32 devices in a mesh: dp: 8 (over y, x, core), tensor: 4 (over z).
Axes of the slice: x: 2, y: 2, z: 4, core: 2. Of those that a mesh axis runs over, the one named last changes fastest.
Arguments:
- tokens: bfloat16 [16384, 1024], P(('dp', 'tensor')), may hold values from -6 to 6
- norm_gains: float32 [2, 1024], replicated, may hold values from 0.5 to 1.5
- attn_qkv: bfloat16 [3, 1024, 1024], P(None, None, 'tensor'), may hold values from -0.09375 to 0.09375
- attn_out: bfloat16 [1024, 1024], P('tensor'), may hold values from -1.5 to 1.5
- ffn_in: bfloat16 [2, 1024, 2816], P(None, None, 'tensor'), may hold values from -0.1875 to 0.1875
- ffn_out: bfloat16 [2816, 1024], P('tensor'), may hold values from -0.109375 to 0.109375
- position_tables: float32 [3, 32, 16], P(None, None, 'tensor'), may hold values from -5 to 5
- page_counts: int32 [16], P('dp'), may hold values from 64 to 1024, as said below
- layout_cells: int32 [2, 16384], P(None, 'dp'), may hold values from 0 to 63
- cotangent: bfloat16 [16384, 1024], P(('dp', 'tensor')), may hold values from -6 to 6
Outputs:
- layer_out: bfloat16 [16384, 1024], P(('dp', 'tensor'))
- tokens_grad: float32 [16384, 1024], P(('dp', 'tensor'))
- gains_grad: float32 [2, 1024], P(None, ('dp', 'tensor'))
- qkv_grad: float32 [3, 1024, 1024], P(None, 'dp', 'tensor')
- out_grad: float32 [1024, 1024], P('tensor', 'dp')
- inner_grad: float32 [2, 1024, 2816], P(None, 'dp', 'tensor')
- outer_grad: float32 [2816, 1024], P('tensor', 'dp')
- tables_grad: float32 [3, 32, 16], P(None, 'dp', 'tensor')
The draws below stay inside these ranges and needn't reach their ends.
Inputs may be any that keep to these rules, and one draw needn't show every extreme that they name: `page_counts`: true token count of each page; a page's tokens at or past it are padding that no query attends to. Some page is full and some page has the least count in every draw.
All inputs are finite; a program needn't handle non-finite values.
Results may differ from the reference program's by a relative error of at most 0.022.
Values may be sent and summed in bfloat16 or wider, within the bound.
A program may use at most 256 MiB of HBM per device.

```python
import math
import jax
import jax.numpy as jnp
import numpy as np
from jax import lax

D = 1024
HEADS = 16
HEAD_DIM = 64
FF = 2816
BUCKETS = 32
REL_REACH = 128
CELLS = 64
PAGE_LEN = 1024
PAGES = 16
TOKENS = 16384
N_TENSOR = 4


def draw_page_counts(key, part):
    count_key, order_key = jax.random.split(key)
    lowest = PAGE_LEN // 16
    counts = jax.random.randint(count_key, (PAGES,), lowest, PAGE_LEN + 1)
    order = jax.random.permutation(order_key, PAGES)
    counts = counts.at[order[0]].set(PAGE_LEN)
    counts = counts.at[order[1]].set(lowest)
    return counts.astype(jnp.int32)


def place_ends(values, stream_key, least, high):
    spot = [jax.random.randint(jax.random.fold_in(stream_key, axis), (), 0, length) for axis, length in enumerate(values.shape)]
    longest = values.shape.index(max(values.shape))
    beside = spot[:longest] + [(spot[longest] + 1) % values.shape[longest]] + spot[longest + 1:]
    return values.at[tuple(spot)].set(least).at[tuple(beside)].set(high)


def spiked(entries, rng, source, target, shards_of, factor):
    owner, partner = [(jnp.arange(entries.shape[dim]) // (entries.shape[dim] // shards_of)).reshape([-1 if axis == dim else 1 for axis in range(entries.ndim)]) for dim in (source, target)]
    chosen = jax.random.permutation(rng, shards_of)[partner]
    strong = (owner == chosen) | (owner == (partner + shards_of // 2) % shards_of)
    return jnp.where(strong, factor * entries, entries)


def block_scale(rng, extent, pieces, least, top_value):
    level = 1.0
    for axis_at, shards_of in pieces:
        heights = jax.random.uniform(jax.random.fold_in(jax.random.fold_in(rng, 6), axis_at), (shards_of,), jnp.float32, least / len(pieces), top_value / len(pieces))
        level = level * jnp.repeat(jnp.exp(heights), extent[axis_at] // shards_of).reshape((-1,) + (1,) * (len(extent) - 1 - axis_at))
    return level


def noise(stream_key, shape, spread, most, pieces=(), held_as=jnp.bfloat16):
    factor_of = block_scale(stream_key, shape, pieces, -0.22, 0.18) if pieces else 1.0
    entries = jax.random.normal(stream_key, shape, jnp.float32) * spread * factor_of
    return jnp.minimum(jnp.maximum(entries, -most), most).astype(held_as)


def bell_draw_with(stream_key, shape, scale, most, shards, heavy, dtype=jnp.bfloat16):
    drawn = scale * jax.random.normal(stream_key, shape, jnp.float32)
    if shards:
        drawn = drawn * block_scale(stream_key, shape, shards, -0.22, 0.18)
    return jnp.clip(spiked(drawn, jax.random.fold_in(stream_key, 3), *heavy), -most, most).astype(dtype)


def setup_inputs(seed: int = 0) -> dict:
    streams_of = jax.random.split(jax.random.key(seed), 11)
    return {
        "tokens": noise(streams_of[0], (TOKENS, D), 1.0, 6.0, ((0, 32),)),
        "norm_gains": jnp.clip(1.0 + 0.1 * jax.random.normal(streams_of[1], (2, D), jnp.float32), 0.5, 1.5),
        "attn_qkv": noise(streams_of[2], (3, D, D), (4 * D) ** -0.5, 0.09375, ((2, 4),)),
        "attn_out": noise(streams_of[3], (D, D), (D // 64) ** -0.5, 1.5, ((0, 4),)),
        "ffn_in": noise(streams_of[4], (2, D, FF), D ** -0.5, 0.1875, ((2, 4),)),
        "ffn_out": noise(streams_of[5], (FF, D), FF ** -0.5, 0.109375, ((0, 4),)),
        "position_tables": noise(streams_of[6], (3, BUCKETS, HEADS), 1.0, 5.0, ((2, 4),), jnp.float32),
        "page_counts": draw_page_counts(jax.random.fold_in(streams_of[10], 71), 0),
        "layout_cells": place_ends(jax.random.randint(streams_of[8], (2, TOKENS), 0, CELLS), jax.random.fold_in(streams_of[8], 1), 0, CELLS - 1).astype(jnp.int32),
        "cotangent": bell_draw_with(streams_of[9], (TOKENS, D), 1.0, 6.0, ((0, 32),), (0, 1, 32, 2.75)),
    }


HIGHEST_PRECISION = lax.Precision.HIGHEST
NORM_EPSILON = 1e-06
MASK_VALUE = -1e+30

@jax.custom_vjp
def low(v):
    return lax.optimization_barrier(v.astype(jnp.bfloat16)).astype(jnp.float32)

@jax.custom_vjp
def low_back(v):
    return v

def low_keep(v):
    return (low(v), None)

def low_pass(kept, grad):
    return (grad,)

def back_keep(v):
    return (v, None)

def back_low(kept, grad):
    return (low(grad),)
low.defvjp(low_keep, low_pass)
low_back.defvjp(back_keep, back_low)

def bucket_table(offsets, bucket_total, max_reach):
    half_total = bucket_total // 2
    exact_limit = half_total // 2
    distance = np.abs(offsets).astype(np.int32)
    upper_side = (offsets > 0).astype(np.int32) * half_total
    safe_dist = np.maximum(distance, 1).astype(np.float32)
    ratio = np.log(safe_dist / np.float32(exact_limit)) / np.float32(math.log(max_reach / exact_limit))
    far_bucket = exact_limit + np.floor(ratio * np.float32(half_total - exact_limit)).astype(np.int32)
    far_bucket = np.minimum(far_bucket, half_total - 1)
    return (upper_side + np.where(distance < exact_limit, distance, far_bucket)).astype(np.int32)

def rms_scale(rows, gain):
    return rows * lax.rsqrt(lax.optimization_barrier(jnp.mean(rows * rows, axis=1, keepdims=True)) + NORM_EPSILON) * gain

def gelu_tanh(values):
    return jax.nn.gelu(values, approximate=True)

def reference(tokens, norm_gains, attn_qkv, attn_out, ffn_in, ffn_out, position_tables, page_counts, layout_cells, cotangent):
    length = PAGE_LEN
    groups = N_TENSOR
    group_cols = D // groups
    group_units = FF // groups
    positions = np.arange(length)
    rel_index = jnp.asarray(bucket_table(positions[None, :] - positions[:, None], BUCKETS, REL_REACH))
    cell_range = np.arange(CELLS)
    layout_index = jnp.asarray(bucket_table(cell_range[None, :] - cell_range[:, None], BUCKETS, CELLS))
    cells_pages = layout_cells.reshape(2, PAGES, length).transpose(1, 0, 2)

    def page_attention(query, key_rows, value_rows, count, page_cells, tables):
        scores = low_back(jnp.einsum('ihd,jhd->hij', query, key_rows, precision=HIGHEST_PRECISION))
        bias = tables[0][rel_index]
        bias = bias + tables[1][layout_index[page_cells[0][:, None], page_cells[0][None, :]]]
        bias = bias + tables[2][layout_index[page_cells[1][:, None], page_cells[1][None, :]]]
        scores = scores + jnp.transpose(bias, (2, 0, 1))
        valid = jnp.arange(length) < count
        scores = jnp.where(valid[None, None, :], scores, MASK_VALUE)
        prob = jax.nn.softmax(scores, axis=-1)
        return jnp.einsum('hij,jhd->ihd', low(prob), value_rows, precision=HIGHEST_PRECISION)
    checked = jax.checkpoint(page_attention)

    def forward(token_rows, gains, qkv_w, out_w, in_w, outer_w, tables):
        normed_one = low(rms_scale(token_rows, gains[0]))
        proj_parts = []
        for group in range(groups):
            shared = low_back(normed_one)
            part = jnp.einsum('td,cdk->ctk', shared, qkv_w[:, :, group * group_cols:(group + 1) * group_cols], precision=HIGHEST_PRECISION)
            proj_parts.append(low(low_back(part)))
        projected = jnp.concatenate(proj_parts, axis=2)
        split = projected.reshape(3, PAGES, length, HEADS, HEAD_DIM)

        def one_page(items):
            return checked(items[0], items[1], items[2], items[3], items[4], tables)
        context = lax.map(one_page, (split[0], split[1], split[2], page_counts, cells_pages))
        context = low(low_back(context.reshape(TOKENS, D)))
        attn_total = jnp.zeros((TOKENS, D), jnp.float32)
        for group in range(groups):
            columns = slice(group * group_cols, (group + 1) * group_cols)
            attn_total = attn_total + low(low_back(jnp.dot(context[:, columns], out_w[columns, :], precision=HIGHEST_PRECISION)))
        resid = token_rows + attn_total
        normed_two = low(rms_scale(resid, gains[1]))
        ffn_total = jnp.zeros((TOKENS, D), jnp.float32)
        for group in range(groups):
            units = slice(group * group_units, (group + 1) * group_units)
            shared = low_back(normed_two)
            gate = low_back(jnp.dot(shared, in_w[0][:, units], precision=HIGHEST_PRECISION))
            upward = low_back(jnp.dot(shared, in_w[1][:, units], precision=HIGHEST_PRECISION))
            hidden = low(gelu_tanh(gate) * upward)
            ffn_total = ffn_total + low(jnp.dot(hidden, outer_w[units, :], precision=HIGHEST_PRECISION))
        return resid + ffn_total
    result, vjp_fn = jax.vjp(forward, tokens.astype(jnp.float32), norm_gains, attn_qkv.astype(jnp.float32), attn_out.astype(jnp.float32), ffn_in.astype(jnp.float32), ffn_out.astype(jnp.float32), position_tables)
    grads = vjp_fn(cotangent.astype(jnp.float32))
    return (result.astype(jnp.bfloat16), grads[0], grads[1], grads[2], grads[3], grads[4], grads[5], grads[6])
```

```python
import math

import jax
import jax.numpy as jnp
import numpy as np
from jax import lax
from jax.experimental import pallas as pl
from jax.experimental.pallas import tpu as pltpu
from jax.sharding import PartitionSpec as P

HEAD_DIM = 64
BUCKETS = 32
REL_REACH = 128
CELLS = 64
PAGE_LEN = 1024


HIGHEST_PRECISION = lax.Precision.HIGHEST
TABLE_PRECISION = lax.Precision.HIGH
NORM_EPSILON = 1e-06
MASK_VALUE = -1e30


def bucket_table(offsets, bucket_total, max_reach):
    half_total = bucket_total // 2
    exact_limit = half_total // 2
    distance = np.abs(offsets).astype(np.int32)
    upper_side = (offsets > 0).astype(np.int32) * half_total
    safe_dist = np.maximum(distance, 1).astype(np.float32)
    ratio = np.log(safe_dist / np.float32(exact_limit)) / np.float32(
        math.log(max_reach / exact_limit)
    )
    far_bucket = exact_limit + np.floor(ratio * np.float32(half_total - exact_limit)).astype(
        np.int32
    )
    far_bucket = np.minimum(far_bucket, half_total - 1)
    return (upper_side + np.where(distance < exact_limit, distance, far_bucket)).astype(np.int32)


def offset_onehot(length):
    offsets = np.arange(2 * length - 1) - (length - 1)
    buckets = bucket_table(offsets, BUCKETS, REL_REACH)
    return jnp.asarray((buckets[:, None] == np.arange(BUCKETS)[None, :]).astype(np.float32))


def layout_onehot():
    cell_range = np.arange(CELLS)
    buckets = bucket_table(cell_range[None, :] - cell_range[:, None], BUCKETS, CELLS)
    return jnp.asarray(
        (buckets.reshape(-1)[:, None] == np.arange(BUCKETS)[None, :]).astype(np.float32)
    )


def gelu_tanh(values):
    return jax.nn.gelu(values, approximate=True)


def relative_bias(table_rows, length):
    values = jnp.dot(offset_onehot(length), table_rows, precision=HIGHEST_PRECISION).T
    heads_dev = values.shape[0]
    padded = jnp.pad(values, ((0, 0), (0, 1)))
    tiled = jnp.tile(padded, (1, length))
    skewed = tiled[:, : length * (2 * length - 1)].reshape(heads_dev, length, 2 * length - 1)
    return skewed[:, :, length - 1 :]


def relative_sums(dscore, length):
    heads_dev = dscore.shape[0]
    placed = jnp.pad(dscore, ((0, 0), (0, 0), (length - 1, 0)))
    flat = jnp.pad(placed.reshape(heads_dev, length * (2 * length - 1)), ((0, 0), (0, length)))
    return jnp.sum(flat.reshape(heads_dev, length, 2 * length), axis=1)[:, : 2 * length - 1]


def layout_values(tables):
    values = jnp.einsum("mn,snh->shm", layout_onehot(), tables[1:], precision=HIGHEST_PRECISION)
    return values.reshape(2, tables.shape[2], CELLS, CELLS)


def cell_onehots(page_cells):
    onehot = (page_cells[:, :, None] == jnp.arange(CELLS)[None, None, :]).astype(jnp.float32)
    length = page_cells.shape[1]
    joined = onehot.transpose(1, 0, 2).reshape(length, 2 * CELLS)
    return (onehot, joined)


def layout_bias(page_cells, lay_vals):
    onehot, joined = cell_onehots(page_cells)
    length = page_cells.shape[1]
    heads_dev = lay_vals.shape[1]
    rows_side = jnp.einsum("sia,shab->hisb", onehot, lay_vals, precision=TABLE_PRECISION)
    rows_side = rows_side.reshape(heads_dev, length, 2 * CELLS)
    return jnp.einsum("hic,jc->hij", rows_side, joined, precision=TABLE_PRECISION)


def layout_sums(dscore, page_cells):
    onehot, joined = cell_onehots(page_cells)
    length = page_cells.shape[1]
    heads_dev = dscore.shape[0]
    partial_rows = jnp.einsum("hij,jc->hic", dscore, joined, precision=TABLE_PRECISION)
    partial_rows = partial_rows.reshape(heads_dev, length, 2, CELLS)
    return jnp.einsum("sia,hisb->shab", onehot, partial_rows, precision=TABLE_PRECISION)


def page_scores(query, key_rows, count, page_cells, rel_bias, lay_vals):
    length = query.shape[0]
    scores = jnp.einsum("ihd,jhd->hij", query, key_rows, preferred_element_type=jnp.float32)
    scores = scores + rel_bias + layout_bias(page_cells, lay_vals)
    valid = jnp.arange(length) < count
    return jnp.where(valid[None, None, :], scores, MASK_VALUE)


def attend(projected, page_counts, layout_cells, rel_bias, lay_vals):
    total_rows = projected.shape[1]
    pages = page_counts.shape[0]
    length = total_rows // pages
    heads_dev = projected.shape[2] // HEAD_DIM
    split = projected.reshape(3, pages, length, heads_dev, HEAD_DIM)
    cells_pages = layout_cells.reshape(2, pages, length).transpose(1, 0, 2)

    def one_page(items):
        query, key_rows, value_rows, count, page_cells = items
        scores = page_scores(query, key_rows, count, page_cells, rel_bias, lay_vals)
        log_total = jax.nn.logsumexp(scores, axis=2)
        prob_low = jnp.exp(scores - log_total[:, :, None]).astype(jnp.bfloat16)
        context = jnp.einsum(
            "hij,jhd->ihd", prob_low, value_rows, preferred_element_type=jnp.float32
        )
        return (context.astype(jnp.bfloat16).reshape(length, heads_dev * HEAD_DIM), log_total)

    context, log_totals = lax.map(
        one_page, (split[0], split[1], split[2], page_counts, cells_pages)
    )
    return (context.reshape(total_rows, heads_dev * HEAD_DIM), log_totals)


def attend_back(projected, grad_context, log_totals, page_counts, layout_cells, rel_bias, lay_vals):
    total_rows = projected.shape[1]
    pages = page_counts.shape[0]
    length = total_rows // pages
    heads_dev = projected.shape[2] // HEAD_DIM
    split = projected.reshape(3, pages, length, heads_dev, HEAD_DIM)
    grad_split = grad_context.reshape(pages, length, heads_dev, HEAD_DIM)
    cells_pages = layout_cells.reshape(2, pages, length).transpose(1, 0, 2)

    def page_step(carry, items):
        rel_acc, lay_acc = carry
        query, key_rows, value_rows, grad_ctx, page_lse, count, page_cells = items
        scores = page_scores(query, key_rows, count, page_cells, rel_bias, lay_vals)
        prob = jnp.exp(scores - page_lse[:, :, None])
        grad_prob = jnp.einsum(
            "ihd,jhd->hij", grad_ctx, value_rows, preferred_element_type=jnp.float32
        )
        delta = jnp.sum(grad_prob * prob, axis=2, keepdims=True)
        dscore = prob * (grad_prob - delta)
        rel_acc = rel_acc + relative_sums(dscore, length)
        lay_acc = lay_acc + layout_sums(dscore, page_cells)
        score_low = dscore.astype(jnp.bfloat16)
        grad_query = jnp.einsum(
            "hij,jhd->ihd", score_low, key_rows, preferred_element_type=jnp.float32
        ).astype(jnp.bfloat16)
        grad_key = jnp.einsum(
            "hij,ihd->jhd", score_low, query, preferred_element_type=jnp.float32
        ).astype(jnp.bfloat16)
        grad_value = jnp.einsum(
            "hij,ihd->jhd", prob.astype(jnp.bfloat16), grad_ctx, preferred_element_type=jnp.float32
        ).astype(jnp.bfloat16)
        stacked = jnp.stack([grad_query, grad_key, grad_value]).reshape(
            3, length, heads_dev * HEAD_DIM
        )
        return ((rel_acc, lay_acc), stacked)

    init_sums = (
        jnp.zeros((heads_dev, 2 * length - 1), jnp.float32),
        jnp.zeros((2, heads_dev, CELLS, CELLS), jnp.float32),
    )
    (rel_acc, lay_acc), grads = lax.scan(
        page_step,
        init_sums,
        (split[0], split[1], split[2], grad_split, log_totals, page_counts, cells_pages),
    )
    grad_proj = grads.transpose(1, 0, 2, 3).reshape(3, total_rows, heads_dev * HEAD_DIM)
    rel_grad = jnp.dot(offset_onehot(length).T, rel_acc.T, precision=HIGHEST_PRECISION)
    lay_grad = jnp.einsum(
        "shm,mn->snh",
        lay_acc.reshape(2, heads_dev, CELLS * CELLS),
        layout_onehot(),
        precision=HIGHEST_PRECISION,
    )
    return (grad_proj, jnp.concatenate([rel_grad[None], lay_grad], axis=0))


def norm_back(rows, scale, gain, grad_normed):
    weighted = grad_normed * gain
    return scale * weighted - rows * scale**3 * jnp.mean(rows * weighted, axis=1, keepdims=True)


def forward_core(
    token_rows,
    norm_gains,
    attn_qkv,
    attn_out,
    ffn_in,
    page_counts,
    layout_cells,
    rel_bias,
    lay_vals,
):
    scale_one = lax.rsqrt(jnp.mean(token_rows * token_rows, axis=1, keepdims=True) + NORM_EPSILON)
    normed_one = (token_rows * scale_one * norm_gains[0]).astype(jnp.bfloat16)
    gathered_one = lax.all_gather(normed_one, "tensor", axis=0, tiled=True)
    projected = jnp.einsum(
        "td,cdk->ctk", gathered_one, attn_qkv, preferred_element_type=jnp.float32
    ).astype(jnp.bfloat16)
    context, log_totals = attend(projected, page_counts, layout_cells, rel_bias, lay_vals)
    attn_total = lax.psum_scatter(
        jnp.dot(context, attn_out, preferred_element_type=jnp.float32)
        .astype(jnp.bfloat16)
        .astype(jnp.float32)
        .astype(jnp.bfloat16),
        "tensor",
        scatter_dimension=0,
        tiled=True,
    ).astype(jnp.float32)
    resid = token_rows + attn_total
    scale_two = lax.rsqrt(jnp.mean(resid * resid, axis=1, keepdims=True) + NORM_EPSILON)
    normed_two = (resid * scale_two * norm_gains[1]).astype(jnp.bfloat16)
    gathered_two = lax.all_gather(normed_two, "tensor", axis=0, tiled=True)
    gate_up = jnp.einsum("td,cdf->ctf", gathered_two, ffn_in, preferred_element_type=jnp.float32)
    hidden = (gelu_tanh(gate_up[0]) * gate_up[1]).astype(jnp.bfloat16)
    return (
        scale_one,
        gathered_one,
        projected,
        context,
        log_totals,
        resid,
        scale_two,
        gathered_two,
        gate_up,
        hidden,
    )


def general_body(
    tokens,
    norm_gains,
    attn_qkv,
    attn_out,
    ffn_in,
    ffn_out,
    position_tables,
    page_counts,
    layout_cells,
    cotangent,
):
    token_rows = tokens.astype(jnp.float32)
    rel_bias = relative_bias(position_tables[0], PAGE_LEN)
    lay_vals = layout_values(position_tables)
    first = forward_core(
        token_rows,
        norm_gains,
        attn_qkv,
        attn_out,
        ffn_in,
        page_counts,
        layout_cells,
        rel_bias,
        lay_vals,
    )
    first_hidden = first[9]
    rows_part = first_hidden
    ffn_total = lax.psum_scatter(
        jnp.dot(rows_part, ffn_out, preferred_element_type=jnp.float32)
        .astype(jnp.bfloat16)
        .astype(jnp.float32)
        .astype(jnp.bfloat16),
        "tensor",
        scatter_dimension=0,
        tiled=True,
    ).astype(jnp.float32)
    layer_out = (first[5] + ffn_total).astype(jnp.bfloat16)
    cot_rows = lax.all_gather(cotangent, "tensor", axis=0, tiled=True)
    again_rows, cot_rows = lax.optimization_barrier((token_rows, cot_rows))
    saved = forward_core(
        again_rows,
        norm_gains,
        attn_qkv,
        attn_out,
        ffn_in,
        page_counts,
        layout_cells,
        rel_bias,
        lay_vals,
    )
    (
        scale_one,
        gathered_one,
        projected,
        context,
        log_totals,
        resid,
        scale_two,
        gathered_two,
        gate_up,
        hidden,
    ) = saved
    grad_hidden = jnp.einsum("td,fd->tf", cot_rows, ffn_out, preferred_element_type=jnp.float32)
    outer_grad = jnp.einsum("tf,td->fd", hidden, cot_rows, preferred_element_type=jnp.float32)
    gelu_value, gelu_back = jax.vjp(gelu_tanh, gate_up[0])
    grad_gate = gelu_back(grad_hidden * gate_up[1])[0].astype(jnp.bfloat16)
    grad_up = (grad_hidden * gelu_value).astype(jnp.bfloat16)
    grad_gate_up = jnp.stack([grad_gate, grad_up])
    inner_grad = jnp.einsum(
        "td,ctf->cdf", gathered_two, grad_gate_up, preferred_element_type=jnp.float32
    )
    rows_part = grad_gate_up
    grad_normed_two = lax.psum_scatter(
        jnp.einsum("ctf,cdf->td", rows_part, ffn_in, preferred_element_type=jnp.float32)
        .astype(jnp.bfloat16)
        .astype(jnp.float32)
        .astype(jnp.bfloat16),
        "tensor",
        scatter_dimension=0,
        tiled=True,
    ).astype(jnp.float32)
    grad_resid = cotangent.astype(jnp.float32) + norm_back(
        resid, scale_two, norm_gains[1], grad_normed_two
    )
    gain_two = jnp.sum(grad_normed_two * resid * scale_two, axis=0)
    resid_rows = lax.all_gather(grad_resid.astype(jnp.bfloat16), "tensor", axis=0, tiled=True)
    out_grad = jnp.einsum("tk,td->kd", context, resid_rows, preferred_element_type=jnp.float32)
    grad_context = jnp.einsum(
        "td,kd->tk", resid_rows, attn_out, preferred_element_type=jnp.float32
    ).astype(jnp.bfloat16)
    grad_proj, tables_grad = attend_back(
        projected, grad_context, log_totals, page_counts, layout_cells, rel_bias, lay_vals
    )
    qkv_grad = jnp.einsum(
        "td,ctk->cdk", gathered_one, grad_proj, preferred_element_type=jnp.float32
    )
    rows_part = grad_proj
    grad_normed_one = lax.psum_scatter(
        jnp.einsum("ctk,cdk->td", rows_part, attn_qkv, preferred_element_type=jnp.float32)
        .astype(jnp.bfloat16)
        .astype(jnp.float32)
        .astype(jnp.bfloat16),
        "tensor",
        scatter_dimension=0,
        tiled=True,
    ).astype(jnp.float32)
    tokens_grad = grad_resid + norm_back(token_rows, scale_one, norm_gains[0], grad_normed_one)
    gain_one = jnp.sum(grad_normed_one * token_rows * scale_one, axis=0)
    gains_grad = lax.psum_scatter(
        jnp.stack([gain_one, gain_two]), ("dp", "tensor"), scatter_dimension=1, tiled=True
    )
    qkv_summed, inner_summed, out_summed, outer_summed, tables_summed = (
        lax.psum_scatter(
            qkv_grad.astype(jnp.bfloat16), "dp", scatter_dimension=1, tiled=True
        ).astype(jnp.float32),
        lax.psum_scatter(
            inner_grad.astype(jnp.bfloat16), "dp", scatter_dimension=1, tiled=True
        ).astype(jnp.float32),
        lax.psum_scatter(
            out_grad.astype(jnp.bfloat16), "dp", scatter_dimension=1, tiled=True
        ).astype(jnp.float32),
        lax.psum_scatter(
            outer_grad.astype(jnp.bfloat16), "dp", scatter_dimension=1, tiled=True
        ).astype(jnp.float32),
        lax.psum_scatter(
            tables_grad.astype(jnp.bfloat16), "dp", scatter_dimension=1, tiled=True
        ).astype(jnp.float32),
    )
    return (
        layer_out,
        tokens_grad,
        gains_grad,
        qkv_summed,
        out_summed,
        inner_summed,
        outer_summed,
        tables_summed,
    )


AXES = ("dp", "tensor")
PLANES = 4
RING = 4
CORES = 2
BLOCK = 256
HALF = 128
ATT = 512
UNITS = 384
FFW = 3 * UNITS
VMEM_BYTES = 60 * 1024 * 1024
F32 = jnp.float32
BF16 = jnp.bfloat16
NT = (((1,), (1,)), ((), ()))
TN = (((0,), (0,)), ((), ()))
NN = (((1,), (0,)), ((), ()))


def page_plan(mesh):
    return mesh.shape["dp"] == PLANES * CORES and mesh.shape["tensor"] == RING


def pairs(target):
    found = []
    for plane in range(PLANES):
        for core in range(CORES):
            for ring in range(RING):
                goal = target(plane, core, ring)
                if goal is not None:
                    source = (plane * CORES + core) * RING + ring
                    found.append((source, (goal[0] * CORES + goal[1]) * RING + goal[2]))
    return found


TO_X = pairs(lambda plane, core, ring: (plane ^ 1, core, ring))
TO_Y = pairs(lambda plane, core, ring: (plane ^ 2, core, ring))
TO_CORE = pairs(lambda plane, core, ring: (plane, 1 - core, ring))
SWAP = pairs(
    lambda plane, core, ring: (plane, 1 - core, ring ^ 1) if core != ring % 2 else None
)
FROM_RING = [
    pairs(lambda plane, core, ring, k=k: (plane, core, (ring - k) % RING)) for k in range(RING)
]
RING_SAME = [
    pairs(lambda plane, core, ring, k=k: (plane, core, (ring + k) % RING)) for k in range(RING)
]
RING_CROSS = [
    pairs(lambda plane, core, ring, k=k: (plane, 1 - core, (ring + k) % RING)) for k in range(RING)
]


def send(values, route):
    return lax.ppermute(values, AXES, route)


def dot(left, right, dims=NN):
    return lax.dot_general(left, right, dims, preferred_element_type=F32)


def call(kernel, name, out_shape, args, flops=0, prefetch=0, scratch=(), grid=None, **specs):
    in_bytes = sum(a.size * a.dtype.itemsize for a in args)
    outs = jax.tree.leaves(out_shape)
    out_bytes = sum(math.prod(o.shape) * o.dtype.itemsize for o in outs)
    whole = pl.BlockSpec(memory_space=pltpu.VMEM)
    scalar = pl.BlockSpec(memory_space=pltpu.SMEM)
    if grid is None:
        extra = dict(
            in_specs=[scalar] * prefetch + [whole] * (len(args) - prefetch),
            out_specs=jax.tree.map(lambda o: whole, out_shape),
            scratch_shapes=list(scratch),
        )
    else:
        extra = dict(grid=grid, scratch_shapes=list(scratch), **specs)
    return pl.pallas_call(
        kernel,
        out_shape=out_shape,
        name=name,
        cost_estimate=pl.CostEstimate(
            flops=int(flops), bytes_accessed=int(in_bytes + out_bytes), transcendentals=0
        ),
        compiler_params=pltpu.CompilerParams(vmem_limit_bytes=VMEM_BYTES),
        **extra,
    )(*args)


def shaped(shape, dtype=BF16):
    return jax.ShapeDtypeStruct(shape, dtype)


def columns(plane, r):
    return pl.ds(pl.multiple_of((plane ^ r) * BLOCK, BLOCK), BLOCK)


def split_pieces(outs, r, lanes, value):
    if r < 3:
        outs[r][:, lanes] = value
    else:
        outs[3][:, lanes] = value[:HALF]
        outs[4][:, lanes] = value[HALF:]


def own_attention_kernel(where, qkv, out, *outs):
    core, plane = where[0], where[1]
    for r in range(PLANES):
        rows = columns(plane, r)
        split_pieces(
            outs,
            r,
            slice(0, HALF),
            out[pl.ds(pl.multiple_of(core * HALF, HALF), HALF), rows].astype(F32).T.astype(BF16),
        )
        for m in range(3):
            lanes = slice((m + 1) * HALF, (m + 2) * HALF)
            split_pieces(
                outs, r, lanes, qkv[m, rows, pl.ds(pl.multiple_of(core * HALF, HALF), HALF)]
            )


def own_ffn_kernel(where, inner, outer, *outs):
    core, plane = where[0], where[1]
    units = inner.shape[2]
    for which, first, count in ((0, 0, UNITS), (1, UNITS, units - UNITS)):

        @pl.when(core == which)
        def _():
            for r in range(PLANES):
                rows = columns(plane, r)
                flipped = outer[first : first + count, rows].astype(F32).T.astype(BF16)
                parts = [flipped, inner[0, rows, first : first + count]]
                parts.append(inner[1, rows, first : first + count])
                for m, part in enumerate(parts):
                    if count < UNITS:
                        part = jnp.concatenate(
                            [part, jnp.zeros((BLOCK, UNITS - count), BF16)], axis=1
                        )
                    split_pieces(outs, r, slice(m * UNITS, (m + 1) * UNITS), part)


def piece_shapes(width):
    return [shaped((BLOCK, width))] * 3 + [shaped((HALF, width))] * 2


def spread_plane(piece):
    from_x = send(piece, TO_X)
    from_y = send(piece, TO_Y)
    corner_a = send(from_x[:HALF], TO_Y)
    corner_b = send(from_y[HALF:], TO_X)
    return [piece, from_x, from_y, corner_a, corner_b]


def join_pieces(target, pieces, lanes=slice(None)):
    for r in range(3):
        target[r * BLOCK : (r + 1) * BLOCK, :] = pieces[r][:, lanes]
    target[3 * BLOCK : 3 * BLOCK + HALF, :] = pieces[3][:, lanes]
    target[3 * BLOCK + HALF :, :] = pieces[4][:, lanes]


def grad_shapes(width):
    return [shaped((2, HALF, width))] * 2 + [shaped((HALF, width))] * 4


def split_grads(outs, lanes, grad):
    to_x, to_y, upper0, upper2, lower0, lower1 = outs
    part = [
        [grad[r * BLOCK : r * BLOCK + HALF], grad[r * BLOCK + HALF : (r + 1) * BLOCK]]
        for r in range(PLANES)
    ]
    part = [[half.astype(BF16) for half in pair] for pair in part]
    to_x[0, :, lanes] = part[1][0]
    to_x[1, :, lanes] = part[3][0]
    to_y[0, :, lanes] = part[2][1]
    to_y[1, :, lanes] = part[3][1]
    upper0[:, lanes] = part[0][0]
    upper2[:, lanes] = part[2][0]
    lower0[:, lanes] = part[0][1]
    lower1[:, lanes] = part[1][1]


def reduce_plane(grads, core):
    to_x, to_y, upper0, upper2, lower0, lower1 = grads
    got_x = send(to_x, TO_X).astype(F32)
    got_y = send(to_y, TO_Y).astype(F32)
    on_y = send((upper2.astype(F32) + got_x[1]).astype(BF16), TO_Y)
    on_x = send((lower1.astype(F32) + got_y[1]).astype(BF16), TO_X)
    upper = upper0.astype(F32) + got_x[0] + on_y.astype(F32)
    lower = lower0.astype(F32) + got_y[0] + on_x.astype(F32)
    mine = jnp.where(core == 0, upper, lower).astype(BF16)
    other = jnp.where(core == 0, lower, upper).astype(BF16)
    return mine, other


def reduce_ring(chunks):
    same, cross = [], []
    for k, (mine, other) in enumerate(chunks):
        same.append(mine if k == 0 else send(mine, RING_SAME[k]))
        cross.append(send(other, RING_CROSS[k]))
    return same + cross


def gather_sum(refs):
    total = refs[0][...].astype(F32)
    for ref in refs[1:]:
        total = total + ref[...].astype(F32)
    return total


def attention_grads_kernel(where, *refs):
    core = where[0]
    ins, (qkv_grad, out_grad) = refs[: 2 * RING], refs[2 * RING :]
    same, cross = gather_sum(ins[:RING]), gather_sum(ins[RING:])
    low = jnp.where(core == 0, same, cross)
    high = jnp.where(core == 0, cross, same)
    for m in range(3):
        lanes = slice((m + 1) * HALF, (m + 2) * HALF)
        qkv_grad[m, :, 0:HALF] = low[:, lanes]
        qkv_grad[m, :, HALF : 2 * HALF] = high[:, lanes]
    out_grad[0:HALF, :] = low[:, 0:HALF].T
    out_grad[HALF : 2 * HALF, :] = high[:, 0:HALF].T


def ffn_grads_kernel(where, *refs):
    core = where[0]
    ins, (inner_grad, outer_grad) = refs[: 2 * RING], refs[2 * RING :]
    rest = inner_grad.shape[2] - UNITS
    same, cross = gather_sum(ins[:RING]), gather_sum(ins[RING:])
    low = jnp.where(core == 0, same, cross)
    high = jnp.where(core == 0, cross, same)
    for m in range(2):
        first = (m + 1) * UNITS
        inner_grad[m, :, 0:UNITS] = low[:, first : first + UNITS]
        inner_grad[m, :, UNITS : UNITS + rest] = high[:, first : first + rest]
    outer_grad[0:UNITS, :] = low[:, 0:UNITS].T
    outer_grad[UNITS : UNITS + rest, :] = high[:, 0:UNITS].T[0:rest]


def place_rows_kernel(where, near, far, full, flipped):
    core, plane = where[0], where[1]
    rows = near.shape[0]
    for source, half in ((near, core), (far, 1 - core)):
        for r in range(PLANES):
            full[pl.ds(pl.multiple_of(half * rows, rows), rows), r * BLOCK : (r + 1) * BLOCK] = (
                source[:, columns(plane, r)]
            )
    for r in range(PLANES):
        lanes = slice(r * BLOCK, (r + 1) * BLOCK)
        flipped[lanes, :] = full[:, lanes].astype(F32).T.astype(BF16)


def first_norm_kernel(where, near, far, gains, full, gains_here, normed, flipped):
    core, plane = where[0], where[1]
    rows = near.shape[0]
    for r in range(PLANES):
        gains_here[:, r * BLOCK : (r + 1) * BLOCK] = gains[:, columns(plane, r)]
    for source, half in ((near, core), (far, 1 - core)):
        for r in range(PLANES):
            full[pl.ds(pl.multiple_of(half * rows, rows), rows), r * BLOCK : (r + 1) * BLOCK] = (
                source[:, columns(plane, r)]
            )
    for i in range(full.shape[0] // BLOCK):
        span = slice(i * BLOCK, (i + 1) * BLOCK)
        x = full[span, :].astype(F32)
        scale = lax.rsqrt(jnp.mean(x * x, axis=1, keepdims=True) + NORM_EPSILON)
        value = x * scale * gains_here[0:1, :]
        normed[span, :] = value.astype(BF16)
        flipped[:, span] = value.T.astype(BF16)


def second_norm_kernel(full, mine, other, gains_here, resid, normed, flipped):
    for i in range(full.shape[0] // BLOCK):
        span = slice(i * BLOCK, (i + 1) * BLOCK)
        row = full[span, :].astype(F32) + (
            mine[span, :].astype(F32) + other[span, :].astype(F32)
        )
        resid[span, :] = row
        scale = lax.rsqrt(jnp.mean(row * row, axis=1, keepdims=True) + NORM_EPSILON)
        value = row * scale * gains_here[1:2, :]
        normed[span, :] = value.astype(BF16)
        flipped[:, span] = value.T.astype(BF16)


def resid_grad_kernel(where, resid, cot, mine, other, gains_here, half_grad, low, flipped, gain):
    core, plane = where[0], where[1]
    rows = half_grad.shape[0]
    total = jnp.zeros((1, resid.shape[1]), F32)
    for i in range(resid.shape[0] // BLOCK):
        span = slice(i * BLOCK, (i + 1) * BLOCK)
        row = resid[span, :]
        grad = mine[span, :].astype(F32) + other[span, :].astype(F32)
        scale = lax.rsqrt(jnp.mean(row * row, axis=1, keepdims=True) + NORM_EPSILON)
        weighted = grad * gains_here[1:2, :]
        center = jnp.mean(row * weighted, axis=1, keepdims=True)
        value = cot[span, :].astype(F32) + scale * weighted - row * (scale * scale * scale * center)
        low[span, :] = value.astype(BF16)
        flipped[:, span] = value.T.astype(BF16)
        in_half = core == (i * BLOCK) // rows
        share = jnp.sum(grad * row * scale, axis=0, keepdims=True)
        total = total + jnp.where(in_half, share, 0.0)

        @pl.when(in_half)
        def _():
            first = (i * BLOCK) % rows
            half_grad[first : first + BLOCK, :] = value

    for r in range(PLANES):
        gain[:, columns(plane, r)] = total[:, r * BLOCK : (r + 1) * BLOCK]


def tokens_grad_kernel(where, full, half_grad, mine, other, gains_here, grad_out, low_out, gain):
    core, plane = where[0], where[1]
    rows = half_grad.shape[0]
    total = jnp.zeros((1, full.shape[1]), F32)
    for i in range(rows // BLOCK):
        span = slice(i * BLOCK, (i + 1) * BLOCK)
        page_span = pl.ds(pl.multiple_of(core * rows + i * BLOCK, BLOCK), BLOCK)
        x = full[page_span, :].astype(F32)
        grad = mine[span, :].astype(F32) + other[span, :].astype(F32)
        scale = lax.rsqrt(jnp.mean(x * x, axis=1, keepdims=True) + NORM_EPSILON)
        weighted = grad * gains_here[0:1, :]
        center = jnp.mean(x * weighted, axis=1, keepdims=True)
        value = half_grad[span, :] + scale * weighted - x * (scale * scale * scale * center)
        total = total + jnp.sum(grad * x * scale, axis=0, keepdims=True)
        for r in range(PLANES):
            block = value[:, r * BLOCK : (r + 1) * BLOCK]
            grad_out[span, columns(plane, r)] = block
            low_out[span, columns(plane, r)] = block.astype(BF16)
    for r in range(PLANES):
        gain[:, columns(plane, r)] = total[:, r * BLOCK : (r + 1) * BLOCK]


def layer_out_kernel(where, resid, mine, other, out):
    core, plane = where[0], where[1]
    rows = out.shape[0]
    page_span = pl.ds(pl.multiple_of(core * rows, rows), rows)
    row = resid[page_span, :] + (mine[...].astype(F32) + other[...].astype(F32))
    for r in range(PLANES):
        out[:, columns(plane, r)] = row[:, r * BLOCK : (r + 1) * BLOCK].astype(BF16)


def pair_lane(rows):
    return lax.broadcasted_iota(jnp.int32, (rows, 2 * HEAD_DIM), 1)


def key_columns(keys, qkv, cells_twice, cell_tail, mine):
    keys[:, :HALF] = jnp.where(
        mine, qkv[:, HALF : 2 * HALF].astype(F32), cells_twice[...].astype(F32)
    ).astype(BF16)
    keys[:, HALF:] = cell_tail[...]


def attention_kernel(
    far, normed, a0, a1, a2, a3, a4, cells, cells_twice, cell_tail, layout, near,
    qkv, prob, context, inverse,
    weights, queries, keys, scores,
):
    h = pl.program_id(0)
    rows = normed.shape[0]
    count = rows // HALF

    @pl.when(h == 0)
    def _():
        join_pieces(weights, (a0, a1, a2, a3, a4), slice(HALF, ATT))
        qkv[...] = dot(normed[...], weights[...]).astype(BF16)

    lane = pair_lane(rows)
    mine = (lane // HEAD_DIM) == h
    side = dot(cells[...], layout[0])
    queries[:, :HALF] = jnp.where(mine, qkv[:, :HALF].astype(F32), side[:, :HALF]).astype(BF16)
    block = lax.broadcasted_iota(jnp.int32, (rows, HALF), 0) // HALF
    other = lane % 8
    is_left, is_right = other < block - 1, other > block + 1
    high = jnp.where(is_left, far[h, 0], jnp.where(is_right, far[h, 2], 0.0))
    low = jnp.where(is_left, far[h, 1], jnp.where(is_right, far[h, 3], 0.0))
    tail = jnp.where(lane < HEAD_DIM, side[:, HALF:], jnp.where(lane == HEAD_DIM + 16, 1.0, 0.0))
    tail = jnp.where((lane >= HEAD_DIM) & (lane < HEAD_DIM + 8), high, tail)
    tail = jnp.where((lane >= HEAD_DIM + 8) & (lane < HEAD_DIM + 16), low, tail)
    queries[:, HALF:] = tail.astype(BF16)
    key_columns(keys, qkv, cells_twice, cell_tail, mine)
    scores[...] = dot(queries[...], keys[...], NT)

    spread = jnp.broadcast_to(near[0], (HALF, 4 * HALF))
    strip = pltpu.roll(spread, 3 * HALF, 1, stride=1, stride_axis=0)[:, : 3 * HALF]
    for i in range(count):
        first, last = max(i - 1, 0), min(i + 2, count)
        part = strip[:, (first - i + 1) * HALF : (last - i + 1) * HALF]
        span = slice(i * HALF, (i + 1) * HALF)
        scores[span, first * HALF : last * HALF] = scores[span, first * HALF : last * HALF] + part
        row = scores[span, :]
        top = jnp.max(row, axis=1, keepdims=True)
        prob[0, span, :] = jnp.exp(row - top).astype(BF16)

    values = jnp.where(mine, qkv[:, 2 * HALF :].astype(F32), 1.0).astype(BF16)
    mixed = dot(prob[0], values)
    inv = 1.0 / pltpu.roll(mixed, HEAD_DIM, 1)
    mixed = (mixed * inv).astype(BF16)

    @pl.when(h == 0)
    def _():
        context[...] = mixed
        inverse[...] = inv

    @pl.when(h == 1)
    def _():
        context[...] = jnp.where(mine, mixed.astype(F32), context[...].astype(F32)).astype(BF16)
        inverse[...] = jnp.where(mine, inv, inverse[...])


def attention(far, normed, pieces, cells, cells_twice, cell_tail, layout, near):
    rows = normed.shape[0]
    full = lambda a: pl.BlockSpec(a.shape, lambda h: (0,) * a.ndim)
    per_head = lambda a: pl.BlockSpec((1,) + a.shape[1:], lambda h: (h,) + (0,) * (a.ndim - 1))
    outs = [
        shaped((rows, 3 * HALF)), shaped((2, rows, rows)), shaped((rows, HALF)),
        shaped((rows, HALF), F32),
    ]
    args = [far, normed, *pieces, cells, cells_twice, cell_tail, layout, near]
    in_specs = [pl.BlockSpec(memory_space=pltpu.SMEM)] + [full(a) for a in args[1:-2]]
    in_specs += [per_head(layout), per_head(near)]
    out_specs = [full(outs[0]), per_head(outs[1]), full(outs[2]), full(outs[3])]
    return call(
        attention_kernel, "attention", outs, args,
        flops=2 * rows * 1024 * 384 + 4 * rows * rows * 384 * 4,
        grid=(2,), in_specs=in_specs, out_specs=out_specs,
        scratch=[
            pltpu.VMEM((PLANES * BLOCK, 3 * HALF), BF16),
            pltpu.VMEM((rows, 2 * HALF), BF16),
            pltpu.VMEM((rows, 2 * HALF), BF16),
            pltpu.VMEM((rows, rows), F32),
        ],
    )


def attention_back_kernel(
    low, low_flipped, normed_flipped, a0, a1, a2, a3, a4, qkv, prob, context, inverse,
    cells_twice, cell_tail, cells_flipped,
    grad_qkv, to_x, to_y, upper0, upper2, lower0, lower1, strip_out, far_out, layout_out,
    weights, scaled, scaled_low, keys, dscores,
):
    h = pl.program_id(0)
    rows = low.shape[0]
    count = rows // HALF
    lane = pair_lane(rows)
    mine = (lane // HEAD_DIM) == h

    @pl.when(h == 0)
    def _():
        join_pieces(weights, (a0, a1, a2, a3, a4), slice(0, HALF))
        grad_context = dot(low[...], weights[...]).astype(BF16).astype(F32)
        value = grad_context * inverse[...]
        scaled[...] = value
        scaled_low[...] = value.astype(BF16)

    value = scaled[...]
    delta = -jnp.sum(jnp.where(mine, value * context[...].astype(F32), 0.0), axis=1, keepdims=True)
    delta_high = delta.astype(BF16).astype(F32)
    spare = HEAD_DIM * (1 - h)
    left = jnp.where(
        mine,
        value,
        jnp.where(lane == spare, delta_high, jnp.where(lane == spare + 1, delta - delta_high, 0.0)),
    ).astype(BF16)
    ones = jnp.where((lane == spare) | (lane == spare + 1), 1.0, 0.0)
    right = jnp.where(mine, qkv[:, 2 * HALF :].astype(F32), ones).astype(BF16)
    strip = jnp.zeros((HALF, 3 * HALF), F32)
    strips = [jnp.zeros((HALF, HALF), F32) for _ in range(3)]
    for i in range(rows // BLOCK):
        span = slice(i * BLOCK, (i + 1) * BLOCK)
        dscore = prob[0, span, :].astype(F32) * dot(left[span, :], right, NT)
        dscores[span, :] = dscore.astype(BF16)
        for part in range(BLOCK // HALF):
            at = i * (BLOCK // HALF) + part
            for step in range(3):
                block = at + step - 1
                if 0 <= block < count:
                    strips[step] = (
                        strips[step]
                        + dscore[
                            part * HALF : (part + 1) * HALF, block * HALF : (block + 1) * HALF
                        ]
                    )
    for step in range(3):
        strip_out[0, :, step * HALF : (step + 1) * HALF] = strips[step]

    key_columns(keys, qkv, cells_twice, cell_tail, mine)
    grad_left = dot(dscores[...], keys[...])
    grad_key = dot(dscores[...], qkv[:, :HALF], TN)
    grad_value = dot(prob[0], scaled_low[...], TN)
    new = [grad_left[:, :HALF], grad_key, grad_value]

    @pl.when(h == 0)
    def _():
        for m in range(3):
            grad_qkv[:, m * HALF : (m + 1) * HALF] = new[m].astype(BF16)

    @pl.when(h == 1)
    def _():
        for m in range(3):
            lanes = slice(m * HALF, (m + 1) * HALF)
            grad_qkv[:, lanes] = jnp.where(mine, new[m], grad_qkv[:, lanes].astype(F32)).astype(BF16)

    for m in range(2):
        lanes = slice(m * HALF, (m + 1) * HALF)
        table = grad_left[:, lanes]
        if m == 0:
            table = jnp.where(mine, pltpu.roll(table, HEAD_DIM, 1), table)
        table_high = table.astype(BF16)
        rest = (table - table_high.astype(F32)).astype(BF16)
        layout_out[0, :, lanes] = dot(cells_flipped[...], table_high) + dot(
            cells_flipped[...], rest
        )
    block = lax.broadcasted_iota(jnp.int32, (rows, HALF), 0) // HALF
    tail = grad_left[:, HALF:]
    far_left = jnp.sum(jnp.where(lane % 8 < block - 1, tail, 0.0), axis=0, keepdims=True)
    far_right = jnp.sum(jnp.where(lane % 8 > block + 1, tail, 0.0), axis=0, keepdims=True)
    far_out[0, 0:1, :] = far_left
    far_out[0, 1:2, :] = far_right

    @pl.when(h == 1)
    def _():
        outs = (to_x, to_y, upper0, upper2, lower0, lower1)
        split_grads(outs, slice(0, HALF), dot(low_flipped[...], context[...]))
        split_grads(outs, slice(HALF, ATT), dot(normed_flipped[...], grad_qkv[...]))


def attention_back(low, low_flipped, normed_flipped, pieces, saved, cells_twice, cell_tail, cells_flipped):
    qkv, prob, context, inverse = saved
    rows = low.shape[0]
    full = lambda a: pl.BlockSpec(a.shape, lambda h: (0,) * a.ndim)
    per_head = lambda a: pl.BlockSpec((1,) + a.shape[1:], lambda h: (h,) + (0,) * (a.ndim - 1))
    args = [low, low_flipped, normed_flipped, *pieces, qkv, prob, context, inverse]
    args += [cells_twice, cell_tail, cells_flipped]
    in_specs = [per_head(a) if a is prob else full(a) for a in args]
    outs = [shaped((rows, 3 * HALF))] + grad_shapes(ATT)
    tables = [shaped((2, HALF, 3 * HALF), F32), shaped((2, 2, HALF), F32), shaped((2, HALF, 2 * HALF), F32)]
    out_specs = [full(o) for o in outs] + [per_head(o) for o in tables]
    return call(
        attention_back_kernel, "attention_back", outs + tables, args,
        flops=4 * rows * 1024 * 512 + 4 * rows * rows * 1024 * 2,
        grid=(2,), in_specs=in_specs, out_specs=out_specs,
        scratch=[
            pltpu.VMEM((PLANES * BLOCK, HALF), BF16),
            pltpu.VMEM((rows, HALF), F32),
            pltpu.VMEM((rows, HALF), BF16),
            pltpu.VMEM((rows, 2 * HALF), BF16),
            pltpu.VMEM((rows, rows), BF16),
        ],
    )


def sum_products_kernel(width, lanes, row_spans, *refs):
    lefts = refs[:RING]
    pieces = [refs[RING + 5 * k : RING + 5 * k + 5] for k in range(RING)]
    out, left, right = refs[6 * RING :]
    for k in range(RING):
        at = slice(k * width, (k + 1) * width)
        left[:, at] = lefts[k][:, lanes[0]]
        for r in range(3):
            right[r * BLOCK : (r + 1) * BLOCK, at] = pieces[k][r][:, lanes[1]]
        right[3 * BLOCK : 3 * BLOCK + HALF, at] = pieces[k][3][:, lanes[1]]
        right[3 * BLOCK + HALF :, at] = pieces[k][4][:, lanes[1]]
    for i in range(left.shape[0] // BLOCK):
        span = slice(i * BLOCK, (i + 1) * BLOCK)
        out[span, :] = dot(left[span, :], right[...], NT).astype(BF16)


def sum_products(name, lefts, left_lanes, pieces, right_lanes):
    rows = lefts[0].shape[0]
    width = right_lanes.stop - right_lanes.start

    def kernel(*refs):
        sum_products_kernel(width, (left_lanes, right_lanes), None, *refs)

    args = list(lefts) + [piece for quarter in pieces for piece in quarter]
    return call(
        kernel, name, shaped((rows, PLANES * BLOCK)), args,
        flops=2 * rows * PLANES * BLOCK * width * RING,
        scratch=[
            pltpu.VMEM((rows, RING * width), BF16),
            pltpu.VMEM((PLANES * BLOCK, RING * width), BF16),
        ],
    )


def ffn_kernel(
    normed, normed_flipped, cot, cot_flipped, f0, f1, f2, f3, f4,
    hidden, to_x, to_y, upper0, upper2, lower0, lower1,
    weights,
):
    join_pieces(weights, (f0, f1, f2, f3, f4))
    for i in range(normed.shape[0] // BLOCK):
        span = slice(i * BLOCK, (i + 1) * BLOCK)
        both = dot(normed[span, :], weights[:, UNITS:])
        grad_hidden = dot(cot[span, :], weights[:, :UNITS])
        gate, up = both[:, :UNITS], both[:, UNITS:]
        square = gate * gate
        ratio = math.sqrt(2.0 / math.pi)
        bend = jnp.tanh(ratio * gate * (1.0 + 0.044715 * square))
        half_gate = 0.5 * gate
        value = half_gate + half_gate * bend
        slope = 0.5 + 0.5 * bend + half_gate * (1.0 - bend * bend) * (
            ratio * (1.0 + 3.0 * 0.044715 * square)
        )
        hidden[span, :UNITS] = (value * up).astype(BF16)
        hidden[span, UNITS : 2 * UNITS] = (grad_hidden * up * slope).astype(BF16)
        hidden[span, 2 * UNITS :] = (grad_hidden * value).astype(BF16)
    outs = (to_x, to_y, upper0, upper2, lower0, lower1)
    split_grads(outs, slice(0, UNITS), dot(cot_flipped[...], hidden[:, :UNITS]))
    split_grads(outs, slice(UNITS, FFW), dot(normed_flipped[...], hidden[:, UNITS:]))


def ffn(normed, normed_flipped, cot, cot_flipped, pieces):
    rows = normed.shape[0]
    outs = [shaped((rows, FFW))] + grad_shapes(FFW)
    return call(
        ffn_kernel, "ffn", outs, [normed, normed_flipped, cot, cot_flipped, *pieces],
        flops=4 * rows * PLANES * BLOCK * FFW,
        scratch=[pltpu.VMEM((PLANES * BLOCK, FFW), BF16)],
    )


def near_onehot():
    offsets = np.arange(4 * HALF) - 2 * HALF
    buckets = bucket_table(offsets, BUCKETS, REL_REACH)
    return (buckets[:, None] == np.arange(BUCKETS)[None, :]).astype(np.float32)


def strip_onehot():
    offsets = np.arange(3 * HALF)[None, :] - HALF - np.arange(HALF)[:, None]
    return bucket_table(offsets, BUCKETS, REL_REACH)


def bias_inputs(tables):
    heads = tables.shape[2]
    near = jnp.einsum("ub,bh->hu", near_onehot(), tables[0], precision=HIGHEST_PRECISION)
    ends = jnp.stack([tables[0, BUCKETS // 2 - 1], tables[0, BUCKETS - 1]], axis=1)
    ends_high = ends.astype(BF16).astype(F32)
    far = jnp.stack([ends_high, ends - ends_high], axis=2).reshape(heads, 4)
    cells = layout_values(tables).astype(BF16)
    gap = jnp.zeros((heads, CELLS, CELLS), BF16)
    top = jnp.concatenate([cells[0], cells[0], gap, gap], axis=2)
    bottom = jnp.concatenate([gap, gap, cells[1], gap], axis=2)
    return near[:, None, :], far, jnp.concatenate([top, bottom], axis=1)


def table_sums(strips, fars, layouts):
    strips, fars, layouts = (jnp.concatenate(a, axis=0) for a in (strips, fars, layouts))
    heads = strips.shape[0]
    strip_bucket = jnp.asarray(strip_onehot())
    near = jnp.stack(
        [
            jnp.sum(jnp.where(strip_bucket == b, strips, 0.0), axis=(1, 2))
            for b in range(BUCKETS)
        ]
    )
    ends = jnp.sum(fars[:, :, HEAD_DIM : HEAD_DIM + 8], axis=2)
    left = (np.arange(BUCKETS) == BUCKETS // 2 - 1).astype(np.float32)[:, None]
    right = (np.arange(BUCKETS) == BUCKETS - 1).astype(np.float32)[:, None]
    rel = near + left * ends[None, :, 0] + right * ends[None, :, 1]
    cells_x = layouts[:, :CELLS, :CELLS]
    cells_y = layouts[:, CELLS:, 2 * CELLS : 3 * CELLS]
    both = jnp.stack([cells_x, cells_y]).reshape(2, heads, CELLS * CELLS)
    lay = jnp.einsum("shm,mn->snh", both, layout_onehot(), precision=HIGHEST_PRECISION)
    return jnp.concatenate([rel[None], lay], axis=0)


def page_body(
    tokens,
    norm_gains,
    attn_qkv,
    attn_out,
    ffn_in,
    ffn_out,
    position_tables,
    page_counts,
    layout_cells,
    cotangent,
):
    group, ring = lax.axis_index("dp"), lax.axis_index("tensor")
    core, plane = group % CORES, group // CORES
    where = jnp.stack([core, plane]).astype(jnp.int32)
    native = core == ring % 2
    rows = tokens.shape[0]
    length = 2 * rows

    near_x = jnp.where(native, tokens, send(tokens, SWAP))
    far_x = send(near_x, TO_CORE)
    att_own = call(own_attention_kernel, "own_attention", piece_shapes(ATT), [where, attn_qkv, attn_out], prefetch=1)
    ffn_own = call(own_ffn_kernel, "own_ffn", piece_shapes(FFW), [where, ffn_in, ffn_out], prefetch=1)
    att_pieces = [att_own] + [spread_plane(send(att_own[0], FROM_RING[k])) for k in range(1, RING)]
    near_g = jnp.where(native, cotangent, send(cotangent, SWAP))
    far_g = send(near_g, TO_CORE)
    ffn_pieces = [ffn_own] + [spread_plane(send(ffn_own[0], FROM_RING[k])) for k in range(1, RING)]

    table_parts = [position_tables] + [send(position_tables, FROM_RING[k]) for k in range(1, RING)]
    tables = jnp.concatenate(
        [lax.dynamic_slice_in_dim(part, 2 * core, 2, axis=2) for part in table_parts], axis=2
    )
    near, far, layout = bias_inputs(tables)
    other_counts = send(page_counts, TO_CORE)
    other_cells = send(layout_cells, TO_CORE)
    counts = jnp.where(native, page_counts, other_counts)
    cell_rows = jnp.where(native, layout_cells, other_cells).reshape(2, 2, length)
    valid_count = lax.dynamic_index_in_dim(counts, ring // 2, 0, keepdims=False)
    cell_rows = lax.dynamic_index_in_dim(cell_rows, ring // 2, 1, keepdims=False)
    onehot = (cell_rows[:, :, None] == jnp.arange(CELLS)[None, None, :]).astype(BF16)
    cells = jnp.concatenate([onehot[0], onehot[1]], axis=1)
    cells_twice = jnp.concatenate([onehot[0], onehot[0]], axis=1)
    position = jnp.arange(length)
    spot = jnp.arange(HEAD_DIM)[None, :]
    block_tail = ((spot < 16) & (spot % 8 == position[:, None] // HALF)).astype(F32)
    hide = jnp.where(position >= valid_count, MASK_VALUE, 0.0)[:, None]
    block_tail = jnp.where(spot == 16, hide, block_tail).astype(BF16)
    cell_tail = jnp.concatenate([onehot[1], block_tail], axis=1)
    cells_flipped = cells.T

    full, gains_here, normed_one, normed_one_t = call(
        first_norm_kernel, "first_norm",
        [shaped((length, 1024)), shaped((2, 1024), F32), shaped((length, 1024)), shaped((1024, length))],
        [where, near_x, far_x, norm_gains], prefetch=1,
    )
    saved = []
    for k in range(RING):
        span = slice(2 * k, 2 * k + 2)
        saved.append(
            attention(far[span], normed_one, att_pieces[k], cells, cells_twice, cell_tail, layout[span], near[span])
        )
    attn_mine = sum_products(
        "attn_out", [s[2] for s in saved], slice(0, HALF), att_pieces, slice(0, HALF)
    )
    attn_other = send(attn_mine, TO_CORE)
    resid, normed_two, normed_two_t = call(
        second_norm_kernel, "second_norm",
        [shaped((length, 1024), F32), shaped((length, 1024)), shaped((1024, length))],
        [full, attn_mine, attn_other, gains_here],
    )

    cot, cot_t = call(
        place_rows_kernel, "place_rows", [shaped((length, 1024)), shaped((1024, length))],
        [where, near_g, far_g], prefetch=1,
    )
    hiddens, ffn_chunks = [], []
    for k in range(RING):
        hidden, *grads = ffn(normed_two, normed_two_t, cot, cot_t, ffn_pieces[k])
        hiddens.append(hidden)
        ffn_chunks.append(reduce_plane(grads, core))
    grad_mine = sum_products(
        "grad_normed_two", hiddens, slice(UNITS, FFW), ffn_pieces, slice(UNITS, FFW)
    )
    grad_other = send(grad_mine, TO_CORE)
    half_grad, low, low_t, gain_two = call(
        resid_grad_kernel, "resid_grad",
        [shaped((rows, 1024), F32), shaped((length, 1024)), shaped((1024, length)), shaped((1, 1024), F32)],
        [where, resid, cot, grad_mine, grad_other, gains_here], prefetch=1,
    )

    att_chunks, grad_qkvs, strips, fars, layouts = [], [], [], [], []
    for k in range(RING):
        back = attention_back(low, low_t, normed_one_t, att_pieces[k], saved[k], cells_twice, cell_tail, cells_flipped)
        grad_qkvs.append(back[0])
        att_chunks.append(reduce_plane(back[1:7], core))
        strips.append(back[7])
        fars.append(back[8])
        layouts.append(back[9])
    one_mine = sum_products("grad_normed_one", grad_qkvs, slice(0, 3 * HALF), att_pieces, slice(HALF, ATT))
    here = lax.dynamic_slice_in_dim(one_mine, core * rows, rows, axis=0)
    there = lax.dynamic_slice_in_dim(one_mine, (1 - core) * rows, rows, axis=0)
    one_other = send(there, TO_CORE)
    page_grad, page_grad_low, gain_one = call(
        tokens_grad_kernel, "tokens_grad",
        [shaped((rows, 1024), F32), shaped((rows, 1024)), shaped((1, 1024), F32)],
        [where, full, half_grad, here, one_other, gains_here], prefetch=1,
    )
    tokens_grad = jnp.where(native, page_grad, send(page_grad_low, SWAP).astype(F32))

    out_mine = sum_products("ffn_out", hiddens, slice(0, UNITS), ffn_pieces, slice(0, UNITS))
    out_here = lax.dynamic_slice_in_dim(out_mine, core * rows, rows, axis=0)
    out_there = lax.dynamic_slice_in_dim(out_mine, (1 - core) * rows, rows, axis=0)
    out_other = send(out_there, TO_CORE)
    page_out = call(
        layer_out_kernel, "layer_out", shaped((rows, 1024)),
        [where, resid, out_here, out_other], prefetch=1,
    )
    layer_out = jnp.where(native, page_out, send(page_out, SWAP))

    units = ffn_in.shape[2]
    inner_grad, outer_grad = call(
        ffn_grads_kernel, "ffn_grads",
        [shaped((2, HALF, units), F32), shaped((units, HALF), F32)],
        [where] + reduce_ring(ffn_chunks), prefetch=1,
    )
    qkv_grad, out_grad = call(
        attention_grads_kernel, "attention_grads",
        [shaped((3, HALF, 2 * HALF), F32), shaped((2 * HALF, HALF), F32)],
        [where] + reduce_ring(att_chunks), prefetch=1,
    )

    sums = table_sums(strips, fars, layouts)
    by_ring = sums.reshape(3, BUCKETS, RING, 2)
    by_ring = jnp.stack(
        [
            jnp.stack([by_ring[:, :, (q - z) % RING] for q in range(RING)], axis=2)
            for z in range(RING)
        ]
    )
    by_ring = lax.dynamic_index_in_dim(by_ring, ring, 0, keepdims=False)
    slots = jnp.where(jnp.arange(CORES)[None, None, None, :, None] == core, by_ring[:, :, :, None, :], 0.0)
    packed = jnp.concatenate(
        [gain_one.reshape(-1), gain_two.reshape(-1), slots.reshape(-1), jnp.zeros((512,), F32)]
    ).reshape(32, HALF)
    packed = packed + send(packed, TO_CORE)
    packed = packed + send(packed, TO_X)
    packed = packed + send(packed, TO_Y)
    packed = packed + (
        send(packed, FROM_RING[1]) + (send(packed, FROM_RING[2]) + send(packed, FROM_RING[3]))
    )
    flat = packed.reshape(-1)
    gains_grad = lax.dynamic_slice_in_dim(
        flat[:2048].reshape(2, 1024), (group * RING + ring) * 32, 32, axis=1
    )
    all_tables = flat[2048 : 2048 + 3 * BUCKETS * 16].reshape(3, BUCKETS, 16)
    tables_grad = lax.dynamic_slice(all_tables, (0, group * 4, ring * 4), (3, 4, 4))
    return (
        layer_out,
        tokens_grad,
        gains_grad,
        qkv_grad,
        out_grad,
        inner_grad,
        outer_grad,
        tables_grad,
    )


def solution(mesh):
    return jax.shard_map(
        page_body if page_plan(mesh) else general_body,
        mesh=mesh,
        in_specs=(
            P(("dp", "tensor"), None),
            P(),
            P(None, None, "tensor"),
            P("tensor", None),
            P(None, None, "tensor"),
            P("tensor", None),
            P(None, None, "tensor"),
            P("dp"),
            P(None, "dp"),
            P(("dp", "tensor"), None),
        ),
        out_specs=(
            P(("dp", "tensor"), None),
            P(("dp", "tensor"), None),
            P(None, ("dp", "tensor")),
            P(None, "dp", "tensor"),
            P("tensor", "dp"),
            P(None, "dp", "tensor"),
            P("tensor", "dp"),
            P(None, "dp", "tensor"),
        ),
        check_vma=False,
    )
```

```python
import math

import jax
import jax.numpy as jnp
import numpy as np
from jax import lax
from jax.experimental import pallas as pl
from jax.experimental.pallas import tpu as pltpu
from jax.sharding import PartitionSpec as P

HEAD_DIM = 64
BUCKETS = 32
REL_REACH = 128
CELLS = 64
PAGE_LEN = 1024


HIGHEST_PRECISION = lax.Precision.HIGHEST
TABLE_PRECISION = lax.Precision.HIGH
NORM_EPSILON = 1e-06
MASK_VALUE = -1e30


def bucket_table(offsets, bucket_total, max_reach):
    half_total = bucket_total // 2
    exact_limit = half_total // 2
    distance = np.abs(offsets).astype(np.int32)
    upper_side = (offsets > 0).astype(np.int32) * half_total
    safe_dist = np.maximum(distance, 1).astype(np.float32)
    ratio = np.log(safe_dist / np.float32(exact_limit)) / np.float32(
        math.log(max_reach / exact_limit)
    )
    far_bucket = exact_limit + np.floor(ratio * np.float32(half_total - exact_limit)).astype(
        np.int32
    )
    far_bucket = np.minimum(far_bucket, half_total - 1)
    return (upper_side + np.where(distance < exact_limit, distance, far_bucket)).astype(np.int32)


def offset_onehot(length):
    offsets = np.arange(2 * length - 1) - (length - 1)
    buckets = bucket_table(offsets, BUCKETS, REL_REACH)
    return jnp.asarray((buckets[:, None] == np.arange(BUCKETS)[None, :]).astype(np.float32))


def layout_onehot():
    cell_range = np.arange(CELLS)
    buckets = bucket_table(cell_range[None, :] - cell_range[:, None], BUCKETS, CELLS)
    return jnp.asarray(
        (buckets.reshape(-1)[:, None] == np.arange(BUCKETS)[None, :]).astype(np.float32)
    )


def gelu_tanh(values):
    return jax.nn.gelu(values, approximate=True)


def relative_bias(table_rows, length):
    values = jnp.dot(offset_onehot(length), table_rows, precision=HIGHEST_PRECISION).T
    heads_dev = values.shape[0]
    padded = jnp.pad(values, ((0, 0), (0, 1)))
    tiled = jnp.tile(padded, (1, length))
    skewed = tiled[:, : length * (2 * length - 1)].reshape(heads_dev, length, 2 * length - 1)
    return skewed[:, :, length - 1 :]


def relative_sums(dscore, length):
    heads_dev = dscore.shape[0]
    placed = jnp.pad(dscore, ((0, 0), (0, 0), (length - 1, 0)))
    flat = jnp.pad(placed.reshape(heads_dev, length * (2 * length - 1)), ((0, 0), (0, length)))
    return jnp.sum(flat.reshape(heads_dev, length, 2 * length), axis=1)[:, : 2 * length - 1]


def layout_values(tables):
    values = jnp.einsum("mn,snh->shm", layout_onehot(), tables[1:], precision=HIGHEST_PRECISION)
    return values.reshape(2, tables.shape[2], CELLS, CELLS)


def cell_onehots(page_cells):
    onehot = (page_cells[:, :, None] == jnp.arange(CELLS)[None, None, :]).astype(jnp.float32)
    length = page_cells.shape[1]
    joined = onehot.transpose(1, 0, 2).reshape(length, 2 * CELLS)
    return (onehot, joined)


def layout_bias(page_cells, lay_vals):
    onehot, joined = cell_onehots(page_cells)
    length = page_cells.shape[1]
    heads_dev = lay_vals.shape[1]
    rows_side = jnp.einsum("sia,shab->hisb", onehot, lay_vals, precision=TABLE_PRECISION)
    rows_side = rows_side.reshape(heads_dev, length, 2 * CELLS)
    return jnp.einsum("hic,jc->hij", rows_side, joined, precision=TABLE_PRECISION)


def layout_sums(dscore, page_cells):
    onehot, joined = cell_onehots(page_cells)
    length = page_cells.shape[1]
    heads_dev = dscore.shape[0]
    partial_rows = jnp.einsum("hij,jc->hic", dscore, joined, precision=TABLE_PRECISION)
    partial_rows = partial_rows.reshape(heads_dev, length, 2, CELLS)
    return jnp.einsum("sia,hisb->shab", onehot, partial_rows, precision=TABLE_PRECISION)


def page_scores(query, key_rows, count, page_cells, rel_bias, lay_vals):
    length = query.shape[0]
    scores = jnp.einsum("ihd,jhd->hij", query, key_rows, preferred_element_type=jnp.float32)
    scores = scores + rel_bias + layout_bias(page_cells, lay_vals)
    valid = jnp.arange(length) < count
    return jnp.where(valid[None, None, :], scores, MASK_VALUE)


def attend(projected, page_counts, layout_cells, rel_bias, lay_vals):
    total_rows = projected.shape[1]
    pages = page_counts.shape[0]
    length = total_rows // pages
    heads_dev = projected.shape[2] // HEAD_DIM
    split = projected.reshape(3, pages, length, heads_dev, HEAD_DIM)
    cells_pages = layout_cells.reshape(2, pages, length).transpose(1, 0, 2)

    def one_page(items):
        query, key_rows, value_rows, count, page_cells = items
        scores = page_scores(query, key_rows, count, page_cells, rel_bias, lay_vals)
        log_total = jax.nn.logsumexp(scores, axis=2)
        prob_low = jnp.exp(scores - log_total[:, :, None]).astype(jnp.bfloat16)
        context = jnp.einsum(
            "hij,jhd->ihd", prob_low, value_rows, preferred_element_type=jnp.float32
        )
        return (context.astype(jnp.bfloat16).reshape(length, heads_dev * HEAD_DIM), log_total)

    context, log_totals = lax.map(
        one_page, (split[0], split[1], split[2], page_counts, cells_pages)
    )
    return (context.reshape(total_rows, heads_dev * HEAD_DIM), log_totals)


def attend_back(projected, grad_context, log_totals, page_counts, layout_cells, rel_bias, lay_vals):
    total_rows = projected.shape[1]
    pages = page_counts.shape[0]
    length = total_rows // pages
    heads_dev = projected.shape[2] // HEAD_DIM
    split = projected.reshape(3, pages, length, heads_dev, HEAD_DIM)
    grad_split = grad_context.reshape(pages, length, heads_dev, HEAD_DIM)
    cells_pages = layout_cells.reshape(2, pages, length).transpose(1, 0, 2)

    def page_step(carry, items):
        rel_acc, lay_acc = carry
        query, key_rows, value_rows, grad_ctx, page_lse, count, page_cells = items
        scores = page_scores(query, key_rows, count, page_cells, rel_bias, lay_vals)
        prob = jnp.exp(scores - page_lse[:, :, None])
        grad_prob = jnp.einsum(
            "ihd,jhd->hij", grad_ctx, value_rows, preferred_element_type=jnp.float32
        )
        delta = jnp.sum(grad_prob * prob, axis=2, keepdims=True)
        dscore = prob * (grad_prob - delta)
        rel_acc = rel_acc + relative_sums(dscore, length)
        lay_acc = lay_acc + layout_sums(dscore, page_cells)
        score_low = dscore.astype(jnp.bfloat16)
        grad_query = jnp.einsum(
            "hij,jhd->ihd", score_low, key_rows, preferred_element_type=jnp.float32
        ).astype(jnp.bfloat16)
        grad_key = jnp.einsum(
            "hij,ihd->jhd", score_low, query, preferred_element_type=jnp.float32
        ).astype(jnp.bfloat16)
        grad_value = jnp.einsum(
            "hij,ihd->jhd", prob.astype(jnp.bfloat16), grad_ctx, preferred_element_type=jnp.float32
        ).astype(jnp.bfloat16)
        stacked = jnp.stack([grad_query, grad_key, grad_value]).reshape(
            3, length, heads_dev * HEAD_DIM
        )
        return ((rel_acc, lay_acc), stacked)

    init_sums = (
        jnp.zeros((heads_dev, 2 * length - 1), jnp.float32),
        jnp.zeros((2, heads_dev, CELLS, CELLS), jnp.float32),
    )
    (rel_acc, lay_acc), grads = lax.scan(
        page_step,
        init_sums,
        (split[0], split[1], split[2], grad_split, log_totals, page_counts, cells_pages),
    )
    grad_proj = grads.transpose(1, 0, 2, 3).reshape(3, total_rows, heads_dev * HEAD_DIM)
    rel_grad = jnp.dot(offset_onehot(length).T, rel_acc.T, precision=HIGHEST_PRECISION)
    lay_grad = jnp.einsum(
        "shm,mn->snh",
        lay_acc.reshape(2, heads_dev, CELLS * CELLS),
        layout_onehot(),
        precision=HIGHEST_PRECISION,
    )
    return (grad_proj, jnp.concatenate([rel_grad[None], lay_grad], axis=0))


def norm_back(rows, scale, gain, grad_normed):
    weighted = grad_normed * gain
    return scale * weighted - rows * scale**3 * jnp.mean(rows * weighted, axis=1, keepdims=True)


def forward_core(
    token_rows,
    norm_gains,
    attn_qkv,
    attn_out,
    ffn_in,
    page_counts,
    layout_cells,
    rel_bias,
    lay_vals,
):
    scale_one = lax.rsqrt(jnp.mean(token_rows * token_rows, axis=1, keepdims=True) + NORM_EPSILON)
    normed_one = (token_rows * scale_one * norm_gains[0]).astype(jnp.bfloat16)
    gathered_one = lax.all_gather(normed_one, "tensor", axis=0, tiled=True)
    projected = jnp.einsum(
        "td,cdk->ctk", gathered_one, attn_qkv, preferred_element_type=jnp.float32
    ).astype(jnp.bfloat16)
    context, log_totals = attend(projected, page_counts, layout_cells, rel_bias, lay_vals)
    attn_total = lax.psum_scatter(
        jnp.dot(context, attn_out, preferred_element_type=jnp.float32)
        .astype(jnp.bfloat16)
        .astype(jnp.float32)
        .astype(jnp.bfloat16),
        "tensor",
        scatter_dimension=0,
        tiled=True,
    ).astype(jnp.float32)
    resid = token_rows + attn_total
    scale_two = lax.rsqrt(jnp.mean(resid * resid, axis=1, keepdims=True) + NORM_EPSILON)
    normed_two = (resid * scale_two * norm_gains[1]).astype(jnp.bfloat16)
    gathered_two = lax.all_gather(normed_two, "tensor", axis=0, tiled=True)
    gate_up = jnp.einsum("td,cdf->ctf", gathered_two, ffn_in, preferred_element_type=jnp.float32)
    hidden = (gelu_tanh(gate_up[0]) * gate_up[1]).astype(jnp.bfloat16)
    return (
        scale_one,
        gathered_one,
        projected,
        context,
        log_totals,
        resid,
        scale_two,
        gathered_two,
        gate_up,
        hidden,
    )


def general_body(
    tokens,
    norm_gains,
    attn_qkv,
    attn_out,
    ffn_in,
    ffn_out,
    position_tables,
    page_counts,
    layout_cells,
    cotangent,
):
    token_rows = tokens.astype(jnp.float32)
    rel_bias = relative_bias(position_tables[0], PAGE_LEN)
    lay_vals = layout_values(position_tables)
    first = forward_core(
        token_rows,
        norm_gains,
        attn_qkv,
        attn_out,
        ffn_in,
        page_counts,
        layout_cells,
        rel_bias,
        lay_vals,
    )
    first_hidden = first[9]
    rows_part = first_hidden
    ffn_total = lax.psum_scatter(
        jnp.dot(rows_part, ffn_out, preferred_element_type=jnp.float32)
        .astype(jnp.bfloat16)
        .astype(jnp.float32)
        .astype(jnp.bfloat16),
        "tensor",
        scatter_dimension=0,
        tiled=True,
    ).astype(jnp.float32)
    layer_out = (first[5] + ffn_total).astype(jnp.bfloat16)
    cot_rows = lax.all_gather(cotangent, "tensor", axis=0, tiled=True)
    again_rows, cot_rows = lax.optimization_barrier((token_rows, cot_rows))
    saved = forward_core(
        again_rows,
        norm_gains,
        attn_qkv,
        attn_out,
        ffn_in,
        page_counts,
        layout_cells,
        rel_bias,
        lay_vals,
    )
    (
        scale_one,
        gathered_one,
        projected,
        context,
        log_totals,
        resid,
        scale_two,
        gathered_two,
        gate_up,
        hidden,
    ) = saved
    grad_hidden = jnp.einsum("td,fd->tf", cot_rows, ffn_out, preferred_element_type=jnp.float32)
    outer_grad = jnp.einsum("tf,td->fd", hidden, cot_rows, preferred_element_type=jnp.float32)
    gelu_value, gelu_back = jax.vjp(gelu_tanh, gate_up[0])
    grad_gate = gelu_back(grad_hidden * gate_up[1])[0].astype(jnp.bfloat16)
    grad_up = (grad_hidden * gelu_value).astype(jnp.bfloat16)
    grad_gate_up = jnp.stack([grad_gate, grad_up])
    inner_grad = jnp.einsum(
        "td,ctf->cdf", gathered_two, grad_gate_up, preferred_element_type=jnp.float32
    )
    rows_part = grad_gate_up
    grad_normed_two = lax.psum_scatter(
        jnp.einsum("ctf,cdf->td", rows_part, ffn_in, preferred_element_type=jnp.float32)
        .astype(jnp.bfloat16)
        .astype(jnp.float32)
        .astype(jnp.bfloat16),
        "tensor",
        scatter_dimension=0,
        tiled=True,
    ).astype(jnp.float32)
    grad_resid = cotangent.astype(jnp.float32) + norm_back(
        resid, scale_two, norm_gains[1], grad_normed_two
    )
    gain_two = jnp.sum(grad_normed_two * resid * scale_two, axis=0)
    resid_rows = lax.all_gather(grad_resid.astype(jnp.bfloat16), "tensor", axis=0, tiled=True)
    out_grad = jnp.einsum("tk,td->kd", context, resid_rows, preferred_element_type=jnp.float32)
    grad_context = jnp.einsum(
        "td,kd->tk", resid_rows, attn_out, preferred_element_type=jnp.float32
    ).astype(jnp.bfloat16)
    grad_proj, tables_grad = attend_back(
        projected, grad_context, log_totals, page_counts, layout_cells, rel_bias, lay_vals
    )
    qkv_grad = jnp.einsum(
        "td,ctk->cdk", gathered_one, grad_proj, preferred_element_type=jnp.float32
    )
    rows_part = grad_proj
    grad_normed_one = lax.psum_scatter(
        jnp.einsum("ctk,cdk->td", rows_part, attn_qkv, preferred_element_type=jnp.float32)
        .astype(jnp.bfloat16)
        .astype(jnp.float32)
        .astype(jnp.bfloat16),
        "tensor",
        scatter_dimension=0,
        tiled=True,
    ).astype(jnp.float32)
    tokens_grad = grad_resid + norm_back(token_rows, scale_one, norm_gains[0], grad_normed_one)
    gain_one = jnp.sum(grad_normed_one * token_rows * scale_one, axis=0)
    gains_grad = lax.psum_scatter(
        jnp.stack([gain_one, gain_two]), ("dp", "tensor"), scatter_dimension=1, tiled=True
    )
    qkv_summed, inner_summed, out_summed, outer_summed, tables_summed = (
        lax.psum_scatter(
            qkv_grad.astype(jnp.bfloat16), "dp", scatter_dimension=1, tiled=True
        ).astype(jnp.float32),
        lax.psum_scatter(
            inner_grad.astype(jnp.bfloat16), "dp", scatter_dimension=1, tiled=True
        ).astype(jnp.float32),
        lax.psum_scatter(
            out_grad.astype(jnp.bfloat16), "dp", scatter_dimension=1, tiled=True
        ).astype(jnp.float32),
        lax.psum_scatter(
            outer_grad.astype(jnp.bfloat16), "dp", scatter_dimension=1, tiled=True
        ).astype(jnp.float32),
        lax.psum_scatter(
            tables_grad.astype(jnp.bfloat16), "dp", scatter_dimension=1, tiled=True
        ).astype(jnp.float32),
    )
    return (
        layer_out,
        tokens_grad,
        gains_grad,
        qkv_summed,
        out_summed,
        inner_summed,
        outer_summed,
        tables_summed,
    )


AXES = ("dp", "tensor")
PLANES = 4
RING = 4
CORES = 2
BLOCK = 256
HALF = 128
ATT = 512
UNITS = 384
FFW = 3 * UNITS
VMEM_BYTES = 60 * 1024 * 1024
F32 = jnp.float32
BF16 = jnp.bfloat16
NT = (((1,), (1,)), ((), ()))
TN = (((0,), (0,)), ((), ()))
NN = (((1,), (0,)), ((), ()))


def page_plan(mesh):
    return mesh.shape["dp"] == PLANES * CORES and mesh.shape["tensor"] == RING


def pairs(target):
    found = []
    for plane in range(PLANES):
        for core in range(CORES):
            for ring in range(RING):
                goal = target(plane, core, ring)
                if goal is not None:
                    source = (plane * CORES + core) * RING + ring
                    found.append((source, (goal[0] * CORES + goal[1]) * RING + goal[2]))
    return found


TO_X = pairs(lambda plane, core, ring: (plane ^ 1, core, ring))
TO_Y = pairs(lambda plane, core, ring: (plane ^ 2, core, ring))
TO_CORE = pairs(lambda plane, core, ring: (plane, 1 - core, ring))
SWAP = pairs(
    lambda plane, core, ring: (plane, 1 - core, ring ^ 1) if core != ring % 2 else None
)
FROM_RING = [
    pairs(lambda plane, core, ring, k=k: (plane, core, (ring - k) % RING)) for k in range(RING)
]
RING_SAME = [
    pairs(lambda plane, core, ring, k=k: (plane, core, (ring + k) % RING)) for k in range(RING)
]
RING_CROSS = [
    pairs(lambda plane, core, ring, k=k: (plane, 1 - core, (ring + k) % RING)) for k in range(RING)
]


def send(values, route):
    return lax.ppermute(values, AXES, route)


def dot(left, right, dims=NN):
    return lax.dot_general(left, right, dims, preferred_element_type=F32)


def call(kernel, name, out_shape, args, flops=0, prefetch=0, scratch=(), grid=None, **specs):
    in_bytes = sum(a.size * a.dtype.itemsize for a in args)
    outs = jax.tree.leaves(out_shape)
    out_bytes = sum(math.prod(o.shape) * o.dtype.itemsize for o in outs)
    whole = pl.BlockSpec(memory_space=pltpu.VMEM)
    scalar = pl.BlockSpec(memory_space=pltpu.SMEM)
    if grid is None:
        extra = dict(
            in_specs=[scalar] * prefetch + [whole] * (len(args) - prefetch),
            out_specs=jax.tree.map(lambda o: whole, out_shape),
            scratch_shapes=list(scratch),
        )
    else:
        extra = dict(grid=grid, scratch_shapes=list(scratch), **specs)
    return pl.pallas_call(
        kernel,
        out_shape=out_shape,
        name=name,
        cost_estimate=pl.CostEstimate(
            flops=int(flops), bytes_accessed=int(in_bytes + out_bytes), transcendentals=0
        ),
        compiler_params=pltpu.CompilerParams(vmem_limit_bytes=VMEM_BYTES),
        **extra,
    )(*args)


def shaped(shape, dtype=BF16):
    return jax.ShapeDtypeStruct(shape, dtype)


def columns(plane, r):
    return pl.ds(pl.multiple_of((plane ^ r) * BLOCK, BLOCK), BLOCK)


def split_pieces(outs, r, lanes, value):
    if r < 3:
        outs[r][:, lanes] = value
    else:
        outs[3][:, lanes] = value[:HALF]
        outs[4][:, lanes] = value[HALF:]


def own_attention_kernel(where, qkv, out, *outs):
    core, plane = where[0], where[1]
    for r in range(PLANES):
        rows = columns(plane, r)
        split_pieces(
            outs,
            r,
            slice(0, HALF),
            out[pl.ds(pl.multiple_of(core * HALF, HALF), HALF), rows].astype(F32).T.astype(BF16),
        )
        for m in range(3):
            lanes = slice((m + 1) * HALF, (m + 2) * HALF)
            split_pieces(
                outs, r, lanes, qkv[m, rows, pl.ds(pl.multiple_of(core * HALF, HALF), HALF)]
            )


def own_ffn_kernel(where, inner, outer, *outs):
    core, plane = where[0], where[1]
    units = inner.shape[2]
    for which, first, count in ((0, 0, UNITS), (1, UNITS, units - UNITS)):

        @pl.when(core == which)
        def _():
            for r in range(PLANES):
                rows = columns(plane, r)
                flipped = outer[first : first + count, rows].astype(F32).T.astype(BF16)
                parts = [flipped, inner[0, rows, first : first + count]]
                parts.append(inner[1, rows, first : first + count])
                for m, part in enumerate(parts):
                    if count < UNITS:
                        part = jnp.concatenate(
                            [part, jnp.zeros((BLOCK, UNITS - count), BF16)], axis=1
                        )
                    split_pieces(outs, r, slice(m * UNITS, (m + 1) * UNITS), part)


def piece_shapes(width):
    return [shaped((BLOCK, width))] * 3 + [shaped((HALF, width))] * 2


def spread_plane(piece):
    from_x = send(piece, TO_X)
    from_y = send(piece, TO_Y)
    corner_a = send(from_x[:HALF], TO_Y)
    corner_b = send(from_y[HALF:], TO_X)
    return [piece, from_x, from_y, corner_a, corner_b]


def join_pieces(target, pieces, lanes=slice(None)):
    for r in range(3):
        target[r * BLOCK : (r + 1) * BLOCK, :] = pieces[r][:, lanes]
    target[3 * BLOCK : 3 * BLOCK + HALF, :] = pieces[3][:, lanes]
    target[3 * BLOCK + HALF :, :] = pieces[4][:, lanes]


def grad_shapes(width):
    return [shaped((2, HALF, width))] * 2 + [shaped((HALF, width))] * 4


def split_grads(outs, lanes, grad):
    to_x, to_y, upper0, upper2, lower0, lower1 = outs
    part = [
        [grad[r * BLOCK : r * BLOCK + HALF], grad[r * BLOCK + HALF : (r + 1) * BLOCK]]
        for r in range(PLANES)
    ]
    part = [[half.astype(BF16) for half in pair] for pair in part]
    to_x[0, :, lanes] = part[1][0]
    to_x[1, :, lanes] = part[3][0]
    to_y[0, :, lanes] = part[2][1]
    to_y[1, :, lanes] = part[3][1]
    upper0[:, lanes] = part[0][0]
    upper2[:, lanes] = part[2][0]
    lower0[:, lanes] = part[0][1]
    lower1[:, lanes] = part[1][1]


def reduce_plane(grads, core):
    to_x, to_y, upper0, upper2, lower0, lower1 = grads
    got_x = send(to_x, TO_X).astype(F32)
    got_y = send(to_y, TO_Y).astype(F32)
    on_y = send((upper2.astype(F32) + got_x[1]).astype(BF16), TO_Y)
    on_x = send((lower1.astype(F32) + got_y[1]).astype(BF16), TO_X)
    upper = upper0.astype(F32) + got_x[0] + on_y.astype(F32)
    lower = lower0.astype(F32) + got_y[0] + on_x.astype(F32)
    mine = jnp.where(core == 0, upper, lower).astype(BF16)
    other = jnp.where(core == 0, lower, upper).astype(BF16)
    return mine, other


def reduce_ring(chunks):
    same, cross = [], []
    for k, (mine, other) in enumerate(chunks):
        same.append(mine if k == 0 else send(mine, RING_SAME[k]))
        cross.append(send(other, RING_CROSS[k]))
    return same + cross


def gather_sum(refs):
    total = refs[0][...].astype(F32)
    for ref in refs[1:]:
        total = total + ref[...].astype(F32)
    return total


def attention_grads_kernel(where, *refs):
    core = where[0]
    ins, (qkv_grad, out_grad) = refs[: 2 * RING], refs[2 * RING :]
    same, cross = gather_sum(ins[:RING]), gather_sum(ins[RING:])
    low = jnp.where(core == 0, same, cross)
    high = jnp.where(core == 0, cross, same)
    for m in range(3):
        lanes = slice((m + 1) * HALF, (m + 2) * HALF)
        qkv_grad[m, :, 0:HALF] = low[:, lanes]
        qkv_grad[m, :, HALF : 2 * HALF] = high[:, lanes]
    out_grad[0:HALF, :] = low[:, 0:HALF].T
    out_grad[HALF : 2 * HALF, :] = high[:, 0:HALF].T


def ffn_grads_kernel(where, *refs):
    core = where[0]
    ins, (inner_grad, outer_grad) = refs[: 2 * RING], refs[2 * RING :]
    rest = inner_grad.shape[2] - UNITS
    same, cross = gather_sum(ins[:RING]), gather_sum(ins[RING:])
    low = jnp.where(core == 0, same, cross)
    high = jnp.where(core == 0, cross, same)
    for m in range(2):
        first = (m + 1) * UNITS
        inner_grad[m, :, 0:UNITS] = low[:, first : first + UNITS]
        inner_grad[m, :, UNITS : UNITS + rest] = high[:, first : first + rest]
    outer_grad[0:UNITS, :] = low[:, 0:UNITS].T
    outer_grad[UNITS : UNITS + rest, :] = high[:, 0:UNITS].T[0:rest]


def place_rows_kernel(where, near, far, full, flipped):
    core, plane = where[0], where[1]
    rows = near.shape[0]
    for source, half in ((near, core), (far, 1 - core)):
        for r in range(PLANES):
            full[pl.ds(pl.multiple_of(half * rows, rows), rows), r * BLOCK : (r + 1) * BLOCK] = (
                source[:, columns(plane, r)]
            )
    for r in range(PLANES):
        lanes = slice(r * BLOCK, (r + 1) * BLOCK)
        flipped[lanes, :] = full[:, lanes].astype(F32).T.astype(BF16)


def first_norm_kernel(where, near, far, gains, full, gains_here, normed, flipped):
    core, plane = where[0], where[1]
    rows = near.shape[0]
    for r in range(PLANES):
        gains_here[:, r * BLOCK : (r + 1) * BLOCK] = gains[:, columns(plane, r)]
    for source, half in ((near, core), (far, 1 - core)):
        for r in range(PLANES):
            full[pl.ds(pl.multiple_of(half * rows, rows), rows), r * BLOCK : (r + 1) * BLOCK] = (
                source[:, columns(plane, r)]
            )
    for i in range(full.shape[0] // BLOCK):
        span = slice(i * BLOCK, (i + 1) * BLOCK)
        x = full[span, :].astype(F32)
        scale = lax.rsqrt(jnp.mean(x * x, axis=1, keepdims=True) + NORM_EPSILON)
        value = x * scale * gains_here[0:1, :]
        normed[span, :] = value.astype(BF16)
        flipped[:, span] = value.T.astype(BF16)


def second_norm_kernel(full, mine, other, gains_here, resid, normed, flipped):
    for i in range(full.shape[0] // BLOCK):
        span = slice(i * BLOCK, (i + 1) * BLOCK)
        row = full[span, :].astype(F32) + (
            mine[span, :].astype(F32) + other[span, :].astype(F32)
        )
        resid[span, :] = row
        scale = lax.rsqrt(jnp.mean(row * row, axis=1, keepdims=True) + NORM_EPSILON)
        value = row * scale * gains_here[1:2, :]
        normed[span, :] = value.astype(BF16)
        flipped[:, span] = value.T.astype(BF16)


def resid_grad_kernel(where, resid, cot, mine, other, gains_here, half_grad, low, flipped, gain):
    core, plane = where[0], where[1]
    rows = half_grad.shape[0]
    total = jnp.zeros((1, resid.shape[1]), F32)
    for i in range(resid.shape[0] // BLOCK):
        span = slice(i * BLOCK, (i + 1) * BLOCK)
        row = resid[span, :]
        grad = mine[span, :].astype(F32) + other[span, :].astype(F32)
        scale = lax.rsqrt(jnp.mean(row * row, axis=1, keepdims=True) + NORM_EPSILON)
        weighted = grad * gains_here[1:2, :]
        center = jnp.mean(row * weighted, axis=1, keepdims=True)
        value = cot[span, :].astype(F32) + scale * weighted - row * (scale * scale * scale * center)
        low[span, :] = value.astype(BF16)
        flipped[:, span] = value.T.astype(BF16)
        in_half = core == (i * BLOCK) // rows
        share = jnp.sum(grad * row * scale, axis=0, keepdims=True)
        total = total + jnp.where(in_half, share, 0.0)

        @pl.when(in_half)
        def _():
            first = (i * BLOCK) % rows
            half_grad[first : first + BLOCK, :] = value

    for r in range(PLANES):
        gain[:, columns(plane, r)] = total[:, r * BLOCK : (r + 1) * BLOCK]


def tokens_grad_kernel(where, full, half_grad, mine, other, gains_here, grad_out, low_out, gain):
    core, plane = where[0], where[1]
    rows = half_grad.shape[0]
    total = jnp.zeros((1, full.shape[1]), F32)
    for i in range(rows // BLOCK):
        span = slice(i * BLOCK, (i + 1) * BLOCK)
        page_span = pl.ds(pl.multiple_of(core * rows + i * BLOCK, BLOCK), BLOCK)
        x = full[page_span, :].astype(F32)
        grad = mine[span, :].astype(F32) + other[span, :].astype(F32)
        scale = lax.rsqrt(jnp.mean(x * x, axis=1, keepdims=True) + NORM_EPSILON)
        weighted = grad * gains_here[0:1, :]
        center = jnp.mean(x * weighted, axis=1, keepdims=True)
        value = half_grad[span, :] + scale * weighted - x * (scale * scale * scale * center)
        total = total + jnp.sum(grad * x * scale, axis=0, keepdims=True)
        for r in range(PLANES):
            block = value[:, r * BLOCK : (r + 1) * BLOCK]
            grad_out[span, columns(plane, r)] = block
            low_out[span, columns(plane, r)] = block.astype(BF16)
    for r in range(PLANES):
        gain[:, columns(plane, r)] = total[:, r * BLOCK : (r + 1) * BLOCK]


def layer_out_kernel(where, resid, mine, other, out):
    core, plane = where[0], where[1]
    rows = out.shape[0]
    page_span = pl.ds(pl.multiple_of(core * rows, rows), rows)
    row = resid[page_span, :] + (mine[...].astype(F32) + other[...].astype(F32))
    for r in range(PLANES):
        out[:, columns(plane, r)] = row[:, r * BLOCK : (r + 1) * BLOCK].astype(BF16)


def pair_lane(rows):
    return lax.broadcasted_iota(jnp.int32, (rows, 2 * HEAD_DIM), 1)


def key_columns(keys, qkv, cells_twice, cell_tail, mine):
    keys[:, :HALF] = jnp.where(
        mine, qkv[:, HALF : 2 * HALF].astype(F32), cells_twice[...].astype(F32)
    ).astype(BF16)
    keys[:, HALF:] = cell_tail[...]


def attention_kernel(
    far, normed, a0, a1, a2, a3, a4, cells, cells_twice, cell_tail, layout, near,
    qkv, prob, context, inverse,
    weights, queries, keys, scores,
):
    h = pl.program_id(0)
    rows = normed.shape[0]
    count = rows // HALF

    @pl.when(h == 0)
    def _():
        join_pieces(weights, (a0, a1, a2, a3, a4), slice(HALF, ATT))
        qkv[...] = dot(normed[...], weights[...]).astype(BF16)

    lane = pair_lane(rows)
    mine = (lane // HEAD_DIM) == h
    side = dot(cells[...], layout[0])
    queries[:, :HALF] = jnp.where(mine, qkv[:, :HALF].astype(F32), side[:, :HALF]).astype(BF16)
    block = lax.broadcasted_iota(jnp.int32, (rows, HALF), 0) // HALF
    other = lane % 8
    is_left, is_right = other < block - 1, other > block + 1
    high = jnp.where(is_left, far[h, 0], jnp.where(is_right, far[h, 2], 0.0))
    low = jnp.where(is_left, far[h, 1], jnp.where(is_right, far[h, 3], 0.0))
    tail = jnp.where(lane < HEAD_DIM, side[:, HALF:], jnp.where(lane == HEAD_DIM + 16, 1.0, 0.0))
    tail = jnp.where((lane >= HEAD_DIM) & (lane < HEAD_DIM + 8), high, tail)
    tail = jnp.where((lane >= HEAD_DIM + 8) & (lane < HEAD_DIM + 16), low, tail)
    queries[:, HALF:] = tail.astype(BF16)
    key_columns(keys, qkv, cells_twice, cell_tail, mine)
    scores[...] = dot(queries[...], keys[...], NT)

    spread = jnp.broadcast_to(near[0], (HALF, 4 * HALF))
    strip = pltpu.roll(spread, 3 * HALF, 1, stride=1, stride_axis=0)[:, : 3 * HALF]
    for i in range(count):
        first, last = max(i - 1, 0), min(i + 2, count)
        part = strip[:, (first - i + 1) * HALF : (last - i + 1) * HALF]
        span = slice(i * HALF, (i + 1) * HALF)
        scores[span, first * HALF : last * HALF] = scores[span, first * HALF : last * HALF] + part
        row = scores[span, :]
        top = jnp.max(row, axis=1, keepdims=True)
        prob[0, span, :] = jnp.exp(row - top).astype(BF16)

    values = jnp.where(mine, qkv[:, 2 * HALF :].astype(F32), 1.0).astype(BF16)
    mixed = dot(prob[0], values)
    inv = 1.0 / pltpu.roll(mixed, HEAD_DIM, 1)
    mixed = (mixed * inv).astype(BF16)

    @pl.when(h == 0)
    def _():
        context[...] = mixed
        inverse[...] = inv

    @pl.when(h == 1)
    def _():
        context[...] = jnp.where(mine, mixed.astype(F32), context[...].astype(F32)).astype(BF16)
        inverse[...] = jnp.where(mine, inv, inverse[...])


def attention(far, normed, pieces, cells, cells_twice, cell_tail, layout, near):
    rows = normed.shape[0]
    full = lambda a: pl.BlockSpec(a.shape, lambda h: (0,) * a.ndim)
    per_head = lambda a: pl.BlockSpec((1,) + a.shape[1:], lambda h: (h,) + (0,) * (a.ndim - 1))
    outs = [
        shaped((rows, 3 * HALF)), shaped((2, rows, rows)), shaped((rows, HALF)),
        shaped((rows, HALF), F32),
    ]
    args = [far, normed, *pieces, cells, cells_twice, cell_tail, layout, near]
    in_specs = [pl.BlockSpec(memory_space=pltpu.SMEM)] + [full(a) for a in args[1:-2]]
    in_specs += [per_head(layout), per_head(near)]
    out_specs = [full(outs[0]), per_head(outs[1]), full(outs[2]), full(outs[3])]
    return call(
        attention_kernel, "attention", outs, args,
        flops=2 * rows * 1024 * 384 + 4 * rows * rows * 384 * 4,
        grid=(2,), in_specs=in_specs, out_specs=out_specs,
        scratch=[
            pltpu.VMEM((PLANES * BLOCK, 3 * HALF), BF16),
            pltpu.VMEM((rows, 2 * HALF), BF16),
            pltpu.VMEM((rows, 2 * HALF), BF16),
            pltpu.VMEM((rows, rows), F32),
        ],
    )


def attention_back_kernel(
    low, low_flipped, normed_flipped, a0, a1, a2, a3, a4, qkv, prob, context, inverse,
    cells_twice, cell_tail, cells_flipped,
    grad_qkv, to_x, to_y, upper0, upper2, lower0, lower1, strip_out, far_out, layout_out,
    weights, scaled, scaled_low, keys, dscores,
):
    h = pl.program_id(0)
    rows = low.shape[0]
    count = rows // HALF
    lane = pair_lane(rows)
    mine = (lane // HEAD_DIM) == h

    @pl.when(h == 0)
    def _():
        join_pieces(weights, (a0, a1, a2, a3, a4), slice(0, HALF))
        grad_context = dot(low[...], weights[...]).astype(BF16).astype(F32)
        value = grad_context * inverse[...]
        scaled[...] = value
        scaled_low[...] = value.astype(BF16)

    value = scaled[...]
    delta = -jnp.sum(jnp.where(mine, value * context[...].astype(F32), 0.0), axis=1, keepdims=True)
    delta_high = delta.astype(BF16).astype(F32)
    spare = HEAD_DIM * (1 - h)
    left = jnp.where(
        mine,
        value,
        jnp.where(lane == spare, delta_high, jnp.where(lane == spare + 1, delta - delta_high, 0.0)),
    ).astype(BF16)
    ones = jnp.where((lane == spare) | (lane == spare + 1), 1.0, 0.0)
    right = jnp.where(mine, qkv[:, 2 * HALF :].astype(F32), ones).astype(BF16)
    strip = jnp.zeros((HALF, 3 * HALF), F32)
    strips = [jnp.zeros((HALF, HALF), F32) for _ in range(3)]
    for i in range(rows // BLOCK):
        span = slice(i * BLOCK, (i + 1) * BLOCK)
        dscore = prob[0, span, :].astype(F32) * dot(left[span, :], right, NT)
        dscores[span, :] = dscore.astype(BF16)
        for part in range(BLOCK // HALF):
            at = i * (BLOCK // HALF) + part
            for step in range(3):
                block = at + step - 1
                if 0 <= block < count:
                    strips[step] = (
                        strips[step]
                        + dscore[
                            part * HALF : (part + 1) * HALF, block * HALF : (block + 1) * HALF
                        ]
                    )
    for step in range(3):
        strip_out[0, :, step * HALF : (step + 1) * HALF] = strips[step]

    key_columns(keys, qkv, cells_twice, cell_tail, mine)
    grad_left = dot(dscores[...], keys[...])
    grad_key = dot(dscores[...], qkv[:, :HALF], TN)
    grad_value = dot(prob[0], scaled_low[...], TN)
    new = [grad_left[:, :HALF], grad_key, grad_value]

    @pl.when(h == 0)
    def _():
        for m in range(3):
            grad_qkv[:, m * HALF : (m + 1) * HALF] = new[m].astype(BF16)

    @pl.when(h == 1)
    def _():
        for m in range(3):
            lanes = slice(m * HALF, (m + 1) * HALF)
            grad_qkv[:, lanes] = jnp.where(mine, new[m], grad_qkv[:, lanes].astype(F32)).astype(BF16)

    for m in range(2):
        lanes = slice(m * HALF, (m + 1) * HALF)
        table = grad_left[:, lanes]
        if m == 0:
            table = jnp.where(mine, pltpu.roll(table, HEAD_DIM, 1), table)
        table_high = table.astype(BF16)
        rest = (table - table_high.astype(F32)).astype(BF16)
        layout_out[0, :, lanes] = dot(cells_flipped[...], table_high) + dot(
            cells_flipped[...], rest
        )
    block = lax.broadcasted_iota(jnp.int32, (rows, HALF), 0) // HALF
    tail = grad_left[:, HALF:]
    far_left = jnp.sum(jnp.where(lane % 8 < block - 1, tail, 0.0), axis=0, keepdims=True)
    far_right = jnp.sum(jnp.where(lane % 8 > block + 1, tail, 0.0), axis=0, keepdims=True)
    far_out[0, 0:1, :] = far_left
    far_out[0, 1:2, :] = far_right

    @pl.when(h == 1)
    def _():
        outs = (to_x, to_y, upper0, upper2, lower0, lower1)
        split_grads(outs, slice(0, HALF), dot(low_flipped[...], context[...]))
        split_grads(outs, slice(HALF, ATT), dot(normed_flipped[...], grad_qkv[...]))


def attention_back(low, low_flipped, normed_flipped, pieces, saved, cells_twice, cell_tail, cells_flipped):
    qkv, prob, context, inverse = saved
    rows = low.shape[0]
    full = lambda a: pl.BlockSpec(a.shape, lambda h: (0,) * a.ndim)
    per_head = lambda a: pl.BlockSpec((1,) + a.shape[1:], lambda h: (h,) + (0,) * (a.ndim - 1))
    args = [low, low_flipped, normed_flipped, *pieces, qkv, prob, context, inverse]
    args += [cells_twice, cell_tail, cells_flipped]
    in_specs = [per_head(a) if a is prob else full(a) for a in args]
    outs = [shaped((rows, 3 * HALF))] + grad_shapes(ATT)
    tables = [shaped((2, HALF, 3 * HALF), F32), shaped((2, 2, HALF), F32), shaped((2, HALF, 2 * HALF), F32)]
    out_specs = [full(o) for o in outs] + [per_head(o) for o in tables]
    return call(
        attention_back_kernel, "attention_back", outs + tables, args,
        flops=4 * rows * 1024 * 512 + 4 * rows * rows * 1024 * 2,
        grid=(2,), in_specs=in_specs, out_specs=out_specs,
        scratch=[
            pltpu.VMEM((PLANES * BLOCK, HALF), BF16),
            pltpu.VMEM((rows, HALF), F32),
            pltpu.VMEM((rows, HALF), BF16),
            pltpu.VMEM((rows, 2 * HALF), BF16),
            pltpu.VMEM((rows, rows), BF16),
        ],
    )


def sum_products_kernel(width, lanes, row_spans, *refs):
    lefts = refs[:RING]
    pieces = [refs[RING + 5 * k : RING + 5 * k + 5] for k in range(RING)]
    out, left, right = refs[6 * RING :]
    for k in range(RING):
        at = slice(k * width, (k + 1) * width)
        left[:, at] = lefts[k][:, lanes[0]]
        for r in range(3):
            right[r * BLOCK : (r + 1) * BLOCK, at] = pieces[k][r][:, lanes[1]]
        right[3 * BLOCK : 3 * BLOCK + HALF, at] = pieces[k][3][:, lanes[1]]
        right[3 * BLOCK + HALF :, at] = pieces[k][4][:, lanes[1]]
    for i in range(left.shape[0] // BLOCK):
        span = slice(i * BLOCK, (i + 1) * BLOCK)
        out[span, :] = dot(left[span, :], right[...], NT).astype(BF16)


def sum_products(name, lefts, left_lanes, pieces, right_lanes):
    rows = lefts[0].shape[0]
    width = right_lanes.stop - right_lanes.start

    def kernel(*refs):
        sum_products_kernel(width, (left_lanes, right_lanes), None, *refs)

    args = list(lefts) + [piece for quarter in pieces for piece in quarter]
    return call(
        kernel, name, shaped((rows, PLANES * BLOCK)), args,
        flops=2 * rows * PLANES * BLOCK * width * RING,
        scratch=[
            pltpu.VMEM((rows, RING * width), BF16),
            pltpu.VMEM((PLANES * BLOCK, RING * width), BF16),
        ],
    )


def ffn_kernel(
    normed, normed_flipped, cot, cot_flipped, f0, f1, f2, f3, f4,
    hidden, to_x, to_y, upper0, upper2, lower0, lower1,
    weights,
):
    join_pieces(weights, (f0, f1, f2, f3, f4))
    for i in range(normed.shape[0] // BLOCK):
        span = slice(i * BLOCK, (i + 1) * BLOCK)
        both = dot(normed[span, :], weights[:, UNITS:])
        grad_hidden = dot(cot[span, :], weights[:, :UNITS])
        gate, up = both[:, :UNITS], both[:, UNITS:]
        square = gate * gate
        ratio = math.sqrt(2.0 / math.pi)
        bend = jnp.tanh(ratio * gate * (1.0 + 0.044715 * square))
        half_gate = 0.5 * gate
        value = half_gate + half_gate * bend
        slope = 0.5 + 0.5 * bend + half_gate * (1.0 - bend * bend) * (
            ratio * (1.0 + 3.0 * 0.044715 * square)
        )
        hidden[span, :UNITS] = (value * up).astype(BF16)
        hidden[span, UNITS : 2 * UNITS] = (grad_hidden * up * slope).astype(BF16)
        hidden[span, 2 * UNITS :] = (grad_hidden * value).astype(BF16)
    outs = (to_x, to_y, upper0, upper2, lower0, lower1)
    split_grads(outs, slice(0, UNITS), dot(cot_flipped[...], hidden[:, :UNITS]))
    split_grads(outs, slice(UNITS, FFW), dot(normed_flipped[...], hidden[:, UNITS:]))


def ffn(normed, normed_flipped, cot, cot_flipped, pieces):
    rows = normed.shape[0]
    outs = [shaped((rows, FFW))] + grad_shapes(FFW)
    return call(
        ffn_kernel, "ffn", outs, [normed, normed_flipped, cot, cot_flipped, *pieces],
        flops=4 * rows * PLANES * BLOCK * FFW,
        scratch=[pltpu.VMEM((PLANES * BLOCK, FFW), BF16)],
    )


MESH = pl.DeviceIdType.MESH


def here():
    group, ring = lax.axis_index("dp"), lax.axis_index("tensor")
    return group // CORES, group % CORES, ring


def device(plane, core, ring):
    return (plane * CORES + core, ring)


def greet(partners):
    barrier = pltpu.get_barrier_semaphore()
    for partner in partners:
        pl.semaphore_signal(barrier, inc=1, device_id=partner, device_id_type=MESH)
    pl.semaphore_wait(barrier, len(partners))


class Lines:
    def __init__(self, send_sems, recv_sems):
        self.send_sems, self.recv_sems, self.open = send_sems, recv_sems, {}

    def make(self, name, source, target, partner):
        at = len(self.open)
        self.open[name] = pltpu.make_async_remote_copy(
            src_ref=source,
            dst_ref=target,
            send_sem=self.send_sems.at[at],
            recv_sem=self.recv_sems.at[at],
            device_id=partner,
            device_id_type=MESH,
        )
        return self.open[name]

    def start(self, name, source, target, partner):
        self.make(name, source, target, partner).start()

    def arrived(self, *names):
        for name in names:
            self.open[name].wait_recv()

    def sent(self, *names):
        for name in names or list(self.open):
            self.open[name].wait_send()


class Gather:
    def __init__(self, lines, tag, own, full, where):
        self.lines, self.tag, self.own, self.full = lines, tag, own, full
        self.plane, self.core, self.ring = where

    def ring_start(self, k):
        self.lines.start(
            (self.tag, "z", k),
            self.own.at[0:BLOCK],
            self.full.at[k, 0:BLOCK],
            device(self.plane, self.core, (self.ring + RING - k) % RING),
        )

    def plane_start(self, k):
        self.lines.arrived((self.tag, "z", k))
        for name, r in (("x", 1), ("y", 2)):
            self.lines.start(
                (self.tag, name, k),
                self.full.at[k, 0:BLOCK],
                self.full.at[k, r * BLOCK : (r + 1) * BLOCK],
                device(self.plane ^ r, self.core, self.ring),
            )

    def corner_start(self, k):
        for name, r, half, goal in (("x", 1, 0, 2), ("y", 2, 1, 1)):
            self.lines.arrived((self.tag, name, k))
            self.lines.start(
                (self.tag, "corner" + name, k),
                self.full.at[k, r * BLOCK + half * HALF : r * BLOCK + (half + 1) * HALF],
                self.full.at[k, 3 * BLOCK + half * HALF : 3 * BLOCK + (half + 1) * HALF],
                device(self.plane ^ goal, self.core, self.ring),
            )

    def finish(self, k):
        self.lines.arrived((self.tag, "cornerx", k), (self.tag, "cornery", k))


def own_attention(core, plane, qkv, out, target):
    for r in range(PLANES):
        rows, place = columns(plane, r), slice(r * BLOCK, (r + 1) * BLOCK)
        mine = pl.ds(pl.multiple_of(core * HALF, HALF), HALF)
        target[place, 0:HALF] = out[mine, rows].astype(F32).T.astype(BF16)
        for m in range(3):
            target[place, (m + 1) * HALF : (m + 2) * HALF] = qkv[m, rows, mine]


def own_ffn(core, plane, inner, outer, target):
    units = inner.shape[2]
    for which, first, count in ((0, 0, UNITS), (1, UNITS, units - UNITS)):

        @pl.when(core == which)
        def _():
            for r in range(PLANES):
                rows, place = columns(plane, r), slice(r * BLOCK, (r + 1) * BLOCK)
                parts = [outer[first : first + count, rows].astype(F32).T.astype(BF16)]
                parts += [inner[m, rows, first : first + count] for m in range(2)]
                for m, part in enumerate(parts):
                    target[place, m * UNITS : m * UNITS + count] = part
                    if count < UNITS:
                        target[place, m * UNITS + count : (m + 1) * UNITS] = jnp.zeros(
                            (BLOCK, UNITS - count), BF16
                        )


def place_rows(plane, core, near, far, full):
    rows = near.shape[0]
    for source, half in ((near, core), (far, 1 - core)):
        for r in range(PLANES):
            full[pl.ds(pl.multiple_of(half * rows, rows), rows), r * BLOCK : (r + 1) * BLOCK] = (
                source[:, columns(plane, r)]
            )


def split_bf16(values):
    parts = []
    for _ in range(3):
        part = values.astype(BF16)
        parts.append(part)
        values = values - part.astype(F32)
    return parts


def bias_pieces(tables, near_hot, cell_hot, layout, near):
    parts = split_bf16(tables)
    rel = sum(dot(part, near_hot[...]) for part in parts)
    cells = dot(parts[0], cell_hot[...])
    heads = tables.shape[0] // 3
    for h in range(heads):
        near[h] = rel[h : h + 1, :]
        toeplitz = []
        for axis in range(2):
            row = jnp.broadcast_to(cells[(axis + 1) * heads + h : (axis + 1) * heads + h + 1], (CELLS, HALF))
            toeplitz.append(pltpu.roll(row, CELLS, 1, stride=1, stride_axis=0))
        side = lax.broadcasted_iota(jnp.int32, (CELLS, HALF), 1)
        first = toeplitz[0]
        layout[h, 0:CELLS, 0:HALF] = jnp.where(
            side < CELLS, first, pltpu.roll(first, CELLS, 1)
        ).astype(BF16)
        layout[h, 0:CELLS, HALF:] = jnp.zeros((CELLS, HALF), BF16)
        layout[h, CELLS:, 0:HALF] = jnp.zeros((CELLS, HALF), BF16)
        layout[h, CELLS:, HALF:] = jnp.where(side < CELLS, toeplitz[1], 0.0).astype(BF16)


def forward_kernel(
    tokens, cot, gains, qkv_w, out_w, ffn_in, ffn_out, tables, ints, near_hot, cell_hot,
    att_full, ffn_full, prob_full, full, gains_here, normed_t, resid, normed_two, normed_two_t,
    cot_full, cot_t, qkv, context, inverse, cells_t, cells_twice, cell_tail,
    near_x, far_x, near_g, far_g, other_ints, table_parts, table_rows, layout, near,
    own_ffn_w, ffn_in_v, ffn_out_v, normed, weights, cells, queries, keys, scores, prob,
    mixed_all, out_rows, mine_out, other_out,
    send_sems, recv_sems, local_sems,
):
    plane, core, ring = where = here()
    native = core == ring % 2
    rows = tokens.shape[0]
    length = 2 * rows
    partner = device(plane, 1 - core, ring)
    swap = device(plane, 1 - core, ring ^ 1)
    ring_others = [device(plane, core, (ring + RING - k) % RING) for k in range(1, RING)]
    neighbours = [device(plane ^ 1, core, ring), device(plane ^ 2, core, ring)]
    lines = Lines(send_sems, recv_sems)
    load_in = pltpu.make_async_copy(ffn_in, ffn_in_v, local_sems.at[0])
    load_out = pltpu.make_async_copy(ffn_out, ffn_out_v, local_sems.at[1])
    load_in.start()
    load_out.start()
    greet([partner, swap] + ring_others + neighbours)

    def swap_rows(tag, source, near_rows, far_rows):
        lines.make((tag, "swap"), source, near_rows, swap)
        lines.make((tag, "give"), source, far_rows, partner)
        lines.make((tag, "pass"), near_rows, far_rows, partner)

        @pl.when(native)
        def _():
            lines.open[tag, "give"].start()
            keep = pltpu.make_async_copy(source, near_rows, local_sems.at[2])
            keep.start()
            keep.wait()

        @pl.when(jnp.logical_not(native))
        def _():
            lines.open[tag, "swap"].start()

    def swap_pass(tag):
        @pl.when(jnp.logical_not(native))
        def _():
            lines.arrived((tag, "swap"))
            lines.open[tag, "pass"].start()
            lines.arrived((tag, "give"))

        @pl.when(native)
        def _():
            lines.arrived((tag, "pass"))

    def swap_sent(tag):
        @pl.when(jnp.logical_not(native))
        def _():
            lines.sent((tag, "swap"), (tag, "pass"))

        @pl.when(native)
        def _():
            lines.sent((tag, "give"))

    swap_rows("x", tokens, near_x, far_x)
    lines.start("ints", ints, other_ints, partner)
    table_parts[0] = tables[...]
    for k in range(1, RING):
        lines.start(("tables", k), tables, table_parts.at[k], ring_others[k - 1])
    own_attention(core, plane, qkv_w, out_w, weights)
    keep_weights = pltpu.make_async_copy(weights, att_full.at[0], local_sems.at[3])
    keep_weights.start()
    att = Gather(lines, "att", weights, att_full, where)
    ffn = Gather(lines, "ffn", own_ffn_w, ffn_full, where)
    keep_weights.wait()
    att.own = att_full.at[0]
    for k in range(1, RING):
        att.ring_start(k)

    lines.arrived("ints")
    page = ring // 2
    picked = []
    for first in (0, 2, 4):
        own_row = ints[pl.ds(first + page, 1), :]
        other_row = other_ints[pl.ds(first + page, 1), :]
        picked.append(jnp.where(native, own_row, other_row))
    spot = lax.broadcasted_iota(jnp.int32, (CELLS, length), 0)
    cells_x = (jnp.broadcast_to(picked[0], (CELLS, length)) == spot).astype(F32)
    cells_y = (jnp.broadcast_to(picked[1], (CELLS, length)) == spot).astype(F32)
    position = lax.broadcasted_iota(jnp.int32, (CELLS, length), 1)
    tail = jnp.where((spot < 16) & (spot % 8 == position // HALF), 1.0, 0.0)
    hidden_key = (spot == 16) & (position >= jnp.broadcast_to(picked[2], (CELLS, length)))
    tail = jnp.where(hidden_key, MASK_VALUE, tail)
    cells_t[0:CELLS, :] = cells_x.astype(BF16)
    cells_t[CELLS:, :] = cells_y.astype(BF16)
    cells[...] = jnp.concatenate([cells_x, cells_y], axis=0).T.astype(BF16)
    cells_twice[...] = jnp.concatenate([cells_x, cells_x], axis=0).T.astype(BF16)
    cell_tail[...] = jnp.concatenate([cells_y, tail], axis=0).T.astype(BF16)
    for k in range(1, RING):
        lines.arrived(("tables", k))
    for k in range(RING):
        for axis in range(3):
            first = axis * 2 * RING + 2 * k
            table_rows[first : first + 2, :] = table_parts[k, pl.ds(4 * axis + 2 * core, 2), :]
    bias_pieces(table_rows[...], near_hot, cell_hot, layout, near)

    for r in range(PLANES):
        gains_here[:, r * BLOCK : (r + 1) * BLOCK] = gains[:, columns(plane, r)]
    swap_pass("x")
    place_rows(plane, core, near_x, far_x, full)
    for i in range(length // BLOCK):
        span = slice(i * BLOCK, (i + 1) * BLOCK)
        x = full[span, :].astype(F32)
        scale = lax.rsqrt(jnp.mean(x * x, axis=1, keepdims=True) + NORM_EPSILON)
        value = x * scale * gains_here[0:1, :]
        normed[span, :] = value.astype(BF16)
        normed_t[:, span] = value.T.astype(BF16)
    swap_rows("g", cot, near_g, far_g)

    def head(k, h):
        at = 2 * k + h
        lane = pair_lane(length)
        mine = (lane // HEAD_DIM) == h
        side = dot(cells[...], layout[at])
        queries[:, :HALF] = jnp.where(mine, qkv[k, :, :HALF].astype(F32), side[:, :HALF]).astype(BF16)
        block = lax.broadcasted_iota(jnp.int32, (length, HALF), 0) // HALF
        is_left, is_right = lane % 8 < block - 1, lane % 8 > block + 1
        left, right = near[at, :, 0:1], near[at, :, 4 * HALF - 1 :]
        left_high, right_high = left.astype(BF16).astype(F32), right.astype(BF16).astype(F32)
        high = jnp.where(is_left, left_high, jnp.where(is_right, right_high, 0.0))
        low = jnp.where(is_left, left - left_high, jnp.where(is_right, right - right_high, 0.0))
        ends = jnp.where(lane < HEAD_DIM, side[:, HALF:], jnp.where(lane == HEAD_DIM + 16, 1.0, 0.0))
        ends = jnp.where((lane >= HEAD_DIM) & (lane < HEAD_DIM + 8), high, ends)
        ends = jnp.where((lane >= HEAD_DIM + 8) & (lane < HEAD_DIM + 16), low, ends)
        queries[:, HALF:] = ends.astype(BF16)
        keys[:, :HALF] = jnp.where(
            mine, qkv[k, :, HALF : 2 * HALF].astype(F32), cells_twice[...].astype(F32)
        ).astype(BF16)
        keys[:, HALF:] = cell_tail[...]
        scores[...] = dot(queries[...], keys[...], NT)
        spread = jnp.broadcast_to(near[at], (HALF, 4 * HALF))
        strip = pltpu.roll(spread, 3 * HALF, 1, stride=1, stride_axis=0)[:, : 3 * HALF]
        count = length // HALF
        store = pltpu.make_async_copy(prob.at[h], prob_full.at[at], local_sems.at[4 + h])
        if k > 0:
            store.wait()
        for i in range(count):
            first, last = max(i - 1, 0), min(i + 2, count)
            part = strip[:, (first - i + 1) * HALF : (last - i + 1) * HALF]
            span, near_span = slice(i * HALF, (i + 1) * HALF), slice(first * HALF, last * HALF)
            scores[span, near_span] = scores[span, near_span] + part
            row = scores[span, :]
            top = jnp.max(row, axis=1, keepdims=True)
            prob[h, span, :] = jnp.exp(row - top).astype(BF16)
        values = jnp.where(mine, qkv[k, :, 2 * HALF :].astype(F32), 1.0).astype(BF16)
        mixed = dot(prob[h], values)
        inv = 1.0 / pltpu.roll(mixed, HEAD_DIM, 1)
        mixed = (mixed * inv).astype(BF16)
        store.start()
        if h == 0:
            context[k] = mixed
            inverse[k] = inv
        else:
            context[k] = jnp.where(mine, mixed.astype(F32), context[k].astype(F32)).astype(BF16)
            inverse[k] = jnp.where(mine, inv, inverse[k])

    def project(k):
        if k > 0:
            load = pltpu.make_async_copy(att_full.at[k], weights, local_sems.at[3])
            load.start()
            load.wait()
        qkv[k] = dot(normed[...], weights[:, HALF:]).astype(BF16)
        mixed_all[:, k * HALF : (k + 1) * HALF] = weights[:, 0:HALF]

    def after_head(k, h):
        if (k, h) == (0, 0):
            att.plane_start(2)
            att.corner_start(1)
        if (k, h) == (0, 1):
            att.plane_start(3)
            att.corner_start(2)
            for step in range(1, RING):
                ffn.ring_start(step)
        if (k, h) == (1, 0):
            att.corner_start(3)
        if (k, h) == (2, 0):
            swap_pass("g")
            ffn.plane_start(1)
        if (k, h) == (3, 0):
            ffn.plane_start(2)
            ffn.corner_start(1)

    for k in range(RING):
        if k > 0:
            att.finish(k)
        project(k)
        if k == 0:
            att.plane_start(1)
            load_in.wait()
            load_out.wait()
            own_ffn(core, plane, ffn_in_v, ffn_out_v, own_ffn_w)
        for h in range(2):
            head(k, h)
            after_head(k, h)

    for k in range(RING):
        out_rows[:, k * HALF : (k + 1) * HALF] = context[k]
    for i in range(length // BLOCK):
        span = slice(i * BLOCK, (i + 1) * BLOCK)
        mine_out[span, :] = dot(out_rows[span, :], mixed_all[...], NT).astype(BF16)
        lines.start(("out", i), mine_out.at[span], other_out.at[span], partner)
    place_rows(plane, core, near_g, far_g, cot_full)
    for r in range(PLANES):
        lanes = slice(r * BLOCK, (r + 1) * BLOCK)
        cot_t[lanes, :] = cot_full[:, lanes].astype(F32).T.astype(BF16)
    for i in range(length // BLOCK):
        span = slice(i * BLOCK, (i + 1) * BLOCK)
        lines.arrived(("out", i))
        row = full[span, :].astype(F32) + (
            mine_out[span, :].astype(F32) + other_out[span, :].astype(F32)
        )
        resid[span, :] = row
        scale = lax.rsqrt(jnp.mean(row * row, axis=1, keepdims=True) + NORM_EPSILON)
        value = row * scale * gains_here[1:2, :]
        normed_two[span, :] = value.astype(BF16)
        normed_two_t[:, span] = value.T.astype(BF16)

    ffn.plane_start(3)
    ffn.corner_start(2)
    ffn.finish(1)
    ffn.corner_start(3)
    ffn.finish(2)
    ffn.finish(3)
    for h in range(2):
        pltpu.make_async_copy(prob.at[h], prob_full.at[2 * (RING - 1) + h], local_sems.at[4 + h]).wait()
    swap_sent("x")
    swap_sent("g")
    lines.sent(*[name for name in lines.open if name[0] not in ("x", "g")])
    keep_ffn = pltpu.make_async_copy(own_ffn_w, ffn_full.at[0], local_sems.at[3])
    keep_ffn.start()
    keep_ffn.wait()


def hot(reach, width):
    offsets = np.arange(width) - width // 2
    found = bucket_table(offsets, BUCKETS, reach)[None, :] == np.arange(HALF)[:, None]
    return jnp.asarray(found.astype(np.float32), BF16)


def forward(tokens, cotangent, gains, qkv_w, out_w, ffn_in, ffn_out, position_tables, page_counts, layout_cells):
    rows = tokens.shape[0]
    length = 2 * rows
    features = PLANES * BLOCK
    tables = position_tables.transpose(0, 2, 1).reshape(12, BUCKETS)
    tables = jnp.pad(tables, ((0, 4), (0, HALF - BUCKETS)))
    ints = jnp.concatenate(
        [
            layout_cells.reshape(4, length),
            jnp.broadcast_to(page_counts[:, None], (2, length)),
            jnp.zeros((2, length), jnp.int32),
        ]
    )
    args = [tokens, cotangent, gains, qkv_w, out_w, ffn_in, ffn_out, tables, ints]
    args += [hot(REL_REACH, 4 * HALF), hot(CELLS, HALF)]
    whole = pl.BlockSpec(memory_space=pltpu.VMEM)
    outside = pl.BlockSpec(memory_space=pl.ANY)
    outs = [
        shaped((RING, features, ATT)), shaped((RING, features, FFW)), shaped((2 * RING, length, length)),
        shaped((length, features)), shaped((2, features), F32), shaped((features, length)),
        shaped((length, features), F32), shaped((length, features)), shaped((features, length)),
        shaped((length, features)), shaped((features, length)),
        shaped((RING, length, 3 * HALF)), shaped((RING, length, HALF)), shaped((RING, length, HALF), F32),
        shaped((HALF, length)), shaped((length, HALF)), shaped((length, HALF)),
    ]
    scratch = [pltpu.VMEM((rows, features), BF16)] * 4 + [
        pltpu.VMEM(ints.shape, jnp.int32),
        pltpu.VMEM((RING,) + tables.shape, F32),
        pltpu.VMEM((6 * RING, HALF), F32),
        pltpu.VMEM((2 * RING, HALF, 2 * HALF), BF16),
        pltpu.VMEM((2 * RING, 1, 4 * HALF), F32),
        pltpu.VMEM((features, FFW), BF16),
        pltpu.VMEM(ffn_in.shape, BF16),
        pltpu.VMEM(ffn_out.shape, BF16),
        pltpu.VMEM((length, features), BF16),
        pltpu.VMEM((features, ATT), BF16),
        pltpu.VMEM((length, HALF), BF16),
        pltpu.VMEM((length, 2 * HALF), BF16),
        pltpu.VMEM((length, 2 * HALF), BF16),
        pltpu.VMEM((length, length), F32),
        pltpu.VMEM((2, length, length), BF16),
        pltpu.VMEM((features, RING * HALF), BF16),
        pltpu.VMEM((length, RING * HALF), BF16),
        pltpu.VMEM((length, features), BF16),
        pltpu.VMEM((length, features), BF16),
        pltpu.SemaphoreType.DMA((48,)),
        pltpu.SemaphoreType.DMA((48,)),
        pltpu.SemaphoreType.DMA((6,)),
    ]
    in_specs = [whole, outside, whole, whole, whole, outside, outside] + [whole] * 4
    out_specs = [outside] * 3 + [whole] * 14
    return pl.pallas_call(
        forward_kernel,
        out_shape=outs,
        in_specs=in_specs,
        out_specs=out_specs,
        scratch_shapes=scratch,
        name="forward",
        cost_estimate=pl.CostEstimate(flops=10**10, bytes_accessed=10**8, transcendentals=0),
        compiler_params=pltpu.CompilerParams(
            vmem_limit_bytes=63 * 1024 * 1024, collective_id=0, has_side_effects=True
        ),
    )(*args)


def near_onehot():
    offsets = np.arange(4 * HALF) - 2 * HALF
    buckets = bucket_table(offsets, BUCKETS, REL_REACH)
    return (buckets[:, None] == np.arange(BUCKETS)[None, :]).astype(np.float32)


def strip_onehot():
    offsets = np.arange(3 * HALF)[None, :] - HALF - np.arange(HALF)[:, None]
    return bucket_table(offsets, BUCKETS, REL_REACH)


def bias_inputs(tables):
    heads = tables.shape[2]
    near = jnp.einsum("ub,bh->hu", near_onehot(), tables[0], precision=HIGHEST_PRECISION)
    ends = jnp.stack([tables[0, BUCKETS // 2 - 1], tables[0, BUCKETS - 1]], axis=1)
    ends_high = ends.astype(BF16).astype(F32)
    far = jnp.stack([ends_high, ends - ends_high], axis=2).reshape(heads, 4)
    cells = layout_values(tables).astype(BF16)
    gap = jnp.zeros((heads, CELLS, CELLS), BF16)
    top = jnp.concatenate([cells[0], cells[0], gap, gap], axis=2)
    bottom = jnp.concatenate([gap, gap, cells[1], gap], axis=2)
    return near[:, None, :], far, jnp.concatenate([top, bottom], axis=1)


def table_sums(strips, fars, layouts):
    strips, fars, layouts = (jnp.concatenate(a, axis=0) for a in (strips, fars, layouts))
    heads = strips.shape[0]
    strip_bucket = jnp.asarray(strip_onehot())
    near = jnp.stack(
        [
            jnp.sum(jnp.where(strip_bucket == b, strips, 0.0), axis=(1, 2))
            for b in range(BUCKETS)
        ]
    )
    ends = jnp.sum(fars[:, :, HEAD_DIM : HEAD_DIM + 8], axis=2)
    left = (np.arange(BUCKETS) == BUCKETS // 2 - 1).astype(np.float32)[:, None]
    right = (np.arange(BUCKETS) == BUCKETS - 1).astype(np.float32)[:, None]
    rel = near + left * ends[None, :, 0] + right * ends[None, :, 1]
    cells_x = layouts[:, :CELLS, :CELLS]
    cells_y = layouts[:, CELLS:, 2 * CELLS : 3 * CELLS]
    both = jnp.stack([cells_x, cells_y]).reshape(2, heads, CELLS * CELLS)
    lay = jnp.einsum("shm,mn->snh", both, layout_onehot(), precision=HIGHEST_PRECISION)
    return jnp.concatenate([rel[None], lay], axis=0)


def page_body(
    tokens,
    norm_gains,
    attn_qkv,
    attn_out,
    ffn_in,
    ffn_out,
    position_tables,
    page_counts,
    layout_cells,
    cotangent,
):
    group, ring = lax.axis_index("dp"), lax.axis_index("tensor")
    core, plane = group % CORES, group // CORES
    where = jnp.stack([core, plane]).astype(jnp.int32)
    native = core == ring % 2
    rows = tokens.shape[0]
    length = 2 * rows

    (
        att_full, ffn_full, prob, full, gains_here, normed_one_t, resid, normed_two, normed_two_t,
        cot, cot_t, qkv, context, inverse, cells_flipped, cells_twice, cell_tail,
    ) = forward(
        tokens, cotangent, norm_gains, attn_qkv, attn_out, ffn_in, ffn_out, position_tables,
        page_counts, layout_cells,
    )

    def pieces(full_columns, k):
        cuts = [slice(r * BLOCK, (r + 1) * BLOCK) for r in range(3)]
        cuts += [slice(3 * BLOCK, 3 * BLOCK + HALF), slice(3 * BLOCK + HALF, 4 * BLOCK)]
        return [full_columns[k, cut] for cut in cuts]

    att_pieces = [pieces(att_full, k) for k in range(RING)]
    ffn_pieces = [pieces(ffn_full, k) for k in range(RING)]
    saved = [(qkv[k], prob[2 * k : 2 * k + 2], context[k], inverse[k]) for k in range(RING)]

    hiddens, ffn_chunks = [], []
    for k in range(RING):
        hidden, *grads = ffn(normed_two, normed_two_t, cot, cot_t, ffn_pieces[k])
        hiddens.append(hidden)
        ffn_chunks.append(reduce_plane(grads, core))
    grad_mine = sum_products(
        "grad_normed_two", hiddens, slice(UNITS, FFW), ffn_pieces, slice(UNITS, FFW)
    )
    grad_other = send(grad_mine, TO_CORE)
    half_grad, low, low_t, gain_two = call(
        resid_grad_kernel, "resid_grad",
        [shaped((rows, 1024), F32), shaped((length, 1024)), shaped((1024, length)), shaped((1, 1024), F32)],
        [where, resid, cot, grad_mine, grad_other, gains_here], prefetch=1,
    )

    att_chunks, grad_qkvs, strips, fars, layouts = [], [], [], [], []
    for k in range(RING):
        back = attention_back(low, low_t, normed_one_t, att_pieces[k], saved[k], cells_twice, cell_tail, cells_flipped)
        grad_qkvs.append(back[0])
        att_chunks.append(reduce_plane(back[1:7], core))
        strips.append(back[7])
        fars.append(back[8])
        layouts.append(back[9])
    one_mine = sum_products("grad_normed_one", grad_qkvs, slice(0, 3 * HALF), att_pieces, slice(HALF, ATT))
    here = lax.dynamic_slice_in_dim(one_mine, core * rows, rows, axis=0)
    there = lax.dynamic_slice_in_dim(one_mine, (1 - core) * rows, rows, axis=0)
    one_other = send(there, TO_CORE)
    page_grad, page_grad_low, gain_one = call(
        tokens_grad_kernel, "tokens_grad",
        [shaped((rows, 1024), F32), shaped((rows, 1024)), shaped((1, 1024), F32)],
        [where, full, half_grad, here, one_other, gains_here], prefetch=1,
    )
    tokens_grad = jnp.where(native, page_grad, send(page_grad_low, SWAP).astype(F32))

    out_mine = sum_products("ffn_out", hiddens, slice(0, UNITS), ffn_pieces, slice(0, UNITS))
    out_here = lax.dynamic_slice_in_dim(out_mine, core * rows, rows, axis=0)
    out_there = lax.dynamic_slice_in_dim(out_mine, (1 - core) * rows, rows, axis=0)
    out_other = send(out_there, TO_CORE)
    page_out = call(
        layer_out_kernel, "layer_out", shaped((rows, 1024)),
        [where, resid, out_here, out_other], prefetch=1,
    )
    layer_out = jnp.where(native, page_out, send(page_out, SWAP))

    units = ffn_in.shape[2]
    inner_grad, outer_grad = call(
        ffn_grads_kernel, "ffn_grads",
        [shaped((2, HALF, units), F32), shaped((units, HALF), F32)],
        [where] + reduce_ring(ffn_chunks), prefetch=1,
    )
    qkv_grad, out_grad = call(
        attention_grads_kernel, "attention_grads",
        [shaped((3, HALF, 2 * HALF), F32), shaped((2 * HALF, HALF), F32)],
        [where] + reduce_ring(att_chunks), prefetch=1,
    )

    sums = table_sums(strips, fars, layouts)
    by_ring = sums.reshape(3, BUCKETS, RING, 2)
    by_ring = jnp.stack(
        [
            jnp.stack([by_ring[:, :, (q - z) % RING] for q in range(RING)], axis=2)
            for z in range(RING)
        ]
    )
    by_ring = lax.dynamic_index_in_dim(by_ring, ring, 0, keepdims=False)
    slots = jnp.where(jnp.arange(CORES)[None, None, None, :, None] == core, by_ring[:, :, :, None, :], 0.0)
    packed = jnp.concatenate(
        [gain_one.reshape(-1), gain_two.reshape(-1), slots.reshape(-1), jnp.zeros((512,), F32)]
    ).reshape(32, HALF)
    packed = packed + send(packed, TO_CORE)
    packed = packed + send(packed, TO_X)
    packed = packed + send(packed, TO_Y)
    packed = packed + (
        send(packed, FROM_RING[1]) + (send(packed, FROM_RING[2]) + send(packed, FROM_RING[3]))
    )
    flat = packed.reshape(-1)
    gains_grad = lax.dynamic_slice_in_dim(
        flat[:2048].reshape(2, 1024), (group * RING + ring) * 32, 32, axis=1
    )
    all_tables = flat[2048 : 2048 + 3 * BUCKETS * 16].reshape(3, BUCKETS, 16)
    tables_grad = lax.dynamic_slice(all_tables, (0, group * 4, ring * 4), (3, 4, 4))
    return (
        layer_out,
        tokens_grad,
        gains_grad,
        qkv_grad,
        out_grad,
        inner_grad,
        outer_grad,
        tables_grad,
    )


def solution(mesh):
    return jax.shard_map(
        page_body if page_plan(mesh) else general_body,
        mesh=mesh,
        in_specs=(
            P(("dp", "tensor"), None),
            P(),
            P(None, None, "tensor"),
            P("tensor", None),
            P(None, None, "tensor"),
            P("tensor", None),
            P(None, None, "tensor"),
            P("dp"),
            P(None, "dp"),
            P(("dp", "tensor"), None),
        ),
        out_specs=(
            P(("dp", "tensor"), None),
            P(("dp", "tensor"), None),
            P(None, ("dp", "tensor")),
            P(None, "dp", "tensor"),
            P("tensor", "dp"),
            P(None, "dp", "tensor"),
            P("tensor", "dp"),
            P(None, "dp", "tensor"),
        ),
        check_vma=False,
    )
```

```python
import math

import jax
import jax.numpy as jnp
import numpy as np
from jax import lax
from jax.experimental import pallas as pl
from jax.experimental.pallas import tpu as pltpu
from jax.sharding import PartitionSpec as P

HEAD_DIM = 64
BUCKETS = 32
REL_REACH = 128
CELLS = 64
PAGE_LEN = 1024


HIGHEST_PRECISION = lax.Precision.HIGHEST
TABLE_PRECISION = lax.Precision.HIGH
NORM_EPSILON = 1e-06
MASK_VALUE = -1e30


def bucket_table(offsets, bucket_total, max_reach):
    half_total = bucket_total // 2
    exact_limit = half_total // 2
    distance = np.abs(offsets).astype(np.int32)
    upper_side = (offsets > 0).astype(np.int32) * half_total
    safe_dist = np.maximum(distance, 1).astype(np.float32)
    ratio = np.log(safe_dist / np.float32(exact_limit)) / np.float32(
        math.log(max_reach / exact_limit)
    )
    far_bucket = exact_limit + np.floor(ratio * np.float32(half_total - exact_limit)).astype(
        np.int32
    )
    far_bucket = np.minimum(far_bucket, half_total - 1)
    return (upper_side + np.where(distance < exact_limit, distance, far_bucket)).astype(np.int32)


def offset_onehot(length):
    offsets = np.arange(2 * length - 1) - (length - 1)
    buckets = bucket_table(offsets, BUCKETS, REL_REACH)
    return jnp.asarray((buckets[:, None] == np.arange(BUCKETS)[None, :]).astype(np.float32))


def layout_onehot():
    cell_range = np.arange(CELLS)
    buckets = bucket_table(cell_range[None, :] - cell_range[:, None], BUCKETS, CELLS)
    return jnp.asarray(
        (buckets.reshape(-1)[:, None] == np.arange(BUCKETS)[None, :]).astype(np.float32)
    )


def gelu_tanh(values):
    return jax.nn.gelu(values, approximate=True)


def relative_bias(table_rows, length):
    values = jnp.dot(offset_onehot(length), table_rows, precision=HIGHEST_PRECISION).T
    heads_dev = values.shape[0]
    padded = jnp.pad(values, ((0, 0), (0, 1)))
    tiled = jnp.tile(padded, (1, length))
    skewed = tiled[:, : length * (2 * length - 1)].reshape(heads_dev, length, 2 * length - 1)
    return skewed[:, :, length - 1 :]


def relative_sums(dscore, length):
    heads_dev = dscore.shape[0]
    placed = jnp.pad(dscore, ((0, 0), (0, 0), (length - 1, 0)))
    flat = jnp.pad(placed.reshape(heads_dev, length * (2 * length - 1)), ((0, 0), (0, length)))
    return jnp.sum(flat.reshape(heads_dev, length, 2 * length), axis=1)[:, : 2 * length - 1]


def layout_values(tables):
    values = jnp.einsum("mn,snh->shm", layout_onehot(), tables[1:], precision=HIGHEST_PRECISION)
    return values.reshape(2, tables.shape[2], CELLS, CELLS)


def cell_onehots(page_cells):
    onehot = (page_cells[:, :, None] == jnp.arange(CELLS)[None, None, :]).astype(jnp.float32)
    length = page_cells.shape[1]
    joined = onehot.transpose(1, 0, 2).reshape(length, 2 * CELLS)
    return (onehot, joined)


def layout_bias(page_cells, lay_vals):
    onehot, joined = cell_onehots(page_cells)
    length = page_cells.shape[1]
    heads_dev = lay_vals.shape[1]
    rows_side = jnp.einsum("sia,shab->hisb", onehot, lay_vals, precision=TABLE_PRECISION)
    rows_side = rows_side.reshape(heads_dev, length, 2 * CELLS)
    return jnp.einsum("hic,jc->hij", rows_side, joined, precision=TABLE_PRECISION)


def layout_sums(dscore, page_cells):
    onehot, joined = cell_onehots(page_cells)
    length = page_cells.shape[1]
    heads_dev = dscore.shape[0]
    partial_rows = jnp.einsum("hij,jc->hic", dscore, joined, precision=TABLE_PRECISION)
    partial_rows = partial_rows.reshape(heads_dev, length, 2, CELLS)
    return jnp.einsum("sia,hisb->shab", onehot, partial_rows, precision=TABLE_PRECISION)


def page_scores(query, key_rows, count, page_cells, rel_bias, lay_vals):
    length = query.shape[0]
    scores = jnp.einsum("ihd,jhd->hij", query, key_rows, preferred_element_type=jnp.float32)
    scores = scores + rel_bias + layout_bias(page_cells, lay_vals)
    valid = jnp.arange(length) < count
    return jnp.where(valid[None, None, :], scores, MASK_VALUE)


def attend(projected, page_counts, layout_cells, rel_bias, lay_vals):
    total_rows = projected.shape[1]
    pages = page_counts.shape[0]
    length = total_rows // pages
    heads_dev = projected.shape[2] // HEAD_DIM
    split = projected.reshape(3, pages, length, heads_dev, HEAD_DIM)
    cells_pages = layout_cells.reshape(2, pages, length).transpose(1, 0, 2)

    def one_page(items):
        query, key_rows, value_rows, count, page_cells = items
        scores = page_scores(query, key_rows, count, page_cells, rel_bias, lay_vals)
        log_total = jax.nn.logsumexp(scores, axis=2)
        prob_low = jnp.exp(scores - log_total[:, :, None]).astype(jnp.bfloat16)
        context = jnp.einsum(
            "hij,jhd->ihd", prob_low, value_rows, preferred_element_type=jnp.float32
        )
        return (context.astype(jnp.bfloat16).reshape(length, heads_dev * HEAD_DIM), log_total)

    context, log_totals = lax.map(
        one_page, (split[0], split[1], split[2], page_counts, cells_pages)
    )
    return (context.reshape(total_rows, heads_dev * HEAD_DIM), log_totals)


def attend_back(projected, grad_context, log_totals, page_counts, layout_cells, rel_bias, lay_vals):
    total_rows = projected.shape[1]
    pages = page_counts.shape[0]
    length = total_rows // pages
    heads_dev = projected.shape[2] // HEAD_DIM
    split = projected.reshape(3, pages, length, heads_dev, HEAD_DIM)
    grad_split = grad_context.reshape(pages, length, heads_dev, HEAD_DIM)
    cells_pages = layout_cells.reshape(2, pages, length).transpose(1, 0, 2)

    def page_step(carry, items):
        rel_acc, lay_acc = carry
        query, key_rows, value_rows, grad_ctx, page_lse, count, page_cells = items
        scores = page_scores(query, key_rows, count, page_cells, rel_bias, lay_vals)
        prob = jnp.exp(scores - page_lse[:, :, None])
        grad_prob = jnp.einsum(
            "ihd,jhd->hij", grad_ctx, value_rows, preferred_element_type=jnp.float32
        )
        delta = jnp.sum(grad_prob * prob, axis=2, keepdims=True)
        dscore = prob * (grad_prob - delta)
        rel_acc = rel_acc + relative_sums(dscore, length)
        lay_acc = lay_acc + layout_sums(dscore, page_cells)
        score_low = dscore.astype(jnp.bfloat16)
        grad_query = jnp.einsum(
            "hij,jhd->ihd", score_low, key_rows, preferred_element_type=jnp.float32
        ).astype(jnp.bfloat16)
        grad_key = jnp.einsum(
            "hij,ihd->jhd", score_low, query, preferred_element_type=jnp.float32
        ).astype(jnp.bfloat16)
        grad_value = jnp.einsum(
            "hij,ihd->jhd", prob.astype(jnp.bfloat16), grad_ctx, preferred_element_type=jnp.float32
        ).astype(jnp.bfloat16)
        stacked = jnp.stack([grad_query, grad_key, grad_value]).reshape(
            3, length, heads_dev * HEAD_DIM
        )
        return ((rel_acc, lay_acc), stacked)

    init_sums = (
        jnp.zeros((heads_dev, 2 * length - 1), jnp.float32),
        jnp.zeros((2, heads_dev, CELLS, CELLS), jnp.float32),
    )
    (rel_acc, lay_acc), grads = lax.scan(
        page_step,
        init_sums,
        (split[0], split[1], split[2], grad_split, log_totals, page_counts, cells_pages),
    )
    grad_proj = grads.transpose(1, 0, 2, 3).reshape(3, total_rows, heads_dev * HEAD_DIM)
    rel_grad = jnp.dot(offset_onehot(length).T, rel_acc.T, precision=HIGHEST_PRECISION)
    lay_grad = jnp.einsum(
        "shm,mn->snh",
        lay_acc.reshape(2, heads_dev, CELLS * CELLS),
        layout_onehot(),
        precision=HIGHEST_PRECISION,
    )
    return (grad_proj, jnp.concatenate([rel_grad[None], lay_grad], axis=0))


def norm_back(rows, scale, gain, grad_normed):
    weighted = grad_normed * gain
    return scale * weighted - rows * scale**3 * jnp.mean(rows * weighted, axis=1, keepdims=True)


def forward_core(
    token_rows,
    norm_gains,
    attn_qkv,
    attn_out,
    ffn_in,
    page_counts,
    layout_cells,
    rel_bias,
    lay_vals,
):
    scale_one = lax.rsqrt(jnp.mean(token_rows * token_rows, axis=1, keepdims=True) + NORM_EPSILON)
    normed_one = (token_rows * scale_one * norm_gains[0]).astype(jnp.bfloat16)
    gathered_one = lax.all_gather(normed_one, "tensor", axis=0, tiled=True)
    projected = jnp.einsum(
        "td,cdk->ctk", gathered_one, attn_qkv, preferred_element_type=jnp.float32
    ).astype(jnp.bfloat16)
    context, log_totals = attend(projected, page_counts, layout_cells, rel_bias, lay_vals)
    attn_total = lax.psum_scatter(
        jnp.dot(context, attn_out, preferred_element_type=jnp.float32)
        .astype(jnp.bfloat16)
        .astype(jnp.float32)
        .astype(jnp.bfloat16),
        "tensor",
        scatter_dimension=0,
        tiled=True,
    ).astype(jnp.float32)
    resid = token_rows + attn_total
    scale_two = lax.rsqrt(jnp.mean(resid * resid, axis=1, keepdims=True) + NORM_EPSILON)
    normed_two = (resid * scale_two * norm_gains[1]).astype(jnp.bfloat16)
    gathered_two = lax.all_gather(normed_two, "tensor", axis=0, tiled=True)
    gate_up = jnp.einsum("td,cdf->ctf", gathered_two, ffn_in, preferred_element_type=jnp.float32)
    hidden = (gelu_tanh(gate_up[0]) * gate_up[1]).astype(jnp.bfloat16)
    return (
        scale_one,
        gathered_one,
        projected,
        context,
        log_totals,
        resid,
        scale_two,
        gathered_two,
        gate_up,
        hidden,
    )


def general_body(
    tokens,
    norm_gains,
    attn_qkv,
    attn_out,
    ffn_in,
    ffn_out,
    position_tables,
    page_counts,
    layout_cells,
    cotangent,
):
    token_rows = tokens.astype(jnp.float32)
    rel_bias = relative_bias(position_tables[0], PAGE_LEN)
    lay_vals = layout_values(position_tables)
    first = forward_core(
        token_rows,
        norm_gains,
        attn_qkv,
        attn_out,
        ffn_in,
        page_counts,
        layout_cells,
        rel_bias,
        lay_vals,
    )
    first_hidden = first[9]
    rows_part = first_hidden
    ffn_total = lax.psum_scatter(
        jnp.dot(rows_part, ffn_out, preferred_element_type=jnp.float32)
        .astype(jnp.bfloat16)
        .astype(jnp.float32)
        .astype(jnp.bfloat16),
        "tensor",
        scatter_dimension=0,
        tiled=True,
    ).astype(jnp.float32)
    layer_out = (first[5] + ffn_total).astype(jnp.bfloat16)
    cot_rows = lax.all_gather(cotangent, "tensor", axis=0, tiled=True)
    again_rows, cot_rows = lax.optimization_barrier((token_rows, cot_rows))
    saved = forward_core(
        again_rows,
        norm_gains,
        attn_qkv,
        attn_out,
        ffn_in,
        page_counts,
        layout_cells,
        rel_bias,
        lay_vals,
    )
    (
        scale_one,
        gathered_one,
        projected,
        context,
        log_totals,
        resid,
        scale_two,
        gathered_two,
        gate_up,
        hidden,
    ) = saved
    grad_hidden = jnp.einsum("td,fd->tf", cot_rows, ffn_out, preferred_element_type=jnp.float32)
    outer_grad = jnp.einsum("tf,td->fd", hidden, cot_rows, preferred_element_type=jnp.float32)
    gelu_value, gelu_back = jax.vjp(gelu_tanh, gate_up[0])
    grad_gate = gelu_back(grad_hidden * gate_up[1])[0].astype(jnp.bfloat16)
    grad_up = (grad_hidden * gelu_value).astype(jnp.bfloat16)
    grad_gate_up = jnp.stack([grad_gate, grad_up])
    inner_grad = jnp.einsum(
        "td,ctf->cdf", gathered_two, grad_gate_up, preferred_element_type=jnp.float32
    )
    rows_part = grad_gate_up
    grad_normed_two = lax.psum_scatter(
        jnp.einsum("ctf,cdf->td", rows_part, ffn_in, preferred_element_type=jnp.float32)
        .astype(jnp.bfloat16)
        .astype(jnp.float32)
        .astype(jnp.bfloat16),
        "tensor",
        scatter_dimension=0,
        tiled=True,
    ).astype(jnp.float32)
    grad_resid = cotangent.astype(jnp.float32) + norm_back(
        resid, scale_two, norm_gains[1], grad_normed_two
    )
    gain_two = jnp.sum(grad_normed_two * resid * scale_two, axis=0)
    resid_rows = lax.all_gather(grad_resid.astype(jnp.bfloat16), "tensor", axis=0, tiled=True)
    out_grad = jnp.einsum("tk,td->kd", context, resid_rows, preferred_element_type=jnp.float32)
    grad_context = jnp.einsum(
        "td,kd->tk", resid_rows, attn_out, preferred_element_type=jnp.float32
    ).astype(jnp.bfloat16)
    grad_proj, tables_grad = attend_back(
        projected, grad_context, log_totals, page_counts, layout_cells, rel_bias, lay_vals
    )
    qkv_grad = jnp.einsum(
        "td,ctk->cdk", gathered_one, grad_proj, preferred_element_type=jnp.float32
    )
    rows_part = grad_proj
    grad_normed_one = lax.psum_scatter(
        jnp.einsum("ctk,cdk->td", rows_part, attn_qkv, preferred_element_type=jnp.float32)
        .astype(jnp.bfloat16)
        .astype(jnp.float32)
        .astype(jnp.bfloat16),
        "tensor",
        scatter_dimension=0,
        tiled=True,
    ).astype(jnp.float32)
    tokens_grad = grad_resid + norm_back(token_rows, scale_one, norm_gains[0], grad_normed_one)
    gain_one = jnp.sum(grad_normed_one * token_rows * scale_one, axis=0)
    gains_grad = lax.psum_scatter(
        jnp.stack([gain_one, gain_two]), ("dp", "tensor"), scatter_dimension=1, tiled=True
    )
    qkv_summed, inner_summed, out_summed, outer_summed, tables_summed = (
        lax.psum_scatter(
            qkv_grad.astype(jnp.bfloat16), "dp", scatter_dimension=1, tiled=True
        ).astype(jnp.float32),
        lax.psum_scatter(
            inner_grad.astype(jnp.bfloat16), "dp", scatter_dimension=1, tiled=True
        ).astype(jnp.float32),
        lax.psum_scatter(
            out_grad.astype(jnp.bfloat16), "dp", scatter_dimension=1, tiled=True
        ).astype(jnp.float32),
        lax.psum_scatter(
            outer_grad.astype(jnp.bfloat16), "dp", scatter_dimension=1, tiled=True
        ).astype(jnp.float32),
        lax.psum_scatter(
            tables_grad.astype(jnp.bfloat16), "dp", scatter_dimension=1, tiled=True
        ).astype(jnp.float32),
    )
    return (
        layer_out,
        tokens_grad,
        gains_grad,
        qkv_summed,
        out_summed,
        inner_summed,
        outer_summed,
        tables_summed,
    )


PLANES = 4
RING = 4
CORES = 2
BLOCK = 256
HALF = 128
ATT = 512
UNITS = 384
FFW = 3 * UNITS
VMEM_BYTES = 60 * 1024 * 1024
F32 = jnp.float32
BF16 = jnp.bfloat16
NT = (((1,), (1,)), ((), ()))
TN = (((0,), (0,)), ((), ()))
NN = (((1,), (0,)), ((), ()))


def page_plan(mesh):
    return mesh.shape["dp"] == PLANES * CORES and mesh.shape["tensor"] == RING


def dot(left, right, dims=NN):
    return lax.dot_general(left, right, dims, preferred_element_type=F32)


def shaped(shape, dtype=BF16):
    return jax.ShapeDtypeStruct(shape, dtype)


def columns(plane, r):
    return pl.ds(pl.multiple_of((plane ^ r) * BLOCK, BLOCK), BLOCK)


def pair_lane(rows):
    return lax.broadcasted_iota(jnp.int32, (rows, 2 * HEAD_DIM), 1)


MESH = pl.DeviceIdType.MESH


def here():
    group, ring = lax.axis_index("dp"), lax.axis_index("tensor")
    return group // CORES, group % CORES, ring


def device(plane, core, ring):
    return (plane * CORES + core, ring)


def greet(partners):
    barrier = pltpu.get_barrier_semaphore()
    for partner in partners:
        pl.semaphore_signal(barrier, inc=1, device_id=partner, device_id_type=MESH)
    pl.semaphore_wait(barrier, len(partners))


class Lines:
    def __init__(self, send_sems, recv_sems):
        self.send_sems, self.recv_sems, self.open = send_sems, recv_sems, {}

    def make(self, name, source, target, partner):
        at = len(self.open)
        self.open[name] = pltpu.make_async_remote_copy(
            src_ref=source,
            dst_ref=target,
            send_sem=self.send_sems.at[at],
            recv_sem=self.recv_sems.at[at],
            device_id=partner,
            device_id_type=MESH,
        )
        return self.open[name]

    def start(self, name, source, target, partner):
        self.make(name, source, target, partner).start()

    def arrived(self, *names):
        for name in names:
            self.open[name].wait_recv()

    def sent(self, *names):
        for name in names or list(self.open):
            self.open[name].wait_send()


class Gather:
    def __init__(self, lines, tag, own, full, where):
        self.lines, self.tag, self.own, self.full = lines, tag, own, full
        self.plane, self.core, self.ring = where

    def ring_start(self, k):
        self.lines.start(
            (self.tag, "z", k),
            self.own.at[0:BLOCK],
            self.full.at[k, 0:BLOCK],
            device(self.plane, self.core, (self.ring + RING - k) % RING),
        )

    def plane_start(self, k):
        self.lines.arrived((self.tag, "z", k))
        for name, r in (("x", 1), ("y", 2)):
            self.lines.start(
                (self.tag, name, k),
                self.full.at[k, 0:BLOCK],
                self.full.at[k, r * BLOCK : (r + 1) * BLOCK],
                device(self.plane ^ r, self.core, self.ring),
            )

    def corner_start(self, k):
        for name, r, half, goal in (("x", 1, 0, 2), ("y", 2, 1, 1)):
            self.lines.arrived((self.tag, name, k))
            self.lines.start(
                (self.tag, "corner" + name, k),
                self.full.at[k, r * BLOCK + half * HALF : r * BLOCK + (half + 1) * HALF],
                self.full.at[k, 3 * BLOCK + half * HALF : 3 * BLOCK + (half + 1) * HALF],
                device(self.plane ^ goal, self.core, self.ring),
            )

    def finish(self, k):
        self.lines.arrived((self.tag, "cornerx", k), (self.tag, "cornery", k))


def own_attention(core, plane, qkv, out, target):
    for r in range(PLANES):
        rows, place = columns(plane, r), slice(r * BLOCK, (r + 1) * BLOCK)
        mine = pl.ds(pl.multiple_of(core * HALF, HALF), HALF)
        target[place, 0:HALF] = out[mine, rows].astype(F32).T.astype(BF16)
        for m in range(3):
            target[place, (m + 1) * HALF : (m + 2) * HALF] = qkv[m, rows, mine]


def own_ffn(core, plane, inner, outer, target):
    units = inner.shape[2]
    for which, first, count in ((0, 0, UNITS), (1, UNITS, units - UNITS)):

        @pl.when(core == which)
        def _():
            for r in range(PLANES):
                rows, place = columns(plane, r), slice(r * BLOCK, (r + 1) * BLOCK)
                parts = [outer[first : first + count, rows].astype(F32).T.astype(BF16)]
                parts += [inner[m, rows, first : first + count] for m in range(2)]
                for m, part in enumerate(parts):
                    target[place, m * UNITS : m * UNITS + count] = part
                    if count < UNITS:
                        target[place, m * UNITS + count : (m + 1) * UNITS] = jnp.zeros(
                            (BLOCK, UNITS - count), BF16
                        )


def place_rows(plane, core, near, far, full):
    rows = near.shape[0]
    for source, half in ((near, core), (far, 1 - core)):
        for r in range(PLANES):
            full[pl.ds(pl.multiple_of(half * rows, rows), rows), r * BLOCK : (r + 1) * BLOCK] = (
                source[:, columns(plane, r)]
            )


def split_bf16(values):
    parts = []
    for _ in range(3):
        part = values.astype(BF16)
        parts.append(part)
        values = values - part.astype(F32)
    return parts


def bias_pieces(tables, near_hot, cell_hot, layout, near):
    parts = split_bf16(tables)
    rel = sum(dot(part, near_hot[...]) for part in parts)
    cells = dot(parts[0], cell_hot[...])
    heads = tables.shape[0] // 3
    for h in range(heads):
        near[h] = rel[h : h + 1, :]
        toeplitz = []
        for axis in range(2):
            row = jnp.broadcast_to(cells[(axis + 1) * heads + h : (axis + 1) * heads + h + 1], (CELLS, HALF))
            toeplitz.append(pltpu.roll(row, CELLS, 1, stride=1, stride_axis=0))
        side = lax.broadcasted_iota(jnp.int32, (CELLS, HALF), 1)
        first = toeplitz[0]
        layout[h, 0:CELLS, 0:HALF] = jnp.where(
            side < CELLS, first, pltpu.roll(first, CELLS, 1)
        ).astype(BF16)
        layout[h, 0:CELLS, HALF:] = jnp.zeros((CELLS, HALF), BF16)
        layout[h, CELLS:, 0:HALF] = jnp.zeros((CELLS, HALF), BF16)
        layout[h, CELLS:, HALF:] = jnp.where(side < CELLS, toeplitz[1], 0.0).astype(BF16)


def forward_kernel(
    tokens, cot, gains, qkv_w, out_w, ffn_in, ffn_out, tables, ints, near_hot, cell_hot,
    att_full, ffn_full, prob_full, full, gains_here, normed_t, resid, normed_two, normed_two_t,
    cot_full, cot_t, qkv, context, inverse, cells_t, cells_twice, cell_tail,
    near_x, far_x, near_g, far_g, other_ints, table_parts, table_rows, layout, near,
    own_ffn_w, ffn_in_v, ffn_out_v, normed, weights, cells, queries, keys, scores, prob,
    mixed_all, out_rows, mine_out, other_out,
    send_sems, recv_sems, local_sems,
):
    plane, core, ring = where = here()
    native = core == ring % 2
    rows = tokens.shape[0]
    length = 2 * rows
    partner = device(plane, 1 - core, ring)
    swap = device(plane, 1 - core, ring ^ 1)
    ring_others = [device(plane, core, (ring + RING - k) % RING) for k in range(1, RING)]
    neighbours = [device(plane ^ 1, core, ring), device(plane ^ 2, core, ring)]
    lines = Lines(send_sems, recv_sems)
    load_in = pltpu.make_async_copy(ffn_in, ffn_in_v, local_sems.at[0])
    load_out = pltpu.make_async_copy(ffn_out, ffn_out_v, local_sems.at[1])
    load_in.start()
    load_out.start()
    greet([partner, swap] + ring_others + neighbours)

    def swap_rows(tag, source, near_rows, far_rows):
        lines.make((tag, "swap"), source, near_rows, swap)
        lines.make((tag, "give"), source, far_rows, partner)
        lines.make((tag, "pass"), near_rows, far_rows, partner)

        @pl.when(native)
        def _():
            lines.open[tag, "give"].start()
            keep = pltpu.make_async_copy(source, near_rows, local_sems.at[2])
            keep.start()
            keep.wait()

        @pl.when(jnp.logical_not(native))
        def _():
            lines.open[tag, "swap"].start()

    def swap_pass(tag):
        @pl.when(jnp.logical_not(native))
        def _():
            lines.arrived((tag, "swap"))
            lines.open[tag, "pass"].start()
            lines.arrived((tag, "give"))

        @pl.when(native)
        def _():
            lines.arrived((tag, "pass"))

    def swap_sent(tag):
        @pl.when(jnp.logical_not(native))
        def _():
            lines.sent((tag, "swap"), (tag, "pass"))

        @pl.when(native)
        def _():
            lines.sent((tag, "give"))

    swap_rows("x", tokens, near_x, far_x)
    lines.start("ints", ints, other_ints, partner)
    table_parts[0] = tables[...]
    for k in range(1, RING):
        lines.start(("tables", k), tables, table_parts.at[k], ring_others[k - 1])
    own_attention(core, plane, qkv_w, out_w, weights)
    keep_weights = pltpu.make_async_copy(weights, att_full.at[0], local_sems.at[3])
    keep_weights.start()
    att = Gather(lines, "att", weights, att_full, where)
    ffn = Gather(lines, "ffn", own_ffn_w, ffn_full, where)
    keep_weights.wait()
    att.own = att_full.at[0]
    for k in range(1, RING):
        att.ring_start(k)

    lines.arrived("ints")
    page = ring // 2
    picked = []
    for first in (0, 2, 4):
        own_row = ints[pl.ds(first + page, 1), :]
        other_row = other_ints[pl.ds(first + page, 1), :]
        picked.append(jnp.where(native, own_row, other_row))
    spot = lax.broadcasted_iota(jnp.int32, (CELLS, length), 0)
    cells_x = (jnp.broadcast_to(picked[0], (CELLS, length)) == spot).astype(F32)
    cells_y = (jnp.broadcast_to(picked[1], (CELLS, length)) == spot).astype(F32)
    position = lax.broadcasted_iota(jnp.int32, (CELLS, length), 1)
    tail = jnp.where((spot < 16) & (spot % 8 == position // HALF), 1.0, 0.0)
    hidden_key = (spot == 16) & (position >= jnp.broadcast_to(picked[2], (CELLS, length)))
    tail = jnp.where(hidden_key, MASK_VALUE, tail)
    flipped = CELLS - 1 - spot
    for axis in range(2):
        turned = (jnp.broadcast_to(picked[axis], (CELLS, length)) == flipped).astype(F32)
        cells_t[axis * CELLS : (axis + 1) * CELLS, :] = turned.astype(BF16)
    cells[...] = jnp.concatenate([cells_x, cells_y], axis=0).T.astype(BF16)
    cells_twice[...] = jnp.concatenate([cells_x, cells_x], axis=0).T.astype(BF16)
    cell_tail[...] = jnp.concatenate([cells_y, tail], axis=0).T.astype(BF16)
    for k in range(1, RING):
        lines.arrived(("tables", k))
    for k in range(RING):
        for axis in range(3):
            first = axis * 2 * RING + 2 * k
            table_rows[first : first + 2, :] = table_parts[k, pl.ds(4 * axis + 2 * core, 2), :]
    bias_pieces(table_rows[...], near_hot, cell_hot, layout, near)

    for r in range(PLANES):
        gains_here[:, r * BLOCK : (r + 1) * BLOCK] = gains[:, columns(plane, r)]
    swap_pass("x")
    place_rows(plane, core, near_x, far_x, full)
    for i in range(length // BLOCK):
        span = slice(i * BLOCK, (i + 1) * BLOCK)
        x = full[span, :].astype(F32)
        scale = lax.rsqrt(jnp.mean(x * x, axis=1, keepdims=True) + NORM_EPSILON)
        value = x * scale * gains_here[0:1, :]
        normed[span, :] = value.astype(BF16)
        normed_t[:, span] = value.T.astype(BF16)
    swap_rows("g", cot, near_g, far_g)

    def head(k, h):
        at = 2 * k + h
        lane = pair_lane(length)
        mine = (lane // HEAD_DIM) == h
        side = dot(cells[...], layout[at])
        queries[:, :HALF] = jnp.where(mine, qkv[k, :, :HALF].astype(F32), side[:, :HALF]).astype(BF16)
        block = lax.broadcasted_iota(jnp.int32, (length, HALF), 0) // HALF
        is_left, is_right = lane % 8 < block - 1, lane % 8 > block + 1
        left, right = near[at, :, 0:1], near[at, :, 4 * HALF - 1 :]
        left_high, right_high = left.astype(BF16).astype(F32), right.astype(BF16).astype(F32)
        high = jnp.where(is_left, left_high, jnp.where(is_right, right_high, 0.0))
        low = jnp.where(is_left, left - left_high, jnp.where(is_right, right - right_high, 0.0))
        ends = jnp.where(lane < HEAD_DIM, side[:, HALF:], jnp.where(lane == HEAD_DIM + 16, 1.0, 0.0))
        ends = jnp.where((lane >= HEAD_DIM) & (lane < HEAD_DIM + 8), high, ends)
        ends = jnp.where((lane >= HEAD_DIM + 8) & (lane < HEAD_DIM + 16), low, ends)
        queries[:, HALF:] = ends.astype(BF16)
        keys[:, :HALF] = jnp.where(
            mine, qkv[k, :, HALF : 2 * HALF].astype(F32), cells_twice[...].astype(F32)
        ).astype(BF16)
        keys[:, HALF:] = cell_tail[...]
        scores[...] = dot(queries[...], keys[...], NT)
        spread = jnp.broadcast_to(near[at], (HALF, 4 * HALF))
        strip = pltpu.roll(spread, 3 * HALF, 1, stride=1, stride_axis=0)[:, : 3 * HALF]
        count = length // HALF
        store = pltpu.make_async_copy(prob.at[h], prob_full.at[at], local_sems.at[4 + h])
        if k > 0:
            store.wait()
        for i in range(count):
            first, last = max(i - 1, 0), min(i + 2, count)
            part = strip[:, (first - i + 1) * HALF : (last - i + 1) * HALF]
            span, near_span = slice(i * HALF, (i + 1) * HALF), slice(first * HALF, last * HALF)
            scores[span, near_span] = scores[span, near_span] + part
            row = scores[span, :]
            top = jnp.max(row, axis=1, keepdims=True)
            prob[h, span, :] = jnp.exp(row - top).astype(BF16)
        values = jnp.where(mine, qkv[k, :, 2 * HALF :].astype(F32), 1.0).astype(BF16)
        mixed = dot(prob[h], values)
        inv = 1.0 / pltpu.roll(mixed, HEAD_DIM, 1)
        mixed = (mixed * inv).astype(BF16)
        store.start()
        if h == 0:
            context[k] = mixed
            inverse[k] = inv
        else:
            context[k] = jnp.where(mine, mixed.astype(F32), context[k].astype(F32)).astype(BF16)
            inverse[k] = jnp.where(mine, inv, inverse[k])

    def project(k):
        if k > 0:
            load = pltpu.make_async_copy(att_full.at[k], weights, local_sems.at[3])
            load.start()
            load.wait()
        qkv[k] = dot(normed[...], weights[:, HALF:]).astype(BF16)
        mixed_all[:, k * HALF : (k + 1) * HALF] = weights[:, 0:HALF]

    def after_head(k, h):
        if (k, h) == (0, 0):
            att.plane_start(2)
            att.corner_start(1)
        if (k, h) == (0, 1):
            att.plane_start(3)
            att.corner_start(2)
            for step in range(1, RING):
                ffn.ring_start(step)
        if (k, h) == (1, 0):
            att.corner_start(3)
        if (k, h) == (2, 0):
            swap_pass("g")
            ffn.plane_start(1)
        if (k, h) == (3, 0):
            ffn.plane_start(2)
            ffn.corner_start(1)

    for k in range(RING):
        if k > 0:
            att.finish(k)
        project(k)
        if k == 0:
            att.plane_start(1)
            load_in.wait()
            load_out.wait()
            own_ffn(core, plane, ffn_in_v, ffn_out_v, own_ffn_w)
        for h in range(2):
            head(k, h)
            after_head(k, h)

    for k in range(RING):
        out_rows[:, k * HALF : (k + 1) * HALF] = context[k]
    for i in range(length // BLOCK):
        span = slice(i * BLOCK, (i + 1) * BLOCK)
        mine_out[span, :] = dot(out_rows[span, :], mixed_all[...], NT).astype(BF16)
        lines.start(("out", i), mine_out.at[span], other_out.at[span], partner)
    place_rows(plane, core, near_g, far_g, cot_full)
    for r in range(PLANES):
        lanes = slice(r * BLOCK, (r + 1) * BLOCK)
        cot_t[lanes, :] = cot_full[:, lanes].astype(F32).T.astype(BF16)
    for i in range(length // BLOCK):
        span = slice(i * BLOCK, (i + 1) * BLOCK)
        lines.arrived(("out", i))
        row = full[span, :].astype(F32) + (
            mine_out[span, :].astype(F32) + other_out[span, :].astype(F32)
        )
        resid[span, :] = row
        scale = lax.rsqrt(jnp.mean(row * row, axis=1, keepdims=True) + NORM_EPSILON)
        value = row * scale * gains_here[1:2, :]
        normed_two[span, :] = value.astype(BF16)
        normed_two_t[:, span] = value.T.astype(BF16)

    ffn.plane_start(3)
    ffn.corner_start(2)
    ffn.finish(1)
    ffn.corner_start(3)
    ffn.finish(2)
    ffn.finish(3)
    for h in range(2):
        pltpu.make_async_copy(prob.at[h], prob_full.at[2 * (RING - 1) + h], local_sems.at[4 + h]).wait()
    swap_sent("x")
    swap_sent("g")
    lines.sent(*[name for name in lines.open if name[0] not in ("x", "g")])
    keep_ffn = pltpu.make_async_copy(own_ffn_w, ffn_full.at[0], local_sems.at[3])
    keep_ffn.start()
    keep_ffn.wait()


def hot(reach, width):
    offsets = np.arange(width) - width // 2
    found = bucket_table(offsets, BUCKETS, reach)[None, :] == np.arange(HALF)[:, None]
    return jnp.asarray(found.astype(np.float32), BF16)


def forward(tokens, cotangent, gains, qkv_w, out_w, ffn_in, ffn_out, position_tables, page_counts, layout_cells):
    rows = tokens.shape[0]
    length = 2 * rows
    features = PLANES * BLOCK
    tables = position_tables.transpose(0, 2, 1).reshape(12, BUCKETS)
    tables = jnp.pad(tables, ((0, 4), (0, HALF - BUCKETS)))
    ints = jnp.concatenate(
        [
            layout_cells.reshape(4, length),
            jnp.broadcast_to(page_counts[:, None], (2, length)),
            jnp.zeros((2, length), jnp.int32),
        ]
    )
    args = [tokens, cotangent, gains, qkv_w, out_w, ffn_in, ffn_out, tables, ints]
    args += [hot(REL_REACH, 4 * HALF), hot(CELLS, HALF)]
    whole = pl.BlockSpec(memory_space=pltpu.VMEM)
    outside = pl.BlockSpec(memory_space=pl.ANY)
    outs = [
        shaped((RING, features, ATT)), shaped((RING, features, FFW)), shaped((2 * RING, length, length)),
        shaped((length, features)), shaped((2, features), F32), shaped((features, length)),
        shaped((length, features), F32), shaped((length, features)), shaped((features, length)),
        shaped((length, features)), shaped((features, length)),
        shaped((RING, length, 3 * HALF)), shaped((RING, length, HALF)), shaped((RING, length, HALF), F32),
        shaped((HALF, length)), shaped((length, HALF)), shaped((length, HALF)),
    ]
    scratch = [pltpu.VMEM((rows, features), BF16)] * 4 + [
        pltpu.VMEM(ints.shape, jnp.int32),
        pltpu.VMEM((RING,) + tables.shape, F32),
        pltpu.VMEM((6 * RING, HALF), F32),
        pltpu.VMEM((2 * RING, HALF, 2 * HALF), BF16),
        pltpu.VMEM((2 * RING, 1, 4 * HALF), F32),
        pltpu.VMEM((features, FFW), BF16),
        pltpu.VMEM(ffn_in.shape, BF16),
        pltpu.VMEM(ffn_out.shape, BF16),
        pltpu.VMEM((length, features), BF16),
        pltpu.VMEM((features, ATT), BF16),
        pltpu.VMEM((length, HALF), BF16),
        pltpu.VMEM((length, 2 * HALF), BF16),
        pltpu.VMEM((length, 2 * HALF), BF16),
        pltpu.VMEM((length, length), F32),
        pltpu.VMEM((2, length, length), BF16),
        pltpu.VMEM((features, RING * HALF), BF16),
        pltpu.VMEM((length, RING * HALF), BF16),
        pltpu.VMEM((length, features), BF16),
        pltpu.VMEM((length, features), BF16),
        pltpu.SemaphoreType.DMA((48,)),
        pltpu.SemaphoreType.DMA((48,)),
        pltpu.SemaphoreType.DMA((6,)),
    ]
    in_specs = [whole, outside, whole, whole, whole, outside, outside] + [whole] * 4
    out_specs = [outside] * 3 + [whole] * 14
    return pl.pallas_call(
        forward_kernel,
        out_shape=outs,
        in_specs=in_specs,
        out_specs=out_specs,
        scratch_shapes=scratch,
        name="forward",
        cost_estimate=pl.CostEstimate(flops=10**10, bytes_accessed=10**8, transcendentals=0),
        compiler_params=pltpu.CompilerParams(
            vmem_limit_bytes=63 * 1024 * 1024, collective_id=0, has_side_effects=True
        ),
    )(*args)


def gelu_parts(gate):
    square = gate * gate
    ratio = math.sqrt(2.0 / math.pi)
    bend = jnp.tanh(ratio * gate * (1.0 + 0.044715 * square))
    half_gate = 0.5 * gate
    value = half_gate + half_gate * bend
    slope = 0.5 + 0.5 * bend + half_gate * (1.0 - bend * bend) * (
        ratio * (1.0 + 3.0 * 0.044715 * square)
    )
    return value, slope


def middle_kernel(
    normed, normed_t, cot, cot_t, resid, gains_here, ffn_full,
    grads_full, low, low_t, half_grad, page_out, gain,
    weights, hidden, grads, total_in, total_out, mine, other, mine_out, other_out,
    send_sems, recv_sems, local_sems,
):
    plane, core, ring = here()
    partner = device(plane, 1 - core, ring)
    lines = Lines(send_sems, recv_sems)
    length = normed.shape[0]
    rows = length // 2
    blocks = length // BLOCK

    def load(k):
        return pltpu.make_async_copy(ffn_full.at[k], weights.at[k % 2], local_sems.at[k % 2])

    def store(k):
        return pltpu.make_async_copy(grads.at[k % 2], grads_full.at[k], local_sems.at[2 + k % 2])

    load(0).start()
    greet([partner])
    for k in range(RING):
        if k + 1 < RING:
            load(k + 1).start()
        load(k).wait()
        w = weights.at[k % 2]
        for i in range(blocks):
            span = slice(i * BLOCK, (i + 1) * BLOCK)
            both = dot(normed[span, :], w[:, UNITS:])
            grad_hidden = dot(cot[span, :], w[:, :UNITS])
            gate, up = both[:, :UNITS], both[:, UNITS:]
            value, slope = gelu_parts(gate)
            hidden[span, :UNITS] = (value * up).astype(BF16)
            hidden[span, UNITS : 2 * UNITS] = (grad_hidden * up * slope).astype(BF16)
            hidden[span, 2 * UNITS :] = (grad_hidden * value).astype(BF16)
            part_in = dot(hidden[span, UNITS:], w[:, UNITS:], NT)
            part_out = dot(hidden[span, :UNITS], w[:, :UNITS], NT)
            if k > 0:
                part_in = total_in[span, :] + part_in
                part_out = total_out[span, :] + part_out
            if k + 1 < RING:
                total_in[span, :] = part_in
                total_out[span, :] = part_out
            else:
                mine[span, :] = part_in.astype(BF16)
                lines.start(("in", i), mine.at[span], other.at[span], partner)
                mine_out[span, :] = part_out.astype(BF16)
        if k + 1 == RING:
            far = pl.ds(pl.multiple_of((1 - core) * rows, rows), rows)
            lines.start("out", mine_out.at[far], other_out, partner)
        if k >= 2:
            store(k - 2).wait()
        for i in range(2):
            span = slice(i * 2 * BLOCK, (i + 1) * 2 * BLOCK)
            grads[k % 2, span, :UNITS] = dot(cot_t[span, :], hidden[:, :UNITS]).astype(BF16)
            grads[k % 2, span, UNITS:] = dot(normed_t[span, :], hidden[:, UNITS:]).astype(BF16)
        store(k).start()

    total = jnp.zeros((1, resid.shape[1]), F32)
    for i in range(blocks):
        span = slice(i * BLOCK, (i + 1) * BLOCK)
        lines.arrived(("in", i))
        row = resid[span, :]
        grad = mine[span, :].astype(F32) + other[span, :].astype(F32)
        scale = lax.rsqrt(jnp.mean(row * row, axis=1, keepdims=True) + NORM_EPSILON)
        weighted = grad * gains_here[1:2, :]
        center = jnp.mean(row * weighted, axis=1, keepdims=True)
        value = cot[span, :].astype(F32) + scale * weighted - row * (scale * scale * scale * center)
        low[span, :] = value.astype(BF16)
        low_t[:, span] = value.T.astype(BF16)
        in_half = core == (i * BLOCK) // rows
        total = total + jnp.where(in_half, jnp.sum(grad * row * scale, axis=0, keepdims=True), 0.0)

        @pl.when(in_half)
        def _():
            first = (i * BLOCK) % rows
            half_grad[first : first + BLOCK, :] = value

    for r in range(PLANES):
        gain[:, columns(plane, r)] = total[:, r * BLOCK : (r + 1) * BLOCK]
    lines.arrived("out")
    for i in range(rows // BLOCK):
        span = slice(i * BLOCK, (i + 1) * BLOCK)
        near = pl.ds(pl.multiple_of(core * rows + i * BLOCK, BLOCK), BLOCK)
        row = resid[near, :] + (mine_out[near, :].astype(F32) + other_out[span, :].astype(F32))
        for r in range(PLANES):
            page_out[span, columns(plane, r)] = row[:, r * BLOCK : (r + 1) * BLOCK].astype(BF16)
    store(RING - 2).wait()
    store(RING - 1).wait()
    lines.sent()


def middle(normed, normed_t, cot, cot_t, resid, gains_here, ffn_full):
    length, features = normed.shape
    rows = length // 2
    whole = pl.BlockSpec(memory_space=pltpu.VMEM)
    outside = pl.BlockSpec(memory_space=pl.ANY)
    return pl.pallas_call(
        middle_kernel,
        out_shape=[
            shaped((RING, features, FFW)), shaped((length, features)), shaped((features, length)),
            shaped((rows, features), F32), shaped((rows, features)), shaped((1, features), F32),
        ],
        in_specs=[whole] * 6 + [outside],
        out_specs=[outside] + [whole] * 5,
        scratch_shapes=[
            pltpu.VMEM((2, features, FFW), BF16),
            pltpu.VMEM((length, FFW), BF16),
            pltpu.VMEM((2, features, FFW), BF16),
            pltpu.VMEM((length, features), F32),
            pltpu.VMEM((length, features), F32),
            pltpu.VMEM((length, features), BF16),
            pltpu.VMEM((length, features), BF16),
            pltpu.VMEM((length, features), BF16),
            pltpu.VMEM((rows, features), BF16),
            pltpu.SemaphoreType.DMA((8,)),
            pltpu.SemaphoreType.DMA((8,)),
            pltpu.SemaphoreType.DMA((4,)),
        ],
        name="middle",
        cost_estimate=pl.CostEstimate(flops=27 * 10**9, bytes_accessed=10**8, transcendentals=0),
        compiler_params=pltpu.CompilerParams(
            vmem_limit_bytes=63 * 1024 * 1024, collective_id=1, has_side_effects=True
        ),
    )(normed, normed_t, cot, cot_t, resid, gains_here, ffn_full)


class Scatter:
    def __init__(self, lines, tag, k, grads, kept, buffers, where):
        self.lines, self.tag, self.k, self.grads, self.kept = lines, tag, k, grads, kept
        self.from_x, self.from_y, self.late, self.same, self.cross = buffers
        self.plane, self.core, self.ring = where
        self.to_x = device(self.plane ^ 1, self.core, self.ring)
        self.to_y = device(self.plane ^ 2, self.core, self.ring)

    def name(self, step):
        return (self.tag, step, self.k)

    def rows(self, r, half):
        return slice(r * BLOCK + half * HALF, r * BLOCK + (half + 1) * HALF)

    def start(self):
        k = self.k
        for step, r, half, target, goal in (
            ("x1", 3, 0, self.from_x.at[k, 1], self.to_x),
            ("y1", 3, 1, self.from_y.at[k, 1], self.to_y),
            ("x0", 1, 0, self.from_x.at[k, 0], self.to_x),
            ("y0", 2, 1, self.from_y.at[k, 0], self.to_y),
        ):
            self.lines.start(self.name(step), self.grads.at[self.rows(r, half)], target, goal)

    def middle(self):
        k = self.k
        self.lines.arrived(self.name("x1"), self.name("y1"))
        for source, r, half, at, goal, step in (
            (self.from_x, 2, 0, 0, self.to_y, "late0"),
            (self.from_y, 1, 1, 1, self.to_x, "late1"),
        ):
            kept = self.kept(r, half).astype(F32)
            source[k, 1] = (kept + source[k, 1].astype(F32)).astype(BF16)
            self.lines.start(self.name(step), source.at[k, 1], self.late.at[k, at], goal)

    def last(self):
        k, late = self.k, self.late
        self.lines.arrived(*[self.name(step) for step in ("x0", "y0", "late0", "late1")])
        upper = self.kept(0, 0).astype(F32) + self.from_x[k, 0].astype(F32) + late[k, 0].astype(F32)
        lower = self.kept(0, 1).astype(F32) + self.from_y[k, 0].astype(F32) + late[k, 1].astype(F32)
        late[k, 0] = jnp.where(self.core == 0, upper, lower).astype(BF16)
        late[k, 1] = jnp.where(self.core == 0, lower, upper).astype(BF16)
        goal = (self.ring + k) % RING
        if k > 0:
            self.lines.start(
                self.name("same"), late.at[k, 0], self.same.at[k - 1], device(self.plane, self.core, goal)
            )
        self.lines.start(
            self.name("cross"), late.at[k, 1], self.cross.at[k], device(self.plane, 1 - self.core, goal)
        )


def sum_ring(lines, tag, late, same, cross):
    for k in range(RING):
        if k > 0:
            lines.arrived((tag, "same", k))
        lines.arrived((tag, "cross", k))
    mine = late[0, 0].astype(F32)
    for k in range(1, RING):
        mine = mine + same[k - 1].astype(F32)
    other = cross[0].astype(F32)
    for k in range(1, RING):
        other = other + cross[k].astype(F32)
    return mine, other


def backward_kernel(
    low, low_t, normed_t, half_grad, full, gains_here, qkv, context, inverse,
    cells_t, cells_twice, cell_tail, near_hot, cell_hot, gain_two,
    att_full, prob_full, ffn_grads, page_out,
    layer_out, tokens_grad, qkv_grad, out_grad, inner_grad, outer_grad, small_out,
    weights, prob, scaled, scaled_low, keys, dscores, grad_qkv, att_grads, total, mine_half, far_half,
    other_half, page_low, swapped, ffn_kept,
    att_x, att_y, att_late, att_same, att_cross, ffn_x, ffn_y, ffn_late, ffn_same, ffn_cross,
    diag_near, diag_cell, gain_one, small, small_ring, small_plane, small_core,
    send_sems, recv_sems, local_sems,
):
    plane, core, ring = where = here()
    native = core == ring % 2
    length = low.shape[0]
    rows = length // 2
    count = length // HALF
    partner = device(plane, 1 - core, ring)
    swap = device(plane, 1 - core, ring ^ 1)
    partners = [partner, swap, device(plane ^ 1, core, ring), device(plane ^ 2, core, ring)]
    for k in range(1, RING):
        partners += [device(plane, core, (ring + k) % RING), device(plane, 1 - core, (ring + k) % RING)]
    lines = Lines(send_sems, recv_sems)

    def load_prob(at):
        return pltpu.make_async_copy(prob_full.at[at], prob.at[at % 2], local_sems.at[at % 2])

    def load_weights(k):
        return pltpu.make_async_copy(att_full.at[k], weights.at[k % 2], local_sems.at[2 + k % 2])

    def load_kept(k):
        return [
            pltpu.make_async_copy(
                ffn_grads.at[k, first : first + BLOCK],
                ffn_kept.at[k % 2, at : at + BLOCK],
                local_sems.at[4 + 2 * (k % 2) + i],
            )
            for i, (first, at) in enumerate(((0, 0), (3 * HALF, BLOCK)))
        ]

    load_prob(0).start()
    load_prob(1).start()
    load_weights(0).start()
    goals = [partner, device(plane ^ 1, core, ring), device(plane ^ 2, core, ring)] + partners[4:]
    greet(goals)

    def kept_ffn(k):
        spots = {(0, 0): 0, (0, 1): HALF, (1, 1): BLOCK, (2, 0): BLOCK + HALF}
        return lambda r, half: ffn_kept[k % 2, spots[r, half] : spots[r, half] + HALF]

    def kept_att(k):
        def read(r, half):
            first = r * BLOCK + half * HALF
            return att_grads[k, first : first + HALF]

        return read

    ffn = [
        Scatter(lines, "ffn", k, ffn_grads.at[k], kept_ffn(k), (ffn_x, ffn_y, ffn_late, ffn_same, ffn_cross), where)
        for k in range(RING)
    ]
    att = [
        Scatter(lines, "att", k, att_grads.at[k], kept_att(k), (att_x, att_y, att_late, att_same, att_cross), where)
        for k in range(RING)
    ]

    def ffn_start(k):
        for copy in load_kept(k):
            copy.start()
        ffn[k].start()

    def ffn_middle(k):
        for copy in load_kept(k):
            copy.wait()
        ffn[k].middle()

    ffn_start(0)
    ffn_start(1)
    lines.make("layer", page_out, layer_out, swap)
    keep_layer = pltpu.make_async_copy(page_out, layer_out, local_sems.at[8])

    @pl.when(native)
    def _():
        keep_layer.start()

    @pl.when(jnp.logical_not(native))
    def _():
        lines.open["layer"].start()

    lane = pair_lane(length)
    row_block = lax.broadcasted_iota(jnp.int32, (length, HALF), 0) // HALF
    flip_at = lax.broadcasted_iota(jnp.int32, (HALF, HALF), 0)
    flip_to = lax.broadcasted_iota(jnp.int32, (HALF, HALF), 1)
    flip = jnp.where(flip_at + flip_to == HALF - 1, 1.0, 0.0).astype(BF16)

    def enter(k):
        if k + 1 < RING:
            load_weights(k + 1).start()
        load_weights(k).wait()
        grad_context = dot(low[...], weights[k % 2, :, 0:HALF]).astype(BF16).astype(F32)
        value = grad_context * inverse[k]
        scaled[...] = value
        scaled_low[...] = value.astype(BF16)

    def head(k, h):
        at = 2 * k + h
        mine = (lane // HEAD_DIM) == h
        value = scaled[...]
        delta = -jnp.sum(
            jnp.where(mine, value * context[k].astype(F32), 0.0), axis=1, keepdims=True
        )
        delta_high = delta.astype(BF16).astype(F32)
        spare = HEAD_DIM * (1 - h)
        fill = jnp.where(lane == spare + 1, delta - delta_high, 0.0)
        left = jnp.where(mine, value, jnp.where(lane == spare, delta_high, fill)).astype(BF16)
        ones = jnp.where((lane == spare) | (lane == spare + 1), 1.0, 0.0)
        right = jnp.where(mine, qkv[k, :, 2 * HALF :].astype(F32), ones).astype(BF16)
        load_prob(at).wait()
        strips = [jnp.zeros((HALF, HALF), F32) for _ in range(3)]
        for i in range(length // BLOCK):
            span = slice(i * BLOCK, (i + 1) * BLOCK)
            dscore = prob[at % 2, span, :].astype(F32) * dot(left[span, :], right, NT)
            dscores[span, :] = dscore.astype(BF16)
            for part in range(BLOCK // HALF):
                for step in range(3):
                    block = i * (BLOCK // HALF) + part + step - 1
                    if 0 <= block < count:
                        strips[step] = strips[step] + dscore[
                            part * HALF : (part + 1) * HALF, block * HALF : (block + 1) * HALF
                        ]
        keys[:, :HALF] = jnp.where(
            mine, qkv[k, :, HALF : 2 * HALF].astype(F32), cells_twice[...].astype(F32)
        ).astype(BF16)
        keys[:, HALF:] = cell_tail[...]
        grad_left = dot(dscores[...], keys[...])
        grad_key = dot(dscores[...], qkv[k, :, :HALF], TN)
        grad_value = dot(prob[at % 2], scaled_low[...], TN)
        if at + 2 < 2 * RING:
            load_prob(at + 2).start()
        for m, new in enumerate((grad_left[:, :HALF], grad_key, grad_value)):
            lanes = slice(m * HALF, (m + 1) * HALF)
            if h == 1:
                new = jnp.where(mine, new, grad_qkv[:, lanes].astype(F32))
            grad_qkv[:, lanes] = new.astype(BF16)

        skewed = jnp.zeros((HALF, 3 * HALF), F32)
        strip = jnp.concatenate(strips, axis=1)
        for part in split_bf16(strip):
            skewed = skewed + dot(flip, part)
        skewed = jnp.concatenate([skewed, jnp.zeros((HALF, HALF), F32)], axis=1)
        sums = jnp.sum(pltpu.roll(skewed, 1, 1, stride=1, stride_axis=0), axis=0, keepdims=True)
        tail = grad_left[:, HALF:]
        in_tail = (lane >= HEAD_DIM) & (lane < HEAD_DIM + 8)
        far_left = jnp.sum(jnp.where(in_tail & (lane % 8 < row_block - 1), tail, 0.0), axis=0, keepdims=True)
        far_right = jnp.sum(jnp.where(in_tail & (lane % 8 > row_block + 1), tail, 0.0), axis=0, keepdims=True)
        wide = lax.broadcasted_iota(jnp.int32, (1, 4 * HALF), 1)
        sums = sums + jnp.where(wide == 0, jnp.sum(far_left, axis=1, keepdims=True), 0.0)
        sums = sums + jnp.where(wide == 4 * HALF - 1, jnp.sum(far_right, axis=1, keepdims=True), 0.0)
        diag_near[at : at + 1, :] = sums
        by_cell = grad_left[:, :HALF]
        by_cell = jnp.where(mine, pltpu.roll(by_cell, HEAD_DIM, 1), by_cell)
        for axis, table in enumerate((by_cell, tail)):
            table_high = table.astype(BF16)
            rest = (table - table_high.astype(F32)).astype(BF16)
            side = cells_t[axis * CELLS : (axis + 1) * CELLS, :]
            grid = dot(side, table_high) + dot(side, rest)
            cell_lane = lax.broadcasted_iota(jnp.int32, (CELLS, HALF), 1)
            grid = jnp.where(cell_lane < CELLS, grid, 0.0)
            grid = pltpu.roll(grid, 1, 1, stride=1, stride_axis=0)
            row = axis * 2 * RING + at
            diag_cell[row : row + 1, :] = jnp.sum(grid, axis=0, keepdims=True)

    def leave(k):
        w = weights[k % 2, :, HALF:]
        att_grads[k, :, 0:HALF] = dot(low_t[...], context[k]).astype(BF16)
        att_grads[k, :, HALF:] = dot(normed_t[...], grad_qkv[...]).astype(BF16)
        for i in range(length // BLOCK):
            span = slice(i * BLOCK, (i + 1) * BLOCK)
            part = dot(grad_qkv[span, :], w, NT)
            total[span, :] = part if k == 0 else total[span, :] + part

    enter(0)
    head(0, 0)
    head(0, 1)
    ffn_middle(0)
    leave(0)
    enter(1)
    head(1, 0)
    ffn_middle(1)
    ffn[0].last()
    ffn_start(2)
    head(1, 1)
    leave(1)
    enter(2)
    head(2, 0)
    ffn[1].last()
    ffn_start(3)
    head(2, 1)
    ffn_middle(2)
    att[0].start()
    att[1].start()
    leave(2)
    enter(3)
    head(3, 0)
    ffn[2].last()
    att[2].start()
    head(3, 1)
    ffn_middle(3)
    leave(3)
    att[3].start()

    near = pl.ds(pl.multiple_of(core * rows, rows), rows)
    far = pl.ds(pl.multiple_of((1 - core) * rows, rows), rows)
    far_half[...] = total[far, :].astype(BF16)
    lines.start("half", far_half, other_half, partner)
    mine_half[...] = total[near, :].astype(BF16)
    att[0].middle()
    att[1].middle()
    lines.arrived("half")
    gain = jnp.zeros((1, full.shape[1]), F32)
    for i in range(rows // BLOCK):
        span = slice(i * BLOCK, (i + 1) * BLOCK)
        x = full[pl.ds(pl.multiple_of(core * rows + i * BLOCK, BLOCK), BLOCK), :].astype(F32)
        grad = mine_half[span, :].astype(F32) + other_half[span, :].astype(F32)
        scale = lax.rsqrt(jnp.mean(x * x, axis=1, keepdims=True) + NORM_EPSILON)
        weighted = grad * gains_here[0:1, :]
        center = jnp.mean(x * weighted, axis=1, keepdims=True)
        value = half_grad[span, :] + scale * weighted - x * (scale * scale * scale * center)
        gain = gain + jnp.sum(grad * x * scale, axis=0, keepdims=True)
        for r in range(PLANES):
            block = value[:, r * BLOCK : (r + 1) * BLOCK]
            tokens_grad[span, columns(plane, r)] = block
            page_low[span, columns(plane, r)] = block.astype(BF16)
    for r in range(PLANES):
        gain_one[:, columns(plane, r)] = gain[:, r * BLOCK : (r + 1) * BLOCK]
    lines.make("swap", page_low, swapped, swap)

    @pl.when(jnp.logical_not(native))
    def _():
        lines.open["swap"].start()

    near_sums = sum(dot(part, near_hot[...], NT) for part in split_bf16(diag_near[...]))
    cell_sums = sum(dot(part, cell_hot[...], NT) for part in split_bf16(diag_cell[...]))
    for k in range(RING):
        small[k, 0:2, :] = near_sums[2 * k : 2 * k + 2, :]
        for axis in range(2):
            first = axis * 2 * RING + 2 * k
            small[k, 2 * axis + 2 : 2 * axis + 4, :] = cell_sums[first : first + 2, :]
        small[k, 6:8, :] = jnp.zeros((2, HALF), F32)
        for j in range(8):
            lanes = slice(j * HALF, (j + 1) * HALF)
            small[k, 8 + j : 9 + j, :] = gain_one[:, lanes]
            small[k, 16 + j : 17 + j, :] = gain_two[:, lanes]
    for k in range(1, RING):
        lines.start(("small", k), small.at[k], small_ring.at[k], device(plane, core, (ring + k) % RING))
    ffn[3].last()
    att[0].last()
    att[2].middle()
    att[1].last()
    att[3].middle()
    for k in range(1, RING):
        lines.arrived(("small", k))
    small_plane[0] = small[0] + (small_ring[1] + (small_ring[2] + small_ring[3]))
    lines.start("smallx", small_plane.at[0], small_plane.at[1], device(plane ^ 1, core, ring))
    att[2].last()
    lines.arrived("smallx")
    small_plane[2] = small_plane[0] + small_plane[1]
    lines.start("smally", small_plane.at[2], small_plane.at[3], device(plane ^ 2, core, ring))
    att[3].last()
    lines.arrived("smally")
    small_core[0] = small_plane[2] + small_plane[3]
    lines.start("smallc", small_core.at[0], small_core.at[1], partner)

    mine, other = sum_ring(lines, "ffn", ffn_late, ffn_same, ffn_cross)
    rest = inner_grad.shape[2] - UNITS
    first_core = jnp.where(core == 0, mine, other)
    second_core = jnp.where(core == 0, other, mine)
    for m in range(2):
        at = (m + 1) * UNITS
        inner_grad[m, :, 0:UNITS] = first_core[:, at : at + UNITS]
        inner_grad[m, :, UNITS : UNITS + rest] = second_core[:, at : at + rest]
    outer_grad[0:UNITS, :] = first_core[:, 0:UNITS].T
    outer_grad[UNITS : UNITS + rest, :] = second_core[:, 0:UNITS].T[0:rest]

    @pl.when(jnp.logical_not(native))
    def _():
        lines.arrived("swap")
        tokens_grad[...] = swapped[...].astype(F32)

    mine, other = sum_ring(lines, "att", att_late, att_same, att_cross)
    first_core = jnp.where(core == 0, mine, other)
    second_core = jnp.where(core == 0, other, mine)
    for m in range(3):
        lanes = slice((m + 1) * HALF, (m + 2) * HALF)
        qkv_grad[m, :, 0:HALF] = first_core[:, lanes]
        qkv_grad[m, :, HALF : 2 * HALF] = second_core[:, lanes]
    out_grad[0:HALF, :] = first_core[:, 0:HALF].T
    out_grad[HALF : 2 * HALF, :] = second_core[:, 0:HALF].T

    lines.arrived("smallc")
    low_core = jnp.where(core == 0, small_core[0], small_core[1])
    high_core = jnp.where(core == 0, small_core[1], small_core[0])
    small_out[0] = low_core
    small_out[1] = high_core

    @pl.when(native)
    def _():
        keep_layer.wait()

    @pl.when(jnp.logical_not(native))
    def _():
        lines.arrived("layer")
        lines.sent("layer", "swap")

    lines.sent(*[name for name in lines.open if name not in ("layer", "swap")])


def backward(low, low_t, normed_t, half_grad, full, gains_here, qkv, context, inverse, cells_t, cells_twice, cell_tail, gain_two, att_full, prob_full, ffn_grads, page_out, units):
    length, features = low.shape
    rows = length // 2
    whole = pl.BlockSpec(memory_space=pltpu.VMEM)
    outside = pl.BlockSpec(memory_space=pl.ANY)
    args = [low, low_t, normed_t, half_grad, full, gains_here, qkv, context, inverse]
    args += [cells_t, cells_twice, cell_tail, hot(REL_REACH, 4 * HALF), hot(CELLS, HALF), gain_two]
    args += [att_full, prob_full, ffn_grads, page_out]

    def buffers(width):
        return [
            pltpu.VMEM((RING, 2, HALF, width), BF16),
            pltpu.VMEM((RING, 2, HALF, width), BF16),
            pltpu.VMEM((RING, 2, HALF, width), BF16),
            pltpu.VMEM((RING - 1, HALF, width), BF16),
            pltpu.VMEM((RING, HALF, width), BF16),
        ]

    return pl.pallas_call(
        backward_kernel,
        out_shape=[
            shaped((rows, features)), shaped((rows, features), F32),
            shaped((3, HALF, 2 * HALF), F32), shaped((2 * HALF, HALF), F32),
            shaped((2, HALF, units), F32), shaped((units, HALF), F32), shaped((2, 24, HALF), F32),
        ],
        in_specs=[whole] * 15 + [outside] * 4,
        out_specs=[outside] + [whole] * 6,
        scratch_shapes=[
            pltpu.VMEM((2, features, ATT), BF16),
            pltpu.VMEM((2, length, length), BF16),
            pltpu.VMEM((length, HALF), F32),
            pltpu.VMEM((length, HALF), BF16),
            pltpu.VMEM((length, 2 * HALF), BF16),
            pltpu.VMEM((length, length), BF16),
            pltpu.VMEM((length, 3 * HALF), BF16),
            pltpu.VMEM((RING, features, ATT), BF16),
            pltpu.VMEM((length, features), F32),
            pltpu.VMEM((rows, features), BF16),
            pltpu.VMEM((rows, features), BF16),
            pltpu.VMEM((rows, features), BF16),
            pltpu.VMEM((rows, features), BF16),
            pltpu.VMEM((rows, features), BF16),
            pltpu.VMEM((2, 2 * BLOCK, FFW), BF16),
            *buffers(ATT),
            *buffers(FFW),
            pltpu.VMEM((2 * RING, 4 * HALF), F32),
            pltpu.VMEM((4 * RING, HALF), F32),
            pltpu.VMEM((1, features), F32),
            pltpu.VMEM((RING, 24, HALF), F32),
            pltpu.VMEM((RING, 24, HALF), F32),
            pltpu.VMEM((4, 24, HALF), F32),
            pltpu.VMEM((2, 24, HALF), F32),
            pltpu.SemaphoreType.DMA((80,)),
            pltpu.SemaphoreType.DMA((80,)),
            pltpu.SemaphoreType.DMA((9,)),
        ],
        name="backward",
        cost_estimate=pl.CostEstimate(flops=3 * 10**10, bytes_accessed=10**8, transcendentals=0),
        compiler_params=pltpu.CompilerParams(
            vmem_limit_bytes=63 * 1024 * 1024, collective_id=2, has_side_effects=True
        ),
    )(*args)


def page_body(
    tokens,
    norm_gains,
    attn_qkv,
    attn_out,
    ffn_in,
    ffn_out,
    position_tables,
    page_counts,
    layout_cells,
    cotangent,
):
    group, ring = lax.axis_index("dp"), lax.axis_index("tensor")
    (
        att_full, ffn_full, prob, full, gains_here, normed_one_t, resid, normed_two, normed_two_t,
        cot, cot_t, qkv, context, inverse, cells_t, cells_twice, cell_tail,
    ) = forward(
        tokens, cotangent, norm_gains, attn_qkv, attn_out, ffn_in, ffn_out, position_tables,
        page_counts, layout_cells,
    )
    ffn_grads, low, low_t, half_grad, page_out, gain_two = middle(
        normed_two, normed_two_t, cot, cot_t, resid, gains_here, ffn_full
    )
    layer_out, tokens_grad, qkv_grad, out_grad, inner_grad, outer_grad, small = backward(
        low, low_t, normed_one_t, half_grad, full, gains_here, qkv, context, inverse, cells_t,
        cells_twice, cell_tail, gain_two, att_full, prob, ffn_grads, page_out, ffn_in.shape[2],
    )
    gains = (small[0, 8:] + small[1, 8:]).reshape(2, 1024)
    gains_grad = lax.dynamic_slice_in_dim(gains, (group * RING + ring) * 32, 32, axis=1)
    tables = small[:, 0:6, :BUCKETS].reshape(CORES, 3, 2, BUCKETS).transpose(1, 3, 0, 2)
    tables = tables.reshape(3, BUCKETS, 2 * CORES)
    tables_grad = lax.dynamic_slice_in_dim(tables, group * 4, 4, axis=1)
    return (
        layer_out,
        tokens_grad,
        gains_grad,
        qkv_grad,
        out_grad,
        inner_grad,
        outer_grad,
        tables_grad,
    )


def solution(mesh):
    return jax.shard_map(
        page_body if page_plan(mesh) else general_body,
        mesh=mesh,
        in_specs=(
            P(("dp", "tensor"), None),
            P(),
            P(None, None, "tensor"),
            P("tensor", None),
            P(None, None, "tensor"),
            P("tensor", None),
            P(None, None, "tensor"),
            P("dp"),
            P(None, "dp"),
            P(("dp", "tensor"), None),
        ),
        out_specs=(
            P(("dp", "tensor"), None),
            P(("dp", "tensor"), None),
            P(None, ("dp", "tensor")),
            P(None, "dp", "tensor"),
            P("tensor", "dp"),
            P(None, "dp", "tensor"),
            P("tensor", "dp"),
            P(None, "dp", "tensor"),
        ),
        check_vma=False,
    )
```

```python
import math

import jax
import jax.numpy as jnp
import numpy as np
from jax import lax
from jax.experimental import pallas as pl
from jax.experimental.pallas import tpu as pltpu
from jax.sharding import PartitionSpec as P

HEAD_DIM = 64
BUCKETS = 32
REL_REACH = 128
CELLS = 64
PAGE_LEN = 1024


HIGHEST_PRECISION = lax.Precision.HIGHEST
TABLE_PRECISION = lax.Precision.HIGH
NORM_EPSILON = 1e-06
MASK_VALUE = -1e30


def bucket_table(offsets, bucket_total, max_reach):
    half_total = bucket_total // 2
    exact_limit = half_total // 2
    distance = np.abs(offsets).astype(np.int32)
    upper_side = (offsets > 0).astype(np.int32) * half_total
    safe_dist = np.maximum(distance, 1).astype(np.float32)
    ratio = np.log(safe_dist / np.float32(exact_limit)) / np.float32(
        math.log(max_reach / exact_limit)
    )
    far_bucket = exact_limit + np.floor(ratio * np.float32(half_total - exact_limit)).astype(
        np.int32
    )
    far_bucket = np.minimum(far_bucket, half_total - 1)
    return (upper_side + np.where(distance < exact_limit, distance, far_bucket)).astype(np.int32)


def offset_onehot(length):
    offsets = np.arange(2 * length - 1) - (length - 1)
    buckets = bucket_table(offsets, BUCKETS, REL_REACH)
    return jnp.asarray((buckets[:, None] == np.arange(BUCKETS)[None, :]).astype(np.float32))


def layout_onehot():
    cell_range = np.arange(CELLS)
    buckets = bucket_table(cell_range[None, :] - cell_range[:, None], BUCKETS, CELLS)
    return jnp.asarray(
        (buckets.reshape(-1)[:, None] == np.arange(BUCKETS)[None, :]).astype(np.float32)
    )


def gelu_tanh(values):
    return jax.nn.gelu(values, approximate=True)


def relative_bias(table_rows, length):
    values = jnp.dot(offset_onehot(length), table_rows, precision=HIGHEST_PRECISION).T
    heads_dev = values.shape[0]
    padded = jnp.pad(values, ((0, 0), (0, 1)))
    tiled = jnp.tile(padded, (1, length))
    skewed = tiled[:, : length * (2 * length - 1)].reshape(heads_dev, length, 2 * length - 1)
    return skewed[:, :, length - 1 :]


def relative_sums(dscore, length):
    heads_dev = dscore.shape[0]
    placed = jnp.pad(dscore, ((0, 0), (0, 0), (length - 1, 0)))
    flat = jnp.pad(placed.reshape(heads_dev, length * (2 * length - 1)), ((0, 0), (0, length)))
    return jnp.sum(flat.reshape(heads_dev, length, 2 * length), axis=1)[:, : 2 * length - 1]


def layout_values(tables):
    values = jnp.einsum("mn,snh->shm", layout_onehot(), tables[1:], precision=HIGHEST_PRECISION)
    return values.reshape(2, tables.shape[2], CELLS, CELLS)


def cell_onehots(page_cells):
    onehot = (page_cells[:, :, None] == jnp.arange(CELLS)[None, None, :]).astype(jnp.float32)
    length = page_cells.shape[1]
    joined = onehot.transpose(1, 0, 2).reshape(length, 2 * CELLS)
    return (onehot, joined)


def layout_bias(page_cells, lay_vals):
    onehot, joined = cell_onehots(page_cells)
    length = page_cells.shape[1]
    heads_dev = lay_vals.shape[1]
    rows_side = jnp.einsum("sia,shab->hisb", onehot, lay_vals, precision=TABLE_PRECISION)
    rows_side = rows_side.reshape(heads_dev, length, 2 * CELLS)
    return jnp.einsum("hic,jc->hij", rows_side, joined, precision=TABLE_PRECISION)


def layout_sums(dscore, page_cells):
    onehot, joined = cell_onehots(page_cells)
    length = page_cells.shape[1]
    heads_dev = dscore.shape[0]
    partial_rows = jnp.einsum("hij,jc->hic", dscore, joined, precision=TABLE_PRECISION)
    partial_rows = partial_rows.reshape(heads_dev, length, 2, CELLS)
    return jnp.einsum("sia,hisb->shab", onehot, partial_rows, precision=TABLE_PRECISION)


def page_scores(query, key_rows, count, page_cells, rel_bias, lay_vals):
    length = query.shape[0]
    scores = jnp.einsum("ihd,jhd->hij", query, key_rows, preferred_element_type=jnp.float32)
    scores = scores + rel_bias + layout_bias(page_cells, lay_vals)
    valid = jnp.arange(length) < count
    return jnp.where(valid[None, None, :], scores, MASK_VALUE)


def attend(projected, page_counts, layout_cells, rel_bias, lay_vals):
    total_rows = projected.shape[1]
    pages = page_counts.shape[0]
    length = total_rows // pages
    heads_dev = projected.shape[2] // HEAD_DIM
    split = projected.reshape(3, pages, length, heads_dev, HEAD_DIM)
    cells_pages = layout_cells.reshape(2, pages, length).transpose(1, 0, 2)

    def one_page(items):
        query, key_rows, value_rows, count, page_cells = items
        scores = page_scores(query, key_rows, count, page_cells, rel_bias, lay_vals)
        log_total = jax.nn.logsumexp(scores, axis=2)
        prob_low = jnp.exp(scores - log_total[:, :, None]).astype(jnp.bfloat16)
        context = jnp.einsum(
            "hij,jhd->ihd", prob_low, value_rows, preferred_element_type=jnp.float32
        )
        return (context.astype(jnp.bfloat16).reshape(length, heads_dev * HEAD_DIM), log_total)

    context, log_totals = lax.map(
        one_page, (split[0], split[1], split[2], page_counts, cells_pages)
    )
    return (context.reshape(total_rows, heads_dev * HEAD_DIM), log_totals)


def attend_back(projected, grad_context, log_totals, page_counts, layout_cells, rel_bias, lay_vals):
    total_rows = projected.shape[1]
    pages = page_counts.shape[0]
    length = total_rows // pages
    heads_dev = projected.shape[2] // HEAD_DIM
    split = projected.reshape(3, pages, length, heads_dev, HEAD_DIM)
    grad_split = grad_context.reshape(pages, length, heads_dev, HEAD_DIM)
    cells_pages = layout_cells.reshape(2, pages, length).transpose(1, 0, 2)

    def page_step(carry, items):
        rel_acc, lay_acc = carry
        query, key_rows, value_rows, grad_ctx, page_lse, count, page_cells = items
        scores = page_scores(query, key_rows, count, page_cells, rel_bias, lay_vals)
        prob = jnp.exp(scores - page_lse[:, :, None])
        grad_prob = jnp.einsum(
            "ihd,jhd->hij", grad_ctx, value_rows, preferred_element_type=jnp.float32
        )
        delta = jnp.sum(grad_prob * prob, axis=2, keepdims=True)
        dscore = prob * (grad_prob - delta)
        rel_acc = rel_acc + relative_sums(dscore, length)
        lay_acc = lay_acc + layout_sums(dscore, page_cells)
        score_low = dscore.astype(jnp.bfloat16)
        grad_query = jnp.einsum(
            "hij,jhd->ihd", score_low, key_rows, preferred_element_type=jnp.float32
        ).astype(jnp.bfloat16)
        grad_key = jnp.einsum(
            "hij,ihd->jhd", score_low, query, preferred_element_type=jnp.float32
        ).astype(jnp.bfloat16)
        grad_value = jnp.einsum(
            "hij,ihd->jhd", prob.astype(jnp.bfloat16), grad_ctx, preferred_element_type=jnp.float32
        ).astype(jnp.bfloat16)
        stacked = jnp.stack([grad_query, grad_key, grad_value]).reshape(
            3, length, heads_dev * HEAD_DIM
        )
        return ((rel_acc, lay_acc), stacked)

    init_sums = (
        jnp.zeros((heads_dev, 2 * length - 1), jnp.float32),
        jnp.zeros((2, heads_dev, CELLS, CELLS), jnp.float32),
    )
    (rel_acc, lay_acc), grads = lax.scan(
        page_step,
        init_sums,
        (split[0], split[1], split[2], grad_split, log_totals, page_counts, cells_pages),
    )
    grad_proj = grads.transpose(1, 0, 2, 3).reshape(3, total_rows, heads_dev * HEAD_DIM)
    rel_grad = jnp.dot(offset_onehot(length).T, rel_acc.T, precision=HIGHEST_PRECISION)
    lay_grad = jnp.einsum(
        "shm,mn->snh",
        lay_acc.reshape(2, heads_dev, CELLS * CELLS),
        layout_onehot(),
        precision=HIGHEST_PRECISION,
    )
    return (grad_proj, jnp.concatenate([rel_grad[None], lay_grad], axis=0))


def norm_back(rows, scale, gain, grad_normed):
    weighted = grad_normed * gain
    return scale * weighted - rows * scale**3 * jnp.mean(rows * weighted, axis=1, keepdims=True)


def forward_core(
    token_rows,
    norm_gains,
    attn_qkv,
    attn_out,
    ffn_in,
    page_counts,
    layout_cells,
    rel_bias,
    lay_vals,
):
    scale_one = lax.rsqrt(jnp.mean(token_rows * token_rows, axis=1, keepdims=True) + NORM_EPSILON)
    normed_one = (token_rows * scale_one * norm_gains[0]).astype(jnp.bfloat16)
    gathered_one = lax.all_gather(normed_one, "tensor", axis=0, tiled=True)
    projected = jnp.einsum(
        "td,cdk->ctk", gathered_one, attn_qkv, preferred_element_type=jnp.float32
    ).astype(jnp.bfloat16)
    context, log_totals = attend(projected, page_counts, layout_cells, rel_bias, lay_vals)
    attn_total = lax.psum_scatter(
        jnp.dot(context, attn_out, preferred_element_type=jnp.float32)
        .astype(jnp.bfloat16)
        .astype(jnp.float32)
        .astype(jnp.bfloat16),
        "tensor",
        scatter_dimension=0,
        tiled=True,
    ).astype(jnp.float32)
    resid = token_rows + attn_total
    scale_two = lax.rsqrt(jnp.mean(resid * resid, axis=1, keepdims=True) + NORM_EPSILON)
    normed_two = (resid * scale_two * norm_gains[1]).astype(jnp.bfloat16)
    gathered_two = lax.all_gather(normed_two, "tensor", axis=0, tiled=True)
    gate_up = jnp.einsum("td,cdf->ctf", gathered_two, ffn_in, preferred_element_type=jnp.float32)
    hidden = (gelu_tanh(gate_up[0]) * gate_up[1]).astype(jnp.bfloat16)
    return (
        scale_one,
        gathered_one,
        projected,
        context,
        log_totals,
        resid,
        scale_two,
        gathered_two,
        gate_up,
        hidden,
    )


def general_body(
    tokens,
    norm_gains,
    attn_qkv,
    attn_out,
    ffn_in,
    ffn_out,
    position_tables,
    page_counts,
    layout_cells,
    cotangent,
):
    token_rows = tokens.astype(jnp.float32)
    rel_bias = relative_bias(position_tables[0], PAGE_LEN)
    lay_vals = layout_values(position_tables)
    first = forward_core(
        token_rows,
        norm_gains,
        attn_qkv,
        attn_out,
        ffn_in,
        page_counts,
        layout_cells,
        rel_bias,
        lay_vals,
    )
    first_hidden = first[9]
    rows_part = first_hidden
    ffn_total = lax.psum_scatter(
        jnp.dot(rows_part, ffn_out, preferred_element_type=jnp.float32)
        .astype(jnp.bfloat16)
        .astype(jnp.float32)
        .astype(jnp.bfloat16),
        "tensor",
        scatter_dimension=0,
        tiled=True,
    ).astype(jnp.float32)
    layer_out = (first[5] + ffn_total).astype(jnp.bfloat16)
    cot_rows = lax.all_gather(cotangent, "tensor", axis=0, tiled=True)
    again_rows, cot_rows = lax.optimization_barrier((token_rows, cot_rows))
    saved = forward_core(
        again_rows,
        norm_gains,
        attn_qkv,
        attn_out,
        ffn_in,
        page_counts,
        layout_cells,
        rel_bias,
        lay_vals,
    )
    (
        scale_one,
        gathered_one,
        projected,
        context,
        log_totals,
        resid,
        scale_two,
        gathered_two,
        gate_up,
        hidden,
    ) = saved
    grad_hidden = jnp.einsum("td,fd->tf", cot_rows, ffn_out, preferred_element_type=jnp.float32)
    outer_grad = jnp.einsum("tf,td->fd", hidden, cot_rows, preferred_element_type=jnp.float32)
    gelu_value, gelu_back = jax.vjp(gelu_tanh, gate_up[0])
    grad_gate = gelu_back(grad_hidden * gate_up[1])[0].astype(jnp.bfloat16)
    grad_up = (grad_hidden * gelu_value).astype(jnp.bfloat16)
    grad_gate_up = jnp.stack([grad_gate, grad_up])
    inner_grad = jnp.einsum(
        "td,ctf->cdf", gathered_two, grad_gate_up, preferred_element_type=jnp.float32
    )
    rows_part = grad_gate_up
    grad_normed_two = lax.psum_scatter(
        jnp.einsum("ctf,cdf->td", rows_part, ffn_in, preferred_element_type=jnp.float32)
        .astype(jnp.bfloat16)
        .astype(jnp.float32)
        .astype(jnp.bfloat16),
        "tensor",
        scatter_dimension=0,
        tiled=True,
    ).astype(jnp.float32)
    grad_resid = cotangent.astype(jnp.float32) + norm_back(
        resid, scale_two, norm_gains[1], grad_normed_two
    )
    gain_two = jnp.sum(grad_normed_two * resid * scale_two, axis=0)
    resid_rows = lax.all_gather(grad_resid.astype(jnp.bfloat16), "tensor", axis=0, tiled=True)
    out_grad = jnp.einsum("tk,td->kd", context, resid_rows, preferred_element_type=jnp.float32)
    grad_context = jnp.einsum(
        "td,kd->tk", resid_rows, attn_out, preferred_element_type=jnp.float32
    ).astype(jnp.bfloat16)
    grad_proj, tables_grad = attend_back(
        projected, grad_context, log_totals, page_counts, layout_cells, rel_bias, lay_vals
    )
    qkv_grad = jnp.einsum(
        "td,ctk->cdk", gathered_one, grad_proj, preferred_element_type=jnp.float32
    )
    rows_part = grad_proj
    grad_normed_one = lax.psum_scatter(
        jnp.einsum("ctk,cdk->td", rows_part, attn_qkv, preferred_element_type=jnp.float32)
        .astype(jnp.bfloat16)
        .astype(jnp.float32)
        .astype(jnp.bfloat16),
        "tensor",
        scatter_dimension=0,
        tiled=True,
    ).astype(jnp.float32)
    tokens_grad = grad_resid + norm_back(token_rows, scale_one, norm_gains[0], grad_normed_one)
    gain_one = jnp.sum(grad_normed_one * token_rows * scale_one, axis=0)
    gains_grad = lax.psum_scatter(
        jnp.stack([gain_one, gain_two]), ("dp", "tensor"), scatter_dimension=1, tiled=True
    )
    qkv_summed, inner_summed, out_summed, outer_summed, tables_summed = (
        lax.psum_scatter(
            qkv_grad.astype(jnp.bfloat16), "dp", scatter_dimension=1, tiled=True
        ).astype(jnp.float32),
        lax.psum_scatter(
            inner_grad.astype(jnp.bfloat16), "dp", scatter_dimension=1, tiled=True
        ).astype(jnp.float32),
        lax.psum_scatter(
            out_grad.astype(jnp.bfloat16), "dp", scatter_dimension=1, tiled=True
        ).astype(jnp.float32),
        lax.psum_scatter(
            outer_grad.astype(jnp.bfloat16), "dp", scatter_dimension=1, tiled=True
        ).astype(jnp.float32),
        lax.psum_scatter(
            tables_grad.astype(jnp.bfloat16), "dp", scatter_dimension=1, tiled=True
        ).astype(jnp.float32),
    )
    return (
        layer_out,
        tokens_grad,
        gains_grad,
        qkv_summed,
        out_summed,
        inner_summed,
        outer_summed,
        tables_summed,
    )


PLANES = 4
RING = 4
CORES = 2
BLOCK = 256
HALF = 128
ORDER = (0, 1, 3, 2)
SLOT = (0, 1, 1, 0)
ATT = 512
UNITS = 384
FFW = 3 * UNITS
VMEM_BYTES = 60 * 1024 * 1024
F32 = jnp.float32
BF16 = jnp.bfloat16
NT = (((1,), (1,)), ((), ()))
TN = (((0,), (0,)), ((), ()))
NN = (((1,), (0,)), ((), ()))


def page_plan(mesh):
    return mesh.shape["dp"] == PLANES * CORES and mesh.shape["tensor"] == RING


def dot(left, right, dims=NN):
    return lax.dot_general(left, right, dims, preferred_element_type=F32)


def shaped(shape, dtype=BF16):
    return jax.ShapeDtypeStruct(shape, dtype)


def columns(plane, r):
    return pl.ds(pl.multiple_of((plane ^ r) * BLOCK, BLOCK), BLOCK)


def pair_lane(rows):
    return lax.broadcasted_iota(jnp.int32, (rows, 2 * HEAD_DIM), 1)


MESH = pl.DeviceIdType.MESH


def here():
    group, ring = lax.axis_index("dp"), lax.axis_index("tensor")
    return group // CORES, group % CORES, ring


def device(plane, core, ring):
    return (plane * CORES + core, ring)


def greet(partners):
    barrier = pltpu.get_barrier_semaphore()
    for partner in partners:
        pl.semaphore_signal(barrier, inc=1, device_id=partner, device_id_type=MESH)
    pl.semaphore_wait(barrier, len(partners))


class Lines:
    def __init__(self, send_sems, recv_sems):
        self.send_sems, self.recv_sems, self.open = send_sems, recv_sems, {}

    def make(self, name, source, target, partner):
        at = len(self.open)
        self.open[name] = pltpu.make_async_remote_copy(
            src_ref=source,
            dst_ref=target,
            send_sem=self.send_sems.at[at],
            recv_sem=self.recv_sems.at[at],
            device_id=partner,
            device_id_type=MESH,
        )
        return self.open[name]

    def start(self, name, source, target, partner):
        self.make(name, source, target, partner).start()

    def arrived(self, *names):
        for name in names:
            self.open[name].wait_recv()

    def sent(self, *names):
        for name in names or list(self.open):
            self.open[name].wait_send()


class Gather:
    def __init__(self, lines, tag, own, full, where):
        self.lines, self.tag, self.own, self.full = lines, tag, own, full
        self.plane, self.core, self.ring = where

    def place(self, ring):
        return device(self.plane, self.core, ring)

    def ring_start(self, k):
        self.lines.start(
            (self.tag, "z", k),
            self.own.at[0:BLOCK],
            self.full.at[k, 0:BLOCK],
            self.place((self.ring + RING - k) % RING),
        )

    def ring_forward(self):
        for name, k, step in (("down", 1, -1), ("up", 3, 1)):
            self.lines.make(
                (self.tag, name),
                self.full.at[k, 0:BLOCK],
                self.full.at[2, 0:BLOCK],
                self.place((self.ring + RING + step) % RING),
            )

        @pl.when((self.ring == 1) | (self.ring == 2))
        def _():
            self.lines.open[self.tag, "down"].start()
            self.lines.open[self.tag, "up"].start()

    def forward_arrived(self):
        @pl.when(self.ring < 2)
        def _():
            self.lines.arrived((self.tag, "down"))

        @pl.when(self.ring >= 2)
        def _():
            self.lines.arrived((self.tag, "up"))

    def forward_sent(self):
        @pl.when((self.ring == 1) | (self.ring == 2))
        def _():
            self.lines.sent((self.tag, "down"), (self.tag, "up"))

    def plane_start(self, k, landed=False):
        if k == 2 and not landed:
            self.forward_arrived()
        elif not landed:
            self.lines.arrived((self.tag, "z", k))
        for name, r in (("x", 1), ("y", 2)):
            self.lines.start(
                (self.tag, name, k),
                self.full.at[k, 0:BLOCK],
                self.full.at[k, r * BLOCK : (r + 1) * BLOCK],
                device(self.plane ^ r, self.core, self.ring),
            )

    def plane_arrived(self, k):
        self.lines.arrived((self.tag, "x", k), (self.tag, "y", k))

    def corner_start(self, k, landed=False):
        if not landed:
            self.plane_arrived(k)
        for name, r, half, goal in (("x", 1, 0, 2), ("y", 2, 1, 1)):
            self.lines.start(
                (self.tag, "corner" + name, k),
                self.full.at[k, r * BLOCK + half * HALF : r * BLOCK + (half + 1) * HALF],
                self.full.at[k, 3 * BLOCK + half * HALF : 3 * BLOCK + (half + 1) * HALF],
                device(self.plane ^ goal, self.core, self.ring),
            )

    def finish(self, k):
        self.lines.arrived((self.tag, "cornerx", k), (self.tag, "cornery", k))


def own_attention(core, plane, qkv, out, target):
    for r in range(PLANES):
        rows, place = columns(plane, r), slice(r * BLOCK, (r + 1) * BLOCK)
        mine = pl.ds(pl.multiple_of(core * HALF, HALF), HALF)
        target[place, 0:HALF] = out[mine, rows].astype(F32).T.astype(BF16)
        for m in range(3):
            target[place, (m + 1) * HALF : (m + 2) * HALF] = qkv[m, rows, mine]


def own_ffn(core, plane, inner, outer, target):
    units = outer.shape[0]
    for which, first, count in ((0, 0, UNITS), (1, UNITS, units - UNITS)):

        @pl.when(core == which)
        def _():
            for r in range(PLANES):
                rows, place = columns(plane, r), slice(r * BLOCK, (r + 1) * BLOCK)
                parts = [outer[first : first + count, rows]]
                parts += [inner[m, first : first + count, rows] for m in range(2)]
                parts = [part.astype(F32).T.astype(BF16) for part in parts]
                for m, part in enumerate(parts):
                    target[place, m * UNITS : m * UNITS + count] = part
                    if count < UNITS:
                        target[place, m * UNITS + count : (m + 1) * UNITS] = jnp.zeros(
                            (BLOCK, UNITS - count), BF16
                        )


def place_rows(plane, core, near, far, full):
    rows = near.shape[0]
    for source, half in ((near, core), (far, 1 - core)):
        for r in range(PLANES):
            full[pl.ds(pl.multiple_of(half * rows, rows), rows), r * BLOCK : (r + 1) * BLOCK] = (
                source[:, columns(plane, r)]
            )


def split_bf16(values):
    parts = []
    for _ in range(3):
        part = values.astype(BF16)
        parts.append(part)
        values = values - part.astype(F32)
    return parts


def bias_pieces(tables, near_hot, cell_hot, layout, near):
    parts = split_bf16(tables)
    rel = sum(dot(part, near_hot[...]) for part in parts)
    cells = dot(parts[0], cell_hot[...])
    heads = tables.shape[0] // 3
    for h in range(heads):
        near[h] = rel[h : h + 1, :]
        toeplitz = []
        for axis in range(2):
            row = jnp.broadcast_to(cells[(axis + 1) * heads + h : (axis + 1) * heads + h + 1], (CELLS, HALF))
            toeplitz.append(pltpu.roll(row, CELLS, 1, stride=1, stride_axis=0))
        side = lax.broadcasted_iota(jnp.int32, (CELLS, HALF), 1)
        first = toeplitz[0]
        layout[h, 0:CELLS, 0:HALF] = jnp.where(
            side < CELLS, first, pltpu.roll(first, CELLS, 1)
        ).astype(BF16)
        layout[h, 0:CELLS, HALF:] = jnp.zeros((CELLS, HALF), BF16)
        layout[h, CELLS:, 0:HALF] = jnp.zeros((CELLS, HALF), BF16)
        layout[h, CELLS:, HALF:] = jnp.where(side < CELLS, toeplitz[1], 0.0).astype(BF16)


def forward_kernel(
    tokens, cot, gains, qkv_w, out_w, ffn_in, ffn_out, tables, ints, near_hot, cell_hot,
    att_full, ffn_full, prob_full, full, gains_here, normed_t, resid, normed_two, normed_two_t,
    cot_full, cot_t, qkv, context, inverse, cells_t, cells_twice, cell_tail,
    near_x, far_x, near_g, far_g, other_ints, table_parts, table_rows, layout, near,
    own_ffn_w, ffn_in_v, ffn_out_v, normed, weights, cells, queries, keys, scores, prob,
    mixed_all, out_rows, mine_out, other_out,
    send_sems, recv_sems, local_sems,
):
    plane, core, ring = where = here()
    native = core == ring % 2
    rows = tokens.shape[0]
    length = 2 * rows
    partner = device(plane, 1 - core, ring)
    swap = device(plane, 1 - core, ring ^ 1)
    ring_others = [device(plane, core, (ring + RING - k) % RING) for k in range(1, RING)]
    neighbours = [device(plane ^ 1, core, ring), device(plane ^ 2, core, ring)]
    lines = Lines(send_sems, recv_sems)
    load_in = pltpu.make_async_copy(ffn_in, ffn_in_v, local_sems.at[0])
    load_out = pltpu.make_async_copy(ffn_out, ffn_out_v, local_sems.at[1])
    load_in.start()
    load_out.start()
    greet([partner, swap] + ring_others + neighbours)

    def swap_rows(tag, source, near_rows, far_rows):
        lines.make((tag, "swap"), source, near_rows, swap)
        lines.make((tag, "give"), source, far_rows, partner)
        lines.make((tag, "pass"), near_rows, far_rows, partner)

        @pl.when(native)
        def _():
            lines.open[tag, "give"].start()
            keep = pltpu.make_async_copy(source, near_rows, local_sems.at[2])
            keep.start()
            keep.wait()

        @pl.when(jnp.logical_not(native))
        def _():
            lines.open[tag, "swap"].start()

    def swap_pass(tag):
        @pl.when(jnp.logical_not(native))
        def _():
            lines.arrived((tag, "swap"))
            lines.open[tag, "pass"].start()
            lines.arrived((tag, "give"))

        @pl.when(native)
        def _():
            lines.arrived((tag, "pass"))

    def swap_sent(tag):
        @pl.when(jnp.logical_not(native))
        def _():
            lines.sent((tag, "swap"), (tag, "pass"))

        @pl.when(native)
        def _():
            lines.sent((tag, "give"))

    swap_rows("x", tokens, near_x, far_x)
    lines.start("ints", ints, other_ints, partner)
    table_parts[0] = tables[...]
    for k in range(1, RING):
        lines.start(("tables", k), tables, table_parts.at[k], ring_others[k - 1])
    own_attention(core, plane, qkv_w, out_w, weights)
    keep_weights = pltpu.make_async_copy(weights, att_full.at[0], local_sems.at[3])
    keep_weights.start()
    att = Gather(lines, "att", weights, att_full, where)
    ffn = Gather(lines, "ffn", own_ffn_w, ffn_full, where)
    keep_weights.wait()
    att.own = att_full.at[0]

    lines.arrived("ints")
    page = ring // 2
    picked = []
    for first in (0, 2, 4):
        own_row = ints[pl.ds(first + page, 1), :]
        other_row = other_ints[pl.ds(first + page, 1), :]
        picked.append(jnp.where(native, own_row, other_row))
    spot = lax.broadcasted_iota(jnp.int32, (CELLS, length), 0)
    cells_x = (jnp.broadcast_to(picked[0], (CELLS, length)) == spot).astype(F32)
    cells_y = (jnp.broadcast_to(picked[1], (CELLS, length)) == spot).astype(F32)
    position = lax.broadcasted_iota(jnp.int32, (CELLS, length), 1)
    tail = jnp.where((spot < 16) & (spot % 8 == position // HALF), 1.0, 0.0)
    hidden_key = (spot == 16) & (position >= jnp.broadcast_to(picked[2], (CELLS, length)))
    tail = jnp.where(hidden_key, MASK_VALUE, tail)
    flipped = CELLS - 1 - spot
    for axis in range(2):
        turned = (jnp.broadcast_to(picked[axis], (CELLS, length)) == flipped).astype(F32)
        cells_t[axis * CELLS : (axis + 1) * CELLS, :] = turned.astype(BF16)
    cells[...] = jnp.concatenate([cells_x, cells_y], axis=0).T.astype(BF16)
    cells_twice[...] = jnp.concatenate([cells_x, cells_x], axis=0).T.astype(BF16)
    cell_tail[...] = jnp.concatenate([cells_y, tail], axis=0).T.astype(BF16)
    for k in range(1, RING):
        lines.arrived(("tables", k))
    for k in range(RING):
        for axis in range(3):
            first = axis * 2 * RING + 2 * k
            table_rows[first : first + 2, :] = table_parts[k, pl.ds(4 * axis + 2 * core, 2), :]
    bias_pieces(table_rows[...], near_hot, cell_hot, layout, near)

    for r in range(PLANES):
        gains_here[:, r * BLOCK : (r + 1) * BLOCK] = gains[:, columns(plane, r)]
    load_in.wait()
    load_out.wait()
    own_ffn(core, plane, ffn_in_v, ffn_out_v, own_ffn_w)
    keep_ffn = pltpu.make_async_copy(own_ffn_w, ffn_full.at[0], local_sems.at[0])
    keep_ffn.start()
    swap_pass("x")
    att.ring_start(1)
    att.ring_start(3)
    place_rows(plane, core, near_x, far_x, full)
    for i in range(length // BLOCK):
        span = slice(i * BLOCK, (i + 1) * BLOCK)
        x = full[span, :].astype(F32)
        scale = lax.rsqrt(jnp.mean(x * x, axis=1, keepdims=True) + NORM_EPSILON)
        value = x * scale * gains_here[0:1, :]
        normed[span, :] = value.astype(BF16)
        normed_t[:, span] = value.T.astype(BF16)

    def head(k, h):
        at = 2 * k + h
        lane = pair_lane(length)
        mine = (lane // HEAD_DIM) == h
        side = dot(cells[...], layout[at])
        queries[:, :HALF] = jnp.where(mine, qkv[k, :, :HALF].astype(F32), side[:, :HALF]).astype(BF16)
        block = lax.broadcasted_iota(jnp.int32, (length, HALF), 0) // HALF
        is_left, is_right = lane % 8 < block - 1, lane % 8 > block + 1
        left, right = near[at, :, 0:1], near[at, :, 4 * HALF - 1 :]
        left_high, right_high = left.astype(BF16).astype(F32), right.astype(BF16).astype(F32)
        high = jnp.where(is_left, left_high, jnp.where(is_right, right_high, 0.0))
        low = jnp.where(is_left, left - left_high, jnp.where(is_right, right - right_high, 0.0))
        ends = jnp.where(lane < HEAD_DIM, side[:, HALF:], jnp.where(lane == HEAD_DIM + 16, 1.0, 0.0))
        ends = jnp.where((lane >= HEAD_DIM) & (lane < HEAD_DIM + 8), high, ends)
        ends = jnp.where((lane >= HEAD_DIM + 8) & (lane < HEAD_DIM + 16), low, ends)
        queries[:, HALF:] = ends.astype(BF16)
        keys[:, :HALF] = jnp.where(
            mine, qkv[k, :, HALF : 2 * HALF].astype(F32), cells_twice[...].astype(F32)
        ).astype(BF16)
        keys[:, HALF:] = cell_tail[...]
        scores[...] = dot(queries[...], keys[...], NT)
        spread = jnp.broadcast_to(near[at], (HALF, 4 * HALF))
        strip = pltpu.roll(spread, 3 * HALF, 1, stride=1, stride_axis=0)[:, : 3 * HALF]
        count = length // HALF
        store = pltpu.make_async_copy(prob.at[h], prob_full.at[at], local_sems.at[4 + h])
        if k > 0:
            store.wait()
        for i in range(count):
            first, last = max(i - 1, 0), min(i + 2, count)
            part = strip[:, (first - i + 1) * HALF : (last - i + 1) * HALF]
            span, near_span = slice(i * HALF, (i + 1) * HALF), slice(first * HALF, last * HALF)
            scores[span, near_span] = scores[span, near_span] + part
            row = scores[span, :]
            top = jnp.max(row, axis=1, keepdims=True)
            prob[h, span, :] = jnp.exp(row - top).astype(BF16)
        values = jnp.where(mine, qkv[k, :, 2 * HALF :].astype(F32), 1.0).astype(BF16)
        mixed = dot(prob[h], values)
        inv = 1.0 / pltpu.roll(mixed, HEAD_DIM, 1)
        mixed = (mixed * inv).astype(BF16)
        store.start()
        if h == 0:
            context[k] = mixed
            inverse[k] = inv
        else:
            context[k] = jnp.where(mine, mixed.astype(F32), context[k].astype(F32)).astype(BF16)
            inverse[k] = jnp.where(mine, inv, inverse[k])

    def project(k):
        if k > 0:
            load = pltpu.make_async_copy(att_full.at[k], weights, local_sems.at[3])
            load.start()
            load.wait()
        qkv[k] = dot(normed[...], weights[:, HALF:]).astype(BF16)
        mixed_all[:, k * HALF : (k + 1) * HALF] = weights[:, 0:HALF]

    def after_head(k, h):
        if (k, h) == (0, 0):
            att.plane_start(3)
            att.ring_forward()
        if (k, h) == (0, 1):
            att.corner_start(1)
            att.plane_start(2)
            ffn.ring_start(1)
            swap_rows("g", cot, near_g, far_g)
            att.finish(1)
        if (k, h) == (1, 0):
            att.corner_start(3)
        if (k, h) == (1, 1):
            att.corner_start(2)
            ffn.plane_start(1)
            ffn.ring_start(3)
            att.finish(3)
        if (k, h) == (3, 0):
            swap_pass("g")
        if (k, h) == (3, 1):
            ffn.corner_start(1)
            att.finish(2)
        if (k, h) == (2, 0):
            ffn.plane_start(3)
            ffn.ring_forward()

    for k in ORDER:
        project(k)
        if k == 0:
            att.plane_start(1)
        for h in range(2):
            head(k, h)
            after_head(k, h)

    for k in range(RING):
        out_rows[:, k * HALF : (k + 1) * HALF] = context[k]
    for i in range(length // BLOCK):
        span = slice(i * BLOCK, (i + 1) * BLOCK)
        mine_out[span, :] = dot(out_rows[span, :], mixed_all[...], NT).astype(BF16)
        lines.start(("out", i), mine_out.at[span], other_out.at[span], partner)
    place_rows(plane, core, near_g, far_g, cot_full)
    for r in range(PLANES):
        lanes = slice(r * BLOCK, (r + 1) * BLOCK)
        cot_t[lanes, :] = cot_full[:, lanes].astype(F32).T.astype(BF16)
    for i in range(length // BLOCK):
        span = slice(i * BLOCK, (i + 1) * BLOCK)
        lines.arrived(("out", i))
        row = full[span, :].astype(F32) + (
            mine_out[span, :].astype(F32) + other_out[span, :].astype(F32)
        )
        resid[span, :] = row
        scale = lax.rsqrt(jnp.mean(row * row, axis=1, keepdims=True) + NORM_EPSILON)
        value = row * scale * gains_here[1:2, :]
        normed_two[span, :] = value.astype(BF16)
        normed_two_t[:, span] = value.T.astype(BF16)

    ffn.finish(1)
    ffn.plane_arrived(3)
    ffn.forward_arrived()
    keep_ffn.wait()
    for h in range(2):
        pltpu.make_async_copy(prob.at[h], prob_full.at[2 * ORDER[-1] + h], local_sems.at[4 + h]).wait()
    swap_sent("x")
    swap_sent("g")
    att.forward_sent()
    ffn.forward_sent()
    lines.sent(
        *[
            name
            for name in lines.open
            if name[0] not in ("x", "g") and name[1] not in ("down", "up")
        ]
    )


def hot(reach, width):
    offsets = np.arange(width) - width // 2
    found = bucket_table(offsets, BUCKETS, reach)[None, :] == np.arange(HALF)[:, None]
    return jnp.asarray(found.astype(np.float32), BF16)


def forward(tokens, cotangent, gains, qkv_w, out_w, ffn_in, ffn_out, position_tables, page_counts, layout_cells):
    rows = tokens.shape[0]
    length = 2 * rows
    features = PLANES * BLOCK
    tables = position_tables.transpose(0, 2, 1).reshape(12, BUCKETS)
    tables = jnp.pad(tables, ((0, 4), (0, HALF - BUCKETS)))
    ints = jnp.concatenate(
        [
            layout_cells.reshape(4, length),
            jnp.broadcast_to(page_counts[:, None], (2, length)),
            jnp.zeros((2, length), jnp.int32),
        ]
    )
    args = [tokens, cotangent, gains, qkv_w, out_w, ffn_in, ffn_out, tables, ints]
    args += [hot(REL_REACH, 4 * HALF), hot(CELLS, HALF)]
    whole = pl.BlockSpec(memory_space=pltpu.VMEM)
    outside = pl.BlockSpec(memory_space=pl.ANY)
    outs = [
        shaped((RING, features, ATT)), shaped((RING, features, FFW)), shaped((2 * RING, length, length)),
        shaped((length, features)), shaped((2, features), F32), shaped((features, length)),
        shaped((length, features), F32), shaped((length, features)), shaped((features, length)),
        shaped((length, features)), shaped((features, length)),
        shaped((RING, length, 3 * HALF)), shaped((RING, length, HALF)), shaped((RING, length, HALF), F32),
        shaped((HALF, length)), shaped((length, HALF)), shaped((length, HALF)),
    ]
    scratch = [pltpu.VMEM((rows, features), BF16)] * 4 + [
        pltpu.VMEM(ints.shape, jnp.int32),
        pltpu.VMEM((RING,) + tables.shape, F32),
        pltpu.VMEM((6 * RING, HALF), F32),
        pltpu.VMEM((2 * RING, HALF, 2 * HALF), BF16),
        pltpu.VMEM((2 * RING, 1, 4 * HALF), F32),
        pltpu.VMEM((features, FFW), BF16),
        pltpu.VMEM(ffn_in.shape, BF16),
        pltpu.VMEM(ffn_out.shape, BF16),
        pltpu.VMEM((length, features), BF16),
        pltpu.VMEM((features, ATT), BF16),
        pltpu.VMEM((length, HALF), BF16),
        pltpu.VMEM((length, 2 * HALF), BF16),
        pltpu.VMEM((length, 2 * HALF), BF16),
        pltpu.VMEM((length, length), F32),
        pltpu.VMEM((2, length, length), BF16),
        pltpu.VMEM((features, RING * HALF), BF16),
        pltpu.VMEM((length, RING * HALF), BF16),
        pltpu.VMEM((length, features), BF16),
        pltpu.VMEM((length, features), BF16),
        pltpu.SemaphoreType.DMA((48,)),
        pltpu.SemaphoreType.DMA((48,)),
        pltpu.SemaphoreType.DMA((6,)),
    ]
    in_specs = [whole, outside, whole, whole, whole, outside, outside] + [whole] * 4
    out_specs = [outside] * 3 + [whole] * 14
    return pl.pallas_call(
        forward_kernel,
        out_shape=outs,
        in_specs=in_specs,
        out_specs=out_specs,
        scratch_shapes=scratch,
        name="forward",
        cost_estimate=pl.CostEstimate(flops=10**10, bytes_accessed=10**8, transcendentals=0),
        compiler_params=pltpu.CompilerParams(
            vmem_limit_bytes=63 * 1024 * 1024, collective_id=0, has_side_effects=True
        ),
    )(*args)


class Scatter:
    def __init__(self, lines, tag, k, grads, kept, buffers, where):
        self.lines, self.tag, self.k, self.grads, self.kept = lines, tag, k, grads, kept
        self.from_x, self.from_y, self.late, self.same, self.cross = buffers
        self.plane, self.core, self.ring = where
        self.to_x = device(self.plane ^ 1, self.core, self.ring)
        self.to_y = device(self.plane ^ 2, self.core, self.ring)

    def name(self, step):
        return (self.tag, step, self.k)

    def rows(self, r, half):
        return slice(r * BLOCK + half * HALF, r * BLOCK + (half + 1) * HALF)

    def start(self):
        k = self.k
        for step, r, half, target, goal in (
            ("x1", 3, 0, self.from_x.at[k, 1], self.to_x),
            ("y1", 3, 1, self.from_y.at[k, 1], self.to_y),
            ("x0", 1, 0, self.from_x.at[k, 0], self.to_x),
            ("y0", 2, 1, self.from_y.at[k, 0], self.to_y),
        ):
            self.lines.start(self.name(step), self.grads.at[self.rows(r, half)], target, goal)

    def middle(self):
        k = self.k
        self.lines.arrived(self.name("x1"), self.name("y1"))
        for source, r, half, at, goal, step in (
            (self.from_x, 2, 0, 0, self.to_y, "late0"),
            (self.from_y, 1, 1, 1, self.to_x, "late1"),
        ):
            kept = self.kept(r, half).astype(F32)
            source[k, 1] = (kept + source[k, 1].astype(F32)).astype(BF16)
            self.lines.start(self.name(step), source.at[k, 1], self.late.at[k, at], goal)

    def last(self):
        self.combine()
        self.hand_over()

    def combine(self):
        k, late = self.k, self.late
        self.lines.arrived(*[self.name(step) for step in ("x0", "y0", "late0", "late1")])
        upper = self.kept(0, 0).astype(F32) + self.from_x[k, 0].astype(F32) + late[k, 0].astype(F32)
        lower = self.kept(0, 1).astype(F32) + self.from_y[k, 0].astype(F32) + late[k, 1].astype(F32)
        late[k, 0] = jnp.where(self.core == 0, upper, lower).astype(BF16)
        late[k, 1] = jnp.where(self.core == 0, lower, upper).astype(BF16)

    def hand_over(self):
        k, late = self.k, self.late
        goal = (self.ring + k) % RING
        if k > 0:
            self.lines.start(
                self.name("same"), late.at[k, 0], self.same.at[k - 1], device(self.plane, self.core, goal)
            )
        self.lines.start(
            self.name("cross"), late.at[k, 1], self.cross.at[k], device(self.plane, 1 - self.core, goal)
        )


def gelu_parts(gate):
    square = gate * gate
    ratio = math.sqrt(2.0 / math.pi)
    bend = jnp.tanh(ratio * gate * (1.0 + 0.044715 * square))
    half_gate = 0.5 * gate
    value = half_gate + half_gate * bend
    slope = 0.5 + 0.5 * bend + half_gate * (1.0 - bend * bend) * (
        ratio * (1.0 + 3.0 * 0.044715 * square)
    )
    return value, slope


def middle_kernel(
    normed, normed_t, cot, cot_t, resid, gains_here, ffn_before,
    ffn_full, grads_full, low, low_t, half_grad, page_out, gain, late,
    weights, hidden, grads, total_in, total_out, mine, other, mine_out, other_out,
    kept, from_x, from_y,
    send_sems, recv_sems, local_sems,
):
    plane, core, ring = where = here()
    partner = device(plane, 1 - core, ring)
    lines = Lines(send_sems, recv_sems)
    length = normed.shape[0]
    rows = length // 2
    blocks = length // BLOCK

    gather = Gather(lines, "ffn", None, ffn_full, where)

    def load(at):
        return pltpu.make_async_copy(
            ffn_full.at[ORDER[at]], weights.at[at % 2], local_sems.at[at % 2]
        )

    def store(k):
        return pltpu.make_async_copy(grads, grads_full.at[k], local_sems.at[2])

    loads = [
        pltpu.make_async_copy(
            grads_full.at[0, first : first + BLOCK], kept.at[at : at + BLOCK], local_sems.at[3 + i]
        )
        for i, (first, at) in enumerate(((0, 0), (3 * HALF, BLOCK)))
    ]
    spots = {(0, 0): 0, (0, 1): HALF, (1, 1): BLOCK, (2, 0): BLOCK + HALF}
    scatter = Scatter(
        lines, "grads", 0, grads_full.at[0],
        lambda r, half: kept[spots[r, half] : spots[r, half] + HALF],
        (from_x, from_y, late, None, None), where,
    )
    load(0).start()
    load(1).start()
    greet([partner, device(plane ^ 1, core, ring), device(plane ^ 2, core, ring)])
    gather.corner_start(3, landed=True)
    gather.plane_start(2, landed=True)
    for at, k in enumerate(ORDER):
        load(at).wait()
        w = weights.at[at % 2]
        for i in range(blocks):
            span = slice(i * BLOCK, (i + 1) * BLOCK)
            both = dot(normed[span, :], w[:, UNITS:])
            grad_hidden = dot(cot[span, :], w[:, :UNITS])
            gate, up = both[:, :UNITS], both[:, UNITS:]
            value, slope = gelu_parts(gate)
            hidden[span, :UNITS] = (value * up).astype(BF16)
            hidden[span, UNITS : 2 * UNITS] = (grad_hidden * up * slope).astype(BF16)
            hidden[span, 2 * UNITS :] = (grad_hidden * value).astype(BF16)
            part_in = dot(hidden[span, UNITS:], w[:, UNITS:], NT)
            part_out = dot(hidden[span, :UNITS], w[:, :UNITS], NT)
            if at > 0:
                part_in = total_in[span, :] + part_in
                part_out = total_out[span, :] + part_out
            if at + 1 < RING:
                total_in[span, :] = part_in
                total_out[span, :] = part_out
            else:
                mine[span, :] = part_in.astype(BF16)
                lines.start(("in", i), mine.at[span], other.at[span], partner)
                mine_out[span, :] = part_out.astype(BF16)
        if at + 1 == RING:
            far = pl.ds(pl.multiple_of((1 - core) * rows, rows), rows)
            lines.start("out", mine_out.at[far], other_out, partner)
        if at > 0:
            store(ORDER[at - 1]).wait()
        if at == 1:
            gather.finish(3)
            load(2).start()
            gather.corner_start(2)
            scatter.start()
            for copy in loads:
                copy.start()
        if at == 2:
            gather.finish(2)
            load(3).start()
        for i in range(2):
            span = slice(i * 2 * BLOCK, (i + 1) * 2 * BLOCK)
            grads[span, :UNITS] = dot(cot_t[span, :], hidden[:, :UNITS]).astype(BF16)
            grads[span, UNITS:] = dot(normed_t[span, :], hidden[:, UNITS:]).astype(BF16)
        store(k).start()
        if at == 2:
            for copy in loads:
                copy.wait()
            scatter.middle()

    total = jnp.zeros((1, resid.shape[1]), F32)
    for i in range(blocks):
        span = slice(i * BLOCK, (i + 1) * BLOCK)
        lines.arrived(("in", i))
        row = resid[span, :]
        grad = mine[span, :].astype(F32) + other[span, :].astype(F32)
        scale = lax.rsqrt(jnp.mean(row * row, axis=1, keepdims=True) + NORM_EPSILON)
        weighted = grad * gains_here[1:2, :]
        center = jnp.mean(row * weighted, axis=1, keepdims=True)
        value = cot[span, :].astype(F32) + scale * weighted - row * (scale * scale * scale * center)
        low[span, :] = value.astype(BF16)
        low_t[:, span] = value.T.astype(BF16)
        in_half = core == (i * BLOCK) // rows
        total = total + jnp.where(in_half, jnp.sum(grad * row * scale, axis=0, keepdims=True), 0.0)

        @pl.when(in_half)
        def _():
            first = (i * BLOCK) % rows
            half_grad[first : first + BLOCK, :] = value

    for r in range(PLANES):
        gain[:, columns(plane, r)] = total[:, r * BLOCK : (r + 1) * BLOCK]
    lines.arrived("out")
    for i in range(rows // BLOCK):
        span = slice(i * BLOCK, (i + 1) * BLOCK)
        near = pl.ds(pl.multiple_of(core * rows + i * BLOCK, BLOCK), BLOCK)
        row = resid[near, :] + (mine_out[near, :].astype(F32) + other_out[span, :].astype(F32))
        for r in range(PLANES):
            page_out[span, columns(plane, r)] = row[:, r * BLOCK : (r + 1) * BLOCK].astype(BF16)
    scatter.combine()
    store(ORDER[-1]).wait()
    lines.sent()


def middle(normed, normed_t, cot, cot_t, resid, gains_here, ffn_full):
    length, features = normed.shape
    rows = length // 2
    whole = pl.BlockSpec(memory_space=pltpu.VMEM)
    outside = pl.BlockSpec(memory_space=pl.ANY)
    return pl.pallas_call(
        middle_kernel,
        out_shape=[
            shaped((RING, features, FFW)), shaped((RING, features, FFW)),
            shaped((length, features)), shaped((features, length)),
            shaped((rows, features), F32), shaped((rows, features)), shaped((1, features), F32),
            shaped((1, 2, HALF, FFW)),
        ],
        in_specs=[whole] * 6 + [outside],
        out_specs=[outside] * 2 + [whole] * 6,
        input_output_aliases={6: 0},
        scratch_shapes=[
            pltpu.VMEM((2, features, FFW), BF16),
            pltpu.VMEM((length, FFW), BF16),
            pltpu.VMEM((features, FFW), BF16),
            pltpu.VMEM((length, features), F32),
            pltpu.VMEM((length, features), F32),
            pltpu.VMEM((length, features), BF16),
            pltpu.VMEM((length, features), BF16),
            pltpu.VMEM((length, features), BF16),
            pltpu.VMEM((rows, features), BF16),
            pltpu.VMEM((2 * BLOCK, FFW), BF16),
            pltpu.VMEM((1, 2, HALF, FFW), BF16),
            pltpu.VMEM((1, 2, HALF, FFW), BF16),
            pltpu.SemaphoreType.DMA((20,)),
            pltpu.SemaphoreType.DMA((20,)),
            pltpu.SemaphoreType.DMA((5,)),
        ],
        name="middle",
        cost_estimate=pl.CostEstimate(flops=27 * 10**9, bytes_accessed=10**8, transcendentals=0),
        compiler_params=pltpu.CompilerParams(
            vmem_limit_bytes=63 * 1024 * 1024, collective_id=1, has_side_effects=True
        ),
    )(normed, normed_t, cot, cot_t, resid, gains_here, ffn_full)


def sum_ring(lines, tag, late, same, cross):
    for k in range(RING):
        if k > 0:
            lines.arrived((tag, "same", k))
        lines.arrived((tag, "cross", k))
    mine = late[0, 0].astype(F32)
    for k in range(1, RING):
        mine = mine + same[k - 1].astype(F32)
    other = cross[0].astype(F32)
    for k in range(1, RING):
        other = other + cross[k].astype(F32)
    return mine, other


def backward_kernel(
    low, low_t, normed_t, half_grad, full, gains_here, qkv, context, inverse,
    cells_t, cells_twice, cell_tail, near_hot, cell_hot, gain_two, ffn_first,
    att_full, prob_full, ffn_grads, page_out,
    layer_out, tokens_grad, qkv_grad, out_grad, inner_grad, outer_grad, small_out,
    weights, prob, scaled, scaled_low, keys, dscores, grad_qkv, att_grads, total, mine_half, far_half,
    other_half, page_low, swapped, ffn_kept,
    att_x, att_y, att_late, att_same, att_cross, ffn_x, ffn_y, ffn_late, ffn_same, ffn_cross,
    diag_near, diag_cell, gain_one, small, small_ring, small_plane, small_core,
    send_sems, recv_sems, local_sems,
):
    plane, core, ring = where = here()
    native = core == ring % 2
    length = low.shape[0]
    rows = length // 2
    count = length // HALF
    partner = device(plane, 1 - core, ring)
    swap = device(plane, 1 - core, ring ^ 1)
    partners = [partner, swap, device(plane ^ 1, core, ring), device(plane ^ 2, core, ring)]
    for k in range(1, RING):
        partners += [device(plane, core, (ring + k) % RING), device(plane, 1 - core, (ring + k) % RING)]
    lines = Lines(send_sems, recv_sems)

    def load_prob(at):
        head_at = 2 * ORDER[at // 2] + at % 2
        return pltpu.make_async_copy(prob_full.at[head_at], prob.at[at % 2], local_sems.at[at % 2])

    def load_weights(k):
        return pltpu.make_async_copy(att_full.at[k], weights.at[SLOT[k]], local_sems.at[2 + SLOT[k]])

    def load_kept(k):
        slot = SLOT[k]
        return [
            pltpu.make_async_copy(
                ffn_grads.at[k, first : first + BLOCK],
                ffn_kept.at[slot, at : at + BLOCK],
                local_sems.at[4 + 2 * slot + i],
            )
            for i, (first, at) in enumerate(((0, 0), (3 * HALF, BLOCK)))
        ]

    load_prob(0).start()
    load_prob(1).start()
    load_weights(0).start()
    goals = [partner, device(plane ^ 1, core, ring), device(plane ^ 2, core, ring)] + partners[4:]
    greet(goals)

    def kept_ffn(k):
        spots = {(0, 0): 0, (0, 1): HALF, (1, 1): BLOCK, (2, 0): BLOCK + HALF}
        return lambda r, half: ffn_kept[SLOT[k], spots[r, half] : spots[r, half] + HALF]

    def kept_att(k):
        def read(r, half):
            first = r * BLOCK + half * HALF
            return att_grads[k, first : first + HALF]

        return read

    ffn = [
        Scatter(lines, "ffn", k, ffn_grads.at[k], kept_ffn(k), (ffn_x, ffn_y, ffn_late, ffn_same, ffn_cross), where)
        for k in range(RING)
    ]
    att = [
        Scatter(lines, "att", k, att_grads.at[k], kept_att(k), (att_x, att_y, att_late, att_same, att_cross), where)
        for k in range(RING)
    ]

    def ffn_start(k):
        for copy in load_kept(k):
            copy.start()
        ffn[k].start()

    def ffn_middle(k):
        for copy in load_kept(k):
            copy.wait()
        ffn[k].middle()

    ffn_start(1)
    ffn_late[0] = ffn_first[0]
    ffn[0].hand_over()
    lines.make("layer", page_out, layer_out, swap)

    @pl.when(jnp.logical_not(native))
    def _():
        lines.open["layer"].start()

    lane = pair_lane(length)
    row_block = lax.broadcasted_iota(jnp.int32, (length, HALF), 0) // HALF
    flip_at = lax.broadcasted_iota(jnp.int32, (HALF, HALF), 0)
    flip_to = lax.broadcasted_iota(jnp.int32, (HALF, HALF), 1)
    flip = jnp.where(flip_at + flip_to == HALF - 1, 1.0, 0.0).astype(BF16)

    def enter(k):
        at = ORDER.index(k)
        if at + 1 < RING:
            load_weights(ORDER[at + 1]).start()
        load_weights(k).wait()
        grad_context = dot(low[...], weights[SLOT[k], :, 0:HALF]).astype(BF16).astype(F32)
        value = grad_context * inverse[k]
        scaled[...] = value
        scaled_low[...] = value.astype(BF16)

    def head(k, h):
        at = 2 * k + h
        mine = (lane // HEAD_DIM) == h
        value = scaled[...]
        delta = -jnp.sum(
            jnp.where(mine, value * context[k].astype(F32), 0.0), axis=1, keepdims=True
        )
        delta_high = delta.astype(BF16).astype(F32)
        spare = HEAD_DIM * (1 - h)
        fill = jnp.where(lane == spare + 1, delta - delta_high, 0.0)
        left = jnp.where(mine, value, jnp.where(lane == spare, delta_high, fill)).astype(BF16)
        ones = jnp.where((lane == spare) | (lane == spare + 1), 1.0, 0.0)
        right = jnp.where(mine, qkv[k, :, 2 * HALF :].astype(F32), ones).astype(BF16)
        turn = 2 * ORDER.index(k) + h
        load_prob(turn).wait()
        strips = [jnp.zeros((HALF, HALF), F32) for _ in range(3)]
        for i in range(length // BLOCK):
            span = slice(i * BLOCK, (i + 1) * BLOCK)
            dscore = prob[at % 2, span, :].astype(F32) * dot(left[span, :], right, NT)
            dscores[span, :] = dscore.astype(BF16)
            for part in range(BLOCK // HALF):
                for step in range(3):
                    block = i * (BLOCK // HALF) + part + step - 1
                    if 0 <= block < count:
                        strips[step] = strips[step] + dscore[
                            part * HALF : (part + 1) * HALF, block * HALF : (block + 1) * HALF
                        ]
        keys[:, :HALF] = jnp.where(
            mine, qkv[k, :, HALF : 2 * HALF].astype(F32), cells_twice[...].astype(F32)
        ).astype(BF16)
        keys[:, HALF:] = cell_tail[...]
        grad_left = dot(dscores[...], keys[...])
        grad_key = dot(dscores[...], qkv[k, :, :HALF], TN)
        grad_value = dot(prob[at % 2], scaled_low[...], TN)
        if turn + 2 < 2 * RING:
            load_prob(turn + 2).start()
        for m, new in enumerate((grad_left[:, :HALF], grad_key, grad_value)):
            lanes = slice(m * HALF, (m + 1) * HALF)
            if h == 1:
                new = jnp.where(mine, new, grad_qkv[:, lanes].astype(F32))
            grad_qkv[:, lanes] = new.astype(BF16)

        skewed = jnp.zeros((HALF, 3 * HALF), F32)
        strip = jnp.concatenate(strips, axis=1)
        for part in split_bf16(strip):
            skewed = skewed + dot(flip, part)
        skewed = jnp.concatenate([skewed, jnp.zeros((HALF, HALF), F32)], axis=1)
        sums = jnp.sum(pltpu.roll(skewed, 1, 1, stride=1, stride_axis=0), axis=0, keepdims=True)
        tail = grad_left[:, HALF:]
        in_tail = (lane >= HEAD_DIM) & (lane < HEAD_DIM + 8)
        far_left = jnp.sum(jnp.where(in_tail & (lane % 8 < row_block - 1), tail, 0.0), axis=0, keepdims=True)
        far_right = jnp.sum(jnp.where(in_tail & (lane % 8 > row_block + 1), tail, 0.0), axis=0, keepdims=True)
        wide = lax.broadcasted_iota(jnp.int32, (1, 4 * HALF), 1)
        sums = sums + jnp.where(wide == 0, jnp.sum(far_left, axis=1, keepdims=True), 0.0)
        sums = sums + jnp.where(wide == 4 * HALF - 1, jnp.sum(far_right, axis=1, keepdims=True), 0.0)
        diag_near[at : at + 1, :] = sums
        by_cell = grad_left[:, :HALF]
        by_cell = jnp.where(mine, pltpu.roll(by_cell, HEAD_DIM, 1), by_cell)
        for axis, table in enumerate((by_cell, tail)):
            table_high = table.astype(BF16)
            rest = (table - table_high.astype(F32)).astype(BF16)
            side = cells_t[axis * CELLS : (axis + 1) * CELLS, :]
            grid = dot(side, table_high) + dot(side, rest)
            cell_lane = lax.broadcasted_iota(jnp.int32, (CELLS, HALF), 1)
            grid = jnp.where(cell_lane < CELLS, grid, 0.0)
            grid = pltpu.roll(grid, 1, 1, stride=1, stride_axis=0)
            row = axis * 2 * RING + at
            diag_cell[row : row + 1, :] = jnp.sum(grid, axis=0, keepdims=True)

    def leave(k):
        w = weights[SLOT[k], :, HALF:]
        att_grads[k, :, 0:HALF] = dot(low_t[...], context[k]).astype(BF16)
        att_grads[k, :, HALF:] = dot(normed_t[...], grad_qkv[...]).astype(BF16)
        if k == ORDER[-1]:
            att[k].start()
        for i in range(length // BLOCK):
            span = slice(i * BLOCK, (i + 1) * BLOCK)
            part = dot(grad_qkv[span, :], w, NT)
            total[span, :] = part if k == 0 else total[span, :] + part

    enter(0)
    head(0, 0)
    head(0, 1)
    ffn_middle(1)
    ffn_start(3)
    leave(0)
    enter(1)
    head(1, 0)
    head(1, 1)
    leave(1)
    enter(3)
    head(3, 0)
    ffn_middle(3)
    ffn[1].last()
    ffn_start(2)
    att[0].start()
    head(3, 1)
    leave(3)
    enter(2)
    head(2, 0)
    head(2, 1)
    ffn_middle(2)
    att[0].middle()
    att[1].start()
    ffn[3].last()
    att[3].start()
    leave(2)

    near = pl.ds(pl.multiple_of(core * rows, rows), rows)
    far = pl.ds(pl.multiple_of((1 - core) * rows, rows), rows)
    far_half[...] = total[far, :].astype(BF16)
    lines.start("half", far_half, other_half, partner)
    mine_half[...] = total[near, :].astype(BF16)
    lines.arrived("half")
    gain = jnp.zeros((1, full.shape[1]), F32)
    for i in range(rows // BLOCK):
        span = slice(i * BLOCK, (i + 1) * BLOCK)
        x = full[pl.ds(pl.multiple_of(core * rows + i * BLOCK, BLOCK), BLOCK), :].astype(F32)
        grad = mine_half[span, :].astype(F32) + other_half[span, :].astype(F32)
        scale = lax.rsqrt(jnp.mean(x * x, axis=1, keepdims=True) + NORM_EPSILON)
        weighted = grad * gains_here[0:1, :]
        center = jnp.mean(x * weighted, axis=1, keepdims=True)
        value = half_grad[span, :] + scale * weighted - x * (scale * scale * scale * center)
        gain = gain + jnp.sum(grad * x * scale, axis=0, keepdims=True)
        for r in range(PLANES):
            block = value[:, r * BLOCK : (r + 1) * BLOCK]
            tokens_grad[span, columns(plane, r)] = block
            page_low[span, columns(plane, r)] = block.astype(BF16)
    for r in range(PLANES):
        gain_one[:, columns(plane, r)] = gain[:, r * BLOCK : (r + 1) * BLOCK]
    lines.make("swap", page_low, swapped, swap)

    @pl.when(jnp.logical_not(native))
    def _():
        lines.open["swap"].start()

    near_sums = sum(dot(part, near_hot[...], NT) for part in split_bf16(diag_near[...]))
    cell_sums = sum(dot(part, cell_hot[...], NT) for part in split_bf16(diag_cell[...]))
    for k in range(RING):
        small[k, 0:2, :] = near_sums[2 * k : 2 * k + 2, :]
        for axis in range(2):
            first = axis * 2 * RING + 2 * k
            small[k, 2 * axis + 2 : 2 * axis + 4, :] = cell_sums[first : first + 2, :]
        small[k, 6:8, :] = jnp.zeros((2, HALF), F32)
        for j in range(8):
            lanes = slice(j * HALF, (j + 1) * HALF)
            small[k, 8 + j : 9 + j, :] = gain_one[:, lanes]
            small[k, 16 + j : 17 + j, :] = gain_two[:, lanes]
    for k in range(1, RING):
        lines.start(("small", k), small.at[k], small_ring.at[k], device(plane, core, (ring + k) % RING))
    ffn[2].last()
    att[1].middle()
    att[0].last()
    att[3].middle()
    for k in range(1, RING):
        lines.arrived(("small", k))
    small_plane[0] = small[0] + (small_ring[1] + (small_ring[2] + small_ring[3]))
    lines.start("smallx", small_plane.at[0], small_plane.at[1], device(plane ^ 1, core, ring))
    att[1].last()
    att[2].middle()
    lines.arrived("smallx")
    small_plane[2] = small_plane[0] + small_plane[1]
    lines.start("smally", small_plane.at[2], small_plane.at[3], device(plane ^ 2, core, ring))
    att[3].last()
    lines.arrived("smally")
    small_core[0] = small_plane[2] + small_plane[3]
    lines.start("smallc", small_core.at[0], small_core.at[1], partner)
    att[2].last()

    mine, other = sum_ring(lines, "ffn", ffn_late, ffn_same, ffn_cross)
    rest = inner_grad.shape[1] - UNITS
    first_core = jnp.where(core == 0, mine, other)
    second_core = jnp.where(core == 0, other, mine)
    for m in range(2):
        at = (m + 1) * UNITS
        inner_grad[m, 0:UNITS, :] = first_core[:, at : at + UNITS].T
        inner_grad[m, UNITS : UNITS + rest, :] = second_core[:, at : at + UNITS].T[0:rest]
    outer_grad[0:UNITS, :] = first_core[:, 0:UNITS].T
    outer_grad[UNITS : UNITS + rest, :] = second_core[:, 0:UNITS].T[0:rest]

    @pl.when(jnp.logical_not(native))
    def _():
        lines.arrived("swap")
        tokens_grad[...] = swapped[...].astype(F32)

    mine, other = sum_ring(lines, "att", att_late, att_same, att_cross)
    first_core = jnp.where(core == 0, mine, other)
    second_core = jnp.where(core == 0, other, mine)
    for m in range(3):
        lanes = slice((m + 1) * HALF, (m + 2) * HALF)
        qkv_grad[m, :, 0:HALF] = first_core[:, lanes]
        qkv_grad[m, :, HALF : 2 * HALF] = second_core[:, lanes]
    out_grad[0:HALF, :] = first_core[:, 0:HALF].T
    out_grad[HALF : 2 * HALF, :] = second_core[:, 0:HALF].T

    lines.arrived("smallc")
    low_core = jnp.where(core == 0, small_core[0], small_core[1])
    high_core = jnp.where(core == 0, small_core[1], small_core[0])
    small_out[0] = low_core
    small_out[1] = high_core

    @pl.when(jnp.logical_not(native))
    def _():
        lines.arrived("layer")
        lines.sent("layer", "swap")

    lines.sent(*[name for name in lines.open if name not in ("layer", "swap")])


def backward(low, low_t, normed_t, half_grad, full, gains_here, qkv, context, inverse, cells_t, cells_twice, cell_tail, gain_two, ffn_first, att_full, prob_full, ffn_grads, page_out, units):
    length, features = low.shape
    rows = length // 2
    whole = pl.BlockSpec(memory_space=pltpu.VMEM)
    outside = pl.BlockSpec(memory_space=pl.ANY)
    args = [low, low_t, normed_t, half_grad, full, gains_here, qkv, context, inverse]
    args += [cells_t, cells_twice, cell_tail, hot(REL_REACH, 4 * HALF), hot(CELLS, HALF), gain_two, ffn_first]
    args += [att_full, prob_full, ffn_grads, page_out]

    def buffers(width):
        return [
            pltpu.VMEM((RING, 2, HALF, width), BF16),
            pltpu.VMEM((RING, 2, HALF, width), BF16),
            pltpu.VMEM((RING, 2, HALF, width), BF16),
            pltpu.VMEM((RING - 1, HALF, width), BF16),
            pltpu.VMEM((RING, HALF, width), BF16),
        ]

    return pl.pallas_call(
        backward_kernel,
        out_shape=[
            shaped((rows, features)), shaped((rows, features), F32),
            shaped((3, HALF, 2 * HALF), F32), shaped((2 * HALF, HALF), F32),
            shaped((2, units, HALF), F32), shaped((units, HALF), F32), shaped((2, 24, HALF), F32),
        ],
        in_specs=[whole] * 16 + [outside] * 4,
        out_specs=[outside] + [whole] * 6,
        scratch_shapes=[
            pltpu.VMEM((2, features, ATT), BF16),
            pltpu.VMEM((2, length, length), BF16),
            pltpu.VMEM((length, HALF), F32),
            pltpu.VMEM((length, HALF), BF16),
            pltpu.VMEM((length, 2 * HALF), BF16),
            pltpu.VMEM((length, length), BF16),
            pltpu.VMEM((length, 3 * HALF), BF16),
            pltpu.VMEM((RING, features, ATT), BF16),
            pltpu.VMEM((length, features), F32),
            pltpu.VMEM((rows, features), BF16),
            pltpu.VMEM((rows, features), BF16),
            pltpu.VMEM((rows, features), BF16),
            pltpu.VMEM((rows, features), BF16),
            pltpu.VMEM((rows, features), BF16),
            pltpu.VMEM((2, 2 * BLOCK, FFW), BF16),
            *buffers(ATT),
            *buffers(FFW),
            pltpu.VMEM((2 * RING, 4 * HALF), F32),
            pltpu.VMEM((4 * RING, HALF), F32),
            pltpu.VMEM((1, features), F32),
            pltpu.VMEM((RING, 24, HALF), F32),
            pltpu.VMEM((RING, 24, HALF), F32),
            pltpu.VMEM((4, 24, HALF), F32),
            pltpu.VMEM((2, 24, HALF), F32),
            pltpu.SemaphoreType.DMA((80,)),
            pltpu.SemaphoreType.DMA((80,)),
            pltpu.SemaphoreType.DMA((9,)),
        ],
        name="backward",
        cost_estimate=pl.CostEstimate(flops=3 * 10**10, bytes_accessed=10**8, transcendentals=0),
        compiler_params=pltpu.CompilerParams(
            vmem_limit_bytes=63 * 1024 * 1024, collective_id=2, has_side_effects=True
        ),
    )(*args)


def page_body(
    tokens,
    norm_gains,
    attn_qkv,
    attn_out,
    ffn_in,
    ffn_out,
    position_tables,
    page_counts,
    layout_cells,
    cotangent,
):
    group, ring = lax.axis_index("dp"), lax.axis_index("tensor")
    (
        att_full, ffn_full, prob, full, gains_here, normed_one_t, resid, normed_two, normed_two_t,
        cot, cot_t, qkv, context, inverse, cells_t, cells_twice, cell_tail,
    ) = forward(
        tokens, cotangent, norm_gains, attn_qkv, attn_out, ffn_in.transpose(0, 2, 1), ffn_out, position_tables,
        page_counts, layout_cells,
    )
    _, ffn_grads, low, low_t, half_grad, page_out, gain_two, ffn_first = middle(
        normed_two, normed_two_t, cot, cot_t, resid, gains_here, ffn_full
    )
    page_got, tokens_grad, qkv_grad, out_grad, inner_grad, outer_grad, small = backward(
        low, low_t, normed_one_t, half_grad, full, gains_here, qkv, context, inverse, cells_t,
        cells_twice, cell_tail, gain_two, ffn_first, att_full, prob, ffn_grads, page_out, ffn_in.shape[2],
    )
    layer_out = jnp.where(group % CORES == ring % 2, page_out, page_got)
    gains = (small[0, 8:] + small[1, 8:]).reshape(2, 1024)
    gains_grad = lax.dynamic_slice_in_dim(gains, (group * RING + ring) * 32, 32, axis=1)
    tables = small[:, 0:6, :BUCKETS].reshape(CORES, 3, 2, BUCKETS).transpose(1, 3, 0, 2)
    tables = tables.reshape(3, BUCKETS, 2 * CORES)
    tables_grad = lax.dynamic_slice_in_dim(tables, group * 4, 4, axis=1)
    return (
        layer_out,
        tokens_grad,
        gains_grad,
        qkv_grad,
        out_grad,
        inner_grad.transpose(0, 2, 1),
        outer_grad,
        tables_grad,
    )


def solution(mesh):
    return jax.shard_map(
        page_body if page_plan(mesh) else general_body,
        mesh=mesh,
        in_specs=(
            P(("dp", "tensor"), None),
            P(),
            P(None, None, "tensor"),
            P("tensor", None),
            P(None, None, "tensor"),
            P("tensor", None),
            P(None, None, "tensor"),
            P("dp"),
            P(None, "dp"),
            P(("dp", "tensor"), None),
        ),
        out_specs=(
            P(("dp", "tensor"), None),
            P(("dp", "tensor"), None),
            P(None, ("dp", "tensor")),
            P(None, "dp", "tensor"),
            P("tensor", "dp"),
            P(None, "dp", "tensor"),
            P("tensor", "dp"),
            P(None, "dp", "tensor"),
        ),
        check_vma=False,
    )
```

```python
import math

import jax
import jax.numpy as jnp
import numpy as np
from jax import lax
from jax.experimental import pallas as pl
from jax.experimental.pallas import tpu as pltpu
from jax.sharding import PartitionSpec as P

HEAD_DIM = 64
BUCKETS = 32
REL_REACH = 128
CELLS = 64
PAGE_LEN = 1024


HIGHEST_PRECISION = lax.Precision.HIGHEST
TABLE_PRECISION = lax.Precision.HIGH
NORM_EPSILON = 1e-06
MASK_VALUE = -1e30


def bucket_table(offsets, bucket_total, max_reach):
    half_total = bucket_total // 2
    exact_limit = half_total // 2
    distance = np.abs(offsets).astype(np.int32)
    upper_side = (offsets > 0).astype(np.int32) * half_total
    safe_dist = np.maximum(distance, 1).astype(np.float32)
    ratio = np.log(safe_dist / np.float32(exact_limit)) / np.float32(
        math.log(max_reach / exact_limit)
    )
    far_bucket = exact_limit + np.floor(ratio * np.float32(half_total - exact_limit)).astype(
        np.int32
    )
    far_bucket = np.minimum(far_bucket, half_total - 1)
    return (upper_side + np.where(distance < exact_limit, distance, far_bucket)).astype(np.int32)


def offset_onehot(length):
    offsets = np.arange(2 * length - 1) - (length - 1)
    buckets = bucket_table(offsets, BUCKETS, REL_REACH)
    return jnp.asarray((buckets[:, None] == np.arange(BUCKETS)[None, :]).astype(np.float32))


def layout_onehot():
    cell_range = np.arange(CELLS)
    buckets = bucket_table(cell_range[None, :] - cell_range[:, None], BUCKETS, CELLS)
    return jnp.asarray(
        (buckets.reshape(-1)[:, None] == np.arange(BUCKETS)[None, :]).astype(np.float32)
    )


def gelu_tanh(values):
    return jax.nn.gelu(values, approximate=True)


def relative_bias(table_rows, length):
    values = jnp.dot(offset_onehot(length), table_rows, precision=HIGHEST_PRECISION).T
    heads_dev = values.shape[0]
    padded = jnp.pad(values, ((0, 0), (0, 1)))
    tiled = jnp.tile(padded, (1, length))
    skewed = tiled[:, : length * (2 * length - 1)].reshape(heads_dev, length, 2 * length - 1)
    return skewed[:, :, length - 1 :]


def relative_sums(dscore, length):
    heads_dev = dscore.shape[0]
    placed = jnp.pad(dscore, ((0, 0), (0, 0), (length - 1, 0)))
    flat = jnp.pad(placed.reshape(heads_dev, length * (2 * length - 1)), ((0, 0), (0, length)))
    return jnp.sum(flat.reshape(heads_dev, length, 2 * length), axis=1)[:, : 2 * length - 1]


def layout_values(tables):
    values = jnp.einsum("mn,snh->shm", layout_onehot(), tables[1:], precision=HIGHEST_PRECISION)
    return values.reshape(2, tables.shape[2], CELLS, CELLS)


def cell_onehots(page_cells):
    onehot = (page_cells[:, :, None] == jnp.arange(CELLS)[None, None, :]).astype(jnp.float32)
    length = page_cells.shape[1]
    joined = onehot.transpose(1, 0, 2).reshape(length, 2 * CELLS)
    return (onehot, joined)


def layout_bias(page_cells, lay_vals):
    onehot, joined = cell_onehots(page_cells)
    length = page_cells.shape[1]
    heads_dev = lay_vals.shape[1]
    rows_side = jnp.einsum("sia,shab->hisb", onehot, lay_vals, precision=TABLE_PRECISION)
    rows_side = rows_side.reshape(heads_dev, length, 2 * CELLS)
    return jnp.einsum("hic,jc->hij", rows_side, joined, precision=TABLE_PRECISION)


def layout_sums(dscore, page_cells):
    onehot, joined = cell_onehots(page_cells)
    length = page_cells.shape[1]
    heads_dev = dscore.shape[0]
    partial_rows = jnp.einsum("hij,jc->hic", dscore, joined, precision=TABLE_PRECISION)
    partial_rows = partial_rows.reshape(heads_dev, length, 2, CELLS)
    return jnp.einsum("sia,hisb->shab", onehot, partial_rows, precision=TABLE_PRECISION)


def page_scores(query, key_rows, count, page_cells, rel_bias, lay_vals):
    length = query.shape[0]
    scores = jnp.einsum("ihd,jhd->hij", query, key_rows, preferred_element_type=jnp.float32)
    scores = scores + rel_bias + layout_bias(page_cells, lay_vals)
    valid = jnp.arange(length) < count
    return jnp.where(valid[None, None, :], scores, MASK_VALUE)


def attend(projected, page_counts, layout_cells, rel_bias, lay_vals):
    total_rows = projected.shape[1]
    pages = page_counts.shape[0]
    length = total_rows // pages
    heads_dev = projected.shape[2] // HEAD_DIM
    split = projected.reshape(3, pages, length, heads_dev, HEAD_DIM)
    cells_pages = layout_cells.reshape(2, pages, length).transpose(1, 0, 2)

    def one_page(items):
        query, key_rows, value_rows, count, page_cells = items
        scores = page_scores(query, key_rows, count, page_cells, rel_bias, lay_vals)
        log_total = jax.nn.logsumexp(scores, axis=2)
        prob_low = jnp.exp(scores - log_total[:, :, None]).astype(jnp.bfloat16)
        context = jnp.einsum(
            "hij,jhd->ihd", prob_low, value_rows, preferred_element_type=jnp.float32
        )
        return (context.astype(jnp.bfloat16).reshape(length, heads_dev * HEAD_DIM), log_total)

    context, log_totals = lax.map(
        one_page, (split[0], split[1], split[2], page_counts, cells_pages)
    )
    return (context.reshape(total_rows, heads_dev * HEAD_DIM), log_totals)


def attend_back(projected, grad_context, log_totals, page_counts, layout_cells, rel_bias, lay_vals):
    total_rows = projected.shape[1]
    pages = page_counts.shape[0]
    length = total_rows // pages
    heads_dev = projected.shape[2] // HEAD_DIM
    split = projected.reshape(3, pages, length, heads_dev, HEAD_DIM)
    grad_split = grad_context.reshape(pages, length, heads_dev, HEAD_DIM)
    cells_pages = layout_cells.reshape(2, pages, length).transpose(1, 0, 2)

    def page_step(carry, items):
        rel_acc, lay_acc = carry
        query, key_rows, value_rows, grad_ctx, page_lse, count, page_cells = items
        scores = page_scores(query, key_rows, count, page_cells, rel_bias, lay_vals)
        prob = jnp.exp(scores - page_lse[:, :, None])
        grad_prob = jnp.einsum(
            "ihd,jhd->hij", grad_ctx, value_rows, preferred_element_type=jnp.float32
        )
        delta = jnp.sum(grad_prob * prob, axis=2, keepdims=True)
        dscore = prob * (grad_prob - delta)
        rel_acc = rel_acc + relative_sums(dscore, length)
        lay_acc = lay_acc + layout_sums(dscore, page_cells)
        score_low = dscore.astype(jnp.bfloat16)
        grad_query = jnp.einsum(
            "hij,jhd->ihd", score_low, key_rows, preferred_element_type=jnp.float32
        ).astype(jnp.bfloat16)
        grad_key = jnp.einsum(
            "hij,ihd->jhd", score_low, query, preferred_element_type=jnp.float32
        ).astype(jnp.bfloat16)
        grad_value = jnp.einsum(
            "hij,ihd->jhd", prob.astype(jnp.bfloat16), grad_ctx, preferred_element_type=jnp.float32
        ).astype(jnp.bfloat16)
        stacked = jnp.stack([grad_query, grad_key, grad_value]).reshape(
            3, length, heads_dev * HEAD_DIM
        )
        return ((rel_acc, lay_acc), stacked)

    init_sums = (
        jnp.zeros((heads_dev, 2 * length - 1), jnp.float32),
        jnp.zeros((2, heads_dev, CELLS, CELLS), jnp.float32),
    )
    (rel_acc, lay_acc), grads = lax.scan(
        page_step,
        init_sums,
        (split[0], split[1], split[2], grad_split, log_totals, page_counts, cells_pages),
    )
    grad_proj = grads.transpose(1, 0, 2, 3).reshape(3, total_rows, heads_dev * HEAD_DIM)
    rel_grad = jnp.dot(offset_onehot(length).T, rel_acc.T, precision=HIGHEST_PRECISION)
    lay_grad = jnp.einsum(
        "shm,mn->snh",
        lay_acc.reshape(2, heads_dev, CELLS * CELLS),
        layout_onehot(),
        precision=HIGHEST_PRECISION,
    )
    return (grad_proj, jnp.concatenate([rel_grad[None], lay_grad], axis=0))


def norm_back(rows, scale, gain, grad_normed):
    weighted = grad_normed * gain
    return scale * weighted - rows * scale**3 * jnp.mean(rows * weighted, axis=1, keepdims=True)


def forward_core(
    token_rows,
    norm_gains,
    attn_qkv,
    attn_out,
    ffn_in,
    page_counts,
    layout_cells,
    rel_bias,
    lay_vals,
):
    scale_one = lax.rsqrt(jnp.mean(token_rows * token_rows, axis=1, keepdims=True) + NORM_EPSILON)
    normed_one = (token_rows * scale_one * norm_gains[0]).astype(jnp.bfloat16)
    gathered_one = lax.all_gather(normed_one, "tensor", axis=0, tiled=True)
    projected = jnp.einsum(
        "td,cdk->ctk", gathered_one, attn_qkv, preferred_element_type=jnp.float32
    ).astype(jnp.bfloat16)
    context, log_totals = attend(projected, page_counts, layout_cells, rel_bias, lay_vals)
    attn_total = lax.psum_scatter(
        jnp.dot(context, attn_out, preferred_element_type=jnp.float32)
        .astype(jnp.bfloat16)
        .astype(jnp.float32)
        .astype(jnp.bfloat16),
        "tensor",
        scatter_dimension=0,
        tiled=True,
    ).astype(jnp.float32)
    resid = token_rows + attn_total
    scale_two = lax.rsqrt(jnp.mean(resid * resid, axis=1, keepdims=True) + NORM_EPSILON)
    normed_two = (resid * scale_two * norm_gains[1]).astype(jnp.bfloat16)
    gathered_two = lax.all_gather(normed_two, "tensor", axis=0, tiled=True)
    gate_up = jnp.einsum("td,cdf->ctf", gathered_two, ffn_in, preferred_element_type=jnp.float32)
    hidden = (gelu_tanh(gate_up[0]) * gate_up[1]).astype(jnp.bfloat16)
    return (
        scale_one,
        gathered_one,
        projected,
        context,
        log_totals,
        resid,
        scale_two,
        gathered_two,
        gate_up,
        hidden,
    )


def general_body(
    tokens,
    norm_gains,
    attn_qkv,
    attn_out,
    ffn_in,
    ffn_out,
    position_tables,
    page_counts,
    layout_cells,
    cotangent,
):
    token_rows = tokens.astype(jnp.float32)
    rel_bias = relative_bias(position_tables[0], PAGE_LEN)
    lay_vals = layout_values(position_tables)
    first = forward_core(
        token_rows,
        norm_gains,
        attn_qkv,
        attn_out,
        ffn_in,
        page_counts,
        layout_cells,
        rel_bias,
        lay_vals,
    )
    first_hidden = first[9]
    rows_part = first_hidden
    ffn_total = lax.psum_scatter(
        jnp.dot(rows_part, ffn_out, preferred_element_type=jnp.float32)
        .astype(jnp.bfloat16)
        .astype(jnp.float32)
        .astype(jnp.bfloat16),
        "tensor",
        scatter_dimension=0,
        tiled=True,
    ).astype(jnp.float32)
    layer_out = (first[5] + ffn_total).astype(jnp.bfloat16)
    cot_rows = lax.all_gather(cotangent, "tensor", axis=0, tiled=True)
    again_rows, cot_rows = lax.optimization_barrier((token_rows, cot_rows))
    saved = forward_core(
        again_rows,
        norm_gains,
        attn_qkv,
        attn_out,
        ffn_in,
        page_counts,
        layout_cells,
        rel_bias,
        lay_vals,
    )
    (
        scale_one,
        gathered_one,
        projected,
        context,
        log_totals,
        resid,
        scale_two,
        gathered_two,
        gate_up,
        hidden,
    ) = saved
    grad_hidden = jnp.einsum("td,fd->tf", cot_rows, ffn_out, preferred_element_type=jnp.float32)
    outer_grad = jnp.einsum("tf,td->fd", hidden, cot_rows, preferred_element_type=jnp.float32)
    gelu_value, gelu_back = jax.vjp(gelu_tanh, gate_up[0])
    grad_gate = gelu_back(grad_hidden * gate_up[1])[0].astype(jnp.bfloat16)
    grad_up = (grad_hidden * gelu_value).astype(jnp.bfloat16)
    grad_gate_up = jnp.stack([grad_gate, grad_up])
    inner_grad = jnp.einsum(
        "td,ctf->cdf", gathered_two, grad_gate_up, preferred_element_type=jnp.float32
    )
    rows_part = grad_gate_up
    grad_normed_two = lax.psum_scatter(
        jnp.einsum("ctf,cdf->td", rows_part, ffn_in, preferred_element_type=jnp.float32)
        .astype(jnp.bfloat16)
        .astype(jnp.float32)
        .astype(jnp.bfloat16),
        "tensor",
        scatter_dimension=0,
        tiled=True,
    ).astype(jnp.float32)
    grad_resid = cotangent.astype(jnp.float32) + norm_back(
        resid, scale_two, norm_gains[1], grad_normed_two
    )
    gain_two = jnp.sum(grad_normed_two * resid * scale_two, axis=0)
    resid_rows = lax.all_gather(grad_resid.astype(jnp.bfloat16), "tensor", axis=0, tiled=True)
    out_grad = jnp.einsum("tk,td->kd", context, resid_rows, preferred_element_type=jnp.float32)
    grad_context = jnp.einsum(
        "td,kd->tk", resid_rows, attn_out, preferred_element_type=jnp.float32
    ).astype(jnp.bfloat16)
    grad_proj, tables_grad = attend_back(
        projected, grad_context, log_totals, page_counts, layout_cells, rel_bias, lay_vals
    )
    qkv_grad = jnp.einsum(
        "td,ctk->cdk", gathered_one, grad_proj, preferred_element_type=jnp.float32
    )
    rows_part = grad_proj
    grad_normed_one = lax.psum_scatter(
        jnp.einsum("ctk,cdk->td", rows_part, attn_qkv, preferred_element_type=jnp.float32)
        .astype(jnp.bfloat16)
        .astype(jnp.float32)
        .astype(jnp.bfloat16),
        "tensor",
        scatter_dimension=0,
        tiled=True,
    ).astype(jnp.float32)
    tokens_grad = grad_resid + norm_back(token_rows, scale_one, norm_gains[0], grad_normed_one)
    gain_one = jnp.sum(grad_normed_one * token_rows * scale_one, axis=0)
    gains_grad = lax.psum_scatter(
        jnp.stack([gain_one, gain_two]), ("dp", "tensor"), scatter_dimension=1, tiled=True
    )
    qkv_summed, inner_summed, out_summed, outer_summed, tables_summed = (
        lax.psum_scatter(
            qkv_grad.astype(jnp.bfloat16), "dp", scatter_dimension=1, tiled=True
        ).astype(jnp.float32),
        lax.psum_scatter(
            inner_grad.astype(jnp.bfloat16), "dp", scatter_dimension=1, tiled=True
        ).astype(jnp.float32),
        lax.psum_scatter(
            out_grad.astype(jnp.bfloat16), "dp", scatter_dimension=1, tiled=True
        ).astype(jnp.float32),
        lax.psum_scatter(
            outer_grad.astype(jnp.bfloat16), "dp", scatter_dimension=1, tiled=True
        ).astype(jnp.float32),
        lax.psum_scatter(
            tables_grad.astype(jnp.bfloat16), "dp", scatter_dimension=1, tiled=True
        ).astype(jnp.float32),
    )
    return (
        layer_out,
        tokens_grad,
        gains_grad,
        qkv_summed,
        out_summed,
        inner_summed,
        outer_summed,
        tables_summed,
    )


PLANES = 4
RING = 4
CORES = 2
BLOCK = 256
HALF = 128
ORDER = (0, 1, 3, 2)
BACK_ORDER = (2, 1, 3, 0)
SLOT = (1, 1, 0, 0)
KEPT_SLOT = (0, 1, 0, 0)
ATT = 512
UNITS = 384
FFW = 3 * UNITS
VMEM_BYTES = 60 * 1024 * 1024
F32 = jnp.float32
BF16 = jnp.bfloat16
NT = (((1,), (1,)), ((), ()))
TN = (((0,), (0,)), ((), ()))
NN = (((1,), (0,)), ((), ()))


def page_plan(mesh):
    return mesh.shape["dp"] == PLANES * CORES and mesh.shape["tensor"] == RING


def dot(left, right, dims=NN):
    return lax.dot_general(left, right, dims, preferred_element_type=F32)


def shaped(shape, dtype=BF16):
    return jax.ShapeDtypeStruct(shape, dtype)


def columns(plane, r):
    return pl.ds(pl.multiple_of((plane ^ r) * BLOCK, BLOCK), BLOCK)


def pair_lane(rows):
    return lax.broadcasted_iota(jnp.int32, (rows, 2 * HEAD_DIM), 1)


MESH = pl.DeviceIdType.MESH


def here():
    group, ring = lax.axis_index("dp"), lax.axis_index("tensor")
    return group // CORES, group % CORES, ring


def device(plane, core, ring):
    return (plane * CORES + core, ring)


def greet(partners):
    barrier = pltpu.get_barrier_semaphore()
    for partner in partners:
        pl.semaphore_signal(barrier, inc=1, device_id=partner, device_id_type=MESH)
    pl.semaphore_wait(barrier, len(partners))


class Lines:
    def __init__(self, send_sems, recv_sems):
        self.send_sems, self.recv_sems, self.open = send_sems, recv_sems, {}

    def make(self, name, source, target, partner):
        at = len(self.open)
        self.open[name] = pltpu.make_async_remote_copy(
            src_ref=source,
            dst_ref=target,
            send_sem=self.send_sems.at[at],
            recv_sem=self.recv_sems.at[at],
            device_id=partner,
            device_id_type=MESH,
        )
        return self.open[name]

    def start(self, name, source, target, partner):
        self.make(name, source, target, partner).start()

    def arrived(self, *names):
        for name in names:
            self.open[name].wait_recv()

    def sent(self, *names):
        for name in names or list(self.open):
            self.open[name].wait_send()


class Gather:
    def __init__(self, lines, tag, own, full, where):
        self.lines, self.tag, self.own, self.full = lines, tag, own, full
        self.plane, self.core, self.ring = where

    def place(self, ring):
        return device(self.plane, self.core, ring)

    def ring_start(self, k):
        self.lines.start(
            (self.tag, "z", k),
            self.own.at[0:BLOCK],
            self.full.at[k, 0:BLOCK],
            self.place((self.ring + RING - k) % RING),
        )

    def ring_forward(self):
        for name, k, step in (("down", 1, -1), ("up", 3, 1)):
            self.lines.make(
                (self.tag, name),
                self.full.at[k, 0:BLOCK],
                self.full.at[2, 0:BLOCK],
                self.place((self.ring + RING + step) % RING),
            )

        @pl.when((self.ring == 1) | (self.ring == 2))
        def _():
            self.lines.open[self.tag, "down"].start()
            self.lines.open[self.tag, "up"].start()

    def forward_arrived(self):
        @pl.when(self.ring < 2)
        def _():
            self.lines.arrived((self.tag, "down"))

        @pl.when(self.ring >= 2)
        def _():
            self.lines.arrived((self.tag, "up"))

    def forward_sent(self):
        @pl.when((self.ring == 1) | (self.ring == 2))
        def _():
            self.lines.sent((self.tag, "down"), (self.tag, "up"))

    def plane_start(self, k, landed=False):
        if k == 2 and not landed:
            self.forward_arrived()
        elif not landed:
            self.lines.arrived((self.tag, "z", k))
        for name, r in (("x", 1), ("y", 2)):
            self.lines.start(
                (self.tag, name, k),
                self.full.at[k, 0:BLOCK],
                self.full.at[k, r * BLOCK : (r + 1) * BLOCK],
                device(self.plane ^ r, self.core, self.ring),
            )

    def plane_arrived(self, k):
        self.lines.arrived((self.tag, "x", k), (self.tag, "y", k))

    def corner_start(self, k, landed=False):
        if not landed:
            self.plane_arrived(k)
        for name, r, half, goal in (("x", 1, 0, 2), ("y", 2, 1, 1)):
            self.lines.start(
                (self.tag, "corner" + name, k),
                self.full.at[k, r * BLOCK + half * HALF : r * BLOCK + (half + 1) * HALF],
                self.full.at[k, 3 * BLOCK + half * HALF : 3 * BLOCK + (half + 1) * HALF],
                device(self.plane ^ goal, self.core, self.ring),
            )

    def finish(self, k):
        self.lines.arrived((self.tag, "cornerx", k), (self.tag, "cornery", k))


def own_attention(core, plane, qkv, out, target):
    for r in range(PLANES):
        rows, place = columns(plane, r), slice(r * BLOCK, (r + 1) * BLOCK)
        mine = pl.ds(pl.multiple_of(core * HALF, HALF), HALF)
        target[place, 0:HALF] = out[mine, rows].astype(F32).T.astype(BF16)
        for m in range(3):
            target[place, (m + 1) * HALF : (m + 2) * HALF] = qkv[m, rows, mine]


def own_ffn(core, plane, inner, outer, target):
    units = outer.shape[0]
    for which, first, count in ((0, 0, UNITS), (1, UNITS, units - UNITS)):

        @pl.when(core == which)
        def _():
            for r in range(PLANES):
                rows, place = columns(plane, r), slice(r * BLOCK, (r + 1) * BLOCK)
                parts = [outer[first : first + count, rows]]
                parts += [inner[m, first : first + count, rows] for m in range(2)]
                parts = [part.astype(F32).T.astype(BF16) for part in parts]
                for m, part in enumerate(parts):
                    target[place, m * UNITS : m * UNITS + count] = part
                    if count < UNITS:
                        target[place, m * UNITS + count : (m + 1) * UNITS] = jnp.zeros(
                            (BLOCK, UNITS - count), BF16
                        )


def place_rows(plane, core, near, far, full):
    rows = near.shape[0]
    for source, half in ((near, core), (far, 1 - core)):
        for r in range(PLANES):
            full[pl.ds(pl.multiple_of(half * rows, rows), rows), r * BLOCK : (r + 1) * BLOCK] = (
                source[:, columns(plane, r)]
            )


def split_bf16(values):
    parts = []
    for _ in range(3):
        part = values.astype(BF16)
        parts.append(part)
        values = values - part.astype(F32)
    return parts


def bias_pieces(tables, near_hot, cell_hot, layout, near):
    parts = split_bf16(tables)
    rel = sum(dot(part, near_hot[...]) for part in parts)
    cells = dot(parts[0], cell_hot[...])
    heads = tables.shape[0] // 3
    for h in range(heads):
        near[h] = rel[h : h + 1, :]
        toeplitz = []
        for axis in range(2):
            row = jnp.broadcast_to(cells[(axis + 1) * heads + h : (axis + 1) * heads + h + 1], (CELLS, HALF))
            toeplitz.append(pltpu.roll(row, CELLS, 1, stride=1, stride_axis=0))
        side = lax.broadcasted_iota(jnp.int32, (CELLS, HALF), 1)
        first = toeplitz[0]
        layout[h, 0:CELLS, 0:HALF] = jnp.where(
            side < CELLS, first, pltpu.roll(first, CELLS, 1)
        ).astype(BF16)
        layout[h, 0:CELLS, HALF:] = jnp.zeros((CELLS, HALF), BF16)
        layout[h, CELLS:, 0:HALF] = jnp.zeros((CELLS, HALF), BF16)
        layout[h, CELLS:, HALF:] = jnp.where(side < CELLS, toeplitz[1], 0.0).astype(BF16)


def forward_kernel(
    tokens, cot, gains, qkv_w, out_w, ffn_in, ffn_out, tables, ints, near_hot, cell_hot,
    att_full, ffn_full, prob_full, full, gains_here, normed_t, resid, normed_two, normed_two_t,
    cot_full, cot_t, qkv, context, inverse, cells_t, cells_twice, cell_tail,
    near_x, far_x, near_g, far_g, other_ints, table_parts, table_rows, layout, near,
    own_ffn_w, ffn_in_v, ffn_out_v, normed, weights, cells, queries, keys, scores, prob,
    mixed_all, out_rows, mine_out, other_out,
    send_sems, recv_sems, local_sems,
):
    plane, core, ring = where = here()
    native = core == ring % 2
    rows = tokens.shape[0]
    length = 2 * rows
    partner = device(plane, 1 - core, ring)
    swap = device(plane, 1 - core, ring ^ 1)
    ring_others = [device(plane, core, (ring + RING - k) % RING) for k in range(1, RING)]
    neighbours = [device(plane ^ 1, core, ring), device(plane ^ 2, core, ring)]
    lines = Lines(send_sems, recv_sems)
    load_in = pltpu.make_async_copy(ffn_in, ffn_in_v, local_sems.at[0])
    load_out = pltpu.make_async_copy(ffn_out, ffn_out_v, local_sems.at[1])
    load_in.start()
    load_out.start()
    greet([partner, swap] + ring_others + neighbours)

    def swap_rows(tag, source, near_rows, far_rows):
        lines.make((tag, "swap"), source, near_rows, swap)
        lines.make((tag, "give"), source, far_rows, partner)
        lines.make((tag, "pass"), near_rows, far_rows, partner)

        @pl.when(native)
        def _():
            lines.open[tag, "give"].start()
            keep = pltpu.make_async_copy(source, near_rows, local_sems.at[2])
            keep.start()
            keep.wait()

        @pl.when(jnp.logical_not(native))
        def _():
            lines.open[tag, "swap"].start()

    def swap_pass(tag):
        @pl.when(jnp.logical_not(native))
        def _():
            lines.arrived((tag, "swap"))
            lines.open[tag, "pass"].start()
            lines.arrived((tag, "give"))

        @pl.when(native)
        def _():
            lines.arrived((tag, "pass"))

    def swap_sent(tag):
        @pl.when(jnp.logical_not(native))
        def _():
            lines.sent((tag, "swap"), (tag, "pass"))

        @pl.when(native)
        def _():
            lines.sent((tag, "give"))

    swap_rows("x", tokens, near_x, far_x)
    lines.start("ints", ints, other_ints, partner)
    table_parts[0] = tables[...]
    for k in range(1, RING):
        lines.start(("tables", k), tables, table_parts.at[k], ring_others[k - 1])
    own_attention(core, plane, qkv_w, out_w, weights)
    keep_weights = pltpu.make_async_copy(weights, att_full.at[0], local_sems.at[3])
    keep_weights.start()
    att = Gather(lines, "att", weights, att_full, where)
    ffn = Gather(lines, "ffn", own_ffn_w, ffn_full, where)
    keep_weights.wait()
    att.own = att_full.at[0]

    lines.arrived("ints")
    page = ring // 2
    picked = []
    for first in (0, 2, 4):
        own_row = ints[pl.ds(first + page, 1), :]
        other_row = other_ints[pl.ds(first + page, 1), :]
        picked.append(jnp.where(native, own_row, other_row))
    spot = lax.broadcasted_iota(jnp.int32, (CELLS, length), 0)
    cells_x = (jnp.broadcast_to(picked[0], (CELLS, length)) == spot).astype(F32)
    cells_y = (jnp.broadcast_to(picked[1], (CELLS, length)) == spot).astype(F32)
    position = lax.broadcasted_iota(jnp.int32, (CELLS, length), 1)
    tail = jnp.where((spot < 16) & (spot % 8 == position // HALF), 1.0, 0.0)
    hidden_key = (spot == 16) & (position >= jnp.broadcast_to(picked[2], (CELLS, length)))
    tail = jnp.where(hidden_key, MASK_VALUE, tail)
    flipped = CELLS - 1 - spot
    for axis in range(2):
        turned = (jnp.broadcast_to(picked[axis], (CELLS, length)) == flipped).astype(F32)
        cells_t[axis * CELLS : (axis + 1) * CELLS, :] = turned.astype(BF16)
    cells[...] = jnp.concatenate([cells_x, cells_y], axis=0).T.astype(BF16)
    cells_twice[...] = jnp.concatenate([cells_x, cells_x], axis=0).T.astype(BF16)
    cell_tail[...] = jnp.concatenate([cells_y, tail], axis=0).T.astype(BF16)
    for k in range(1, RING):
        lines.arrived(("tables", k))
    for k in range(RING):
        for axis in range(3):
            first = axis * 2 * RING + 2 * k
            table_rows[first : first + 2, :] = table_parts[k, pl.ds(4 * axis + 2 * core, 2), :]
    bias_pieces(table_rows[...], near_hot, cell_hot, layout, near)

    for r in range(PLANES):
        gains_here[:, r * BLOCK : (r + 1) * BLOCK] = gains[:, columns(plane, r)]
    load_in.wait()
    load_out.wait()
    own_ffn(core, plane, ffn_in_v, ffn_out_v, own_ffn_w)
    keep_ffn = pltpu.make_async_copy(own_ffn_w, ffn_full.at[0], local_sems.at[0])
    keep_ffn.start()
    swap_pass("x")
    att.ring_start(1)
    att.ring_start(3)
    place_rows(plane, core, near_x, far_x, full)
    for i in range(length // BLOCK):
        span = slice(i * BLOCK, (i + 1) * BLOCK)
        x = full[span, :].astype(F32)
        scale = lax.rsqrt(jnp.mean(x * x, axis=1, keepdims=True) + NORM_EPSILON)
        value = x * scale * gains_here[0:1, :]
        normed[span, :] = value.astype(BF16)
        normed_t[:, span] = value.T.astype(BF16)

    def head(k, h):
        at = 2 * k + h
        lane = pair_lane(length)
        mine = (lane // HEAD_DIM) == h
        side = dot(cells[...], layout[at])
        queries[:, :HALF] = jnp.where(mine, qkv[k, :, :HALF].astype(F32), side[:, :HALF]).astype(BF16)
        block = lax.broadcasted_iota(jnp.int32, (length, HALF), 0) // HALF
        is_left, is_right = lane % 8 < block - 1, lane % 8 > block + 1
        left, right = near[at, :, 0:1], near[at, :, 4 * HALF - 1 :]
        left_high, right_high = left.astype(BF16).astype(F32), right.astype(BF16).astype(F32)
        high = jnp.where(is_left, left_high, jnp.where(is_right, right_high, 0.0))
        low = jnp.where(is_left, left - left_high, jnp.where(is_right, right - right_high, 0.0))
        ends = jnp.where(lane < HEAD_DIM, side[:, HALF:], jnp.where(lane == HEAD_DIM + 16, 1.0, 0.0))
        ends = jnp.where((lane >= HEAD_DIM) & (lane < HEAD_DIM + 8), high, ends)
        ends = jnp.where((lane >= HEAD_DIM + 8) & (lane < HEAD_DIM + 16), low, ends)
        queries[:, HALF:] = ends.astype(BF16)
        keys[:, :HALF] = jnp.where(
            mine, qkv[k, :, HALF : 2 * HALF].astype(F32), cells_twice[...].astype(F32)
        ).astype(BF16)
        keys[:, HALF:] = cell_tail[...]
        scores[...] = dot(queries[...], keys[...], NT)
        spread = jnp.broadcast_to(near[at], (HALF, 4 * HALF))
        strip = pltpu.roll(spread, 3 * HALF, 1, stride=1, stride_axis=0)[:, : 3 * HALF]
        count = length // HALF
        store = pltpu.make_async_copy(prob.at[h], prob_full.at[at], local_sems.at[4 + h])
        if k > 0:
            store.wait()
        for i in range(count):
            first, last = max(i - 1, 0), min(i + 2, count)
            part = strip[:, (first - i + 1) * HALF : (last - i + 1) * HALF]
            span, near_span = slice(i * HALF, (i + 1) * HALF), slice(first * HALF, last * HALF)
            scores[span, near_span] = scores[span, near_span] + part
            row = scores[span, :]
            top = jnp.max(row, axis=1, keepdims=True)
            prob[h, span, :] = jnp.exp(row - top).astype(BF16)
        values = jnp.where(mine, qkv[k, :, 2 * HALF :].astype(F32), 1.0).astype(BF16)
        mixed = dot(prob[h], values)
        inv = 1.0 / pltpu.roll(mixed, HEAD_DIM, 1)
        mixed = (mixed * inv).astype(BF16)
        store.start()
        if h == 0:
            context[k] = mixed
            inverse[k] = inv
        else:
            context[k] = jnp.where(mine, mixed.astype(F32), context[k].astype(F32)).astype(BF16)
            inverse[k] = jnp.where(mine, inv, inverse[k])

    def project(k):
        if k > 0:
            load = pltpu.make_async_copy(att_full.at[k], weights, local_sems.at[3])
            load.start()
            load.wait()
        qkv[k] = dot(normed[...], weights[:, HALF:]).astype(BF16)
        mixed_all[:, k * HALF : (k + 1) * HALF] = weights[:, 0:HALF]

    def after_head(k, h):
        if (k, h) == (0, 0):
            att.plane_start(3)
            att.ring_forward()
        if (k, h) == (0, 1):
            att.corner_start(1)
            att.plane_start(2)
            ffn.ring_start(1)
            swap_rows("g", cot, near_g, far_g)
            att.finish(1)
        if (k, h) == (1, 0):
            att.corner_start(3)
        if (k, h) == (1, 1):
            att.corner_start(2)
            ffn.plane_start(1)
            ffn.ring_start(3)
            att.finish(3)
        if (k, h) == (3, 0):
            swap_pass("g")
        if (k, h) == (3, 1):
            ffn.corner_start(1)
            att.finish(2)
        if (k, h) == (2, 0):
            ffn.plane_start(3)
            ffn.ring_forward()

    for k in ORDER:
        project(k)
        if k == 0:
            att.plane_start(1)
        for h in range(2):
            head(k, h)
            after_head(k, h)

    for k in range(RING):
        out_rows[:, k * HALF : (k + 1) * HALF] = context[k]
    for i in range(length // BLOCK):
        span = slice(i * BLOCK, (i + 1) * BLOCK)
        mine_out[span, :] = dot(out_rows[span, :], mixed_all[...], NT).astype(BF16)
        lines.start(("out", i), mine_out.at[span], other_out.at[span], partner)
    place_rows(plane, core, near_g, far_g, cot_full)
    for r in range(PLANES):
        lanes = slice(r * BLOCK, (r + 1) * BLOCK)
        cot_t[lanes, :] = cot_full[:, lanes].astype(F32).T.astype(BF16)
    for i in range(length // BLOCK):
        span = slice(i * BLOCK, (i + 1) * BLOCK)
        lines.arrived(("out", i))
        row = full[span, :].astype(F32) + (
            mine_out[span, :].astype(F32) + other_out[span, :].astype(F32)
        )
        resid[span, :] = row
        scale = lax.rsqrt(jnp.mean(row * row, axis=1, keepdims=True) + NORM_EPSILON)
        value = row * scale * gains_here[1:2, :]
        normed_two[span, :] = value.astype(BF16)
        normed_two_t[:, span] = value.T.astype(BF16)

    ffn.finish(1)
    ffn.plane_arrived(3)
    ffn.forward_arrived()
    keep_ffn.wait()
    for h in range(2):
        pltpu.make_async_copy(prob.at[h], prob_full.at[2 * ORDER[-1] + h], local_sems.at[4 + h]).wait()
    swap_sent("x")
    swap_sent("g")
    att.forward_sent()
    ffn.forward_sent()
    lines.sent(
        *[
            name
            for name in lines.open
            if name[0] not in ("x", "g") and name[1] not in ("down", "up")
        ]
    )


def hot(reach, width):
    offsets = np.arange(width) - width // 2
    found = bucket_table(offsets, BUCKETS, reach)[None, :] == np.arange(HALF)[:, None]
    return jnp.asarray(found.astype(np.float32), BF16)


def forward(tokens, cotangent, gains, qkv_w, out_w, ffn_in, ffn_out, position_tables, page_counts, layout_cells):
    rows = tokens.shape[0]
    length = 2 * rows
    features = PLANES * BLOCK
    tables = position_tables.transpose(0, 2, 1).reshape(12, BUCKETS)
    tables = jnp.pad(tables, ((0, 4), (0, HALF - BUCKETS)))
    ints = jnp.concatenate(
        [
            layout_cells.reshape(4, length),
            jnp.broadcast_to(page_counts[:, None], (2, length)),
            jnp.zeros((2, length), jnp.int32),
        ]
    )
    args = [tokens, cotangent, gains, qkv_w, out_w, ffn_in, ffn_out, tables, ints]
    args += [hot(REL_REACH, 4 * HALF), hot(CELLS, HALF)]
    whole = pl.BlockSpec(memory_space=pltpu.VMEM)
    outside = pl.BlockSpec(memory_space=pl.ANY)
    outs = [
        shaped((RING, features, ATT)), shaped((RING, features, FFW)), shaped((2 * RING, length, length)),
        shaped((length, features)), shaped((2, features), F32), shaped((features, length)),
        shaped((length, features), F32), shaped((length, features)), shaped((features, length)),
        shaped((length, features)), shaped((features, length)),
        shaped((RING, length, 3 * HALF)), shaped((RING, length, HALF)), shaped((RING, length, HALF), F32),
        shaped((HALF, length)), shaped((length, HALF)), shaped((length, HALF)),
    ]
    scratch = [pltpu.VMEM((rows, features), BF16)] * 4 + [
        pltpu.VMEM(ints.shape, jnp.int32),
        pltpu.VMEM((RING,) + tables.shape, F32),
        pltpu.VMEM((6 * RING, HALF), F32),
        pltpu.VMEM((2 * RING, HALF, 2 * HALF), BF16),
        pltpu.VMEM((2 * RING, 1, 4 * HALF), F32),
        pltpu.VMEM((features, FFW), BF16),
        pltpu.VMEM(ffn_in.shape, BF16),
        pltpu.VMEM(ffn_out.shape, BF16),
        pltpu.VMEM((length, features), BF16),
        pltpu.VMEM((features, ATT), BF16),
        pltpu.VMEM((length, HALF), BF16),
        pltpu.VMEM((length, 2 * HALF), BF16),
        pltpu.VMEM((length, 2 * HALF), BF16),
        pltpu.VMEM((length, length), F32),
        pltpu.VMEM((2, length, length), BF16),
        pltpu.VMEM((features, RING * HALF), BF16),
        pltpu.VMEM((length, RING * HALF), BF16),
        pltpu.VMEM((length, features), BF16),
        pltpu.VMEM((length, features), BF16),
        pltpu.SemaphoreType.DMA((48,)),
        pltpu.SemaphoreType.DMA((48,)),
        pltpu.SemaphoreType.DMA((6,)),
    ]
    in_specs = [whole, outside, whole, whole, whole, outside, outside] + [whole] * 4
    out_specs = [outside] * 3 + [whole] * 14
    return pl.pallas_call(
        forward_kernel,
        out_shape=outs,
        in_specs=in_specs,
        out_specs=out_specs,
        scratch_shapes=scratch,
        name="forward",
        cost_estimate=pl.CostEstimate(flops=10**10, bytes_accessed=10**8, transcendentals=0),
        compiler_params=pltpu.CompilerParams(
            vmem_limit_bytes=63 * 1024 * 1024, collective_id=0, has_side_effects=True
        ),
    )(*args)


class Scatter:
    def __init__(self, lines, tag, k, grads, kept, buffers, where):
        self.lines, self.tag, self.k, self.grads, self.kept = lines, tag, k, grads, kept
        self.from_x, self.from_y, self.late, self.same, self.cross = buffers
        self.plane, self.core, self.ring = where
        self.to_x = device(self.plane ^ 1, self.core, self.ring)
        self.to_y = device(self.plane ^ 2, self.core, self.ring)

    def name(self, step):
        return (self.tag, step, self.k)

    def rows(self, r, half):
        return slice(r * BLOCK + half * HALF, r * BLOCK + (half + 1) * HALF)

    def start(self):
        k = self.k
        for step, r, half, target, goal in (
            ("x1", 3, 0, self.from_x.at[k, 1], self.to_x),
            ("y1", 3, 1, self.from_y.at[k, 1], self.to_y),
            ("x0", 1, 0, self.from_x.at[k, 0], self.to_x),
            ("y0", 2, 1, self.from_y.at[k, 0], self.to_y),
        ):
            self.lines.start(self.name(step), self.grads.at[self.rows(r, half)], target, goal)

    def middle(self):
        k = self.k
        self.lines.arrived(self.name("x1"), self.name("y1"))
        for source, r, half, at, goal, step in (
            (self.from_x, 2, 0, 0, self.to_y, "late0"),
            (self.from_y, 1, 1, 1, self.to_x, "late1"),
        ):
            kept = self.kept(r, half).astype(F32)
            source[k, 1] = (kept + source[k, 1].astype(F32)).astype(BF16)
            self.lines.start(self.name(step), source.at[k, 1], self.late.at[k, at], goal)

    def last(self):
        self.combine()
        self.hand_over()

    def combine(self):
        k, late = self.k, self.late
        self.lines.arrived(*[self.name(step) for step in ("x0", "y0", "late0", "late1")])
        upper = self.kept(0, 0).astype(F32) + self.from_x[k, 0].astype(F32) + late[k, 0].astype(F32)
        lower = self.kept(0, 1).astype(F32) + self.from_y[k, 0].astype(F32) + late[k, 1].astype(F32)
        late[k, 0] = jnp.where(self.core == 0, upper, lower).astype(BF16)
        late[k, 1] = jnp.where(self.core == 0, lower, upper).astype(BF16)

    def hand_over(self):
        k, late = self.k, self.late
        goal = (self.ring + k) % RING
        if k > 0:
            self.lines.start(
                self.name("same"), late.at[k, 0], self.same.at[k - 1], device(self.plane, self.core, goal)
            )
        self.lines.start(
            self.name("cross"), late.at[k, 1], self.cross.at[k], device(self.plane, 1 - self.core, goal)
        )


def gelu_parts(gate):
    square = gate * gate
    ratio = math.sqrt(2.0 / math.pi)
    bend = jnp.tanh(ratio * gate * (1.0 + 0.044715 * square))
    half_gate = 0.5 * gate
    value = half_gate + half_gate * bend
    slope = 0.5 + 0.5 * bend + half_gate * (1.0 - bend * bend) * (
        ratio * (1.0 + 3.0 * 0.044715 * square)
    )
    return value, slope


def middle_kernel(
    normed, normed_t, cot, cot_t, resid, gains_here, ffn_before,
    ffn_full, grads_full, low, low_t, half_grad, page_out, gain, late,
    weights, hidden, grads, total_in, total_out, mine, other, mine_out, other_out,
    kept, from_x, from_y,
    send_sems, recv_sems, local_sems,
):
    plane, core, ring = where = here()
    partner = device(plane, 1 - core, ring)
    lines = Lines(send_sems, recv_sems)
    length = normed.shape[0]
    rows = length // 2
    blocks = length // BLOCK

    gather = Gather(lines, "ffn", None, ffn_full, where)

    def load(at):
        return pltpu.make_async_copy(
            ffn_full.at[ORDER[at]], weights.at[at % 2], local_sems.at[at % 2]
        )

    def store(k):
        return pltpu.make_async_copy(grads, grads_full.at[k], local_sems.at[2])

    loads = [
        pltpu.make_async_copy(
            grads_full.at[0, first : first + BLOCK], kept.at[at : at + BLOCK], local_sems.at[3 + i]
        )
        for i, (first, at) in enumerate(((0, 0), (3 * HALF, BLOCK)))
    ]
    spots = {(0, 0): 0, (0, 1): HALF, (1, 1): BLOCK, (2, 0): BLOCK + HALF}
    scatter = Scatter(
        lines, "grads", 0, grads_full.at[0],
        lambda r, half: kept[spots[r, half] : spots[r, half] + HALF],
        (from_x, from_y, late, None, None), where,
    )
    load(0).start()
    load(1).start()
    greet([partner, device(plane ^ 1, core, ring), device(plane ^ 2, core, ring)])
    gather.corner_start(3, landed=True)
    gather.plane_start(2, landed=True)
    for at, k in enumerate(ORDER):
        load(at).wait()
        w = weights.at[at % 2]
        for i in range(blocks):
            span = slice(i * BLOCK, (i + 1) * BLOCK)
            both = dot(normed[span, :], w[:, UNITS:])
            grad_hidden = dot(cot[span, :], w[:, :UNITS])
            gate, up = both[:, :UNITS], both[:, UNITS:]
            value, slope = gelu_parts(gate)
            hidden[span, :UNITS] = (value * up).astype(BF16)
            hidden[span, UNITS : 2 * UNITS] = (grad_hidden * up * slope).astype(BF16)
            hidden[span, 2 * UNITS :] = (grad_hidden * value).astype(BF16)
            part_in = dot(hidden[span, UNITS:], w[:, UNITS:], NT)
            part_out = dot(hidden[span, :UNITS], w[:, :UNITS], NT)
            if at > 0:
                part_in = total_in[span, :] + part_in
                part_out = total_out[span, :] + part_out
            if at + 1 < RING:
                total_in[span, :] = part_in
                total_out[span, :] = part_out
            else:
                mine[span, :] = part_in.astype(BF16)
                lines.start(("in", i), mine.at[span], other.at[span], partner)
                mine_out[span, :] = part_out.astype(BF16)
        if at + 1 == RING:
            far = pl.ds(pl.multiple_of((1 - core) * rows, rows), rows)
            lines.start("out", mine_out.at[far], other_out, partner)
        if at > 0:
            store(ORDER[at - 1]).wait()
        if at == 1:
            gather.finish(3)
            load(2).start()
            gather.corner_start(2)
            scatter.start()
            for copy in loads:
                copy.start()
        if at == 2:
            gather.finish(2)
            load(3).start()
        for i in range(2):
            span = slice(i * 2 * BLOCK, (i + 1) * 2 * BLOCK)
            grads[span, :UNITS] = dot(cot_t[span, :], hidden[:, :UNITS]).astype(BF16)
            grads[span, UNITS:] = dot(normed_t[span, :], hidden[:, UNITS:]).astype(BF16)
        store(k).start()
        if at == 2:
            for copy in loads:
                copy.wait()
            scatter.middle()

    total = jnp.zeros((1, resid.shape[1]), F32)
    for i in range(blocks):
        span = slice(i * BLOCK, (i + 1) * BLOCK)
        lines.arrived(("in", i))
        row = resid[span, :]
        grad = mine[span, :].astype(F32) + other[span, :].astype(F32)
        scale = lax.rsqrt(jnp.mean(row * row, axis=1, keepdims=True) + NORM_EPSILON)
        weighted = grad * gains_here[1:2, :]
        center = jnp.mean(row * weighted, axis=1, keepdims=True)
        value = cot[span, :].astype(F32) + scale * weighted - row * (scale * scale * scale * center)
        low[span, :] = value.astype(BF16)
        low_t[:, span] = value.T.astype(BF16)
        in_half = core == (i * BLOCK) // rows
        total = total + jnp.where(in_half, jnp.sum(grad * row * scale, axis=0, keepdims=True), 0.0)

        @pl.when(in_half)
        def _():
            first = (i * BLOCK) % rows
            half_grad[first : first + BLOCK, :] = value

    for r in range(PLANES):
        gain[:, columns(plane, r)] = total[:, r * BLOCK : (r + 1) * BLOCK]
    lines.arrived("out")
    for i in range(rows // BLOCK):
        span = slice(i * BLOCK, (i + 1) * BLOCK)
        near = pl.ds(pl.multiple_of(core * rows + i * BLOCK, BLOCK), BLOCK)
        row = resid[near, :] + (mine_out[near, :].astype(F32) + other_out[span, :].astype(F32))
        for r in range(PLANES):
            page_out[span, columns(plane, r)] = row[:, r * BLOCK : (r + 1) * BLOCK].astype(BF16)
    scatter.combine()
    store(ORDER[-1]).wait()
    lines.sent()


def middle(normed, normed_t, cot, cot_t, resid, gains_here, ffn_full):
    length, features = normed.shape
    rows = length // 2
    whole = pl.BlockSpec(memory_space=pltpu.VMEM)
    outside = pl.BlockSpec(memory_space=pl.ANY)
    return pl.pallas_call(
        middle_kernel,
        out_shape=[
            shaped((RING, features, FFW)), shaped((RING, features, FFW)),
            shaped((length, features)), shaped((features, length)),
            shaped((rows, features), F32), shaped((rows, features)), shaped((1, features), F32),
            shaped((1, 2, HALF, FFW)),
        ],
        in_specs=[whole] * 6 + [outside],
        out_specs=[outside] * 2 + [whole] * 6,
        input_output_aliases={6: 0},
        scratch_shapes=[
            pltpu.VMEM((2, features, FFW), BF16),
            pltpu.VMEM((length, FFW), BF16),
            pltpu.VMEM((features, FFW), BF16),
            pltpu.VMEM((length, features), F32),
            pltpu.VMEM((length, features), F32),
            pltpu.VMEM((length, features), BF16),
            pltpu.VMEM((length, features), BF16),
            pltpu.VMEM((length, features), BF16),
            pltpu.VMEM((rows, features), BF16),
            pltpu.VMEM((2 * BLOCK, FFW), BF16),
            pltpu.VMEM((1, 2, HALF, FFW), BF16),
            pltpu.VMEM((1, 2, HALF, FFW), BF16),
            pltpu.SemaphoreType.DMA((20,)),
            pltpu.SemaphoreType.DMA((20,)),
            pltpu.SemaphoreType.DMA((5,)),
        ],
        name="middle",
        cost_estimate=pl.CostEstimate(flops=27 * 10**9, bytes_accessed=10**8, transcendentals=0),
        compiler_params=pltpu.CompilerParams(
            vmem_limit_bytes=63 * 1024 * 1024, collective_id=1, has_side_effects=True
        ),
    )(normed, normed_t, cot, cot_t, resid, gains_here, ffn_full)


def sum_ring(lines, tag, late, same, cross):
    for k in range(RING):
        if k > 0:
            lines.arrived((tag, "same", k))
        lines.arrived((tag, "cross", k))
    mine = late[0, 0].astype(F32)
    for k in range(1, RING):
        mine = mine + same[k - 1].astype(F32)
    other = cross[0].astype(F32)
    for k in range(1, RING):
        other = other + cross[k].astype(F32)
    return mine, other


def backward_kernel(
    low, low_t, normed_t, half_grad, full, gains_here, qkv, context, inverse,
    cells_t, cells_twice, cell_tail, near_hot, cell_hot, gain_two, ffn_first,
    att_full, prob_full, ffn_grads, page_out,
    layer_out, tokens_grad, qkv_grad, out_grad, inner_grad, outer_grad, small_out,
    weights, prob, scaled, scaled_low, keys, dscores, grad_qkv, att_grads, total, mine_half, far_half,
    other_half, page_low, swapped, ffn_kept,
    att_x, att_y, att_late, att_same, att_cross, ffn_x, ffn_y, ffn_late, ffn_same, ffn_cross,
    diag_near, diag_cell, gain_one, small, small_ring, small_plane, small_core,
    send_sems, recv_sems, local_sems,
):
    plane, core, ring = where = here()
    native = core == ring % 2
    length = low.shape[0]
    rows = length // 2
    count = length // HALF
    partner = device(plane, 1 - core, ring)
    swap = device(plane, 1 - core, ring ^ 1)
    partners = [partner, swap, device(plane ^ 1, core, ring), device(plane ^ 2, core, ring)]
    for k in range(1, RING):
        partners += [device(plane, core, (ring + k) % RING), device(plane, 1 - core, (ring + k) % RING)]
    lines = Lines(send_sems, recv_sems)

    def load_prob(at):
        head_at = 2 * BACK_ORDER[at // 2] + at % 2
        return pltpu.make_async_copy(prob_full.at[head_at], prob.at[at % 2], local_sems.at[at % 2])

    def load_weights(k):
        return pltpu.make_async_copy(att_full.at[k], weights.at[SLOT[k]], local_sems.at[2 + SLOT[k]])

    def load_kept(k):
        slot = KEPT_SLOT[k]
        return [
            pltpu.make_async_copy(
                ffn_grads.at[k, first : first + BLOCK],
                ffn_kept.at[slot, at : at + BLOCK],
                local_sems.at[4 + 2 * slot + i],
            )
            for i, (first, at) in enumerate(((0, 0), (3 * HALF, BLOCK)))
        ]

    load_prob(0).start()
    load_prob(1).start()
    load_weights(BACK_ORDER[0]).start()
    goals = [partner, device(plane ^ 1, core, ring), device(plane ^ 2, core, ring)] + partners[4:]
    greet(goals)

    def kept_ffn(k):
        spots = {(0, 0): 0, (0, 1): HALF, (1, 1): BLOCK, (2, 0): BLOCK + HALF}
        return lambda r, half: ffn_kept[KEPT_SLOT[k], spots[r, half] : spots[r, half] + HALF]

    def kept_att(k):
        def read(r, half):
            first = r * BLOCK + half * HALF
            return att_grads[k, first : first + HALF]

        return read

    ffn = [
        Scatter(lines, "ffn", k, ffn_grads.at[k], kept_ffn(k), (ffn_x, ffn_y, ffn_late, ffn_same, ffn_cross), where)
        for k in range(RING)
    ]
    att = [
        Scatter(lines, "att", k, att_grads.at[k], kept_att(k), (att_x, att_y, att_late, att_same, att_cross), where)
        for k in range(RING)
    ]

    def ffn_start(k):
        for copy in load_kept(k):
            copy.start()
        ffn[k].start()

    def ffn_middle(k):
        for copy in load_kept(k):
            copy.wait()
        ffn[k].middle()

    ffn_start(2)
    ffn_late[0] = ffn_first[0]
    ffn[0].hand_over()
    lines.make("layer", page_out, layer_out, swap)

    @pl.when(jnp.logical_not(native))
    def _():
        lines.open["layer"].start()

    lane = pair_lane(length)
    row_block = lax.broadcasted_iota(jnp.int32, (length, HALF), 0) // HALF
    flip_at = lax.broadcasted_iota(jnp.int32, (HALF, HALF), 0)
    flip_to = lax.broadcasted_iota(jnp.int32, (HALF, HALF), 1)
    flip = jnp.where(flip_at + flip_to == HALF - 1, 1.0, 0.0).astype(BF16)

    def enter(k):
        at = BACK_ORDER.index(k)
        if at + 1 < RING:
            load_weights(BACK_ORDER[at + 1]).start()
        load_weights(k).wait()
        grad_context = dot(low[...], weights[SLOT[k], :, 0:HALF]).astype(BF16).astype(F32)
        value = grad_context * inverse[k]
        scaled[...] = value
        scaled_low[...] = value.astype(BF16)

    def head(k, h):
        at = 2 * k + h
        mine = (lane // HEAD_DIM) == h
        value = scaled[...]
        delta = -jnp.sum(
            jnp.where(mine, value * context[k].astype(F32), 0.0), axis=1, keepdims=True
        )
        delta_high = delta.astype(BF16).astype(F32)
        spare = HEAD_DIM * (1 - h)
        fill = jnp.where(lane == spare + 1, delta - delta_high, 0.0)
        left = jnp.where(mine, value, jnp.where(lane == spare, delta_high, fill)).astype(BF16)
        ones = jnp.where((lane == spare) | (lane == spare + 1), 1.0, 0.0)
        right = jnp.where(mine, qkv[k, :, 2 * HALF :].astype(F32), ones).astype(BF16)
        turn = 2 * BACK_ORDER.index(k) + h
        load_prob(turn).wait()
        strips = [jnp.zeros((HALF, HALF), F32) for _ in range(3)]
        for i in range(length // BLOCK):
            span = slice(i * BLOCK, (i + 1) * BLOCK)
            dscore = prob[at % 2, span, :].astype(F32) * dot(left[span, :], right, NT)
            dscores[span, :] = dscore.astype(BF16)
            for part in range(BLOCK // HALF):
                for step in range(3):
                    block = i * (BLOCK // HALF) + part + step - 1
                    if 0 <= block < count:
                        strips[step] = strips[step] + dscore[
                            part * HALF : (part + 1) * HALF, block * HALF : (block + 1) * HALF
                        ]
        keys[:, :HALF] = jnp.where(
            mine, qkv[k, :, HALF : 2 * HALF].astype(F32), cells_twice[...].astype(F32)
        ).astype(BF16)
        keys[:, HALF:] = cell_tail[...]
        grad_left = dot(dscores[...], keys[...])
        grad_key = dot(dscores[...], qkv[k, :, :HALF], TN)
        grad_value = dot(prob[at % 2], scaled_low[...], TN)
        if turn + 2 < 2 * RING:
            load_prob(turn + 2).start()
        for m, new in enumerate((grad_left[:, :HALF], grad_key, grad_value)):
            lanes = slice(m * HALF, (m + 1) * HALF)
            if h == 1:
                new = jnp.where(mine, new, grad_qkv[:, lanes].astype(F32))
            grad_qkv[:, lanes] = new.astype(BF16)

        skewed = jnp.zeros((HALF, 3 * HALF), F32)
        strip = jnp.concatenate(strips, axis=1)
        for part in split_bf16(strip):
            skewed = skewed + dot(flip, part)
        skewed = jnp.concatenate([skewed, jnp.zeros((HALF, HALF), F32)], axis=1)
        sums = jnp.sum(pltpu.roll(skewed, 1, 1, stride=1, stride_axis=0), axis=0, keepdims=True)
        tail = grad_left[:, HALF:]
        in_tail = (lane >= HEAD_DIM) & (lane < HEAD_DIM + 8)
        far_left = jnp.sum(jnp.where(in_tail & (lane % 8 < row_block - 1), tail, 0.0), axis=0, keepdims=True)
        far_right = jnp.sum(jnp.where(in_tail & (lane % 8 > row_block + 1), tail, 0.0), axis=0, keepdims=True)
        wide = lax.broadcasted_iota(jnp.int32, (1, 4 * HALF), 1)
        sums = sums + jnp.where(wide == 0, jnp.sum(far_left, axis=1, keepdims=True), 0.0)
        sums = sums + jnp.where(wide == 4 * HALF - 1, jnp.sum(far_right, axis=1, keepdims=True), 0.0)
        diag_near[at : at + 1, :] = sums
        by_cell = grad_left[:, :HALF]
        by_cell = jnp.where(mine, pltpu.roll(by_cell, HEAD_DIM, 1), by_cell)
        for axis, table in enumerate((by_cell, tail)):
            table_high = table.astype(BF16)
            rest = (table - table_high.astype(F32)).astype(BF16)
            side = cells_t[axis * CELLS : (axis + 1) * CELLS, :]
            grid = dot(side, table_high) + dot(side, rest)
            cell_lane = lax.broadcasted_iota(jnp.int32, (CELLS, HALF), 1)
            grid = jnp.where(cell_lane < CELLS, grid, 0.0)
            grid = pltpu.roll(grid, 1, 1, stride=1, stride_axis=0)
            row = axis * 2 * RING + at
            diag_cell[row : row + 1, :] = jnp.sum(grid, axis=0, keepdims=True)

    def leave(k):
        w = weights[SLOT[k], :, HALF:]
        att_grads[k, :, 0:HALF] = dot(low_t[...], context[k]).astype(BF16)
        att_grads[k, :, HALF:] = dot(normed_t[...], grad_qkv[...]).astype(BF16)
        if k == BACK_ORDER[-1]:
            att[k].start()
        for i in range(length // BLOCK):
            span = slice(i * BLOCK, (i + 1) * BLOCK)
            part = dot(grad_qkv[span, :], w, NT)
            total[span, :] = part if k == BACK_ORDER[0] else total[span, :] + part

    enter(2)
    head(2, 0)
    head(2, 1)
    ffn_middle(2)
    ffn_start(1)
    leave(2)
    enter(1)
    head(1, 0)
    ffn[2].last()
    head(1, 1)
    leave(1)
    ffn_middle(1)
    ffn_start(3)
    enter(3)
    head(3, 0)
    att[2].start()
    head(3, 1)
    ffn[1].last()
    leave(3)
    enter(0)
    head(0, 0)
    ffn_middle(3)
    att[1].start()
    head(0, 1)
    att[2].middle()
    att[3].start()
    leave(0)
    ffn[3].last()

    near = pl.ds(pl.multiple_of(core * rows, rows), rows)
    far = pl.ds(pl.multiple_of((1 - core) * rows, rows), rows)
    far_half[...] = total[far, :].astype(BF16)
    lines.start("half", far_half, other_half, partner)
    mine_half[...] = total[near, :].astype(BF16)
    lines.arrived("half")
    gain = jnp.zeros((1, full.shape[1]), F32)
    for i in range(rows // BLOCK):
        span = slice(i * BLOCK, (i + 1) * BLOCK)
        x = full[pl.ds(pl.multiple_of(core * rows + i * BLOCK, BLOCK), BLOCK), :].astype(F32)
        grad = mine_half[span, :].astype(F32) + other_half[span, :].astype(F32)
        scale = lax.rsqrt(jnp.mean(x * x, axis=1, keepdims=True) + NORM_EPSILON)
        weighted = grad * gains_here[0:1, :]
        center = jnp.mean(x * weighted, axis=1, keepdims=True)
        value = half_grad[span, :] + scale * weighted - x * (scale * scale * scale * center)
        gain = gain + jnp.sum(grad * x * scale, axis=0, keepdims=True)
        for r in range(PLANES):
            block = value[:, r * BLOCK : (r + 1) * BLOCK]
            tokens_grad[span, columns(plane, r)] = block
            page_low[span, columns(plane, r)] = block.astype(BF16)
    for r in range(PLANES):
        gain_one[:, columns(plane, r)] = gain[:, r * BLOCK : (r + 1) * BLOCK]
    lines.make("swap", page_low, swapped, swap)

    @pl.when(jnp.logical_not(native))
    def _():
        lines.open["swap"].start()

    near_sums = sum(dot(part, near_hot[...], NT) for part in split_bf16(diag_near[...]))
    cell_sums = sum(dot(part, cell_hot[...], NT) for part in split_bf16(diag_cell[...]))
    for k in range(RING):
        small[k, 0:2, :] = near_sums[2 * k : 2 * k + 2, :]
        for axis in range(2):
            first = axis * 2 * RING + 2 * k
            small[k, 2 * axis + 2 : 2 * axis + 4, :] = cell_sums[first : first + 2, :]
        small[k, 6:8, :] = jnp.zeros((2, HALF), F32)
        for j in range(8):
            lanes = slice(j * HALF, (j + 1) * HALF)
            small[k, 8 + j : 9 + j, :] = gain_one[:, lanes]
            small[k, 16 + j : 17 + j, :] = gain_two[:, lanes]
    for k in range(1, RING):
        lines.start(("small", k), small.at[k], small_ring.at[k], device(plane, core, (ring + k) % RING))
    att[2].last()
    att[1].middle()
    att[3].middle()
    for k in range(1, RING):
        lines.arrived(("small", k))
    small_plane[0] = small[0] + (small_ring[1] + (small_ring[2] + small_ring[3]))
    lines.start("smallx", small_plane.at[0], small_plane.at[1], device(plane ^ 1, core, ring))
    att[1].last()
    att[0].middle()
    lines.arrived("smallx")
    small_plane[2] = small_plane[0] + small_plane[1]
    lines.start("smally", small_plane.at[2], small_plane.at[3], device(plane ^ 2, core, ring))
    att[3].last()
    lines.arrived("smally")
    small_core[0] = small_plane[2] + small_plane[3]
    lines.start("smallc", small_core.at[0], small_core.at[1], partner)
    att[0].last()

    mine, other = sum_ring(lines, "ffn", ffn_late, ffn_same, ffn_cross)
    rest = inner_grad.shape[1] - UNITS
    first_core = jnp.where(core == 0, mine, other)
    second_core = jnp.where(core == 0, other, mine)
    for m in range(2):
        at = (m + 1) * UNITS
        inner_grad[m, 0:UNITS, :] = first_core[:, at : at + UNITS].T
        inner_grad[m, UNITS : UNITS + rest, :] = second_core[:, at : at + UNITS].T[0:rest]
    outer_grad[0:UNITS, :] = first_core[:, 0:UNITS].T
    outer_grad[UNITS : UNITS + rest, :] = second_core[:, 0:UNITS].T[0:rest]

    @pl.when(jnp.logical_not(native))
    def _():
        lines.arrived("swap")
        tokens_grad[...] = swapped[...].astype(F32)

    mine, other = sum_ring(lines, "att", att_late, att_same, att_cross)
    first_core = jnp.where(core == 0, mine, other)
    second_core = jnp.where(core == 0, other, mine)
    for m in range(3):
        lanes = slice((m + 1) * HALF, (m + 2) * HALF)
        qkv_grad[m, :, 0:HALF] = first_core[:, lanes]
        qkv_grad[m, :, HALF : 2 * HALF] = second_core[:, lanes]
    out_grad[0:HALF, :] = first_core[:, 0:HALF].T
    out_grad[HALF : 2 * HALF, :] = second_core[:, 0:HALF].T

    lines.arrived("smallc")
    low_core = jnp.where(core == 0, small_core[0], small_core[1])
    high_core = jnp.where(core == 0, small_core[1], small_core[0])
    small_out[0] = low_core
    small_out[1] = high_core

    @pl.when(jnp.logical_not(native))
    def _():
        lines.arrived("layer")
        lines.sent("layer", "swap")

    lines.sent(*[name for name in lines.open if name not in ("layer", "swap")])


def backward(low, low_t, normed_t, half_grad, full, gains_here, qkv, context, inverse, cells_t, cells_twice, cell_tail, gain_two, ffn_first, att_full, prob_full, ffn_grads, page_out, units):
    length, features = low.shape
    rows = length // 2
    whole = pl.BlockSpec(memory_space=pltpu.VMEM)
    outside = pl.BlockSpec(memory_space=pl.ANY)
    args = [low, low_t, normed_t, half_grad, full, gains_here, qkv, context, inverse]
    args += [cells_t, cells_twice, cell_tail, hot(REL_REACH, 4 * HALF), hot(CELLS, HALF), gain_two, ffn_first]
    args += [att_full, prob_full, ffn_grads, page_out]

    def buffers(width):
        return [
            pltpu.VMEM((RING, 2, HALF, width), BF16),
            pltpu.VMEM((RING, 2, HALF, width), BF16),
            pltpu.VMEM((RING, 2, HALF, width), BF16),
            pltpu.VMEM((RING - 1, HALF, width), BF16),
            pltpu.VMEM((RING, HALF, width), BF16),
        ]

    return pl.pallas_call(
        backward_kernel,
        out_shape=[
            shaped((rows, features)), shaped((rows, features), F32),
            shaped((3, HALF, 2 * HALF), F32), shaped((2 * HALF, HALF), F32),
            shaped((2, units, HALF), F32), shaped((units, HALF), F32), shaped((2, 24, HALF), F32),
        ],
        in_specs=[whole] * 16 + [outside] * 4,
        out_specs=[outside] + [whole] * 6,
        scratch_shapes=[
            pltpu.VMEM((2, features, ATT), BF16),
            pltpu.VMEM((2, length, length), BF16),
            pltpu.VMEM((length, HALF), F32),
            pltpu.VMEM((length, HALF), BF16),
            pltpu.VMEM((length, 2 * HALF), BF16),
            pltpu.VMEM((length, length), BF16),
            pltpu.VMEM((length, 3 * HALF), BF16),
            pltpu.VMEM((RING, features, ATT), BF16),
            pltpu.VMEM((length, features), F32),
            pltpu.VMEM((rows, features), BF16),
            pltpu.VMEM((rows, features), BF16),
            pltpu.VMEM((rows, features), BF16),
            pltpu.VMEM((rows, features), BF16),
            pltpu.VMEM((rows, features), BF16),
            pltpu.VMEM((2, 2 * BLOCK, FFW), BF16),
            *buffers(ATT),
            *buffers(FFW),
            pltpu.VMEM((2 * RING, 4 * HALF), F32),
            pltpu.VMEM((4 * RING, HALF), F32),
            pltpu.VMEM((1, features), F32),
            pltpu.VMEM((RING, 24, HALF), F32),
            pltpu.VMEM((RING, 24, HALF), F32),
            pltpu.VMEM((4, 24, HALF), F32),
            pltpu.VMEM((2, 24, HALF), F32),
            pltpu.SemaphoreType.DMA((80,)),
            pltpu.SemaphoreType.DMA((80,)),
            pltpu.SemaphoreType.DMA((9,)),
        ],
        name="backward",
        cost_estimate=pl.CostEstimate(flops=3 * 10**10, bytes_accessed=10**8, transcendentals=0),
        compiler_params=pltpu.CompilerParams(
            vmem_limit_bytes=63 * 1024 * 1024, collective_id=2, has_side_effects=True
        ),
    )(*args)


def page_body(
    tokens,
    norm_gains,
    attn_qkv,
    attn_out,
    ffn_in,
    ffn_out,
    position_tables,
    page_counts,
    layout_cells,
    cotangent,
):
    group, ring = lax.axis_index("dp"), lax.axis_index("tensor")
    (
        att_full, ffn_full, prob, full, gains_here, normed_one_t, resid, normed_two, normed_two_t,
        cot, cot_t, qkv, context, inverse, cells_t, cells_twice, cell_tail,
    ) = forward(
        tokens, cotangent, norm_gains, attn_qkv, attn_out, ffn_in.transpose(0, 2, 1), ffn_out, position_tables,
        page_counts, layout_cells,
    )
    _, ffn_grads, low, low_t, half_grad, page_out, gain_two, ffn_first = middle(
        normed_two, normed_two_t, cot, cot_t, resid, gains_here, ffn_full
    )
    page_got, tokens_grad, qkv_grad, out_grad, inner_grad, outer_grad, small = backward(
        low, low_t, normed_one_t, half_grad, full, gains_here, qkv, context, inverse, cells_t,
        cells_twice, cell_tail, gain_two, ffn_first, att_full, prob, ffn_grads, page_out, ffn_in.shape[2],
    )
    layer_out = jnp.where(group % CORES == ring % 2, page_out, page_got)
    gains = (small[0, 8:] + small[1, 8:]).reshape(2, 1024)
    gains_grad = lax.dynamic_slice_in_dim(gains, (group * RING + ring) * 32, 32, axis=1)
    tables = small[:, 0:6, :BUCKETS].reshape(CORES, 3, 2, BUCKETS).transpose(1, 3, 0, 2)
    tables = tables.reshape(3, BUCKETS, 2 * CORES)
    tables_grad = lax.dynamic_slice_in_dim(tables, group * 4, 4, axis=1)
    return (
        layer_out,
        tokens_grad,
        gains_grad,
        qkv_grad,
        out_grad,
        inner_grad.transpose(0, 2, 1),
        outer_grad,
        tables_grad,
    )


def solution(mesh):
    return jax.shard_map(
        page_body if page_plan(mesh) else general_body,
        mesh=mesh,
        in_specs=(
            P(("dp", "tensor"), None),
            P(),
            P(None, None, "tensor"),
            P("tensor", None),
            P(None, None, "tensor"),
            P("tensor", None),
            P(None, None, "tensor"),
            P("dp"),
            P(None, "dp"),
            P(("dp", "tensor"), None),
        ),
        out_specs=(
            P(("dp", "tensor"), None),
            P(("dp", "tensor"), None),
            P(None, ("dp", "tensor")),
            P(None, "dp", "tensor"),
            P("tensor", "dp"),
            P(None, "dp", "tensor"),
            P("tensor", "dp"),
            P(None, "dp", "tensor"),
        ),
        check_vma=False,
    )
```

```python
import math

import jax
import jax.numpy as jnp
import numpy as np
from jax import lax
from jax.experimental import pallas as pl
from jax.experimental.pallas import tpu as pltpu
from jax.sharding import PartitionSpec as P

HEAD_DIM = 64
BUCKETS = 32
REL_REACH = 128
CELLS = 64
PAGE_LEN = 1024


HIGHEST_PRECISION = lax.Precision.HIGHEST
TABLE_PRECISION = lax.Precision.HIGH
NORM_EPSILON = 1e-06
MASK_VALUE = -1e30


def bucket_table(offsets, bucket_total, max_reach):
    half_total = bucket_total // 2
    exact_limit = half_total // 2
    distance = np.abs(offsets).astype(np.int32)
    upper_side = (offsets > 0).astype(np.int32) * half_total
    safe_dist = np.maximum(distance, 1).astype(np.float32)
    ratio = np.log(safe_dist / np.float32(exact_limit)) / np.float32(
        math.log(max_reach / exact_limit)
    )
    far_bucket = exact_limit + np.floor(ratio * np.float32(half_total - exact_limit)).astype(
        np.int32
    )
    far_bucket = np.minimum(far_bucket, half_total - 1)
    return (upper_side + np.where(distance < exact_limit, distance, far_bucket)).astype(np.int32)


def offset_onehot(length):
    offsets = np.arange(2 * length - 1) - (length - 1)
    buckets = bucket_table(offsets, BUCKETS, REL_REACH)
    return jnp.asarray((buckets[:, None] == np.arange(BUCKETS)[None, :]).astype(np.float32))


def layout_onehot():
    cell_range = np.arange(CELLS)
    buckets = bucket_table(cell_range[None, :] - cell_range[:, None], BUCKETS, CELLS)
    return jnp.asarray(
        (buckets.reshape(-1)[:, None] == np.arange(BUCKETS)[None, :]).astype(np.float32)
    )


def gelu_tanh(values):
    return jax.nn.gelu(values, approximate=True)


def relative_bias(table_rows, length):
    values = jnp.dot(offset_onehot(length), table_rows, precision=HIGHEST_PRECISION).T
    heads_dev = values.shape[0]
    padded = jnp.pad(values, ((0, 0), (0, 1)))
    tiled = jnp.tile(padded, (1, length))
    skewed = tiled[:, : length * (2 * length - 1)].reshape(heads_dev, length, 2 * length - 1)
    return skewed[:, :, length - 1 :]


def relative_sums(dscore, length):
    heads_dev = dscore.shape[0]
    placed = jnp.pad(dscore, ((0, 0), (0, 0), (length - 1, 0)))
    flat = jnp.pad(placed.reshape(heads_dev, length * (2 * length - 1)), ((0, 0), (0, length)))
    return jnp.sum(flat.reshape(heads_dev, length, 2 * length), axis=1)[:, : 2 * length - 1]


def layout_values(tables):
    values = jnp.einsum("mn,snh->shm", layout_onehot(), tables[1:], precision=HIGHEST_PRECISION)
    return values.reshape(2, tables.shape[2], CELLS, CELLS)


def cell_onehots(page_cells):
    onehot = (page_cells[:, :, None] == jnp.arange(CELLS)[None, None, :]).astype(jnp.float32)
    length = page_cells.shape[1]
    joined = onehot.transpose(1, 0, 2).reshape(length, 2 * CELLS)
    return (onehot, joined)


def layout_bias(page_cells, lay_vals):
    onehot, joined = cell_onehots(page_cells)
    length = page_cells.shape[1]
    heads_dev = lay_vals.shape[1]
    rows_side = jnp.einsum("sia,shab->hisb", onehot, lay_vals, precision=TABLE_PRECISION)
    rows_side = rows_side.reshape(heads_dev, length, 2 * CELLS)
    return jnp.einsum("hic,jc->hij", rows_side, joined, precision=TABLE_PRECISION)


def layout_sums(dscore, page_cells):
    onehot, joined = cell_onehots(page_cells)
    length = page_cells.shape[1]
    heads_dev = dscore.shape[0]
    partial_rows = jnp.einsum("hij,jc->hic", dscore, joined, precision=TABLE_PRECISION)
    partial_rows = partial_rows.reshape(heads_dev, length, 2, CELLS)
    return jnp.einsum("sia,hisb->shab", onehot, partial_rows, precision=TABLE_PRECISION)


def page_scores(query, key_rows, count, page_cells, rel_bias, lay_vals):
    length = query.shape[0]
    scores = jnp.einsum("ihd,jhd->hij", query, key_rows, preferred_element_type=jnp.float32)
    scores = scores + rel_bias + layout_bias(page_cells, lay_vals)
    valid = jnp.arange(length) < count
    return jnp.where(valid[None, None, :], scores, MASK_VALUE)


def attend(projected, page_counts, layout_cells, rel_bias, lay_vals):
    total_rows = projected.shape[1]
    pages = page_counts.shape[0]
    length = total_rows // pages
    heads_dev = projected.shape[2] // HEAD_DIM
    split = projected.reshape(3, pages, length, heads_dev, HEAD_DIM)
    cells_pages = layout_cells.reshape(2, pages, length).transpose(1, 0, 2)

    def one_page(items):
        query, key_rows, value_rows, count, page_cells = items
        scores = page_scores(query, key_rows, count, page_cells, rel_bias, lay_vals)
        log_total = jax.nn.logsumexp(scores, axis=2)
        prob_low = jnp.exp(scores - log_total[:, :, None]).astype(jnp.bfloat16)
        context = jnp.einsum(
            "hij,jhd->ihd", prob_low, value_rows, preferred_element_type=jnp.float32
        )
        return (context.astype(jnp.bfloat16).reshape(length, heads_dev * HEAD_DIM), log_total)

    context, log_totals = lax.map(
        one_page, (split[0], split[1], split[2], page_counts, cells_pages)
    )
    return (context.reshape(total_rows, heads_dev * HEAD_DIM), log_totals)


def attend_back(projected, grad_context, log_totals, page_counts, layout_cells, rel_bias, lay_vals):
    total_rows = projected.shape[1]
    pages = page_counts.shape[0]
    length = total_rows // pages
    heads_dev = projected.shape[2] // HEAD_DIM
    split = projected.reshape(3, pages, length, heads_dev, HEAD_DIM)
    grad_split = grad_context.reshape(pages, length, heads_dev, HEAD_DIM)
    cells_pages = layout_cells.reshape(2, pages, length).transpose(1, 0, 2)

    def page_step(carry, items):
        rel_acc, lay_acc = carry
        query, key_rows, value_rows, grad_ctx, page_lse, count, page_cells = items
        scores = page_scores(query, key_rows, count, page_cells, rel_bias, lay_vals)
        prob = jnp.exp(scores - page_lse[:, :, None])
        grad_prob = jnp.einsum(
            "ihd,jhd->hij", grad_ctx, value_rows, preferred_element_type=jnp.float32
        )
        delta = jnp.sum(grad_prob * prob, axis=2, keepdims=True)
        dscore = prob * (grad_prob - delta)
        rel_acc = rel_acc + relative_sums(dscore, length)
        lay_acc = lay_acc + layout_sums(dscore, page_cells)
        score_low = dscore.astype(jnp.bfloat16)
        grad_query = jnp.einsum(
            "hij,jhd->ihd", score_low, key_rows, preferred_element_type=jnp.float32
        ).astype(jnp.bfloat16)
        grad_key = jnp.einsum(
            "hij,ihd->jhd", score_low, query, preferred_element_type=jnp.float32
        ).astype(jnp.bfloat16)
        grad_value = jnp.einsum(
            "hij,ihd->jhd", prob.astype(jnp.bfloat16), grad_ctx, preferred_element_type=jnp.float32
        ).astype(jnp.bfloat16)
        stacked = jnp.stack([grad_query, grad_key, grad_value]).reshape(
            3, length, heads_dev * HEAD_DIM
        )
        return ((rel_acc, lay_acc), stacked)

    init_sums = (
        jnp.zeros((heads_dev, 2 * length - 1), jnp.float32),
        jnp.zeros((2, heads_dev, CELLS, CELLS), jnp.float32),
    )
    (rel_acc, lay_acc), grads = lax.scan(
        page_step,
        init_sums,
        (split[0], split[1], split[2], grad_split, log_totals, page_counts, cells_pages),
    )
    grad_proj = grads.transpose(1, 0, 2, 3).reshape(3, total_rows, heads_dev * HEAD_DIM)
    rel_grad = jnp.dot(offset_onehot(length).T, rel_acc.T, precision=HIGHEST_PRECISION)
    lay_grad = jnp.einsum(
        "shm,mn->snh",
        lay_acc.reshape(2, heads_dev, CELLS * CELLS),
        layout_onehot(),
        precision=HIGHEST_PRECISION,
    )
    return (grad_proj, jnp.concatenate([rel_grad[None], lay_grad], axis=0))


def norm_back(rows, scale, gain, grad_normed):
    weighted = grad_normed * gain
    return scale * weighted - rows * scale**3 * jnp.mean(rows * weighted, axis=1, keepdims=True)


def forward_core(
    token_rows,
    norm_gains,
    attn_qkv,
    attn_out,
    ffn_in,
    page_counts,
    layout_cells,
    rel_bias,
    lay_vals,
):
    scale_one = lax.rsqrt(jnp.mean(token_rows * token_rows, axis=1, keepdims=True) + NORM_EPSILON)
    normed_one = (token_rows * scale_one * norm_gains[0]).astype(jnp.bfloat16)
    gathered_one = lax.all_gather(normed_one, "tensor", axis=0, tiled=True)
    projected = jnp.einsum(
        "td,cdk->ctk", gathered_one, attn_qkv, preferred_element_type=jnp.float32
    ).astype(jnp.bfloat16)
    context, log_totals = attend(projected, page_counts, layout_cells, rel_bias, lay_vals)
    attn_total = lax.psum_scatter(
        jnp.dot(context, attn_out, preferred_element_type=jnp.float32)
        .astype(jnp.bfloat16)
        .astype(jnp.float32)
        .astype(jnp.bfloat16),
        "tensor",
        scatter_dimension=0,
        tiled=True,
    ).astype(jnp.float32)
    resid = token_rows + attn_total
    scale_two = lax.rsqrt(jnp.mean(resid * resid, axis=1, keepdims=True) + NORM_EPSILON)
    normed_two = (resid * scale_two * norm_gains[1]).astype(jnp.bfloat16)
    gathered_two = lax.all_gather(normed_two, "tensor", axis=0, tiled=True)
    gate_up = jnp.einsum("td,cdf->ctf", gathered_two, ffn_in, preferred_element_type=jnp.float32)
    hidden = (gelu_tanh(gate_up[0]) * gate_up[1]).astype(jnp.bfloat16)
    return (
        scale_one,
        gathered_one,
        projected,
        context,
        log_totals,
        resid,
        scale_two,
        gathered_two,
        gate_up,
        hidden,
    )


def general_body(
    tokens,
    norm_gains,
    attn_qkv,
    attn_out,
    ffn_in,
    ffn_out,
    position_tables,
    page_counts,
    layout_cells,
    cotangent,
):
    token_rows = tokens.astype(jnp.float32)
    rel_bias = relative_bias(position_tables[0], PAGE_LEN)
    lay_vals = layout_values(position_tables)
    first = forward_core(
        token_rows,
        norm_gains,
        attn_qkv,
        attn_out,
        ffn_in,
        page_counts,
        layout_cells,
        rel_bias,
        lay_vals,
    )
    first_hidden = first[9]
    rows_part = first_hidden
    ffn_total = lax.psum_scatter(
        jnp.dot(rows_part, ffn_out, preferred_element_type=jnp.float32)
        .astype(jnp.bfloat16)
        .astype(jnp.float32)
        .astype(jnp.bfloat16),
        "tensor",
        scatter_dimension=0,
        tiled=True,
    ).astype(jnp.float32)
    layer_out = (first[5] + ffn_total).astype(jnp.bfloat16)
    cot_rows = lax.all_gather(cotangent, "tensor", axis=0, tiled=True)
    again_rows, cot_rows = lax.optimization_barrier((token_rows, cot_rows))
    saved = forward_core(
        again_rows,
        norm_gains,
        attn_qkv,
        attn_out,
        ffn_in,
        page_counts,
        layout_cells,
        rel_bias,
        lay_vals,
    )
    (
        scale_one,
        gathered_one,
        projected,
        context,
        log_totals,
        resid,
        scale_two,
        gathered_two,
        gate_up,
        hidden,
    ) = saved
    grad_hidden = jnp.einsum("td,fd->tf", cot_rows, ffn_out, preferred_element_type=jnp.float32)
    outer_grad = jnp.einsum("tf,td->fd", hidden, cot_rows, preferred_element_type=jnp.float32)
    gelu_value, gelu_back = jax.vjp(gelu_tanh, gate_up[0])
    grad_gate = gelu_back(grad_hidden * gate_up[1])[0].astype(jnp.bfloat16)
    grad_up = (grad_hidden * gelu_value).astype(jnp.bfloat16)
    grad_gate_up = jnp.stack([grad_gate, grad_up])
    inner_grad = jnp.einsum(
        "td,ctf->cdf", gathered_two, grad_gate_up, preferred_element_type=jnp.float32
    )
    rows_part = grad_gate_up
    grad_normed_two = lax.psum_scatter(
        jnp.einsum("ctf,cdf->td", rows_part, ffn_in, preferred_element_type=jnp.float32)
        .astype(jnp.bfloat16)
        .astype(jnp.float32)
        .astype(jnp.bfloat16),
        "tensor",
        scatter_dimension=0,
        tiled=True,
    ).astype(jnp.float32)
    grad_resid = cotangent.astype(jnp.float32) + norm_back(
        resid, scale_two, norm_gains[1], grad_normed_two
    )
    gain_two = jnp.sum(grad_normed_two * resid * scale_two, axis=0)
    resid_rows = lax.all_gather(grad_resid.astype(jnp.bfloat16), "tensor", axis=0, tiled=True)
    out_grad = jnp.einsum("tk,td->kd", context, resid_rows, preferred_element_type=jnp.float32)
    grad_context = jnp.einsum(
        "td,kd->tk", resid_rows, attn_out, preferred_element_type=jnp.float32
    ).astype(jnp.bfloat16)
    grad_proj, tables_grad = attend_back(
        projected, grad_context, log_totals, page_counts, layout_cells, rel_bias, lay_vals
    )
    qkv_grad = jnp.einsum(
        "td,ctk->cdk", gathered_one, grad_proj, preferred_element_type=jnp.float32
    )
    rows_part = grad_proj
    grad_normed_one = lax.psum_scatter(
        jnp.einsum("ctk,cdk->td", rows_part, attn_qkv, preferred_element_type=jnp.float32)
        .astype(jnp.bfloat16)
        .astype(jnp.float32)
        .astype(jnp.bfloat16),
        "tensor",
        scatter_dimension=0,
        tiled=True,
    ).astype(jnp.float32)
    tokens_grad = grad_resid + norm_back(token_rows, scale_one, norm_gains[0], grad_normed_one)
    gain_one = jnp.sum(grad_normed_one * token_rows * scale_one, axis=0)
    gains_grad = lax.psum_scatter(
        jnp.stack([gain_one, gain_two]), ("dp", "tensor"), scatter_dimension=1, tiled=True
    )
    qkv_summed, inner_summed, out_summed, outer_summed, tables_summed = (
        lax.psum_scatter(
            qkv_grad.astype(jnp.bfloat16), "dp", scatter_dimension=1, tiled=True
        ).astype(jnp.float32),
        lax.psum_scatter(
            inner_grad.astype(jnp.bfloat16), "dp", scatter_dimension=1, tiled=True
        ).astype(jnp.float32),
        lax.psum_scatter(
            out_grad.astype(jnp.bfloat16), "dp", scatter_dimension=1, tiled=True
        ).astype(jnp.float32),
        lax.psum_scatter(
            outer_grad.astype(jnp.bfloat16), "dp", scatter_dimension=1, tiled=True
        ).astype(jnp.float32),
        lax.psum_scatter(
            tables_grad.astype(jnp.bfloat16), "dp", scatter_dimension=1, tiled=True
        ).astype(jnp.float32),
    )
    return (
        layer_out,
        tokens_grad,
        gains_grad,
        qkv_summed,
        out_summed,
        inner_summed,
        outer_summed,
        tables_summed,
    )


PLANES = 4
RING = 4
CORES = 2
BLOCK = 256
HALF = 128
ORDER = (0, 1, 3, 2)
BACK_ORDER = (2, 1, 3, 0)
SLOT = (1, 1, 0, 0)
KEPT_SLOT = (0, 1, 0, 0)
ATT = 512
UNITS = 384
FFW = 3 * UNITS
VMEM_BYTES = 60 * 1024 * 1024
F32 = jnp.float32
BF16 = jnp.bfloat16
NT = (((1,), (1,)), ((), ()))
TN = (((0,), (0,)), ((), ()))
NN = (((1,), (0,)), ((), ()))


def page_plan(mesh):
    return mesh.shape["dp"] == PLANES * CORES and mesh.shape["tensor"] == RING


def dot(left, right, dims=NN):
    return lax.dot_general(left, right, dims, preferred_element_type=F32)


def shaped(shape, dtype=BF16):
    return jax.ShapeDtypeStruct(shape, dtype)


def columns(plane, r):
    return pl.ds(pl.multiple_of((plane ^ r) * BLOCK, BLOCK), BLOCK)


def pair_lane(rows):
    return lax.broadcasted_iota(jnp.int32, (rows, 2 * HEAD_DIM), 1)


MESH = pl.DeviceIdType.MESH


def here():
    group, ring = lax.axis_index("dp"), lax.axis_index("tensor")
    return group // CORES, group % CORES, ring


def device(plane, core, ring):
    return (plane * CORES + core, ring)


def greet(partners):
    barrier = pltpu.get_barrier_semaphore()
    for partner in partners:
        pl.semaphore_signal(barrier, inc=1, device_id=partner, device_id_type=MESH)
    pl.semaphore_wait(barrier, len(partners))


class Lines:
    def __init__(self, send_sems, recv_sems):
        self.send_sems, self.recv_sems, self.open = send_sems, recv_sems, {}

    def make(self, name, source, target, partner):
        at = len(self.open)
        self.open[name] = pltpu.make_async_remote_copy(
            src_ref=source,
            dst_ref=target,
            send_sem=self.send_sems.at[at],
            recv_sem=self.recv_sems.at[at],
            device_id=partner,
            device_id_type=MESH,
        )
        return self.open[name]

    def start(self, name, source, target, partner):
        self.make(name, source, target, partner).start()

    def arrived(self, *names):
        for name in names:
            self.open[name].wait_recv()

    def sent(self, *names):
        for name in names or list(self.open):
            self.open[name].wait_send()


class Gather:
    def __init__(self, lines, tag, own, full, where):
        self.lines, self.tag, self.own, self.full = lines, tag, own, full
        self.plane, self.core, self.ring = where

    def place(self, ring):
        return device(self.plane, self.core, ring)

    def ring_start(self, k):
        self.lines.start(
            (self.tag, "z", k),
            self.own.at[0:BLOCK],
            self.full.at[k, 0:BLOCK],
            self.place((self.ring + RING - k) % RING),
        )

    def ring_forward(self):
        for name, k, step in (("down", 1, -1), ("up", 3, 1)):
            self.lines.make(
                (self.tag, name),
                self.full.at[k, 0:BLOCK],
                self.full.at[2, 0:BLOCK],
                self.place((self.ring + RING + step) % RING),
            )

        @pl.when((self.ring == 1) | (self.ring == 2))
        def _():
            self.lines.open[self.tag, "down"].start()
            self.lines.open[self.tag, "up"].start()

    def forward_arrived(self):
        @pl.when(self.ring < 2)
        def _():
            self.lines.arrived((self.tag, "down"))

        @pl.when(self.ring >= 2)
        def _():
            self.lines.arrived((self.tag, "up"))

    def forward_sent(self):
        @pl.when((self.ring == 1) | (self.ring == 2))
        def _():
            self.lines.sent((self.tag, "down"), (self.tag, "up"))

    def plane_start(self, k, landed=False):
        if k == 2 and not landed:
            self.forward_arrived()
        elif not landed:
            self.lines.arrived((self.tag, "z", k))
        for name, r in (("x", 1), ("y", 2)):
            self.lines.start(
                (self.tag, name, k),
                self.full.at[k, 0:BLOCK],
                self.full.at[k, r * BLOCK : (r + 1) * BLOCK],
                device(self.plane ^ r, self.core, self.ring),
            )

    def plane_arrived(self, k):
        self.lines.arrived((self.tag, "x", k), (self.tag, "y", k))

    def corner_start(self, k, landed=False):
        if not landed:
            self.plane_arrived(k)
        for name, r, half, goal in (("x", 1, 0, 2), ("y", 2, 1, 1)):
            self.lines.start(
                (self.tag, "corner" + name, k),
                self.full.at[k, r * BLOCK + half * HALF : r * BLOCK + (half + 1) * HALF],
                self.full.at[k, 3 * BLOCK + half * HALF : 3 * BLOCK + (half + 1) * HALF],
                device(self.plane ^ goal, self.core, self.ring),
            )

    def finish(self, k):
        self.lines.arrived((self.tag, "cornerx", k), (self.tag, "cornery", k))


def own_attention(core, plane, qkv, out, target):
    for r in range(PLANES):
        rows, place = columns(plane, r), slice(r * BLOCK, (r + 1) * BLOCK)
        mine = pl.ds(pl.multiple_of(core * HALF, HALF), HALF)
        target[place, 0:HALF] = out[mine, rows].astype(F32).T.astype(BF16)
        for m in range(3):
            target[place, (m + 1) * HALF : (m + 2) * HALF] = qkv[m, rows, mine]


def own_ffn(core, plane, inner, outer, target):
    units = outer.shape[0]
    for which, first, count in ((0, 0, UNITS), (1, UNITS, units - UNITS)):

        @pl.when(core == which)
        def _():
            for r in range(PLANES):
                rows, place = columns(plane, r), slice(r * BLOCK, (r + 1) * BLOCK)
                parts = [outer[first : first + count, rows]]
                parts += [inner[m, first : first + count, rows] for m in range(2)]
                parts = [part.astype(F32).T.astype(BF16) for part in parts]
                for m, part in enumerate(parts):
                    target[place, m * UNITS : m * UNITS + count] = part
                    if count < UNITS:
                        target[place, m * UNITS + count : (m + 1) * UNITS] = jnp.zeros(
                            (BLOCK, UNITS - count), BF16
                        )


def place_rows(plane, core, near, far, full):
    rows = near.shape[0]
    for source, half in ((near, core), (far, 1 - core)):
        for r in range(PLANES):
            full[pl.ds(pl.multiple_of(half * rows, rows), rows), r * BLOCK : (r + 1) * BLOCK] = (
                source[:, columns(plane, r)]
            )


def split_bf16(values):
    parts = []
    for _ in range(3):
        part = values.astype(BF16)
        parts.append(part)
        values = values - part.astype(F32)
    return parts


def bias_pieces(tables, near_hot, cell_hot, layout, near):
    parts = split_bf16(tables)
    rel = sum(dot(part, near_hot[...]) for part in parts)
    cells = dot(parts[0], cell_hot[...])
    heads = tables.shape[0] // 3
    for h in range(heads):
        near[h] = rel[h : h + 1, :]
        toeplitz = []
        for axis in range(2):
            row = jnp.broadcast_to(cells[(axis + 1) * heads + h : (axis + 1) * heads + h + 1], (CELLS, HALF))
            toeplitz.append(pltpu.roll(row, CELLS, 1, stride=1, stride_axis=0))
        side = lax.broadcasted_iota(jnp.int32, (CELLS, HALF), 1)
        first = toeplitz[0]
        layout[h, 0:CELLS, 0:HALF] = jnp.where(
            side < CELLS, first, pltpu.roll(first, CELLS, 1)
        ).astype(BF16)
        layout[h, 0:CELLS, HALF:] = jnp.zeros((CELLS, HALF), BF16)
        layout[h, CELLS:, 0:HALF] = jnp.zeros((CELLS, HALF), BF16)
        layout[h, CELLS:, HALF:] = jnp.where(side < CELLS, toeplitz[1], 0.0).astype(BF16)


def forward_kernel(
    tokens, cot, gains, qkv_w, out_w, ffn_in, ffn_out, tables, cell_ids, counts, near_hot, cell_hot,
    att_full, ffn_full, prob_full, full, gains_here, normed_t, resid, normed_two, normed_two_t,
    cot_full, cot_t, qkv, context, inverse, cells_t, cells_twice, cell_tail,
    near_x, far_x, near_g, far_g, other_ids, other_counts, table_parts, table_rows, layout, near,
    own_ffn_w, ffn_in_v, ffn_out_v, normed, weights, cells, queries, keys, scores, prob,
    mixed_all, out_rows, mine_out, other_out,
    send_sems, recv_sems, local_sems,
):
    plane, core, ring = where = here()
    native = core == ring % 2
    rows = tokens.shape[0]
    length = 2 * rows
    partner = device(plane, 1 - core, ring)
    swap = device(plane, 1 - core, ring ^ 1)
    ring_others = [device(plane, core, (ring + RING - k) % RING) for k in range(1, RING)]
    neighbours = [device(plane ^ 1, core, ring), device(plane ^ 2, core, ring)]
    lines = Lines(send_sems, recv_sems)
    load_in = pltpu.make_async_copy(ffn_in, ffn_in_v, local_sems.at[0])
    load_out = pltpu.make_async_copy(ffn_out, ffn_out_v, local_sems.at[1])
    load_in.start()
    load_out.start()
    greet([partner, swap] + ring_others + neighbours)

    def swap_rows(tag, source, near_rows, far_rows):
        lines.make((tag, "swap"), source, near_rows, swap)
        lines.make((tag, "give"), source, far_rows, partner)
        lines.make((tag, "pass"), near_rows, far_rows, partner)

        @pl.when(native)
        def _():
            lines.open[tag, "give"].start()
            keep = pltpu.make_async_copy(source, near_rows, local_sems.at[2])
            keep.start()
            keep.wait()

        @pl.when(jnp.logical_not(native))
        def _():
            lines.open[tag, "swap"].start()

    def swap_pass(tag):
        @pl.when(jnp.logical_not(native))
        def _():
            lines.arrived((tag, "swap"))
            lines.open[tag, "pass"].start()
            lines.arrived((tag, "give"))

        @pl.when(native)
        def _():
            lines.arrived((tag, "pass"))

    def swap_sent(tag):
        @pl.when(jnp.logical_not(native))
        def _():
            lines.sent((tag, "swap"), (tag, "pass"))

        @pl.when(native)
        def _():
            lines.sent((tag, "give"))

    swap_rows("x", tokens, near_x, far_x)
    lines.start("ids", cell_ids, other_ids, partner)
    lines.start("counts", counts, other_counts, partner)
    table_parts[0] = tables[...]
    for k in range(1, RING):
        lines.start(("tables", k), tables, table_parts.at[k], ring_others[k - 1])
    own_attention(core, plane, qkv_w, out_w, weights)
    keep_weights = pltpu.make_async_copy(weights, att_full.at[0], local_sems.at[3])
    keep_weights.start()
    att = Gather(lines, "att", weights, att_full, where)
    ffn = Gather(lines, "ffn", own_ffn_w, ffn_full, where)
    keep_weights.wait()
    att.own = att_full.at[0]

    lines.arrived("ids", "counts")
    page = ring // 2
    picked = []
    for axis in range(2):
        span = pl.ds(pl.multiple_of(page * length, length), length)
        picked.append(
            jnp.where(native, cell_ids[axis : axis + 1, span], other_ids[axis : axis + 1, span])
        )
    picked.append(
        jnp.where(native, counts[pl.ds(page, 1), :], other_counts[pl.ds(page, 1), :])[:, 0:1]
    )
    spot = lax.broadcasted_iota(jnp.int32, (CELLS, length), 0)
    cells_x = (jnp.broadcast_to(picked[0], (CELLS, length)) == spot).astype(F32)
    cells_y = (jnp.broadcast_to(picked[1], (CELLS, length)) == spot).astype(F32)
    position = lax.broadcasted_iota(jnp.int32, (CELLS, length), 1)
    tail = jnp.where((spot < 16) & (spot % 8 == position // HALF), 1.0, 0.0)
    hidden_key = (spot == 16) & (position >= jnp.broadcast_to(picked[2], (CELLS, length)))
    tail = jnp.where(hidden_key, MASK_VALUE, tail)
    flipped = CELLS - 1 - spot
    for axis in range(2):
        turned = (jnp.broadcast_to(picked[axis], (CELLS, length)) == flipped).astype(F32)
        cells_t[axis * CELLS : (axis + 1) * CELLS, :] = turned.astype(BF16)
    cells[...] = jnp.concatenate([cells_x, cells_y], axis=0).T.astype(BF16)
    cells_twice[...] = jnp.concatenate([cells_x, cells_x], axis=0).T.astype(BF16)
    cell_tail[...] = jnp.concatenate([cells_y, tail], axis=0).T.astype(BF16)
    for k in range(1, RING):
        lines.arrived(("tables", k))
    table_rows[...] = jnp.zeros(table_rows.shape, F32)
    for k in range(RING):
        for axis in range(3):
            first = axis * 2 * RING + 2 * k
            table_rows[first : first + 2, 0:BUCKETS] = table_parts[k, axis, pl.ds(2 * core, 2), :]
    bias_pieces(table_rows[...], near_hot, cell_hot, layout, near)

    for r in range(PLANES):
        gains_here[:, r * BLOCK : (r + 1) * BLOCK] = gains[:, columns(plane, r)]
    load_in.wait()
    load_out.wait()
    own_ffn(core, plane, ffn_in_v, ffn_out_v, own_ffn_w)
    keep_ffn = pltpu.make_async_copy(own_ffn_w, ffn_full.at[0], local_sems.at[0])
    keep_ffn.start()
    swap_pass("x")
    att.ring_start(1)
    att.ring_start(3)
    place_rows(plane, core, near_x, far_x, full)
    for i in range(length // BLOCK):
        span = slice(i * BLOCK, (i + 1) * BLOCK)
        x = full[span, :].astype(F32)
        scale = lax.rsqrt(jnp.mean(x * x, axis=1, keepdims=True) + NORM_EPSILON)
        value = x * scale * gains_here[0:1, :]
        normed[span, :] = value.astype(BF16)
        normed_t[:, span] = value.T.astype(BF16)

    def head(k, h):
        at = 2 * k + h
        lane = pair_lane(length)
        mine = (lane // HEAD_DIM) == h
        side = dot(cells[...], layout[at])
        queries[:, :HALF] = jnp.where(mine, qkv[k, :, :HALF].astype(F32), side[:, :HALF]).astype(BF16)
        block = lax.broadcasted_iota(jnp.int32, (length, HALF), 0) // HALF
        is_left, is_right = lane % 8 < block - 1, lane % 8 > block + 1
        left, right = near[at, :, 0:1], near[at, :, 4 * HALF - 1 :]
        left_high, right_high = left.astype(BF16).astype(F32), right.astype(BF16).astype(F32)
        high = jnp.where(is_left, left_high, jnp.where(is_right, right_high, 0.0))
        low = jnp.where(is_left, left - left_high, jnp.where(is_right, right - right_high, 0.0))
        ends = jnp.where(lane < HEAD_DIM, side[:, HALF:], jnp.where(lane == HEAD_DIM + 16, 1.0, 0.0))
        ends = jnp.where((lane >= HEAD_DIM) & (lane < HEAD_DIM + 8), high, ends)
        ends = jnp.where((lane >= HEAD_DIM + 8) & (lane < HEAD_DIM + 16), low, ends)
        queries[:, HALF:] = ends.astype(BF16)
        keys[:, :HALF] = jnp.where(
            mine, qkv[k, :, HALF : 2 * HALF].astype(F32), cells_twice[...].astype(F32)
        ).astype(BF16)
        keys[:, HALF:] = cell_tail[...]
        scores[...] = dot(queries[...], keys[...], NT)
        spread = jnp.broadcast_to(near[at], (HALF, 4 * HALF))
        strip = pltpu.roll(spread, 3 * HALF, 1, stride=1, stride_axis=0)[:, : 3 * HALF]
        count = length // HALF
        store = pltpu.make_async_copy(prob.at[h], prob_full.at[at], local_sems.at[4 + h])
        if k > 0:
            store.wait()
        for i in range(count):
            first, last = max(i - 1, 0), min(i + 2, count)
            part = strip[:, (first - i + 1) * HALF : (last - i + 1) * HALF]
            span, near_span = slice(i * HALF, (i + 1) * HALF), slice(first * HALF, last * HALF)
            scores[span, near_span] = scores[span, near_span] + part
            row = scores[span, :]
            top = jnp.max(row, axis=1, keepdims=True)
            prob[h, span, :] = jnp.exp(row - top).astype(BF16)
        values = jnp.where(mine, qkv[k, :, 2 * HALF :].astype(F32), 1.0).astype(BF16)
        mixed = dot(prob[h], values)
        inv = 1.0 / pltpu.roll(mixed, HEAD_DIM, 1)
        mixed = (mixed * inv).astype(BF16)
        store.start()
        if h == 0:
            context[k] = mixed
            inverse[k] = inv
        else:
            context[k] = jnp.where(mine, mixed.astype(F32), context[k].astype(F32)).astype(BF16)
            inverse[k] = jnp.where(mine, inv, inverse[k])

    def project(k):
        if k > 0:
            load = pltpu.make_async_copy(att_full.at[k], weights, local_sems.at[3])
            load.start()
            load.wait()
        qkv[k] = dot(normed[...], weights[:, HALF:]).astype(BF16)
        mixed_all[:, k * HALF : (k + 1) * HALF] = weights[:, 0:HALF]

    def after_head(k, h):
        if (k, h) == (0, 0):
            att.plane_start(3)
            att.ring_forward()
        if (k, h) == (0, 1):
            att.corner_start(1)
            att.plane_start(2)
            ffn.ring_start(1)
            swap_rows("g", cot, near_g, far_g)
            att.finish(1)
        if (k, h) == (1, 0):
            att.corner_start(3)
        if (k, h) == (1, 1):
            att.corner_start(2)
            ffn.plane_start(1)
            ffn.ring_start(3)
            att.finish(3)
        if (k, h) == (3, 0):
            swap_pass("g")
        if (k, h) == (3, 1):
            ffn.corner_start(1)
            att.finish(2)
        if (k, h) == (2, 0):
            ffn.plane_start(3)
            ffn.ring_forward()

    for k in ORDER:
        project(k)
        if k == 0:
            att.plane_start(1)
        for h in range(2):
            head(k, h)
            after_head(k, h)

    for k in range(RING):
        out_rows[:, k * HALF : (k + 1) * HALF] = context[k]
    for i in range(length // BLOCK):
        span = slice(i * BLOCK, (i + 1) * BLOCK)
        mine_out[span, :] = dot(out_rows[span, :], mixed_all[...], NT).astype(BF16)
        lines.start(("out", i), mine_out.at[span], other_out.at[span], partner)
    place_rows(plane, core, near_g, far_g, cot_full)
    for r in range(PLANES):
        lanes = slice(r * BLOCK, (r + 1) * BLOCK)
        cot_t[lanes, :] = cot_full[:, lanes].astype(F32).T.astype(BF16)
    for i in range(length // BLOCK):
        span = slice(i * BLOCK, (i + 1) * BLOCK)
        lines.arrived(("out", i))
        row = full[span, :].astype(F32) + (
            mine_out[span, :].astype(F32) + other_out[span, :].astype(F32)
        )
        resid[span, :] = row
        scale = lax.rsqrt(jnp.mean(row * row, axis=1, keepdims=True) + NORM_EPSILON)
        value = row * scale * gains_here[1:2, :]
        normed_two[span, :] = value.astype(BF16)
        normed_two_t[:, span] = value.T.astype(BF16)

    ffn.finish(1)
    ffn.plane_arrived(3)
    ffn.forward_arrived()
    keep_ffn.wait()
    for h in range(2):
        pltpu.make_async_copy(prob.at[h], prob_full.at[2 * ORDER[-1] + h], local_sems.at[4 + h]).wait()
    swap_sent("x")
    swap_sent("g")
    att.forward_sent()
    ffn.forward_sent()
    lines.sent(
        *[
            name
            for name in lines.open
            if name[0] not in ("x", "g") and name[1] not in ("down", "up")
        ]
    )


def hot(reach, width):
    offsets = np.arange(width) - width // 2
    found = bucket_table(offsets, BUCKETS, reach)[None, :] == np.arange(HALF)[:, None]
    return jnp.asarray(found.astype(np.float32), BF16)


def forward(tokens, cotangent, gains, qkv_w, out_w, ffn_in, ffn_out, position_tables, page_counts, layout_cells):
    rows = tokens.shape[0]
    length = 2 * rows
    features = PLANES * BLOCK
    tables = position_tables.transpose(0, 2, 1)
    counts = jnp.broadcast_to(page_counts[:, None], (2, HALF))
    args = [tokens, cotangent, gains, qkv_w, out_w, ffn_in, ffn_out, tables, layout_cells, counts]
    args += [hot(REL_REACH, 4 * HALF), hot(CELLS, HALF)]
    whole = pl.BlockSpec(memory_space=pltpu.VMEM)
    outside = pl.BlockSpec(memory_space=pl.ANY)
    outs = [
        shaped((RING, features, ATT)), shaped((RING, features, FFW)), shaped((2 * RING, length, length)),
        shaped((length, features)), shaped((2, features), F32), shaped((features, length)),
        shaped((length, features), F32), shaped((length, features)), shaped((features, length)),
        shaped((length, features)), shaped((features, length)),
        shaped((RING, length, 3 * HALF)), shaped((RING, length, HALF)), shaped((RING, length, HALF), F32),
        shaped((HALF, length)), shaped((length, HALF)), shaped((length, HALF)),
    ]
    scratch = [pltpu.VMEM((rows, features), BF16)] * 4 + [
        pltpu.VMEM(layout_cells.shape, jnp.int32),
        pltpu.VMEM(counts.shape, jnp.int32),
        pltpu.VMEM((RING,) + tables.shape, F32),
        pltpu.VMEM((6 * RING, HALF), F32),
        pltpu.VMEM((2 * RING, HALF, 2 * HALF), BF16),
        pltpu.VMEM((2 * RING, 1, 4 * HALF), F32),
        pltpu.VMEM((features, FFW), BF16),
        pltpu.VMEM(ffn_in.shape, BF16),
        pltpu.VMEM(ffn_out.shape, BF16),
        pltpu.VMEM((length, features), BF16),
        pltpu.VMEM((features, ATT), BF16),
        pltpu.VMEM((length, HALF), BF16),
        pltpu.VMEM((length, 2 * HALF), BF16),
        pltpu.VMEM((length, 2 * HALF), BF16),
        pltpu.VMEM((length, length), F32),
        pltpu.VMEM((2, length, length), BF16),
        pltpu.VMEM((features, RING * HALF), BF16),
        pltpu.VMEM((length, RING * HALF), BF16),
        pltpu.VMEM((length, features), BF16),
        pltpu.VMEM((length, features), BF16),
        pltpu.SemaphoreType.DMA((48,)),
        pltpu.SemaphoreType.DMA((48,)),
        pltpu.SemaphoreType.DMA((6,)),
    ]
    in_specs = [whole, outside, whole, whole, whole, outside, outside] + [whole] * 5
    out_specs = [outside] * 3 + [whole] * 14
    return pl.pallas_call(
        forward_kernel,
        out_shape=outs,
        in_specs=in_specs,
        out_specs=out_specs,
        scratch_shapes=scratch,
        name="forward",
        cost_estimate=pl.CostEstimate(flops=10**10, bytes_accessed=10**8, transcendentals=0),
        compiler_params=pltpu.CompilerParams(
            vmem_limit_bytes=63 * 1024 * 1024, collective_id=0, has_side_effects=True
        ),
    )(*args)


class Scatter:
    def __init__(self, lines, tag, k, grads, kept, buffers, where):
        self.lines, self.tag, self.k, self.grads, self.kept = lines, tag, k, grads, kept
        self.from_x, self.from_y, self.late, self.same, self.cross = buffers
        self.plane, self.core, self.ring = where
        self.to_x = device(self.plane ^ 1, self.core, self.ring)
        self.to_y = device(self.plane ^ 2, self.core, self.ring)

    def name(self, step):
        return (self.tag, step, self.k)

    def rows(self, r, half):
        return slice(r * BLOCK + half * HALF, r * BLOCK + (half + 1) * HALF)

    def start(self):
        k = self.k
        for step, r, half, target, goal in (
            ("x1", 3, 0, self.from_x.at[k, 1], self.to_x),
            ("y1", 3, 1, self.from_y.at[k, 1], self.to_y),
            ("x0", 1, 0, self.from_x.at[k, 0], self.to_x),
            ("y0", 2, 1, self.from_y.at[k, 0], self.to_y),
        ):
            self.lines.start(self.name(step), self.grads.at[self.rows(r, half)], target, goal)

    def middle(self):
        k = self.k
        self.lines.arrived(self.name("x1"), self.name("y1"))
        for source, r, half, at, goal, step in (
            (self.from_x, 2, 0, 0, self.to_y, "late0"),
            (self.from_y, 1, 1, 1, self.to_x, "late1"),
        ):
            kept = self.kept(r, half).astype(F32)
            source[k, 1] = (kept + source[k, 1].astype(F32)).astype(BF16)
            self.lines.start(self.name(step), source.at[k, 1], self.late.at[k, at], goal)

    def last(self):
        self.combine()
        self.hand_over()

    def combine(self):
        k, late = self.k, self.late
        self.lines.arrived(*[self.name(step) for step in ("x0", "y0", "late0", "late1")])
        upper = self.kept(0, 0).astype(F32) + self.from_x[k, 0].astype(F32) + late[k, 0].astype(F32)
        lower = self.kept(0, 1).astype(F32) + self.from_y[k, 0].astype(F32) + late[k, 1].astype(F32)
        late[k, 0] = jnp.where(self.core == 0, upper, lower).astype(BF16)
        late[k, 1] = jnp.where(self.core == 0, lower, upper).astype(BF16)

    def hand_over(self):
        k, late = self.k, self.late
        goal = (self.ring + k) % RING
        if k > 0:
            self.lines.start(
                self.name("same"), late.at[k, 0], self.same.at[k - 1], device(self.plane, self.core, goal)
            )
        self.lines.start(
            self.name("cross"), late.at[k, 1], self.cross.at[k], device(self.plane, 1 - self.core, goal)
        )


def gelu_parts(gate):
    square = gate * gate
    ratio = math.sqrt(2.0 / math.pi)
    bend = jnp.tanh(ratio * gate * (1.0 + 0.044715 * square))
    half_gate = 0.5 * gate
    value = half_gate + half_gate * bend
    slope = 0.5 + 0.5 * bend + half_gate * (1.0 - bend * bend) * (
        ratio * (1.0 + 3.0 * 0.044715 * square)
    )
    return value, slope


def middle_kernel(
    normed, normed_t, cot, cot_t, resid, gains_here, ffn_before,
    ffn_full, grads_full, low, low_t, half_grad, page_out, gain, late,
    weights, hidden, grads, total_in, total_out, mine, other, mine_out, other_out,
    kept, from_x, from_y,
    send_sems, recv_sems, local_sems,
):
    plane, core, ring = where = here()
    partner = device(plane, 1 - core, ring)
    lines = Lines(send_sems, recv_sems)
    length = normed.shape[0]
    rows = length // 2
    blocks = length // BLOCK

    gather = Gather(lines, "ffn", None, ffn_full, where)

    def load(at):
        return pltpu.make_async_copy(
            ffn_full.at[ORDER[at]], weights.at[at % 2], local_sems.at[at % 2]
        )

    def store(k):
        return pltpu.make_async_copy(grads, grads_full.at[k], local_sems.at[2])

    loads = [
        pltpu.make_async_copy(
            grads_full.at[0, first : first + BLOCK], kept.at[at : at + BLOCK], local_sems.at[3 + i]
        )
        for i, (first, at) in enumerate(((0, 0), (3 * HALF, BLOCK)))
    ]
    spots = {(0, 0): 0, (0, 1): HALF, (1, 1): BLOCK, (2, 0): BLOCK + HALF}
    scatter = Scatter(
        lines, "grads", 0, grads_full.at[0],
        lambda r, half: kept[spots[r, half] : spots[r, half] + HALF],
        (from_x, from_y, late, None, None), where,
    )
    load(0).start()
    load(1).start()
    greet([partner, device(plane ^ 1, core, ring), device(plane ^ 2, core, ring)])
    gather.corner_start(3, landed=True)
    gather.plane_start(2, landed=True)
    for at, k in enumerate(ORDER):
        load(at).wait()
        w = weights.at[at % 2]
        for i in range(blocks):
            span = slice(i * BLOCK, (i + 1) * BLOCK)
            both = dot(normed[span, :], w[:, UNITS:])
            grad_hidden = dot(cot[span, :], w[:, :UNITS])
            gate, up = both[:, :UNITS], both[:, UNITS:]
            value, slope = gelu_parts(gate)
            hidden[span, :UNITS] = (value * up).astype(BF16)
            hidden[span, UNITS : 2 * UNITS] = (grad_hidden * up * slope).astype(BF16)
            hidden[span, 2 * UNITS :] = (grad_hidden * value).astype(BF16)
            part_in = dot(hidden[span, UNITS:], w[:, UNITS:], NT)
            part_out = dot(hidden[span, :UNITS], w[:, :UNITS], NT)
            if at > 0:
                part_in = total_in[span, :] + part_in
                part_out = total_out[span, :] + part_out
            if at + 1 < RING:
                total_in[span, :] = part_in
                total_out[span, :] = part_out
            else:
                mine[span, :] = part_in.astype(BF16)
                lines.start(("in", i), mine.at[span], other.at[span], partner)
                mine_out[span, :] = part_out.astype(BF16)
        if at + 1 == RING:
            far = pl.ds(pl.multiple_of((1 - core) * rows, rows), rows)
            lines.start("out", mine_out.at[far], other_out, partner)
        if at > 0:
            store(ORDER[at - 1]).wait()
        if at == 1:
            gather.finish(3)
            load(2).start()
            gather.corner_start(2)
            scatter.start()
            for copy in loads:
                copy.start()
        if at == 2:
            gather.finish(2)
            load(3).start()
        for i in range(2):
            span = slice(i * 2 * BLOCK, (i + 1) * 2 * BLOCK)
            grads[span, :UNITS] = dot(cot_t[span, :], hidden[:, :UNITS]).astype(BF16)
            grads[span, UNITS:] = dot(normed_t[span, :], hidden[:, UNITS:]).astype(BF16)
        store(k).start()
        if at == 2:
            for copy in loads:
                copy.wait()
            scatter.middle()

    total = jnp.zeros((1, resid.shape[1]), F32)
    for i in range(blocks):
        span = slice(i * BLOCK, (i + 1) * BLOCK)
        lines.arrived(("in", i))
        row = resid[span, :]
        grad = mine[span, :].astype(F32) + other[span, :].astype(F32)
        scale = lax.rsqrt(jnp.mean(row * row, axis=1, keepdims=True) + NORM_EPSILON)
        weighted = grad * gains_here[1:2, :]
        center = jnp.mean(row * weighted, axis=1, keepdims=True)
        value = cot[span, :].astype(F32) + scale * weighted - row * (scale * scale * scale * center)
        low[span, :] = value.astype(BF16)
        low_t[:, span] = value.T.astype(BF16)
        in_half = core == (i * BLOCK) // rows
        total = total + jnp.where(in_half, jnp.sum(grad * row * scale, axis=0, keepdims=True), 0.0)

        @pl.when(in_half)
        def _():
            first = (i * BLOCK) % rows
            half_grad[first : first + BLOCK, :] = value

    for r in range(PLANES):
        gain[:, columns(plane, r)] = total[:, r * BLOCK : (r + 1) * BLOCK]
    lines.arrived("out")
    for i in range(rows // BLOCK):
        span = slice(i * BLOCK, (i + 1) * BLOCK)
        near = pl.ds(pl.multiple_of(core * rows + i * BLOCK, BLOCK), BLOCK)
        row = resid[near, :] + (mine_out[near, :].astype(F32) + other_out[span, :].astype(F32))
        for r in range(PLANES):
            page_out[span, columns(plane, r)] = row[:, r * BLOCK : (r + 1) * BLOCK].astype(BF16)
    scatter.combine()
    store(ORDER[-1]).wait()
    lines.sent()


def middle(normed, normed_t, cot, cot_t, resid, gains_here, ffn_full):
    length, features = normed.shape
    rows = length // 2
    whole = pl.BlockSpec(memory_space=pltpu.VMEM)
    outside = pl.BlockSpec(memory_space=pl.ANY)
    return pl.pallas_call(
        middle_kernel,
        out_shape=[
            shaped((RING, features, FFW)), shaped((RING, features, FFW)),
            shaped((length, features)), shaped((features, length)),
            shaped((rows, features), F32), shaped((rows, features)), shaped((1, features), F32),
            shaped((1, 2, HALF, FFW)),
        ],
        in_specs=[whole] * 6 + [outside],
        out_specs=[outside] * 2 + [whole] * 6,
        input_output_aliases={6: 0},
        scratch_shapes=[
            pltpu.VMEM((2, features, FFW), BF16),
            pltpu.VMEM((length, FFW), BF16),
            pltpu.VMEM((features, FFW), BF16),
            pltpu.VMEM((length, features), F32),
            pltpu.VMEM((length, features), F32),
            pltpu.VMEM((length, features), BF16),
            pltpu.VMEM((length, features), BF16),
            pltpu.VMEM((length, features), BF16),
            pltpu.VMEM((rows, features), BF16),
            pltpu.VMEM((2 * BLOCK, FFW), BF16),
            pltpu.VMEM((1, 2, HALF, FFW), BF16),
            pltpu.VMEM((1, 2, HALF, FFW), BF16),
            pltpu.SemaphoreType.DMA((20,)),
            pltpu.SemaphoreType.DMA((20,)),
            pltpu.SemaphoreType.DMA((5,)),
        ],
        name="middle",
        cost_estimate=pl.CostEstimate(flops=27 * 10**9, bytes_accessed=10**8, transcendentals=0),
        compiler_params=pltpu.CompilerParams(
            vmem_limit_bytes=63 * 1024 * 1024, collective_id=1, has_side_effects=True
        ),
    )(normed, normed_t, cot, cot_t, resid, gains_here, ffn_full)


def sum_ring(lines, tag, late, same, cross):
    for k in range(RING):
        if k > 0:
            lines.arrived((tag, "same", k))
        lines.arrived((tag, "cross", k))
    mine = late[0, 0].astype(F32)
    for k in range(1, RING):
        mine = mine + same[k - 1].astype(F32)
    other = cross[0].astype(F32)
    for k in range(1, RING):
        other = other + cross[k].astype(F32)
    return mine, other


def backward_kernel(
    low, low_t, normed_t, half_grad, full, gains_here, qkv, context, inverse,
    cells_t, cells_twice, cell_tail, near_hot, cell_hot, gain_two, ffn_first,
    att_full, prob_full, ffn_grads, page_out,
    layer_out, tokens_grad, qkv_grad, out_grad, inner_grad, outer_grad, small_out,
    weights, prob, scaled, scaled_low, keys, dscores, grad_qkv, att_grads, total, mine_half, far_half,
    other_half, page_low, swapped, ffn_kept,
    att_x, att_y, att_late, att_same, att_cross, ffn_x, ffn_y, ffn_late, ffn_same, ffn_cross,
    diag_near, diag_cell, gain_one, small, small_ring, small_plane, small_core,
    send_sems, recv_sems, local_sems,
):
    plane, core, ring = where = here()
    native = core == ring % 2
    length = low.shape[0]
    rows = length // 2
    count = length // HALF
    partner = device(plane, 1 - core, ring)
    swap = device(plane, 1 - core, ring ^ 1)
    partners = [partner, swap, device(plane ^ 1, core, ring), device(plane ^ 2, core, ring)]
    for k in range(1, RING):
        partners += [device(plane, core, (ring + k) % RING), device(plane, 1 - core, (ring + k) % RING)]
    lines = Lines(send_sems, recv_sems)

    def load_prob(at):
        head_at = 2 * BACK_ORDER[at // 2] + at % 2
        return pltpu.make_async_copy(prob_full.at[head_at], prob.at[at % 2], local_sems.at[at % 2])

    def load_weights(k):
        return pltpu.make_async_copy(att_full.at[k], weights.at[SLOT[k]], local_sems.at[2 + SLOT[k]])

    def load_kept(k):
        slot = KEPT_SLOT[k]
        return [
            pltpu.make_async_copy(
                ffn_grads.at[k, first : first + BLOCK],
                ffn_kept.at[slot, at : at + BLOCK],
                local_sems.at[4 + 2 * slot + i],
            )
            for i, (first, at) in enumerate(((0, 0), (3 * HALF, BLOCK)))
        ]

    load_prob(0).start()
    load_prob(1).start()
    load_weights(BACK_ORDER[0]).start()
    goals = [partner, device(plane ^ 1, core, ring), device(plane ^ 2, core, ring)] + partners[4:]
    greet(goals)

    def kept_ffn(k):
        spots = {(0, 0): 0, (0, 1): HALF, (1, 1): BLOCK, (2, 0): BLOCK + HALF}
        return lambda r, half: ffn_kept[KEPT_SLOT[k], spots[r, half] : spots[r, half] + HALF]

    def kept_att(k):
        def read(r, half):
            first = r * BLOCK + half * HALF
            return att_grads[k, first : first + HALF]

        return read

    ffn = [
        Scatter(lines, "ffn", k, ffn_grads.at[k], kept_ffn(k), (ffn_x, ffn_y, ffn_late, ffn_same, ffn_cross), where)
        for k in range(RING)
    ]
    att = [
        Scatter(lines, "att", k, att_grads.at[k], kept_att(k), (att_x, att_y, att_late, att_same, att_cross), where)
        for k in range(RING)
    ]

    def ffn_start(k):
        for copy in load_kept(k):
            copy.start()
        ffn[k].start()

    def ffn_middle(k):
        for copy in load_kept(k):
            copy.wait()
        ffn[k].middle()

    ffn_start(2)
    ffn_late[0] = ffn_first[0]
    ffn[0].hand_over()
    lines.make("layer", page_out, layer_out, swap)

    @pl.when(jnp.logical_not(native))
    def _():
        lines.open["layer"].start()

    lane = pair_lane(length)
    row_block = lax.broadcasted_iota(jnp.int32, (length, HALF), 0) // HALF
    flip_at = lax.broadcasted_iota(jnp.int32, (HALF, HALF), 0)
    flip_to = lax.broadcasted_iota(jnp.int32, (HALF, HALF), 1)
    flip = jnp.where(flip_at + flip_to == HALF - 1, 1.0, 0.0).astype(BF16)

    def enter(k):
        at = BACK_ORDER.index(k)
        if at + 1 < RING:
            load_weights(BACK_ORDER[at + 1]).start()
        load_weights(k).wait()
        grad_context = dot(low[...], weights[SLOT[k], :, 0:HALF]).astype(BF16).astype(F32)
        value = grad_context * inverse[k]
        scaled[...] = value
        scaled_low[...] = value.astype(BF16)

    def head(k, h):
        at = 2 * k + h
        mine = (lane // HEAD_DIM) == h
        value = scaled[...]
        delta = -jnp.sum(
            jnp.where(mine, value * context[k].astype(F32), 0.0), axis=1, keepdims=True
        )
        delta_high = delta.astype(BF16).astype(F32)
        spare = HEAD_DIM * (1 - h)
        fill = jnp.where(lane == spare + 1, delta - delta_high, 0.0)
        left = jnp.where(mine, value, jnp.where(lane == spare, delta_high, fill)).astype(BF16)
        ones = jnp.where((lane == spare) | (lane == spare + 1), 1.0, 0.0)
        right = jnp.where(mine, qkv[k, :, 2 * HALF :].astype(F32), ones).astype(BF16)
        turn = 2 * BACK_ORDER.index(k) + h
        load_prob(turn).wait()
        strips = [jnp.zeros((HALF, HALF), F32) for _ in range(3)]
        for i in range(length // BLOCK):
            span = slice(i * BLOCK, (i + 1) * BLOCK)
            dscore = prob[at % 2, span, :].astype(F32) * dot(left[span, :], right, NT)
            dscores[span, :] = dscore.astype(BF16)
            for part in range(BLOCK // HALF):
                for step in range(3):
                    block = i * (BLOCK // HALF) + part + step - 1
                    if 0 <= block < count:
                        strips[step] = strips[step] + dscore[
                            part * HALF : (part + 1) * HALF, block * HALF : (block + 1) * HALF
                        ]
        keys[:, :HALF] = jnp.where(
            mine, qkv[k, :, HALF : 2 * HALF].astype(F32), cells_twice[...].astype(F32)
        ).astype(BF16)
        keys[:, HALF:] = cell_tail[...]
        grad_left = dot(dscores[...], keys[...])
        grad_key = dot(dscores[...], qkv[k, :, :HALF], TN)
        grad_value = dot(prob[at % 2], scaled_low[...], TN)
        if turn + 2 < 2 * RING:
            load_prob(turn + 2).start()
        for m, new in enumerate((grad_left[:, :HALF], grad_key, grad_value)):
            lanes = slice(m * HALF, (m + 1) * HALF)
            if h == 1:
                new = jnp.where(mine, new, grad_qkv[:, lanes].astype(F32))
            grad_qkv[:, lanes] = new.astype(BF16)

        skewed = jnp.zeros((HALF, 3 * HALF), F32)
        strip = jnp.concatenate(strips, axis=1)
        for part in split_bf16(strip):
            skewed = skewed + dot(flip, part)
        skewed = jnp.concatenate([skewed, jnp.zeros((HALF, HALF), F32)], axis=1)
        sums = jnp.sum(pltpu.roll(skewed, 1, 1, stride=1, stride_axis=0), axis=0, keepdims=True)
        tail = grad_left[:, HALF:]
        in_tail = (lane >= HEAD_DIM) & (lane < HEAD_DIM + 8)
        far_left = jnp.sum(jnp.where(in_tail & (lane % 8 < row_block - 1), tail, 0.0), axis=0, keepdims=True)
        far_right = jnp.sum(jnp.where(in_tail & (lane % 8 > row_block + 1), tail, 0.0), axis=0, keepdims=True)
        wide = lax.broadcasted_iota(jnp.int32, (1, 4 * HALF), 1)
        sums = sums + jnp.where(wide == 0, jnp.sum(far_left, axis=1, keepdims=True), 0.0)
        sums = sums + jnp.where(wide == 4 * HALF - 1, jnp.sum(far_right, axis=1, keepdims=True), 0.0)
        diag_near[at : at + 1, :] = sums
        by_cell = grad_left[:, :HALF]
        by_cell = jnp.where(mine, pltpu.roll(by_cell, HEAD_DIM, 1), by_cell)
        for axis, table in enumerate((by_cell, tail)):
            table_high = table.astype(BF16)
            rest = (table - table_high.astype(F32)).astype(BF16)
            side = cells_t[axis * CELLS : (axis + 1) * CELLS, :]
            grid = dot(side, table_high) + dot(side, rest)
            cell_lane = lax.broadcasted_iota(jnp.int32, (CELLS, HALF), 1)
            grid = jnp.where(cell_lane < CELLS, grid, 0.0)
            grid = pltpu.roll(grid, 1, 1, stride=1, stride_axis=0)
            row = axis * 2 * RING + at
            diag_cell[row : row + 1, :] = jnp.sum(grid, axis=0, keepdims=True)

    def leave(k):
        w = weights[SLOT[k], :, HALF:]
        att_grads[k, :, 0:HALF] = dot(low_t[...], context[k]).astype(BF16)
        att_grads[k, :, HALF:] = dot(normed_t[...], grad_qkv[...]).astype(BF16)
        if k == BACK_ORDER[-1]:
            att[k].start()
        for i in range(length // BLOCK):
            span = slice(i * BLOCK, (i + 1) * BLOCK)
            part = dot(grad_qkv[span, :], w, NT)
            total[span, :] = part if k == BACK_ORDER[0] else total[span, :] + part

    enter(2)
    head(2, 0)
    head(2, 1)
    ffn_middle(2)
    ffn_start(1)
    leave(2)
    enter(1)
    head(1, 0)
    ffn[2].last()
    head(1, 1)
    leave(1)
    ffn_middle(1)
    ffn_start(3)
    enter(3)
    head(3, 0)
    att[2].start()
    head(3, 1)
    ffn[1].last()
    leave(3)
    enter(0)
    head(0, 0)
    ffn_middle(3)
    att[1].start()
    head(0, 1)
    att[2].middle()
    att[3].start()
    leave(0)
    ffn[3].last()

    near = pl.ds(pl.multiple_of(core * rows, rows), rows)
    far = pl.ds(pl.multiple_of((1 - core) * rows, rows), rows)
    far_half[...] = total[far, :].astype(BF16)
    lines.start("half", far_half, other_half, partner)
    mine_half[...] = total[near, :].astype(BF16)
    lines.arrived("half")
    gain = jnp.zeros((1, full.shape[1]), F32)
    for i in range(rows // BLOCK):
        span = slice(i * BLOCK, (i + 1) * BLOCK)
        x = full[pl.ds(pl.multiple_of(core * rows + i * BLOCK, BLOCK), BLOCK), :].astype(F32)
        grad = mine_half[span, :].astype(F32) + other_half[span, :].astype(F32)
        scale = lax.rsqrt(jnp.mean(x * x, axis=1, keepdims=True) + NORM_EPSILON)
        weighted = grad * gains_here[0:1, :]
        center = jnp.mean(x * weighted, axis=1, keepdims=True)
        value = half_grad[span, :] + scale * weighted - x * (scale * scale * scale * center)
        gain = gain + jnp.sum(grad * x * scale, axis=0, keepdims=True)
        for r in range(PLANES):
            block = value[:, r * BLOCK : (r + 1) * BLOCK]
            tokens_grad[span, columns(plane, r)] = block
            page_low[span, columns(plane, r)] = block.astype(BF16)
    for r in range(PLANES):
        gain_one[:, columns(plane, r)] = gain[:, r * BLOCK : (r + 1) * BLOCK]
    lines.make("swap", page_low, swapped, swap)

    @pl.when(jnp.logical_not(native))
    def _():
        lines.open["swap"].start()

    near_sums = sum(dot(part, near_hot[...], NT) for part in split_bf16(diag_near[...]))
    cell_sums = sum(dot(part, cell_hot[...], NT) for part in split_bf16(diag_cell[...]))
    for k in range(RING):
        small[k, 0:2, :] = near_sums[2 * k : 2 * k + 2, :]
        for axis in range(2):
            first = axis * 2 * RING + 2 * k
            small[k, 2 * axis + 2 : 2 * axis + 4, :] = cell_sums[first : first + 2, :]
        small[k, 6:8, :] = jnp.zeros((2, HALF), F32)
        for j in range(8):
            lanes = slice(j * HALF, (j + 1) * HALF)
            small[k, 8 + j : 9 + j, :] = gain_one[:, lanes]
            small[k, 16 + j : 17 + j, :] = gain_two[:, lanes]
    for k in range(1, RING):
        lines.start(("small", k), small.at[k], small_ring.at[k], device(plane, core, (ring + k) % RING))
    att[2].last()
    att[1].middle()
    att[3].middle()
    for k in range(1, RING):
        lines.arrived(("small", k))
    small_plane[0] = small[0] + (small_ring[1] + (small_ring[2] + small_ring[3]))
    lines.start("smallx", small_plane.at[0], small_plane.at[1], device(plane ^ 1, core, ring))
    att[1].last()
    att[0].middle()
    lines.arrived("smallx")
    small_plane[2] = small_plane[0] + small_plane[1]
    lines.start("smally", small_plane.at[2], small_plane.at[3], device(plane ^ 2, core, ring))
    att[3].last()
    lines.arrived("smally")
    small_core[0] = small_plane[2] + small_plane[3]
    lines.start("smallc", small_core.at[0], small_core.at[1], partner)
    att[0].last()

    mine, other = sum_ring(lines, "ffn", ffn_late, ffn_same, ffn_cross)
    rest = inner_grad.shape[1] - UNITS
    first_core = jnp.where(core == 0, mine, other)
    second_core = jnp.where(core == 0, other, mine)
    for m in range(2):
        at = (m + 1) * UNITS
        inner_grad[m, 0:UNITS, :] = first_core[:, at : at + UNITS].T
        inner_grad[m, UNITS : UNITS + rest, :] = second_core[:, at : at + UNITS].T[0:rest]
    outer_grad[0:UNITS, :] = first_core[:, 0:UNITS].T
    outer_grad[UNITS : UNITS + rest, :] = second_core[:, 0:UNITS].T[0:rest]

    @pl.when(jnp.logical_not(native))
    def _():
        lines.arrived("swap")
        tokens_grad[...] = swapped[...].astype(F32)

    mine, other = sum_ring(lines, "att", att_late, att_same, att_cross)
    first_core = jnp.where(core == 0, mine, other)
    second_core = jnp.where(core == 0, other, mine)
    for m in range(3):
        lanes = slice((m + 1) * HALF, (m + 2) * HALF)
        qkv_grad[m, :, 0:HALF] = first_core[:, lanes]
        qkv_grad[m, :, HALF : 2 * HALF] = second_core[:, lanes]
    out_grad[0:HALF, :] = first_core[:, 0:HALF].T
    out_grad[HALF : 2 * HALF, :] = second_core[:, 0:HALF].T

    lines.arrived("smallc")
    low_core = jnp.where(core == 0, small_core[0], small_core[1])
    high_core = jnp.where(core == 0, small_core[1], small_core[0])
    small_out[0] = low_core
    small_out[1] = high_core

    @pl.when(jnp.logical_not(native))
    def _():
        lines.arrived("layer")
        lines.sent("layer", "swap")

    lines.sent(*[name for name in lines.open if name not in ("layer", "swap")])


def backward(low, low_t, normed_t, half_grad, full, gains_here, qkv, context, inverse, cells_t, cells_twice, cell_tail, gain_two, ffn_first, att_full, prob_full, ffn_grads, page_out, units):
    length, features = low.shape
    rows = length // 2
    whole = pl.BlockSpec(memory_space=pltpu.VMEM)
    outside = pl.BlockSpec(memory_space=pl.ANY)
    args = [low, low_t, normed_t, half_grad, full, gains_here, qkv, context, inverse]
    args += [cells_t, cells_twice, cell_tail, hot(REL_REACH, 4 * HALF), hot(CELLS, HALF), gain_two, ffn_first]
    args += [att_full, prob_full, ffn_grads, page_out]

    def buffers(width):
        return [
            pltpu.VMEM((RING, 2, HALF, width), BF16),
            pltpu.VMEM((RING, 2, HALF, width), BF16),
            pltpu.VMEM((RING, 2, HALF, width), BF16),
            pltpu.VMEM((RING - 1, HALF, width), BF16),
            pltpu.VMEM((RING, HALF, width), BF16),
        ]

    return pl.pallas_call(
        backward_kernel,
        out_shape=[
            shaped((rows, features)), shaped((rows, features), F32),
            shaped((3, HALF, 2 * HALF), F32), shaped((2 * HALF, HALF), F32),
            shaped((2, units, HALF), F32), shaped((units, HALF), F32), shaped((2, 24, HALF), F32),
        ],
        in_specs=[whole] * 16 + [outside] * 4,
        out_specs=[outside] + [whole] * 6,
        scratch_shapes=[
            pltpu.VMEM((2, features, ATT), BF16),
            pltpu.VMEM((2, length, length), BF16),
            pltpu.VMEM((length, HALF), F32),
            pltpu.VMEM((length, HALF), BF16),
            pltpu.VMEM((length, 2 * HALF), BF16),
            pltpu.VMEM((length, length), BF16),
            pltpu.VMEM((length, 3 * HALF), BF16),
            pltpu.VMEM((RING, features, ATT), BF16),
            pltpu.VMEM((length, features), F32),
            pltpu.VMEM((rows, features), BF16),
            pltpu.VMEM((rows, features), BF16),
            pltpu.VMEM((rows, features), BF16),
            pltpu.VMEM((rows, features), BF16),
            pltpu.VMEM((rows, features), BF16),
            pltpu.VMEM((2, 2 * BLOCK, FFW), BF16),
            *buffers(ATT),
            *buffers(FFW),
            pltpu.VMEM((2 * RING, 4 * HALF), F32),
            pltpu.VMEM((4 * RING, HALF), F32),
            pltpu.VMEM((1, features), F32),
            pltpu.VMEM((RING, 24, HALF), F32),
            pltpu.VMEM((RING, 24, HALF), F32),
            pltpu.VMEM((4, 24, HALF), F32),
            pltpu.VMEM((2, 24, HALF), F32),
            pltpu.SemaphoreType.DMA((80,)),
            pltpu.SemaphoreType.DMA((80,)),
            pltpu.SemaphoreType.DMA((9,)),
        ],
        name="backward",
        cost_estimate=pl.CostEstimate(flops=3 * 10**10, bytes_accessed=10**8, transcendentals=0),
        compiler_params=pltpu.CompilerParams(
            vmem_limit_bytes=63 * 1024 * 1024, collective_id=2, has_side_effects=True
        ),
    )(*args)


def page_body(
    tokens,
    norm_gains,
    attn_qkv,
    attn_out,
    ffn_in,
    ffn_out,
    position_tables,
    page_counts,
    layout_cells,
    cotangent,
):
    group, ring = lax.axis_index("dp"), lax.axis_index("tensor")
    (
        att_full, ffn_full, prob, full, gains_here, normed_one_t, resid, normed_two, normed_two_t,
        cot, cot_t, qkv, context, inverse, cells_t, cells_twice, cell_tail,
    ) = forward(
        tokens, cotangent, norm_gains, attn_qkv, attn_out, ffn_in.transpose(0, 2, 1), ffn_out, position_tables,
        page_counts, layout_cells,
    )
    _, ffn_grads, low, low_t, half_grad, page_out, gain_two, ffn_first = middle(
        normed_two, normed_two_t, cot, cot_t, resid, gains_here, ffn_full
    )
    page_got, tokens_grad, qkv_grad, out_grad, inner_grad, outer_grad, small = backward(
        low, low_t, normed_one_t, half_grad, full, gains_here, qkv, context, inverse, cells_t,
        cells_twice, cell_tail, gain_two, ffn_first, att_full, prob, ffn_grads, page_out, ffn_in.shape[2],
    )
    layer_out = jnp.where(group % CORES == ring % 2, page_out, page_got)
    gains = (small[0, 8:] + small[1, 8:]).reshape(2, 1024)
    gains_grad = lax.dynamic_slice_in_dim(gains, (group * RING + ring) * 32, 32, axis=1)
    tables = small[:, 0:6, :BUCKETS].reshape(CORES, 3, 2, BUCKETS).transpose(1, 3, 0, 2)
    tables = tables.reshape(3, BUCKETS, 2 * CORES)
    tables_grad = lax.dynamic_slice_in_dim(tables, group * 4, 4, axis=1)
    return (
        layer_out,
        tokens_grad,
        gains_grad,
        qkv_grad,
        out_grad,
        inner_grad.transpose(0, 2, 1),
        outer_grad,
        tables_grad,
    )


def solution(mesh):
    return jax.shard_map(
        page_body if page_plan(mesh) else general_body,
        mesh=mesh,
        in_specs=(
            P(("dp", "tensor"), None),
            P(),
            P(None, None, "tensor"),
            P("tensor", None),
            P(None, None, "tensor"),
            P("tensor", None),
            P(None, None, "tensor"),
            P("dp"),
            P(None, "dp"),
            P(("dp", "tensor"), None),
        ),
        out_specs=(
            P(("dp", "tensor"), None),
            P(("dp", "tensor"), None),
            P(None, ("dp", "tensor")),
            P(None, "dp", "tensor"),
            P("tensor", "dp"),
            P(None, "dp", "tensor"),
            P("tensor", "dp"),
            P(None, "dp", "tensor"),
        ),
        check_vma=False,
    )
```

```python
import math

import jax
import jax.numpy as jnp
import numpy as np
from jax import lax
from jax.experimental import pallas as pl
from jax.experimental.pallas import tpu as pltpu
from jax.sharding import PartitionSpec as P

HEAD_DIM = 64
BUCKETS = 32
REL_REACH = 128
CELLS = 64
PAGE_LEN = 1024


HIGHEST_PRECISION = lax.Precision.HIGHEST
TABLE_PRECISION = lax.Precision.HIGH
NORM_EPSILON = 1e-06
MASK_VALUE = -1e30


def bucket_table(offsets, bucket_total, max_reach):
    half_total = bucket_total // 2
    exact_limit = half_total // 2
    distance = np.abs(offsets).astype(np.int32)
    upper_side = (offsets > 0).astype(np.int32) * half_total
    safe_dist = np.maximum(distance, 1).astype(np.float32)
    ratio = np.log(safe_dist / np.float32(exact_limit)) / np.float32(
        math.log(max_reach / exact_limit)
    )
    far_bucket = exact_limit + np.floor(ratio * np.float32(half_total - exact_limit)).astype(
        np.int32
    )
    far_bucket = np.minimum(far_bucket, half_total - 1)
    return (upper_side + np.where(distance < exact_limit, distance, far_bucket)).astype(np.int32)


def offset_onehot(length):
    offsets = np.arange(2 * length - 1) - (length - 1)
    buckets = bucket_table(offsets, BUCKETS, REL_REACH)
    return jnp.asarray((buckets[:, None] == np.arange(BUCKETS)[None, :]).astype(np.float32))


def layout_onehot():
    cell_range = np.arange(CELLS)
    buckets = bucket_table(cell_range[None, :] - cell_range[:, None], BUCKETS, CELLS)
    return jnp.asarray(
        (buckets.reshape(-1)[:, None] == np.arange(BUCKETS)[None, :]).astype(np.float32)
    )


def gelu_tanh(values):
    return jax.nn.gelu(values, approximate=True)


def relative_bias(table_rows, length):
    values = jnp.dot(offset_onehot(length), table_rows, precision=HIGHEST_PRECISION).T
    heads_dev = values.shape[0]
    padded = jnp.pad(values, ((0, 0), (0, 1)))
    tiled = jnp.tile(padded, (1, length))
    skewed = tiled[:, : length * (2 * length - 1)].reshape(heads_dev, length, 2 * length - 1)
    return skewed[:, :, length - 1 :]


def relative_sums(dscore, length):
    heads_dev = dscore.shape[0]
    placed = jnp.pad(dscore, ((0, 0), (0, 0), (length - 1, 0)))
    flat = jnp.pad(placed.reshape(heads_dev, length * (2 * length - 1)), ((0, 0), (0, length)))
    return jnp.sum(flat.reshape(heads_dev, length, 2 * length), axis=1)[:, : 2 * length - 1]


def layout_values(tables):
    values = jnp.einsum("mn,snh->shm", layout_onehot(), tables[1:], precision=HIGHEST_PRECISION)
    return values.reshape(2, tables.shape[2], CELLS, CELLS)


def cell_onehots(page_cells):
    onehot = (page_cells[:, :, None] == jnp.arange(CELLS)[None, None, :]).astype(jnp.float32)
    length = page_cells.shape[1]
    joined = onehot.transpose(1, 0, 2).reshape(length, 2 * CELLS)
    return (onehot, joined)


def layout_bias(page_cells, lay_vals):
    onehot, joined = cell_onehots(page_cells)
    length = page_cells.shape[1]
    heads_dev = lay_vals.shape[1]
    rows_side = jnp.einsum("sia,shab->hisb", onehot, lay_vals, precision=TABLE_PRECISION)
    rows_side = rows_side.reshape(heads_dev, length, 2 * CELLS)
    return jnp.einsum("hic,jc->hij", rows_side, joined, precision=TABLE_PRECISION)


def layout_sums(dscore, page_cells):
    onehot, joined = cell_onehots(page_cells)
    length = page_cells.shape[1]
    heads_dev = dscore.shape[0]
    partial_rows = jnp.einsum("hij,jc->hic", dscore, joined, precision=TABLE_PRECISION)
    partial_rows = partial_rows.reshape(heads_dev, length, 2, CELLS)
    return jnp.einsum("sia,hisb->shab", onehot, partial_rows, precision=TABLE_PRECISION)


def page_scores(query, key_rows, count, page_cells, rel_bias, lay_vals):
    length = query.shape[0]
    scores = jnp.einsum("ihd,jhd->hij", query, key_rows, preferred_element_type=jnp.float32)
    scores = scores + rel_bias + layout_bias(page_cells, lay_vals)
    valid = jnp.arange(length) < count
    return jnp.where(valid[None, None, :], scores, MASK_VALUE)


def attend(projected, page_counts, layout_cells, rel_bias, lay_vals):
    total_rows = projected.shape[1]
    pages = page_counts.shape[0]
    length = total_rows // pages
    heads_dev = projected.shape[2] // HEAD_DIM
    split = projected.reshape(3, pages, length, heads_dev, HEAD_DIM)
    cells_pages = layout_cells.reshape(2, pages, length).transpose(1, 0, 2)

    def one_page(items):
        query, key_rows, value_rows, count, page_cells = items
        scores = page_scores(query, key_rows, count, page_cells, rel_bias, lay_vals)
        log_total = jax.nn.logsumexp(scores, axis=2)
        prob_low = jnp.exp(scores - log_total[:, :, None]).astype(jnp.bfloat16)
        context = jnp.einsum(
            "hij,jhd->ihd", prob_low, value_rows, preferred_element_type=jnp.float32
        )
        return (context.astype(jnp.bfloat16).reshape(length, heads_dev * HEAD_DIM), log_total)

    context, log_totals = lax.map(
        one_page, (split[0], split[1], split[2], page_counts, cells_pages)
    )
    return (context.reshape(total_rows, heads_dev * HEAD_DIM), log_totals)


def attend_back(projected, grad_context, log_totals, page_counts, layout_cells, rel_bias, lay_vals):
    total_rows = projected.shape[1]
    pages = page_counts.shape[0]
    length = total_rows // pages
    heads_dev = projected.shape[2] // HEAD_DIM
    split = projected.reshape(3, pages, length, heads_dev, HEAD_DIM)
    grad_split = grad_context.reshape(pages, length, heads_dev, HEAD_DIM)
    cells_pages = layout_cells.reshape(2, pages, length).transpose(1, 0, 2)

    def page_step(carry, items):
        rel_acc, lay_acc = carry
        query, key_rows, value_rows, grad_ctx, page_lse, count, page_cells = items
        scores = page_scores(query, key_rows, count, page_cells, rel_bias, lay_vals)
        prob = jnp.exp(scores - page_lse[:, :, None])
        grad_prob = jnp.einsum(
            "ihd,jhd->hij", grad_ctx, value_rows, preferred_element_type=jnp.float32
        )
        delta = jnp.sum(grad_prob * prob, axis=2, keepdims=True)
        dscore = prob * (grad_prob - delta)
        rel_acc = rel_acc + relative_sums(dscore, length)
        lay_acc = lay_acc + layout_sums(dscore, page_cells)
        score_low = dscore.astype(jnp.bfloat16)
        grad_query = jnp.einsum(
            "hij,jhd->ihd", score_low, key_rows, preferred_element_type=jnp.float32
        ).astype(jnp.bfloat16)
        grad_key = jnp.einsum(
            "hij,ihd->jhd", score_low, query, preferred_element_type=jnp.float32
        ).astype(jnp.bfloat16)
        grad_value = jnp.einsum(
            "hij,ihd->jhd", prob.astype(jnp.bfloat16), grad_ctx, preferred_element_type=jnp.float32
        ).astype(jnp.bfloat16)
        stacked = jnp.stack([grad_query, grad_key, grad_value]).reshape(
            3, length, heads_dev * HEAD_DIM
        )
        return ((rel_acc, lay_acc), stacked)

    init_sums = (
        jnp.zeros((heads_dev, 2 * length - 1), jnp.float32),
        jnp.zeros((2, heads_dev, CELLS, CELLS), jnp.float32),
    )
    (rel_acc, lay_acc), grads = lax.scan(
        page_step,
        init_sums,
        (split[0], split[1], split[2], grad_split, log_totals, page_counts, cells_pages),
    )
    grad_proj = grads.transpose(1, 0, 2, 3).reshape(3, total_rows, heads_dev * HEAD_DIM)
    rel_grad = jnp.dot(offset_onehot(length).T, rel_acc.T, precision=HIGHEST_PRECISION)
    lay_grad = jnp.einsum(
        "shm,mn->snh",
        lay_acc.reshape(2, heads_dev, CELLS * CELLS),
        layout_onehot(),
        precision=HIGHEST_PRECISION,
    )
    return (grad_proj, jnp.concatenate([rel_grad[None], lay_grad], axis=0))


def norm_back(rows, scale, gain, grad_normed):
    weighted = grad_normed * gain
    return scale * weighted - rows * scale**3 * jnp.mean(rows * weighted, axis=1, keepdims=True)


def forward_core(
    token_rows,
    norm_gains,
    attn_qkv,
    attn_out,
    ffn_in,
    page_counts,
    layout_cells,
    rel_bias,
    lay_vals,
):
    scale_one = lax.rsqrt(jnp.mean(token_rows * token_rows, axis=1, keepdims=True) + NORM_EPSILON)
    normed_one = (token_rows * scale_one * norm_gains[0]).astype(jnp.bfloat16)
    gathered_one = lax.all_gather(normed_one, "tensor", axis=0, tiled=True)
    projected = jnp.einsum(
        "td,cdk->ctk", gathered_one, attn_qkv, preferred_element_type=jnp.float32
    ).astype(jnp.bfloat16)
    context, log_totals = attend(projected, page_counts, layout_cells, rel_bias, lay_vals)
    attn_total = lax.psum_scatter(
        jnp.dot(context, attn_out, preferred_element_type=jnp.float32)
        .astype(jnp.bfloat16)
        .astype(jnp.float32)
        .astype(jnp.bfloat16),
        "tensor",
        scatter_dimension=0,
        tiled=True,
    ).astype(jnp.float32)
    resid = token_rows + attn_total
    scale_two = lax.rsqrt(jnp.mean(resid * resid, axis=1, keepdims=True) + NORM_EPSILON)
    normed_two = (resid * scale_two * norm_gains[1]).astype(jnp.bfloat16)
    gathered_two = lax.all_gather(normed_two, "tensor", axis=0, tiled=True)
    gate_up = jnp.einsum("td,cdf->ctf", gathered_two, ffn_in, preferred_element_type=jnp.float32)
    hidden = (gelu_tanh(gate_up[0]) * gate_up[1]).astype(jnp.bfloat16)
    return (
        scale_one,
        gathered_one,
        projected,
        context,
        log_totals,
        resid,
        scale_two,
        gathered_two,
        gate_up,
        hidden,
    )


def general_body(
    tokens,
    norm_gains,
    attn_qkv,
    attn_out,
    ffn_in,
    ffn_out,
    position_tables,
    page_counts,
    layout_cells,
    cotangent,
):
    token_rows = tokens.astype(jnp.float32)
    rel_bias = relative_bias(position_tables[0], PAGE_LEN)
    lay_vals = layout_values(position_tables)
    first = forward_core(
        token_rows,
        norm_gains,
        attn_qkv,
        attn_out,
        ffn_in,
        page_counts,
        layout_cells,
        rel_bias,
        lay_vals,
    )
    first_hidden = first[9]
    rows_part = first_hidden
    ffn_total = lax.psum_scatter(
        jnp.dot(rows_part, ffn_out, preferred_element_type=jnp.float32)
        .astype(jnp.bfloat16)
        .astype(jnp.float32)
        .astype(jnp.bfloat16),
        "tensor",
        scatter_dimension=0,
        tiled=True,
    ).astype(jnp.float32)
    layer_out = (first[5] + ffn_total).astype(jnp.bfloat16)
    cot_rows = lax.all_gather(cotangent, "tensor", axis=0, tiled=True)
    again_rows, cot_rows = lax.optimization_barrier((token_rows, cot_rows))
    saved = forward_core(
        again_rows,
        norm_gains,
        attn_qkv,
        attn_out,
        ffn_in,
        page_counts,
        layout_cells,
        rel_bias,
        lay_vals,
    )
    (
        scale_one,
        gathered_one,
        projected,
        context,
        log_totals,
        resid,
        scale_two,
        gathered_two,
        gate_up,
        hidden,
    ) = saved
    grad_hidden = jnp.einsum("td,fd->tf", cot_rows, ffn_out, preferred_element_type=jnp.float32)
    outer_grad = jnp.einsum("tf,td->fd", hidden, cot_rows, preferred_element_type=jnp.float32)
    gelu_value, gelu_back = jax.vjp(gelu_tanh, gate_up[0])
    grad_gate = gelu_back(grad_hidden * gate_up[1])[0].astype(jnp.bfloat16)
    grad_up = (grad_hidden * gelu_value).astype(jnp.bfloat16)
    grad_gate_up = jnp.stack([grad_gate, grad_up])
    inner_grad = jnp.einsum(
        "td,ctf->cdf", gathered_two, grad_gate_up, preferred_element_type=jnp.float32
    )
    rows_part = grad_gate_up
    grad_normed_two = lax.psum_scatter(
        jnp.einsum("ctf,cdf->td", rows_part, ffn_in, preferred_element_type=jnp.float32)
        .astype(jnp.bfloat16)
        .astype(jnp.float32)
        .astype(jnp.bfloat16),
        "tensor",
        scatter_dimension=0,
        tiled=True,
    ).astype(jnp.float32)
    grad_resid = cotangent.astype(jnp.float32) + norm_back(
        resid, scale_two, norm_gains[1], grad_normed_two
    )
    gain_two = jnp.sum(grad_normed_two * resid * scale_two, axis=0)
    resid_rows = lax.all_gather(grad_resid.astype(jnp.bfloat16), "tensor", axis=0, tiled=True)
    out_grad = jnp.einsum("tk,td->kd", context, resid_rows, preferred_element_type=jnp.float32)
    grad_context = jnp.einsum(
        "td,kd->tk", resid_rows, attn_out, preferred_element_type=jnp.float32
    ).astype(jnp.bfloat16)
    grad_proj, tables_grad = attend_back(
        projected, grad_context, log_totals, page_counts, layout_cells, rel_bias, lay_vals
    )
    qkv_grad = jnp.einsum(
        "td,ctk->cdk", gathered_one, grad_proj, preferred_element_type=jnp.float32
    )
    rows_part = grad_proj
    grad_normed_one = lax.psum_scatter(
        jnp.einsum("ctk,cdk->td", rows_part, attn_qkv, preferred_element_type=jnp.float32)
        .astype(jnp.bfloat16)
        .astype(jnp.float32)
        .astype(jnp.bfloat16),
        "tensor",
        scatter_dimension=0,
        tiled=True,
    ).astype(jnp.float32)
    tokens_grad = grad_resid + norm_back(token_rows, scale_one, norm_gains[0], grad_normed_one)
    gain_one = jnp.sum(grad_normed_one * token_rows * scale_one, axis=0)
    gains_grad = lax.psum_scatter(
        jnp.stack([gain_one, gain_two]), ("dp", "tensor"), scatter_dimension=1, tiled=True
    )
    qkv_summed, inner_summed, out_summed, outer_summed, tables_summed = (
        lax.psum_scatter(
            qkv_grad.astype(jnp.bfloat16), "dp", scatter_dimension=1, tiled=True
        ).astype(jnp.float32),
        lax.psum_scatter(
            inner_grad.astype(jnp.bfloat16), "dp", scatter_dimension=1, tiled=True
        ).astype(jnp.float32),
        lax.psum_scatter(
            out_grad.astype(jnp.bfloat16), "dp", scatter_dimension=1, tiled=True
        ).astype(jnp.float32),
        lax.psum_scatter(
            outer_grad.astype(jnp.bfloat16), "dp", scatter_dimension=1, tiled=True
        ).astype(jnp.float32),
        lax.psum_scatter(
            tables_grad.astype(jnp.bfloat16), "dp", scatter_dimension=1, tiled=True
        ).astype(jnp.float32),
    )
    return (
        layer_out,
        tokens_grad,
        gains_grad,
        qkv_summed,
        out_summed,
        inner_summed,
        outer_summed,
        tables_summed,
    )


PLANES = 4
RING = 4
CORES = 2
BLOCK = 256
HALF = 128
PARTS = 2
ORDER = (0, 1, 3, 2)
BACK_ORDER = (2, 1, 3, 0)
SLOT = (1, 1, 0, 0)
KEPT_SLOT = (0, 1, 0, 0)
ATT = 512
UNITS = 384
FFW = 3 * UNITS
VMEM_BYTES = 60 * 1024 * 1024
F32 = jnp.float32
BF16 = jnp.bfloat16
NT = (((1,), (1,)), ((), ()))
TN = (((0,), (0,)), ((), ()))
NN = (((1,), (0,)), ((), ()))


def page_plan(mesh):
    return mesh.shape["dp"] == PLANES * CORES and mesh.shape["tensor"] == RING


def dot(left, right, dims=NN):
    return lax.dot_general(left, right, dims, preferred_element_type=F32)


def shaped(shape, dtype=BF16):
    return jax.ShapeDtypeStruct(shape, dtype)


def columns(plane, r):
    return pl.ds(pl.multiple_of((plane ^ r) * BLOCK, BLOCK), BLOCK)


def pair_lane(rows):
    return lax.broadcasted_iota(jnp.int32, (rows, 2 * HEAD_DIM), 1)


MESH = pl.DeviceIdType.MESH


def here():
    group, ring = lax.axis_index("dp"), lax.axis_index("tensor")
    return group // CORES, group % CORES, ring


def device(plane, core, ring):
    return (plane * CORES + core, ring)


def greet(partners):
    barrier = pltpu.get_barrier_semaphore()
    for partner in partners:
        pl.semaphore_signal(barrier, inc=1, device_id=partner, device_id_type=MESH)
    pl.semaphore_wait(barrier, len(partners))


class Lines:
    def __init__(self, send_sems, recv_sems):
        self.send_sems, self.recv_sems, self.open = send_sems, recv_sems, {}

    def make(self, name, source, target, partner):
        at = len(self.open)
        self.open[name] = pltpu.make_async_remote_copy(
            src_ref=source,
            dst_ref=target,
            send_sem=self.send_sems.at[at],
            recv_sem=self.recv_sems.at[at],
            device_id=partner,
            device_id_type=MESH,
        )
        return self.open[name]

    def start(self, name, source, target, partner):
        self.make(name, source, target, partner).start()

    def arrived(self, *names):
        for name in names:
            self.open[name].wait_recv()

    def sent(self, *names):
        for name in names or list(self.open):
            self.open[name].wait_send()


class Gather:
    def __init__(self, lines, tag, own, full, where):
        self.lines, self.tag, self.own, self.full = lines, tag, own, full
        self.plane, self.core, self.ring = where

    def place(self, ring):
        return device(self.plane, self.core, ring)

    def ring_start(self, k):
        self.lines.start(
            (self.tag, "z", k),
            self.own.at[0:BLOCK],
            self.full.at[k, 0:BLOCK],
            self.place((self.ring + RING - k) % RING),
        )

    def ring_forward(self):
        for name, k, step in (("down", 1, -1), ("up", 3, 1)):
            self.lines.make(
                (self.tag, name),
                self.full.at[k, 0:BLOCK],
                self.full.at[2, 0:BLOCK],
                self.place((self.ring + RING + step) % RING),
            )

        @pl.when((self.ring == 1) | (self.ring == 2))
        def _():
            self.lines.open[self.tag, "down"].start()
            self.lines.open[self.tag, "up"].start()

    def forward_arrived(self):
        @pl.when(self.ring < 2)
        def _():
            self.lines.arrived((self.tag, "down"))

        @pl.when(self.ring >= 2)
        def _():
            self.lines.arrived((self.tag, "up"))

    def forward_sent(self):
        @pl.when((self.ring == 1) | (self.ring == 2))
        def _():
            self.lines.sent((self.tag, "down"), (self.tag, "up"))

    def plane_start(self, k, landed=False):
        if k == 2 and not landed:
            self.forward_arrived()
        elif not landed:
            self.lines.arrived((self.tag, "z", k))
        for name, r in (("x", 1), ("y", 2)):
            self.lines.start(
                (self.tag, name, k),
                self.full.at[k, 0:BLOCK],
                self.full.at[k, r * BLOCK : (r + 1) * BLOCK],
                device(self.plane ^ r, self.core, self.ring),
            )

    def plane_arrived(self, k):
        self.lines.arrived((self.tag, "x", k), (self.tag, "y", k))

    def corner_start(self, k, landed=False):
        if not landed:
            self.plane_arrived(k)
        for name, r, half, goal in (("x", 1, 0, 2), ("y", 2, 1, 1)):
            self.lines.start(
                (self.tag, "corner" + name, k),
                self.full.at[k, r * BLOCK + half * HALF : r * BLOCK + (half + 1) * HALF],
                self.full.at[k, 3 * BLOCK + half * HALF : 3 * BLOCK + (half + 1) * HALF],
                device(self.plane ^ goal, self.core, self.ring),
            )

    def finish(self, k):
        self.lines.arrived((self.tag, "cornerx", k), (self.tag, "cornery", k))


def own_attention(core, plane, qkv, out, target):
    for r in range(PLANES):
        rows, place = columns(plane, r), slice(r * BLOCK, (r + 1) * BLOCK)
        mine = pl.ds(pl.multiple_of(core * HALF, HALF), HALF)
        target[place, 0:HALF] = out[mine, rows].astype(F32).T.astype(BF16)
        for m in range(3):
            target[place, (m + 1) * HALF : (m + 2) * HALF] = qkv[m, rows, mine]


def own_ffn(core, plane, inner, outer, target):
    units = outer.shape[0]
    for which, first, count in ((0, 0, UNITS), (1, UNITS, units - UNITS)):

        @pl.when(core == which)
        def _():
            for r in range(PLANES):
                rows, place = columns(plane, r), slice(r * BLOCK, (r + 1) * BLOCK)
                parts = [outer[first : first + count, rows]]
                parts += [inner[m, first : first + count, rows] for m in range(2)]
                parts = [part.astype(F32).T.astype(BF16) for part in parts]
                for m, part in enumerate(parts):
                    target[place, m * UNITS : m * UNITS + count] = part
                    if count < UNITS:
                        target[place, m * UNITS + count : (m + 1) * UNITS] = jnp.zeros(
                            (BLOCK, UNITS - count), BF16
                        )


def place_rows(plane, core, near, far, full):
    rows = near.shape[0]
    for source, half in ((near, core), (far, 1 - core)):
        for r in range(PLANES):
            full[pl.ds(pl.multiple_of(half * rows, rows), rows), r * BLOCK : (r + 1) * BLOCK] = (
                source[:, columns(plane, r)]
            )


def split_bf16(values):
    parts = []
    for _ in range(3):
        part = values.astype(BF16)
        parts.append(part)
        values = values - part.astype(F32)
    return parts


def bias_pieces(tables, near_hot, cell_hot, layout, near):
    parts = split_bf16(tables)
    rel = sum(dot(part, near_hot[...]) for part in parts)
    cells = dot(parts[0], cell_hot[...])
    heads = tables.shape[0] // 3
    for h in range(heads):
        near[h] = rel[h : h + 1, :]
        toeplitz = []
        for axis in range(2):
            row = jnp.broadcast_to(cells[(axis + 1) * heads + h : (axis + 1) * heads + h + 1], (CELLS, HALF))
            toeplitz.append(pltpu.roll(row, CELLS, 1, stride=1, stride_axis=0))
        side = lax.broadcasted_iota(jnp.int32, (CELLS, HALF), 1)
        first = toeplitz[0]
        layout[h, 0:CELLS, 0:HALF] = jnp.where(
            side < CELLS, first, pltpu.roll(first, CELLS, 1)
        ).astype(BF16)
        layout[h, 0:CELLS, HALF:] = jnp.zeros((CELLS, HALF), BF16)
        layout[h, CELLS:, 0:HALF] = jnp.zeros((CELLS, HALF), BF16)
        layout[h, CELLS:, HALF:] = jnp.where(side < CELLS, toeplitz[1], 0.0).astype(BF16)


def forward_kernel(
    tokens, cot, gains, qkv_w, out_w, ffn_in, ffn_out, tables, cell_ids, counts, near_hot, cell_hot,
    att_full, ffn_full, prob_full, full, gains_here, normed_t, resid, normed_two, normed_two_t,
    cot_full, cot_t, qkv, context, inverse, cells_t, cells_twice, cell_tail,
    near_x, far_x, near_g, far_g, other_ids, other_counts, table_parts, table_rows, layout, near,
    own_ffn_w, ffn_in_v, ffn_out_v, normed, weights, cells, queries, keys, scores, prob,
    mixed_all, out_rows, mine_out, other_out,
    send_sems, recv_sems, local_sems,
):
    plane, core, ring = where = here()
    native = core == ring % 2
    rows = tokens.shape[0]
    length = 2 * rows
    partner = device(plane, 1 - core, ring)
    swap = device(plane, 1 - core, ring ^ 1)
    ring_others = [device(plane, core, (ring + RING - k) % RING) for k in range(1, RING)]
    neighbours = [device(plane ^ 1, core, ring), device(plane ^ 2, core, ring)]
    lines = Lines(send_sems, recv_sems)
    load_in = pltpu.make_async_copy(ffn_in, ffn_in_v, local_sems.at[0])
    load_out = pltpu.make_async_copy(ffn_out, ffn_out_v, local_sems.at[1])
    load_in.start()
    load_out.start()
    greet([partner, swap] + ring_others + neighbours)

    def swap_rows(tag, source, near_rows, far_rows):
        for part in range(PARTS):
            span = pl.ds(part * (rows // PARTS), rows // PARTS)
            lines.make((tag, "swap", part), source.at[span], near_rows.at[span], swap)
            lines.make((tag, "give", part), source.at[span], far_rows.at[span], partner)
            lines.make((tag, "pass", part), near_rows.at[span], far_rows.at[span], partner)

        @pl.when(native)
        def _():
            for part in range(PARTS):
                lines.open[tag, "give", part].start()
            keep = pltpu.make_async_copy(source, near_rows, local_sems.at[2])
            keep.start()
            keep.wait()

        @pl.when(jnp.logical_not(native))
        def _():
            for part in range(PARTS):
                lines.open[tag, "swap", part].start()

    def swap_pass(tag):
        @pl.when(jnp.logical_not(native))
        def _():
            for part in range(PARTS):
                lines.arrived((tag, "swap", part))
                lines.open[tag, "pass", part].start()
            for part in range(PARTS):
                lines.arrived((tag, "give", part))

        @pl.when(native)
        def _():
            for part in range(PARTS):
                lines.arrived((tag, "pass", part))

    def swap_sent(tag):
        @pl.when(jnp.logical_not(native))
        def _():
            for part in range(PARTS):
                lines.sent((tag, "swap", part), (tag, "pass", part))

        @pl.when(native)
        def _():
            for part in range(PARTS):
                lines.sent((tag, "give", part))

    swap_rows("x", tokens, near_x, far_x)
    lines.start("ids", cell_ids, other_ids, partner)
    lines.start("counts", counts, other_counts, partner)
    table_parts[0] = tables[...]
    for k in range(1, RING):
        lines.start(("tables", k), tables, table_parts.at[k], ring_others[k - 1])
    own_attention(core, plane, qkv_w, out_w, weights)
    keep_weights = pltpu.make_async_copy(weights, att_full.at[0], local_sems.at[3])
    keep_weights.start()
    att = Gather(lines, "att", weights, att_full, where)
    ffn = Gather(lines, "ffn", own_ffn_w, ffn_full, where)
    keep_weights.wait()
    att.own = att_full.at[0]

    lines.arrived("ids", "counts")
    page = ring // 2
    picked = []
    for axis in range(2):
        span = pl.ds(pl.multiple_of(page * length, length), length)
        picked.append(
            jnp.where(native, cell_ids[axis : axis + 1, span], other_ids[axis : axis + 1, span])
        )
    picked.append(
        jnp.where(native, counts[pl.ds(page, 1), :], other_counts[pl.ds(page, 1), :])[:, 0:1]
    )
    spot = lax.broadcasted_iota(jnp.int32, (CELLS, length), 0)
    cells_x = (jnp.broadcast_to(picked[0], (CELLS, length)) == spot).astype(F32)
    cells_y = (jnp.broadcast_to(picked[1], (CELLS, length)) == spot).astype(F32)
    position = lax.broadcasted_iota(jnp.int32, (CELLS, length), 1)
    tail = jnp.where((spot < 16) & (spot % 8 == position // HALF), 1.0, 0.0)
    hidden_key = (spot == 16) & (position >= jnp.broadcast_to(picked[2], (CELLS, length)))
    tail = jnp.where(hidden_key, MASK_VALUE, tail)
    flipped = CELLS - 1 - spot
    for axis in range(2):
        turned = (jnp.broadcast_to(picked[axis], (CELLS, length)) == flipped).astype(F32)
        cells_t[axis * CELLS : (axis + 1) * CELLS, :] = turned.astype(BF16)
    cells[...] = jnp.concatenate([cells_x, cells_y], axis=0).T.astype(BF16)
    cells_twice[...] = jnp.concatenate([cells_x, cells_x], axis=0).T.astype(BF16)
    cell_tail[...] = jnp.concatenate([cells_y, tail], axis=0).T.astype(BF16)
    for k in range(1, RING):
        lines.arrived(("tables", k))
    table_rows[...] = jnp.zeros(table_rows.shape, F32)
    for k in range(RING):
        for axis in range(3):
            first = axis * 2 * RING + 2 * k
            table_rows[first : first + 2, 0:BUCKETS] = table_parts[k, axis, pl.ds(2 * core, 2), :]
    bias_pieces(table_rows[...], near_hot, cell_hot, layout, near)

    for r in range(PLANES):
        gains_here[:, r * BLOCK : (r + 1) * BLOCK] = gains[:, columns(plane, r)]
    load_in.wait()
    load_out.wait()
    own_ffn(core, plane, ffn_in_v, ffn_out_v, own_ffn_w)
    keep_ffn = pltpu.make_async_copy(own_ffn_w, ffn_full.at[0], local_sems.at[0])
    keep_ffn.start()
    swap_pass("x")
    att.ring_start(1)
    att.ring_start(3)
    place_rows(plane, core, near_x, far_x, full)
    for i in range(length // BLOCK):
        span = slice(i * BLOCK, (i + 1) * BLOCK)
        x = full[span, :].astype(F32)
        scale = lax.rsqrt(jnp.mean(x * x, axis=1, keepdims=True) + NORM_EPSILON)
        value = x * scale * gains_here[0:1, :]
        normed[span, :] = value.astype(BF16)
        normed_t[:, span] = value.T.astype(BF16)

    def head(k, h):
        at = 2 * k + h
        lane = pair_lane(length)
        mine = (lane // HEAD_DIM) == h
        side = dot(cells[...], layout[at])
        queries[:, :HALF] = jnp.where(mine, qkv[k, :, :HALF].astype(F32), side[:, :HALF]).astype(BF16)
        block = lax.broadcasted_iota(jnp.int32, (length, HALF), 0) // HALF
        is_left, is_right = lane % 8 < block - 1, lane % 8 > block + 1
        left, right = near[at, :, 0:1], near[at, :, 4 * HALF - 1 :]
        left_high, right_high = left.astype(BF16).astype(F32), right.astype(BF16).astype(F32)
        high = jnp.where(is_left, left_high, jnp.where(is_right, right_high, 0.0))
        low = jnp.where(is_left, left - left_high, jnp.where(is_right, right - right_high, 0.0))
        ends = jnp.where(lane < HEAD_DIM, side[:, HALF:], jnp.where(lane == HEAD_DIM + 16, 1.0, 0.0))
        ends = jnp.where((lane >= HEAD_DIM) & (lane < HEAD_DIM + 8), high, ends)
        ends = jnp.where((lane >= HEAD_DIM + 8) & (lane < HEAD_DIM + 16), low, ends)
        queries[:, HALF:] = ends.astype(BF16)
        keys[:, :HALF] = jnp.where(
            mine, qkv[k, :, HALF : 2 * HALF].astype(F32), cells_twice[...].astype(F32)
        ).astype(BF16)
        keys[:, HALF:] = cell_tail[...]
        scores[...] = dot(queries[...], keys[...], NT)
        spread = jnp.broadcast_to(near[at], (HALF, 4 * HALF))
        strip = pltpu.roll(spread, 3 * HALF, 1, stride=1, stride_axis=0)[:, : 3 * HALF]
        count = length // HALF
        store = pltpu.make_async_copy(prob.at[h], prob_full.at[at], local_sems.at[4 + h])
        if k > 0:
            store.wait()
        for i in range(count):
            first, last = max(i - 1, 0), min(i + 2, count)
            part = strip[:, (first - i + 1) * HALF : (last - i + 1) * HALF]
            span, near_span = slice(i * HALF, (i + 1) * HALF), slice(first * HALF, last * HALF)
            scores[span, near_span] = scores[span, near_span] + part
            row = scores[span, :]
            top = jnp.max(row, axis=1, keepdims=True)
            prob[h, span, :] = jnp.exp(row - top).astype(BF16)
        values = jnp.where(mine, qkv[k, :, 2 * HALF :].astype(F32), 1.0).astype(BF16)
        mixed = dot(prob[h], values)
        inv = 1.0 / pltpu.roll(mixed, HEAD_DIM, 1)
        mixed = (mixed * inv).astype(BF16)
        store.start()
        if h == 0:
            context[k] = mixed
            inverse[k] = inv
        else:
            context[k] = jnp.where(mine, mixed.astype(F32), context[k].astype(F32)).astype(BF16)
            inverse[k] = jnp.where(mine, inv, inverse[k])

    def project(k):
        if k > 0:
            load = pltpu.make_async_copy(att_full.at[k], weights, local_sems.at[3])
            load.start()
            load.wait()
        qkv[k] = dot(normed[...], weights[:, HALF:]).astype(BF16)
        mixed_all[:, k * HALF : (k + 1) * HALF] = weights[:, 0:HALF]

    def after_head(k, h):
        if (k, h) == (0, 0):
            att.plane_start(3)
            att.ring_forward()
        if (k, h) == (0, 1):
            att.corner_start(1)
            att.plane_start(2)
            ffn.ring_start(1)
            swap_rows("g", cot, near_g, far_g)
            att.finish(1)
        if (k, h) == (1, 0):
            att.corner_start(3)
        if (k, h) == (1, 1):
            att.corner_start(2)
            ffn.plane_start(1)
            ffn.ring_start(3)
            att.finish(3)
        if (k, h) == (3, 0):
            swap_pass("g")
        if (k, h) == (3, 1):
            ffn.corner_start(1)
            att.finish(2)
        if (k, h) == (2, 0):
            ffn.plane_start(3)
            ffn.ring_forward()

    for k in ORDER:
        project(k)
        if k == 0:
            att.plane_start(1)
        for h in range(2):
            head(k, h)
            after_head(k, h)

    for k in range(RING):
        out_rows[:, k * HALF : (k + 1) * HALF] = context[k]
    for i in range(length // BLOCK):
        span = slice(i * BLOCK, (i + 1) * BLOCK)
        mine_out[span, :] = dot(out_rows[span, :], mixed_all[...], NT).astype(BF16)
        lines.start(("out", i), mine_out.at[span], other_out.at[span], partner)
    place_rows(plane, core, near_g, far_g, cot_full)
    for r in range(PLANES):
        lanes = slice(r * BLOCK, (r + 1) * BLOCK)
        cot_t[lanes, :] = cot_full[:, lanes].astype(F32).T.astype(BF16)
    for i in range(length // BLOCK):
        span = slice(i * BLOCK, (i + 1) * BLOCK)
        lines.arrived(("out", i))
        row = full[span, :].astype(F32) + (
            mine_out[span, :].astype(F32) + other_out[span, :].astype(F32)
        )
        resid[span, :] = row
        scale = lax.rsqrt(jnp.mean(row * row, axis=1, keepdims=True) + NORM_EPSILON)
        value = row * scale * gains_here[1:2, :]
        normed_two[span, :] = value.astype(BF16)
        normed_two_t[:, span] = value.T.astype(BF16)

    ffn.finish(1)
    ffn.plane_arrived(3)
    ffn.forward_arrived()
    keep_ffn.wait()
    for h in range(2):
        pltpu.make_async_copy(prob.at[h], prob_full.at[2 * ORDER[-1] + h], local_sems.at[4 + h]).wait()
    swap_sent("x")
    swap_sent("g")
    att.forward_sent()
    ffn.forward_sent()
    lines.sent(
        *[
            name
            for name in lines.open
            if name[0] not in ("x", "g") and name[1] not in ("down", "up")
        ]
    )


def hot(reach, width):
    offsets = np.arange(width) - width // 2
    found = bucket_table(offsets, BUCKETS, reach)[None, :] == np.arange(HALF)[:, None]
    return jnp.asarray(found.astype(np.float32), BF16)


def forward(tokens, cotangent, gains, qkv_w, out_w, ffn_in, ffn_out, position_tables, page_counts, layout_cells):
    rows = tokens.shape[0]
    length = 2 * rows
    features = PLANES * BLOCK
    tables = position_tables.transpose(0, 2, 1)
    counts = jnp.broadcast_to(page_counts[:, None], (2, HALF))
    args = [tokens, cotangent, gains, qkv_w, out_w, ffn_in, ffn_out, tables, layout_cells, counts]
    args += [hot(REL_REACH, 4 * HALF), hot(CELLS, HALF)]
    whole = pl.BlockSpec(memory_space=pltpu.VMEM)
    outside = pl.BlockSpec(memory_space=pl.ANY)
    outs = [
        shaped((RING, features, ATT)), shaped((RING, features, FFW)), shaped((2 * RING, length, length)),
        shaped((length, features)), shaped((2, features), F32), shaped((features, length)),
        shaped((length, features), F32), shaped((length, features)), shaped((features, length)),
        shaped((length, features)), shaped((features, length)),
        shaped((RING, length, 3 * HALF)), shaped((RING, length, HALF)), shaped((RING, length, HALF), F32),
        shaped((HALF, length)), shaped((length, HALF)), shaped((length, HALF)),
    ]
    scratch = [pltpu.VMEM((rows, features), BF16)] * 4 + [
        pltpu.VMEM(layout_cells.shape, jnp.int32),
        pltpu.VMEM(counts.shape, jnp.int32),
        pltpu.VMEM((RING,) + tables.shape, F32),
        pltpu.VMEM((6 * RING, HALF), F32),
        pltpu.VMEM((2 * RING, HALF, 2 * HALF), BF16),
        pltpu.VMEM((2 * RING, 1, 4 * HALF), F32),
        pltpu.VMEM((features, FFW), BF16),
        pltpu.VMEM(ffn_in.shape, BF16),
        pltpu.VMEM(ffn_out.shape, BF16),
        pltpu.VMEM((length, features), BF16),
        pltpu.VMEM((features, ATT), BF16),
        pltpu.VMEM((length, HALF), BF16),
        pltpu.VMEM((length, 2 * HALF), BF16),
        pltpu.VMEM((length, 2 * HALF), BF16),
        pltpu.VMEM((length, length), F32),
        pltpu.VMEM((2, length, length), BF16),
        pltpu.VMEM((features, RING * HALF), BF16),
        pltpu.VMEM((length, RING * HALF), BF16),
        pltpu.VMEM((length, features), BF16),
        pltpu.VMEM((length, features), BF16),
        pltpu.SemaphoreType.DMA((56,)),
        pltpu.SemaphoreType.DMA((56,)),
        pltpu.SemaphoreType.DMA((6,)),
    ]
    in_specs = [whole, outside, whole, whole, whole, outside, outside] + [whole] * 5
    out_specs = [outside] * 3 + [whole] * 14
    return pl.pallas_call(
        forward_kernel,
        out_shape=outs,
        in_specs=in_specs,
        out_specs=out_specs,
        scratch_shapes=scratch,
        name="forward",
        cost_estimate=pl.CostEstimate(flops=10**10, bytes_accessed=10**8, transcendentals=0),
        compiler_params=pltpu.CompilerParams(
            vmem_limit_bytes=63 * 1024 * 1024, collective_id=0, has_side_effects=True
        ),
    )(*args)


class Scatter:
    def __init__(self, lines, tag, k, grads, kept, buffers, where):
        self.lines, self.tag, self.k, self.grads, self.kept = lines, tag, k, grads, kept
        self.from_x, self.from_y, self.late, self.same, self.cross = buffers
        self.plane, self.core, self.ring = where
        self.to_x = device(self.plane ^ 1, self.core, self.ring)
        self.to_y = device(self.plane ^ 2, self.core, self.ring)

    def name(self, step):
        return (self.tag, step, self.k)

    def rows(self, r, half):
        return slice(r * BLOCK + half * HALF, r * BLOCK + (half + 1) * HALF)

    def start(self):
        k = self.k
        for step, r, half, target, goal in (
            ("x1", 3, 0, self.from_x.at[k, 1], self.to_x),
            ("y1", 3, 1, self.from_y.at[k, 1], self.to_y),
            ("x0", 1, 0, self.from_x.at[k, 0], self.to_x),
            ("y0", 2, 1, self.from_y.at[k, 0], self.to_y),
        ):
            self.lines.start(self.name(step), self.grads.at[self.rows(r, half)], target, goal)

    def middle(self):
        k = self.k
        self.lines.arrived(self.name("x1"), self.name("y1"))
        for source, r, half, at, goal, step in (
            (self.from_x, 2, 0, 0, self.to_y, "late0"),
            (self.from_y, 1, 1, 1, self.to_x, "late1"),
        ):
            kept = self.kept(r, half).astype(F32)
            source[k, 1] = (kept + source[k, 1].astype(F32)).astype(BF16)
            self.lines.start(self.name(step), source.at[k, 1], self.late.at[k, at], goal)

    def last(self):
        self.combine()
        self.hand_over()

    def combine(self):
        k, late = self.k, self.late
        self.lines.arrived(*[self.name(step) for step in ("x0", "y0", "late0", "late1")])
        upper = self.kept(0, 0).astype(F32) + self.from_x[k, 0].astype(F32) + late[k, 0].astype(F32)
        lower = self.kept(0, 1).astype(F32) + self.from_y[k, 0].astype(F32) + late[k, 1].astype(F32)
        late[k, 0] = jnp.where(self.core == 0, upper, lower).astype(BF16)
        late[k, 1] = jnp.where(self.core == 0, lower, upper).astype(BF16)

    def hand_over(self):
        k, late = self.k, self.late
        goal = (self.ring + k) % RING
        if k > 0:
            self.lines.start(
                self.name("same"), late.at[k, 0], self.same.at[k - 1], device(self.plane, self.core, goal)
            )
        self.lines.start(
            self.name("cross"), late.at[k, 1], self.cross.at[k], device(self.plane, 1 - self.core, goal)
        )


def gelu_parts(gate):
    square = gate * gate
    ratio = math.sqrt(2.0 / math.pi)
    bend = jnp.tanh(ratio * gate * (1.0 + 0.044715 * square))
    half_gate = 0.5 * gate
    value = half_gate + half_gate * bend
    slope = 0.5 + 0.5 * bend + half_gate * (1.0 - bend * bend) * (
        ratio * (1.0 + 3.0 * 0.044715 * square)
    )
    return value, slope


def middle_kernel(
    normed, normed_t, cot, cot_t, resid, gains_here, ffn_before,
    ffn_full, grads_full, low, low_t, half_grad, page_out, gain, late,
    weights, hidden, grads, total_in, total_out, mine, other, mine_out, other_out,
    kept, from_x, from_y,
    send_sems, recv_sems, local_sems,
):
    plane, core, ring = where = here()
    partner = device(plane, 1 - core, ring)
    lines = Lines(send_sems, recv_sems)
    length = normed.shape[0]
    rows = length // 2
    blocks = length // BLOCK

    gather = Gather(lines, "ffn", None, ffn_full, where)

    def load(at):
        return pltpu.make_async_copy(
            ffn_full.at[ORDER[at]], weights.at[at % 2], local_sems.at[at % 2]
        )

    def store(k):
        return pltpu.make_async_copy(grads, grads_full.at[k], local_sems.at[2])

    loads = [
        pltpu.make_async_copy(
            grads_full.at[0, first : first + BLOCK], kept.at[at : at + BLOCK], local_sems.at[3 + i]
        )
        for i, (first, at) in enumerate(((0, 0), (3 * HALF, BLOCK)))
    ]
    spots = {(0, 0): 0, (0, 1): HALF, (1, 1): BLOCK, (2, 0): BLOCK + HALF}
    scatter = Scatter(
        lines, "grads", 0, grads_full.at[0],
        lambda r, half: kept[spots[r, half] : spots[r, half] + HALF],
        (from_x, from_y, late, None, None), where,
    )
    load(0).start()
    load(1).start()
    greet([partner, device(plane ^ 1, core, ring), device(plane ^ 2, core, ring)])
    gather.corner_start(3, landed=True)
    gather.plane_start(2, landed=True)
    for at, k in enumerate(ORDER):
        load(at).wait()
        w = weights.at[at % 2]
        for i in range(blocks):
            span = slice(i * BLOCK, (i + 1) * BLOCK)
            both = dot(normed[span, :], w[:, UNITS:])
            grad_hidden = dot(cot[span, :], w[:, :UNITS])
            gate, up = both[:, :UNITS], both[:, UNITS:]
            value, slope = gelu_parts(gate)
            hidden[span, :UNITS] = (value * up).astype(BF16)
            hidden[span, UNITS : 2 * UNITS] = (grad_hidden * up * slope).astype(BF16)
            hidden[span, 2 * UNITS :] = (grad_hidden * value).astype(BF16)
            part_in = dot(hidden[span, UNITS:], w[:, UNITS:], NT)
            part_out = dot(hidden[span, :UNITS], w[:, :UNITS], NT)
            if at > 0:
                part_in = total_in[span, :] + part_in
                part_out = total_out[span, :] + part_out
            if at + 1 < RING:
                total_in[span, :] = part_in
                total_out[span, :] = part_out
            else:
                mine[span, :] = part_in.astype(BF16)
                lines.start(("in", i), mine.at[span], other.at[span], partner)
                mine_out[span, :] = part_out.astype(BF16)
        if at + 1 == RING:
            far = pl.ds(pl.multiple_of((1 - core) * rows, rows), rows)
            lines.start("out", mine_out.at[far], other_out, partner)
        if at > 0:
            store(ORDER[at - 1]).wait()
        if at == 1:
            gather.finish(3)
            load(2).start()
            gather.corner_start(2)
            scatter.start()
            for copy in loads:
                copy.start()
        if at == 2:
            gather.finish(2)
            load(3).start()
        for i in range(2):
            span = slice(i * 2 * BLOCK, (i + 1) * 2 * BLOCK)
            grads[span, :UNITS] = dot(cot_t[span, :], hidden[:, :UNITS]).astype(BF16)
            grads[span, UNITS:] = dot(normed_t[span, :], hidden[:, UNITS:]).astype(BF16)
        store(k).start()
        if at == 2:
            for copy in loads:
                copy.wait()
            scatter.middle()

    total = jnp.zeros((1, resid.shape[1]), F32)
    for i in range(blocks):
        span = slice(i * BLOCK, (i + 1) * BLOCK)
        lines.arrived(("in", i))
        row = resid[span, :]
        grad = mine[span, :].astype(F32) + other[span, :].astype(F32)
        scale = lax.rsqrt(jnp.mean(row * row, axis=1, keepdims=True) + NORM_EPSILON)
        weighted = grad * gains_here[1:2, :]
        center = jnp.mean(row * weighted, axis=1, keepdims=True)
        value = cot[span, :].astype(F32) + scale * weighted - row * (scale * scale * scale * center)
        low[span, :] = value.astype(BF16)
        low_t[:, span] = value.T.astype(BF16)
        in_half = core == (i * BLOCK) // rows
        total = total + jnp.where(in_half, jnp.sum(grad * row * scale, axis=0, keepdims=True), 0.0)

        @pl.when(in_half)
        def _():
            first = (i * BLOCK) % rows
            half_grad[first : first + BLOCK, :] = value

    for r in range(PLANES):
        gain[:, columns(plane, r)] = total[:, r * BLOCK : (r + 1) * BLOCK]
    lines.arrived("out")
    for i in range(rows // BLOCK):
        span = slice(i * BLOCK, (i + 1) * BLOCK)
        near = pl.ds(pl.multiple_of(core * rows + i * BLOCK, BLOCK), BLOCK)
        row = resid[near, :] + (mine_out[near, :].astype(F32) + other_out[span, :].astype(F32))
        for r in range(PLANES):
            page_out[span, columns(plane, r)] = row[:, r * BLOCK : (r + 1) * BLOCK].astype(BF16)
    scatter.combine()
    store(ORDER[-1]).wait()
    lines.sent()


def middle(normed, normed_t, cot, cot_t, resid, gains_here, ffn_full):
    length, features = normed.shape
    rows = length // 2
    whole = pl.BlockSpec(memory_space=pltpu.VMEM)
    outside = pl.BlockSpec(memory_space=pl.ANY)
    return pl.pallas_call(
        middle_kernel,
        out_shape=[
            shaped((RING, features, FFW)), shaped((RING, features, FFW)),
            shaped((length, features)), shaped((features, length)),
            shaped((rows, features), F32), shaped((rows, features)), shaped((1, features), F32),
            shaped((1, 2, HALF, FFW)),
        ],
        in_specs=[whole] * 6 + [outside],
        out_specs=[outside] * 2 + [whole] * 6,
        input_output_aliases={6: 0},
        scratch_shapes=[
            pltpu.VMEM((2, features, FFW), BF16),
            pltpu.VMEM((length, FFW), BF16),
            pltpu.VMEM((features, FFW), BF16),
            pltpu.VMEM((length, features), F32),
            pltpu.VMEM((length, features), F32),
            pltpu.VMEM((length, features), BF16),
            pltpu.VMEM((length, features), BF16),
            pltpu.VMEM((length, features), BF16),
            pltpu.VMEM((rows, features), BF16),
            pltpu.VMEM((2 * BLOCK, FFW), BF16),
            pltpu.VMEM((1, 2, HALF, FFW), BF16),
            pltpu.VMEM((1, 2, HALF, FFW), BF16),
            pltpu.SemaphoreType.DMA((20,)),
            pltpu.SemaphoreType.DMA((20,)),
            pltpu.SemaphoreType.DMA((5,)),
        ],
        name="middle",
        cost_estimate=pl.CostEstimate(flops=27 * 10**9, bytes_accessed=10**8, transcendentals=0),
        compiler_params=pltpu.CompilerParams(
            vmem_limit_bytes=63 * 1024 * 1024, collective_id=1, has_side_effects=True
        ),
    )(normed, normed_t, cot, cot_t, resid, gains_here, ffn_full)


def sum_ring(lines, tag, late, same, cross):
    for k in range(RING):
        if k > 0:
            lines.arrived((tag, "same", k))
        lines.arrived((tag, "cross", k))
    mine = late[0, 0].astype(F32)
    for k in range(1, RING):
        mine = mine + same[k - 1].astype(F32)
    other = cross[0].astype(F32)
    for k in range(1, RING):
        other = other + cross[k].astype(F32)
    return mine, other


def backward_kernel(
    low, low_t, normed_t, half_grad, full, gains_here, qkv, context, inverse,
    cells_t, cells_twice, cell_tail, near_hot, cell_hot, gain_two, ffn_first,
    att_full, prob_full, ffn_grads, page_out,
    layer_out, tokens_grad, qkv_grad, out_grad, inner_grad, outer_grad, small_out,
    weights, prob, scaled, scaled_low, keys, dscores, grad_qkv, att_grads, total, mine_half, far_half,
    other_half, page_low, swapped, ffn_kept,
    att_x, att_y, att_late, att_same, att_cross, ffn_x, ffn_y, ffn_late, ffn_same, ffn_cross,
    diag_near, diag_cell, gain_one, small, small_ring, small_plane, small_core,
    send_sems, recv_sems, local_sems,
):
    plane, core, ring = where = here()
    native = core == ring % 2
    length = low.shape[0]
    rows = length // 2
    count = length // HALF
    partner = device(plane, 1 - core, ring)
    swap = device(plane, 1 - core, ring ^ 1)
    partners = [partner, swap, device(plane ^ 1, core, ring), device(plane ^ 2, core, ring)]
    for k in range(1, RING):
        partners += [device(plane, core, (ring + k) % RING), device(plane, 1 - core, (ring + k) % RING)]
    lines = Lines(send_sems, recv_sems)

    def load_prob(at):
        head_at = 2 * BACK_ORDER[at // 2] + at % 2
        return pltpu.make_async_copy(prob_full.at[head_at], prob.at[at % 2], local_sems.at[at % 2])

    def load_weights(k):
        return pltpu.make_async_copy(att_full.at[k], weights.at[SLOT[k]], local_sems.at[2 + SLOT[k]])

    def load_kept(k):
        slot = KEPT_SLOT[k]
        return [
            pltpu.make_async_copy(
                ffn_grads.at[k, first : first + BLOCK],
                ffn_kept.at[slot, at : at + BLOCK],
                local_sems.at[4 + 2 * slot + i],
            )
            for i, (first, at) in enumerate(((0, 0), (3 * HALF, BLOCK)))
        ]

    load_prob(0).start()
    load_prob(1).start()
    load_weights(BACK_ORDER[0]).start()
    goals = [partner, device(plane ^ 1, core, ring), device(plane ^ 2, core, ring)] + partners[4:]
    greet(goals)

    def kept_ffn(k):
        spots = {(0, 0): 0, (0, 1): HALF, (1, 1): BLOCK, (2, 0): BLOCK + HALF}
        return lambda r, half: ffn_kept[KEPT_SLOT[k], spots[r, half] : spots[r, half] + HALF]

    def kept_att(k):
        def read(r, half):
            first = r * BLOCK + half * HALF
            return att_grads[k, first : first + HALF]

        return read

    ffn = [
        Scatter(lines, "ffn", k, ffn_grads.at[k], kept_ffn(k), (ffn_x, ffn_y, ffn_late, ffn_same, ffn_cross), where)
        for k in range(RING)
    ]
    att = [
        Scatter(lines, "att", k, att_grads.at[k], kept_att(k), (att_x, att_y, att_late, att_same, att_cross), where)
        for k in range(RING)
    ]

    def ffn_start(k):
        for copy in load_kept(k):
            copy.start()
        ffn[k].start()

    def ffn_middle(k):
        for copy in load_kept(k):
            copy.wait()
        ffn[k].middle()

    ffn_start(2)
    ffn_late[0] = ffn_first[0]
    ffn[0].hand_over()
    lines.make("layer", page_out, layer_out, swap)

    @pl.when(jnp.logical_not(native))
    def _():
        lines.open["layer"].start()

    lane = pair_lane(length)
    row_block = lax.broadcasted_iota(jnp.int32, (length, HALF), 0) // HALF
    flip_at = lax.broadcasted_iota(jnp.int32, (HALF, HALF), 0)
    flip_to = lax.broadcasted_iota(jnp.int32, (HALF, HALF), 1)
    flip = jnp.where(flip_at + flip_to == HALF - 1, 1.0, 0.0).astype(BF16)

    def enter(k):
        at = BACK_ORDER.index(k)
        if at + 1 < RING:
            load_weights(BACK_ORDER[at + 1]).start()
        load_weights(k).wait()
        grad_context = dot(low[...], weights[SLOT[k], :, 0:HALF]).astype(BF16).astype(F32)
        value = grad_context * inverse[k]
        scaled[...] = value
        scaled_low[...] = value.astype(BF16)

    def head(k, h):
        at = 2 * k + h
        mine = (lane // HEAD_DIM) == h
        value = scaled[...]
        delta = -jnp.sum(
            jnp.where(mine, value * context[k].astype(F32), 0.0), axis=1, keepdims=True
        )
        delta_high = delta.astype(BF16).astype(F32)
        spare = HEAD_DIM * (1 - h)
        fill = jnp.where(lane == spare + 1, delta - delta_high, 0.0)
        left = jnp.where(mine, value, jnp.where(lane == spare, delta_high, fill)).astype(BF16)
        ones = jnp.where((lane == spare) | (lane == spare + 1), 1.0, 0.0)
        right = jnp.where(mine, qkv[k, :, 2 * HALF :].astype(F32), ones).astype(BF16)
        turn = 2 * BACK_ORDER.index(k) + h
        load_prob(turn).wait()
        strips = [jnp.zeros((HALF, HALF), F32) for _ in range(3)]
        for i in range(length // BLOCK):
            span = slice(i * BLOCK, (i + 1) * BLOCK)
            dscore = prob[at % 2, span, :].astype(F32) * dot(left[span, :], right, NT)
            dscores[span, :] = dscore.astype(BF16)
            for part in range(BLOCK // HALF):
                for step in range(3):
                    block = i * (BLOCK // HALF) + part + step - 1
                    if 0 <= block < count:
                        strips[step] = strips[step] + dscore[
                            part * HALF : (part + 1) * HALF, block * HALF : (block + 1) * HALF
                        ]
        keys[:, :HALF] = jnp.where(
            mine, qkv[k, :, HALF : 2 * HALF].astype(F32), cells_twice[...].astype(F32)
        ).astype(BF16)
        keys[:, HALF:] = cell_tail[...]
        grad_left = dot(dscores[...], keys[...])
        grad_key = dot(dscores[...], qkv[k, :, :HALF], TN)
        grad_value = dot(prob[at % 2], scaled_low[...], TN)
        if turn + 2 < 2 * RING:
            load_prob(turn + 2).start()
        for m, new in enumerate((grad_left[:, :HALF], grad_key, grad_value)):
            lanes = slice(m * HALF, (m + 1) * HALF)
            if h == 1:
                new = jnp.where(mine, new, grad_qkv[:, lanes].astype(F32))
            grad_qkv[:, lanes] = new.astype(BF16)

        skewed = jnp.zeros((HALF, 3 * HALF), F32)
        strip = jnp.concatenate(strips, axis=1)
        for part in split_bf16(strip):
            skewed = skewed + dot(flip, part)
        skewed = jnp.concatenate([skewed, jnp.zeros((HALF, HALF), F32)], axis=1)
        sums = jnp.sum(pltpu.roll(skewed, 1, 1, stride=1, stride_axis=0), axis=0, keepdims=True)
        tail = grad_left[:, HALF:]
        in_tail = (lane >= HEAD_DIM) & (lane < HEAD_DIM + 8)
        far_left = jnp.sum(jnp.where(in_tail & (lane % 8 < row_block - 1), tail, 0.0), axis=0, keepdims=True)
        far_right = jnp.sum(jnp.where(in_tail & (lane % 8 > row_block + 1), tail, 0.0), axis=0, keepdims=True)
        wide = lax.broadcasted_iota(jnp.int32, (1, 4 * HALF), 1)
        sums = sums + jnp.where(wide == 0, jnp.sum(far_left, axis=1, keepdims=True), 0.0)
        sums = sums + jnp.where(wide == 4 * HALF - 1, jnp.sum(far_right, axis=1, keepdims=True), 0.0)
        diag_near[at : at + 1, :] = sums
        by_cell = grad_left[:, :HALF]
        by_cell = jnp.where(mine, pltpu.roll(by_cell, HEAD_DIM, 1), by_cell)
        for axis, table in enumerate((by_cell, tail)):
            table_high = table.astype(BF16)
            rest = (table - table_high.astype(F32)).astype(BF16)
            side = cells_t[axis * CELLS : (axis + 1) * CELLS, :]
            grid = dot(side, table_high) + dot(side, rest)
            cell_lane = lax.broadcasted_iota(jnp.int32, (CELLS, HALF), 1)
            grid = jnp.where(cell_lane < CELLS, grid, 0.0)
            grid = pltpu.roll(grid, 1, 1, stride=1, stride_axis=0)
            row = axis * 2 * RING + at
            diag_cell[row : row + 1, :] = jnp.sum(grid, axis=0, keepdims=True)

    def leave(k):
        w = weights[SLOT[k], :, HALF:]
        att_grads[k, :, 0:HALF] = dot(low_t[...], context[k]).astype(BF16)
        att_grads[k, :, HALF:] = dot(normed_t[...], grad_qkv[...]).astype(BF16)
        if k == BACK_ORDER[-1]:
            att[k].start()
        for i in range(length // BLOCK):
            span = slice(i * BLOCK, (i + 1) * BLOCK)
            part = dot(grad_qkv[span, :], w, NT)
            total[span, :] = part if k == BACK_ORDER[0] else total[span, :] + part

    enter(2)
    head(2, 0)
    head(2, 1)
    ffn_middle(2)
    ffn_start(1)
    leave(2)
    enter(1)
    head(1, 0)
    ffn[2].last()
    head(1, 1)
    leave(1)
    ffn_middle(1)
    ffn_start(3)
    enter(3)
    head(3, 0)
    att[2].start()
    head(3, 1)
    ffn[1].last()
    leave(3)
    enter(0)
    head(0, 0)
    ffn_middle(3)
    att[1].start()
    head(0, 1)
    att[2].middle()
    att[3].start()
    leave(0)
    ffn[3].last()

    near = pl.ds(pl.multiple_of(core * rows, rows), rows)
    far = pl.ds(pl.multiple_of((1 - core) * rows, rows), rows)
    far_half[...] = total[far, :].astype(BF16)
    lines.start("half", far_half, other_half, partner)
    mine_half[...] = total[near, :].astype(BF16)
    lines.arrived("half")
    gain = jnp.zeros((1, full.shape[1]), F32)
    for i in range(rows // BLOCK):
        span = slice(i * BLOCK, (i + 1) * BLOCK)
        x = full[pl.ds(pl.multiple_of(core * rows + i * BLOCK, BLOCK), BLOCK), :].astype(F32)
        grad = mine_half[span, :].astype(F32) + other_half[span, :].astype(F32)
        scale = lax.rsqrt(jnp.mean(x * x, axis=1, keepdims=True) + NORM_EPSILON)
        weighted = grad * gains_here[0:1, :]
        center = jnp.mean(x * weighted, axis=1, keepdims=True)
        value = half_grad[span, :] + scale * weighted - x * (scale * scale * scale * center)
        gain = gain + jnp.sum(grad * x * scale, axis=0, keepdims=True)
        for r in range(PLANES):
            block = value[:, r * BLOCK : (r + 1) * BLOCK]
            tokens_grad[span, columns(plane, r)] = block
            page_low[span, columns(plane, r)] = block.astype(BF16)
        lines.make(("swap", i), page_low.at[span], swapped.at[span], swap)

        @pl.when(jnp.logical_not(native))
        def _():
            lines.open["swap", i].start()

    for r in range(PLANES):
        gain_one[:, columns(plane, r)] = gain[:, r * BLOCK : (r + 1) * BLOCK]
    near_sums = sum(dot(part, near_hot[...], NT) for part in split_bf16(diag_near[...]))
    cell_sums = sum(dot(part, cell_hot[...], NT) for part in split_bf16(diag_cell[...]))
    for k in range(RING):
        small[k, 0:2, :] = near_sums[2 * k : 2 * k + 2, :]
        for axis in range(2):
            first = axis * 2 * RING + 2 * k
            small[k, 2 * axis + 2 : 2 * axis + 4, :] = cell_sums[first : first + 2, :]
        small[k, 6:8, :] = jnp.zeros((2, HALF), F32)
        for j in range(8):
            lanes = slice(j * HALF, (j + 1) * HALF)
            small[k, 8 + j : 9 + j, :] = gain_one[:, lanes]
            small[k, 16 + j : 17 + j, :] = gain_two[:, lanes]
    for k in range(1, RING):
        lines.start(("small", k), small.at[k], small_ring.at[k], device(plane, core, (ring + k) % RING))
    att[2].last()
    att[1].middle()
    att[3].middle()
    for k in range(1, RING):
        lines.arrived(("small", k))
    small_plane[0] = small[0] + (small_ring[1] + (small_ring[2] + small_ring[3]))
    lines.start("smallx", small_plane.at[0], small_plane.at[1], device(plane ^ 1, core, ring))
    att[1].last()
    att[0].middle()
    lines.arrived("smallx")
    small_plane[2] = small_plane[0] + small_plane[1]
    lines.start("smally", small_plane.at[2], small_plane.at[3], device(plane ^ 2, core, ring))
    att[3].last()
    lines.arrived("smally")
    small_core[0] = small_plane[2] + small_plane[3]
    lines.start("smallc", small_core.at[0], small_core.at[1], partner)
    att[0].last()

    mine, other = sum_ring(lines, "ffn", ffn_late, ffn_same, ffn_cross)
    rest = inner_grad.shape[1] - UNITS
    first_core = jnp.where(core == 0, mine, other)
    second_core = jnp.where(core == 0, other, mine)
    for m in range(2):
        at = (m + 1) * UNITS
        inner_grad[m, 0:UNITS, :] = first_core[:, at : at + UNITS].T
        inner_grad[m, UNITS : UNITS + rest, :] = second_core[:, at : at + UNITS].T[0:rest]
    outer_grad[0:UNITS, :] = first_core[:, 0:UNITS].T
    outer_grad[UNITS : UNITS + rest, :] = second_core[:, 0:UNITS].T[0:rest]

    @pl.when(jnp.logical_not(native))
    def _():
        lines.arrived(("swap", 0), ("swap", 1))
        tokens_grad[...] = swapped[...].astype(F32)

    mine, other = sum_ring(lines, "att", att_late, att_same, att_cross)
    first_core = jnp.where(core == 0, mine, other)
    second_core = jnp.where(core == 0, other, mine)
    for m in range(3):
        lanes = slice((m + 1) * HALF, (m + 2) * HALF)
        qkv_grad[m, :, 0:HALF] = first_core[:, lanes]
        qkv_grad[m, :, HALF : 2 * HALF] = second_core[:, lanes]
    out_grad[0:HALF, :] = first_core[:, 0:HALF].T
    out_grad[HALF : 2 * HALF, :] = second_core[:, 0:HALF].T

    lines.arrived("smallc")
    low_core = jnp.where(core == 0, small_core[0], small_core[1])
    high_core = jnp.where(core == 0, small_core[1], small_core[0])
    small_out[0] = low_core
    small_out[1] = high_core

    @pl.when(jnp.logical_not(native))
    def _():
        lines.arrived("layer")
        lines.sent("layer", ("swap", 0), ("swap", 1))

    lines.sent(*[name for name in lines.open if name != "layer" and name[0] != "swap"])


def backward(low, low_t, normed_t, half_grad, full, gains_here, qkv, context, inverse, cells_t, cells_twice, cell_tail, gain_two, ffn_first, att_full, prob_full, ffn_grads, page_out, units):
    length, features = low.shape
    rows = length // 2
    whole = pl.BlockSpec(memory_space=pltpu.VMEM)
    outside = pl.BlockSpec(memory_space=pl.ANY)
    args = [low, low_t, normed_t, half_grad, full, gains_here, qkv, context, inverse]
    args += [cells_t, cells_twice, cell_tail, hot(REL_REACH, 4 * HALF), hot(CELLS, HALF), gain_two, ffn_first]
    args += [att_full, prob_full, ffn_grads, page_out]

    def buffers(width):
        return [
            pltpu.VMEM((RING, 2, HALF, width), BF16),
            pltpu.VMEM((RING, 2, HALF, width), BF16),
            pltpu.VMEM((RING, 2, HALF, width), BF16),
            pltpu.VMEM((RING - 1, HALF, width), BF16),
            pltpu.VMEM((RING, HALF, width), BF16),
        ]

    return pl.pallas_call(
        backward_kernel,
        out_shape=[
            shaped((rows, features)), shaped((rows, features), F32),
            shaped((3, HALF, 2 * HALF), F32), shaped((2 * HALF, HALF), F32),
            shaped((2, units, HALF), F32), shaped((units, HALF), F32), shaped((2, 24, HALF), F32),
        ],
        in_specs=[whole] * 16 + [outside] * 4,
        out_specs=[outside] + [whole] * 6,
        scratch_shapes=[
            pltpu.VMEM((2, features, ATT), BF16),
            pltpu.VMEM((2, length, length), BF16),
            pltpu.VMEM((length, HALF), F32),
            pltpu.VMEM((length, HALF), BF16),
            pltpu.VMEM((length, 2 * HALF), BF16),
            pltpu.VMEM((length, length), BF16),
            pltpu.VMEM((length, 3 * HALF), BF16),
            pltpu.VMEM((RING, features, ATT), BF16),
            pltpu.VMEM((length, features), F32),
            pltpu.VMEM((rows, features), BF16),
            pltpu.VMEM((rows, features), BF16),
            pltpu.VMEM((rows, features), BF16),
            pltpu.VMEM((rows, features), BF16),
            pltpu.VMEM((rows, features), BF16),
            pltpu.VMEM((2, 2 * BLOCK, FFW), BF16),
            *buffers(ATT),
            *buffers(FFW),
            pltpu.VMEM((2 * RING, 4 * HALF), F32),
            pltpu.VMEM((4 * RING, HALF), F32),
            pltpu.VMEM((1, features), F32),
            pltpu.VMEM((RING, 24, HALF), F32),
            pltpu.VMEM((RING, 24, HALF), F32),
            pltpu.VMEM((4, 24, HALF), F32),
            pltpu.VMEM((2, 24, HALF), F32),
            pltpu.SemaphoreType.DMA((80,)),
            pltpu.SemaphoreType.DMA((80,)),
            pltpu.SemaphoreType.DMA((9,)),
        ],
        name="backward",
        cost_estimate=pl.CostEstimate(flops=3 * 10**10, bytes_accessed=10**8, transcendentals=0),
        compiler_params=pltpu.CompilerParams(
            vmem_limit_bytes=63 * 1024 * 1024, collective_id=2, has_side_effects=True
        ),
    )(*args)


def page_body(
    tokens,
    norm_gains,
    attn_qkv,
    attn_out,
    ffn_in,
    ffn_out,
    position_tables,
    page_counts,
    layout_cells,
    cotangent,
):
    group, ring = lax.axis_index("dp"), lax.axis_index("tensor")
    (
        att_full, ffn_full, prob, full, gains_here, normed_one_t, resid, normed_two, normed_two_t,
        cot, cot_t, qkv, context, inverse, cells_t, cells_twice, cell_tail,
    ) = forward(
        tokens, cotangent, norm_gains, attn_qkv, attn_out, ffn_in.transpose(0, 2, 1), ffn_out, position_tables,
        page_counts, layout_cells,
    )
    _, ffn_grads, low, low_t, half_grad, page_out, gain_two, ffn_first = middle(
        normed_two, normed_two_t, cot, cot_t, resid, gains_here, ffn_full
    )
    page_got, tokens_grad, qkv_grad, out_grad, inner_grad, outer_grad, small = backward(
        low, low_t, normed_one_t, half_grad, full, gains_here, qkv, context, inverse, cells_t,
        cells_twice, cell_tail, gain_two, ffn_first, att_full, prob, ffn_grads, page_out, ffn_in.shape[2],
    )
    layer_out = jnp.where(group % CORES == ring % 2, page_out, page_got)
    gains = (small[0, 8:] + small[1, 8:]).reshape(2, 1024)
    gains_grad = lax.dynamic_slice_in_dim(gains, (group * RING + ring) * 32, 32, axis=1)
    tables = small[:, 0:6, :BUCKETS].reshape(CORES, 3, 2, BUCKETS).transpose(1, 3, 0, 2)
    tables = tables.reshape(3, BUCKETS, 2 * CORES)
    tables_grad = lax.dynamic_slice_in_dim(tables, group * 4, 4, axis=1)
    return (
        layer_out,
        tokens_grad,
        gains_grad,
        qkv_grad,
        out_grad,
        inner_grad.transpose(0, 2, 1),
        outer_grad,
        tables_grad,
    )


def solution(mesh):
    return jax.shard_map(
        page_body if page_plan(mesh) else general_body,
        mesh=mesh,
        in_specs=(
            P(("dp", "tensor"), None),
            P(),
            P(None, None, "tensor"),
            P("tensor", None),
            P(None, None, "tensor"),
            P("tensor", None),
            P(None, None, "tensor"),
            P("dp"),
            P(None, "dp"),
            P(("dp", "tensor"), None),
        ),
        out_specs=(
            P(("dp", "tensor"), None),
            P(("dp", "tensor"), None),
            P(None, ("dp", "tensor")),
            P(None, "dp", "tensor"),
            P("tensor", "dp"),
            P(None, "dp", "tensor"),
            P("tensor", "dp"),
            P(None, "dp", "tensor"),
        ),
        check_vma=False,
    )
```
